32 devices in a mesh: seq: 8 (over y, x, core), head: 4 (over z).
Axes of the slice: x: 2, y: 2, z: 4, core: 2. Of those that a mesh axis runs over, the one named last changes fastest.
Arguments:
- tokens: bfloat16 [8192, 2048], P('seq'), may hold values from -6 to 6
- doc_lengths: int32 [12], replicated, may hold values from 1 to 4096, 8192 in all
- mixer_gain: float32 [2048], replicated, may hold values from 0.5 to 1.5
- query_weight: float32 [2048, 2048], P('seq', 'head'), may hold values from -0.125 to 0.125
- key_weight: float32 [2048, 2048], P('seq', 'head'), may hold values from -0.125 to 0.125
- value_weight: float32 [2048, 4096], P('seq', 'head'), may hold values from -0.125 to 0.125
- gate_weight: float32 [2048, 4096], P('seq', 'head'), may hold values from -0.125 to 0.125
- alpha_weight: float32 [2048, 16], P('seq', 'head'), may hold values from -0.125 to 0.125
- beta_weight: float32 [2048, 16], P('seq', 'head'), may hold values from -0.125 to 0.125
- decay_log: float32 [16], P('head'), may hold values from -6 to 0
- decay_bias: float32 [16], P('head'), may hold values from -4 to -1
- query_taps: float32 [4, 2048], P(None, 'head'), may hold values from -3 to 3
- key_taps: float32 [4, 2048], P(None, 'head'), may hold values from -3 to 3
- value_taps: float32 [4, 4096], P(None, 'head'), may hold values from -3 to 3
- head_gain: float32 [256], replicated, may hold values from 0.5 to 1.5
- output_weight: float32 [4096, 2048], P('head', 'seq'), may hold values from -0.09375 to 0.09375
- ffn_gain: float32 [2048], replicated, may hold values from 0.5 to 1.5
- ffn_gate: float32 [2048, 5632], P('seq', 'head'), may hold values from -0.125 to 0.125
- ffn_up: float32 [2048, 5632], P('seq', 'head'), may hold values from -0.125 to 0.125
- ffn_down: float32 [5632, 2048], P('head', 'seq'), may hold values from -0.078125 to 0.078125
- cotangent: bfloat16 [8192, 2048], P('seq'), may hold values from -6 to 6
Outputs:
- result: bfloat16 [8192, 2048], P('seq')
- tokens_grad: float32 [8192, 2048], P('seq')
- mixer_gain_grad: float32 [2048], replicated
- query_weight_grad: float32 [2048, 2048], P('seq', 'head')
- key_weight_grad: float32 [2048, 2048], P('seq', 'head')
- value_weight_grad: float32 [2048, 4096], P('seq', 'head')
- gate_weight_grad: float32 [2048, 4096], P('seq', 'head')
- alpha_weight_grad: float32 [2048, 16], P('seq', 'head')
- beta_weight_grad: float32 [2048, 16], P('seq', 'head')
- decay_log_grad: float32 [16], P('head')
- decay_bias_grad: float32 [16], P('head')
- query_taps_grad: float32 [4, 2048], P(None, 'head')
- key_taps_grad: float32 [4, 2048], P(None, 'head')
- value_taps_grad: float32 [4, 4096], P(None, 'head')
- head_gain_grad: float32 [256], replicated
- output_weight_grad: float32 [4096, 2048], P('head', 'seq')
- ffn_gain_grad: float32 [2048], replicated
- ffn_gate_grad: float32 [2048, 5632], P('seq', 'head')
- ffn_up_grad: float32 [2048, 5632], P('seq', 'head')
- ffn_down_grad: float32 [5632, 2048], P('head', 'seq')
The draws below stay inside these ranges and needn't reach their ends.
Inputs may be any that keep to these rules, and one draw needn't show every extreme that they name: `doc_lengths`: the 12 documents fill the stream in order; the longest has exactly 4096 tokens.
All inputs are finite; a program needn't handle non-finite values.
Results may differ from the reference program's by a relative error of at most 0.023.
Values may be sent and summed in bfloat16 or wider, within the bound.
A program may use at most 320 MiB of HBM per device.

```python
import math
import jax
import jax.numpy as jnp
import numpy as np
from jax import lax

D = 2048
HEADS = 16
DK = 128
DV = 256
FF = 5632
CONV = 4
GROUP = 64
TOKENS = 8192
KEYS = 2048
VALS = 4096
DOCS = 12
DOC_MOST = 4096


def strengthened(values, stream_key, source, target, parts, factor):
    def block_of(position):
        return (jnp.arange(values.shape[position]) // (values.shape[position] // parts)).reshape((-1,) + (1,) * (values.ndim - 1 - position))

    near = jax.random.permutation(stream_key, parts)[block_of(target)]
    other_side = (block_of(target) + parts // 2) % parts
    return jnp.where((block_of(source) == near) | (block_of(source) == other_side), factor * values, values)


def level_of(rng, shape, split, smallest, top_value):
    def one(axis_at, shards_of):
        draws = jax.random.uniform(jax.random.fold_in(jax.random.fold_in(rng, 6), axis_at), (shards_of,), jnp.float32, smallest / len(split), top_value / len(split))
        return jnp.repeat(jnp.exp(draws), shape[axis_at] // shards_of).reshape((-1,) + (1,) * (len(shape) - axis_at - 1))

    factor_of = one(*split[0])
    for cut in split[1:]:
        factor_of = factor_of * one(*cut)
    return factor_of


def split_up(number_of, total, limit, lean):
    weights = [(1 << 20) // math.isqrt(grade ** lean) + 1 for grade in range(2, number_of + 1)]
    spare, holding = total - limit - (number_of - 1), [1] * (number_of - 1)
    while spare > 0:
        free = [i for i in range(number_of - 1) if holding[i] < limit]
        pool, budget = sum([weights[i] for i in free]), spare
        for i in free:
            extra = min(limit - holding[i], max(1, budget * weights[i] // pool), spare)
            holding[i] = holding[i] + extra
            spare = spare - extra
    return np.array([limit] + holding)


def ragged(rng, count, total, most, slope):
    if count == 2:
        one = jax.random.randint(rng, (), max(1, total - most), min(most, total - 1) + 1)
        return jnp.stack([one, total - one])
    sizes = jnp.asarray(split_up(count, total, most, slope), jnp.int32)
    twos = (count - 1) // 2
    source_of, sink = sizes[1:1 + 2 * twos:2], sizes[2:2 + 2 * twos:2]
    room = jnp.minimum(source_of - 1, most - sink)
    shifted = jax.random.randint(jax.random.fold_in(rng, 1), (twos,), 0, 1 << 20) % (room + 1)
    sizes = sizes.at[1:1 + 2 * twos:2].set(source_of - shifted).at[2:2 + 2 * twos:2].set(sink + shifted)
    return sizes[jax.random.permutation(jax.random.fold_in(rng, 2), count)]


def centred(own_key, dims, spread, most, pieces=(), held_as=jnp.bfloat16):
    drawn = spread * jax.random.normal(own_key, dims, jnp.float32)
    if pieces:
        drawn = drawn * level_of(own_key, dims, pieces, -0.22, 0.18)
    return jnp.clip(drawn, -most, most).astype(held_as)


def heavy_noise(own_key, dims, spread, bound, cuts, heavy, kind=jnp.bfloat16):
    values = spread * jax.random.normal(own_key, dims, jnp.float32)
    if cuts:
        values = values * level_of(own_key, dims, cuts, -0.22, 0.18)
    return jnp.clip(strengthened(values, jax.random.fold_in(own_key, 3), *heavy), -bound, bound).astype(kind)


def setup_inputs(seed: int = 0) -> dict:
    key_list = jax.random.split(jax.random.key(seed), 22)
    return {
        "tokens": centred(key_list[0], (TOKENS, D), 1.0, 6.0, ((0, 8),)),
        "doc_lengths": ragged(key_list[1], DOCS, TOKENS, DOC_MOST, 2).astype(jnp.int32),
        "mixer_gain": jnp.clip(1.0 + 0.1 * jax.random.normal(key_list[2], (D,), jnp.float32), 0.5, 1.5),
        "query_weight": centred(key_list[3], (D, KEYS), D ** -0.5, 0.125, ((0, 8), (1, 4)), jnp.float32),
        "key_weight": centred(key_list[4], (D, KEYS), D ** -0.5, 0.125, ((0, 8), (1, 4)), jnp.float32),
        "value_weight": centred(key_list[5], (D, VALS), D ** -0.5, 0.125, ((0, 8), (1, 4)), jnp.float32),
        "gate_weight": centred(key_list[6], (D, VALS), D ** -0.5, 0.125, ((0, 8), (1, 4)), jnp.float32),
        "alpha_weight": centred(key_list[7], (D, HEADS), D ** -0.5, 0.125, ((0, 8), (1, 4)), jnp.float32),
        "beta_weight": centred(key_list[8], (D, HEADS), D ** -0.5, 0.125, ((0, 8), (1, 4)), jnp.float32),
        "decay_log": jnp.clip(-6.0 + 6.0 * jax.random.uniform(key_list[9], (HEADS,), jnp.float32) ** level_of(key_list[9], (HEADS,), ((0, 4),), -0.2, 0.2), -6.0, 0.0),
        "decay_bias": jnp.clip(-4.0 + 3.0 * jax.random.uniform(key_list[10], (HEADS,), jnp.float32) ** level_of(key_list[10], (HEADS,), ((0, 4),), -0.2, 0.2), -4.0, -1.0),
        "query_taps": centred(key_list[11], (CONV, KEYS), 0.5, 3.0, ((1, 4),), jnp.float32),
        "key_taps": centred(key_list[12], (CONV, KEYS), 0.5, 3.0, ((1, 4),), jnp.float32),
        "value_taps": centred(key_list[13], (CONV, VALS), 0.5, 3.0, ((1, 4),), jnp.float32),
        "head_gain": jnp.clip(1.0 + 0.1 * jax.random.normal(key_list[14], (DV,), jnp.float32), 0.5, 1.5),
        "output_weight": centred(key_list[15], (VALS, D), VALS ** -0.5, 0.09375, ((0, 4), (1, 8)), jnp.float32),
        "ffn_gain": jnp.clip(1.0 + 0.1 * jax.random.normal(key_list[16], (D,), jnp.float32), 0.5, 1.5),
        "ffn_gate": centred(key_list[17], (D, FF), D ** -0.5, 0.125, ((0, 8), (1, 4)), jnp.float32),
        "ffn_up": centred(key_list[18], (D, FF), D ** -0.5, 0.125, ((0, 8), (1, 4)), jnp.float32),
        "ffn_down": centred(key_list[19], (FF, D), FF ** -0.5, 0.078125, ((0, 4), (1, 8)), jnp.float32),
        "cotangent": heavy_noise(key_list[20], (TOKENS, D), 1.0, 6.0, ((0, 8),), (0, 1, 8, 2.0)),
    }


highest = lax.Precision.HIGHEST

@jax.custom_vjp
def low(v):
    return lax.optimization_barrier(v.astype(jnp.bfloat16)).astype(jnp.float32)

@jax.custom_vjp
def low_back(v):
    return v

def low_keep(v):
    return (low(v), None)

def low_pass(kept, grad):
    return (grad,)

def back_keep(v):
    return (v, None)

def back_low(kept, grad):
    return (low(grad),)
low.defvjp(low_keep, low_pass)
low_back.defvjp(back_keep, back_low)

def group_step(carry, blocks):
    state_now, seg_prev = carry
    queries, key_rows, values, log_decay, beta_gate, segment = blocks
    block_size = segment.shape[0]
    cum_decay = jnp.cumsum(log_decay, axis=-1)
    same_doc = segment[:, None] == segment[None, :]
    row_index = lax.broadcasted_iota(jnp.int32, (block_size, block_size), 0)
    col_index = lax.broadcasted_iota(jnp.int32, (block_size, block_size), 1)
    lower_mask = same_doc & (row_index >= col_index)
    strict_mask = same_doc & (row_index > col_index)
    decay_gap = cum_decay[:, :, None] - cum_decay[:, None, :]
    decay_lower = jnp.where(lower_mask, jnp.exp(jnp.where(lower_mask, decay_gap, 0.0)), 0.0)
    decay_strict = jnp.where(strict_mask, decay_lower, 0.0)
    alive_mask = (segment == seg_prev).astype(jnp.float32)
    from_start = jnp.exp(cum_decay) * alive_mask
    key_gram = jnp.einsum('hid,hjd->hij', key_rows, key_rows, precision=highest)
    power_term = -beta_gate[:, :, None] * decay_strict * key_gram
    inverse = jnp.eye(block_size, dtype=jnp.float32) + power_term
    for repeat in range((block_size - 1).bit_length() - 1):
        power_term = jnp.einsum('hij,hjk->hik', power_term, power_term, precision=highest)
        inverse = inverse + jnp.einsum('hij,hjk->hik', inverse, power_term, precision=highest)
    key_state = jnp.einsum('hid,hdv->hiv', key_rows, state_now, precision=highest)
    target = beta_gate[:, :, None] * (values - from_start[:, :, None] * key_state)
    delta_rows = jnp.einsum('hij,hjv->hiv', inverse, target, precision=highest)
    query_key = jnp.einsum('hid,hjd->hij', queries, key_rows, precision=highest)
    query_state = jnp.einsum('hid,hdv->hiv', queries, state_now, precision=highest)
    output = from_start[:, :, None] * query_state + jnp.einsum('hij,hjv->hiv', decay_lower * query_key, delta_rows, precision=highest)
    last_same = (segment == segment[-1])[None, :]
    to_end = jnp.where(last_same, jnp.exp(jnp.where(last_same, cum_decay[:, -1:] - cum_decay, 0.0)), 0.0)
    carried = jnp.exp(cum_decay[:, -1]) * alive_mask[-1]
    state_next = carried[:, None, None] * state_now + jnp.einsum('hjd,hjv->hdv', key_rows * to_end[:, :, None], delta_rows, precision=highest)
    return ((state_next, segment[-1]), output)

def run_groups(state_now, seg_prev, queries, key_rows, values, log_decay, beta_gate, segment, block_size):
    head_count, length = log_decay.shape
    block_count = length // block_size

    def splitter(array):
        shaped = array.reshape((head_count, block_count, block_size) + array.shape[2:])
        return jnp.moveaxis(shaped, 1, 0)
    blocks = (splitter(queries), splitter(key_rows), splitter(values), splitter(log_decay), splitter(beta_gate), segment.reshape(block_count, block_size))
    (state_end, seg_end), outputs = lax.scan(jax.checkpoint(group_step), (state_now, seg_prev), blocks)
    return (jnp.moveaxis(outputs, 0, 1).reshape(head_count, length, -1), state_end)

def rms_scale(array, epsilon):
    return lax.rsqrt(lax.optimization_barrier(jnp.mean(array * array, axis=-1, keepdims=True)) + epsilon)

def unit_rows(array):
    return array * lax.rsqrt(lax.optimization_barrier(jnp.sum(array * array, axis=-1, keepdims=True)) + 1e-06)

def conv_silu(extended, seg_ext, taps):
    reach = taps.shape[0]
    length = extended.shape[0] - reach + 1
    total = jnp.zeros((length, extended.shape[1]), jnp.float32)
    for offset in range(reach):
        match = (seg_ext[offset:offset + length] == seg_ext[reach - 1:]).astype(jnp.float32)
        total = total + taps[offset] * extended[offset:offset + length] * match[:, None]
    return jax.nn.silu(total)

def mixer_inputs(ext_query, ext_key, ext_value, query_taps, key_taps, value_taps, alpha_pre, beta_pre, decay_log, decay_bias, seg_ext):
    head_count = alpha_pre.shape[1]
    conv_query = conv_silu(ext_query, seg_ext, query_taps)
    length = conv_query.shape[0]
    queries = unit_rows(conv_query.reshape(length, head_count, -1))
    key_rows = unit_rows(conv_silu(ext_key, seg_ext, key_taps).reshape(length, head_count, -1))
    values = conv_silu(ext_value, seg_ext, value_taps).reshape(length, head_count, -1)
    log_decay = -jnp.exp(decay_log) * jax.nn.softplus(alpha_pre + decay_bias)
    beta_gate = jax.nn.sigmoid(beta_pre)
    return (jnp.swapaxes(queries, 0, 1), jnp.swapaxes(key_rows, 0, 1), jnp.swapaxes(values, 0, 1), log_decay.T, beta_gate.T)

def head_gate(mixed, gate_pre, head_gain):
    per_token = jnp.swapaxes(mixed, 0, 1)
    length = per_token.shape[0]
    head_count = per_token.shape[1]
    normed = per_token * rms_scale(per_token, 1e-05)
    gate_act = jax.nn.silu(gate_pre.reshape(length, head_count, -1))
    return (normed * head_gain * gate_act).reshape(length, -1)

def matmul(left, right):
    return jnp.dot(left, right, precision=highest, preferred_element_type=jnp.float32)

def forward(stream, mixer_gain, query_weight, key_weight, value_weight, gate_weight, alpha_weight, beta_weight, decay_log, decay_bias, query_taps, key_taps, value_taps, head_gain, output_weight, ffn_gain, ffn_gate, ffn_up, ffn_down, segment, seg_ext):
    first_in = low(stream * rms_scale(stream, 1e-06) * mixer_gain)
    pre_query = low_back(low(matmul(first_in, low(query_weight))))
    pre_key = low_back(low(matmul(first_in, low(key_weight))))
    pre_value = low_back(low(matmul(first_in, low(value_weight))))
    gate_pre = low_back(matmul(first_in, low(gate_weight)))
    alpha_pre = low_back(matmul(first_in, low(alpha_weight)))
    beta_pre = low_back(matmul(first_in, low(beta_weight)))
    reach = query_taps.shape[0]
    ext_query = jnp.concatenate([jnp.zeros((reach - 1, pre_query.shape[1]), jnp.float32), pre_query], axis=0)
    ext_key = jnp.concatenate([jnp.zeros((reach - 1, pre_key.shape[1]), jnp.float32), pre_key], axis=0)
    ext_value = jnp.concatenate([jnp.zeros((reach - 1, pre_value.shape[1]), jnp.float32), pre_value], axis=0)
    queries, key_rows, values, log_decay, beta_gate = mixer_inputs(ext_query, ext_key, ext_value, query_taps, key_taps, value_taps, alpha_pre, beta_pre, decay_log, decay_bias, seg_ext)
    head_count = log_decay.shape[0]
    state_zero = jnp.zeros((head_count, DK, DV), jnp.float32)
    mixed, state_end = run_groups(state_zero, jnp.zeros((), jnp.int32), queries, key_rows, values, log_decay, beta_gate, segment, GROUP)
    mix_out = low(head_gate(mixed, gate_pre, head_gain))
    middle = stream + low_back(matmul(mix_out, low(output_weight)))
    second_in = low(middle * rms_scale(middle, 1e-06) * ffn_gain)
    gate_act = low_back(matmul(second_in, low(ffn_gate)))
    lift_act = low_back(matmul(second_in, low(ffn_up)))
    hidden = low(jax.nn.silu(gate_act) * lift_act)
    return middle + low_back(matmul(hidden, low(ffn_down)))

def reference(tokens, doc_lengths, mixer_gain, query_weight, key_weight, value_weight, gate_weight, alpha_weight, beta_weight, decay_log, decay_bias, query_taps, key_taps, value_taps, head_gain, output_weight, ffn_gain, ffn_gate, ffn_up, ffn_down, cotangent):
    stream = tokens.astype(jnp.float32)
    starts = jnp.cumsum(doc_lengths, dtype=jnp.int32) - doc_lengths
    positions = jnp.arange(1 - CONV, TOKENS, dtype=jnp.int32)
    seg_ext = lax.optimization_barrier(jnp.sum((starts[None, :] <= positions[:, None]).astype(jnp.int32), axis=1, dtype=jnp.int32))
    segment = seg_ext[CONV - 1:]

    def closed(*inputs):
        return forward(*inputs, segment, seg_ext)
    result, backward = jax.vjp(closed, stream, mixer_gain, query_weight, key_weight, value_weight, gate_weight, alpha_weight, beta_weight, decay_log, decay_bias, query_taps, key_taps, value_taps, head_gain, output_weight, ffn_gain, ffn_gate, ffn_up, ffn_down)
    grads = backward(cotangent.astype(jnp.float32))
    return (result.astype(jnp.bfloat16), grads[0], grads[1], grads[2], grads[3], grads[4], grads[5], grads[6], grads[7], grads[8], grads[9], grads[10], grads[11], grads[12], grads[13], grads[14], grads[15], grads[16], grads[17], grads[18])
```

```python
from functools import partial

import jax
import jax.numpy as jnp
from jax import lax
from jax.experimental import pallas as pl
from jax.experimental.pallas import tpu as pltpu
from jax.sharding import PartitionSpec as P

BLOCK = 128
LANES = 128
low = jnp.bfloat16
full = jnp.float32
MIB = 1 << 20


def mm(a, b):
    return jnp.dot(a.astype(low), b.astype(low), preferred_element_type=full)


def mm_nt(a, b):
    return lax.dot_general(
        a.astype(low), b.astype(low), (((1,), (1,)), ((), ())), preferred_element_type=full
    )


def mm_tn(a, b):
    return lax.dot_general(
        a.astype(low), b.astype(low), (((0,), (0,)), ((), ())), preferred_element_type=full
    )


def exact(a, b):
    return jnp.dot(a, b, precision=lax.Precision.HIGHEST, preferred_element_type=full)


def sigmoid(t):
    return 1.0 / (1.0 + jnp.exp(-t))


def softplus(t):
    return jnp.maximum(t, 0.0) + jnp.log(1.0 + jnp.exp(-jnp.abs(t)))


def iotas(size):
    return (
        lax.broadcasted_iota(jnp.int32, (size, size), 0),
        lax.broadcasted_iota(jnp.int32, (size, size), 1),
    )


def conv_sum(ext, taps, meta, first, width, rows):
    total = taps[3:4, first : first + width] * ext[8 : 8 + rows, first : first + width]
    for lag in (1, 2, 3):
        total += (
            taps[3 - lag : 4 - lag, first : first + width]
            * meta[:, lag : lag + 1]
            * ext[8 - lag : 8 - lag + rows, first : first + width]
        )
    return total


def gates(ab, params, heads):
    log_decay = params[0:1, :] * softplus(ab + params[1:2, :])
    beta = sigmoid(ab)
    return log_decay, beta


def decay_parts(cum, cum_t, h, same_low, strict_low, meta):
    size = cum.shape[0]
    col = cum[:, h : h + 1]
    row = cum_t[h : h + 1, :]
    lower = jnp.where(same_low, jnp.exp(jnp.minimum(col - row, 0.0)), 0.0)
    strict = jnp.where(strict_low, lower, 0.0)
    last = cum[size - 1 : size, h : h + 1]
    from_start = jnp.exp(col) * meta[:, 4:5]
    to_end = jnp.exp(last - col) * meta[:, 5:6]
    carried = jnp.exp(last) * meta[size - 1 : size, 4:5]
    return lower, strict, from_start, to_end, carried


def unit_lower_inverse(strict, rows, cols):
    size = strict.shape[0]
    power = jnp.where((rows >> 3) == (cols >> 3), -strict, 0.0)
    inverse = jnp.where(rows == cols, 1.0, power)
    power = mm(power, power)
    inverse = inverse + mm(inverse, power)
    power = mm(power, power)
    inverse = inverse + mm(inverse, power)
    shift = 3
    while (1 << shift) < size:
        off = jnp.where(
            ((rows >> (shift + 1)) == (cols >> (shift + 1))) & ((rows >> shift) != (cols >> shift)),
            strict,
            0.0,
        )
        inverse = inverse - mm(inverse, mm(off, inverse))
        shift += 1
    return inverse


def inverses(stricts, rows, cols):
    size = stricts[0].shape[0]
    near = (rows >> 3) == (cols >> 3)
    powers = [jnp.where(near, -a, 0.0) for a in stricts]
    result = [jnp.where(rows == cols, 1.0, p) for p in powers]
    for _ in range(2):
        powers = [mm(p, p) for p in powers]
        result = [t + mm(t, p) for t, p in zip(result, powers)]
    shift = 3
    while (1 << shift) < size:
        pick = ((rows >> (shift + 1)) == (cols >> (shift + 1))) & (
            (rows >> shift) != (cols >> shift)
        )
        offs = [mm(jnp.where(pick, a, 0.0), t) for a, t in zip(stricts, result)]
        result = [t - mm(t, o) for t, o in zip(result, offs)]
        shift += 1
    return result


def masks(meta, segrow):
    size = meta.shape[0]
    rows, cols = iotas(size)
    same = meta[:, 0:1] == segrow[0:1, :]
    return rows, cols, same & (rows >= cols), same & (rows > cols)


def unit(post):
    return lax.rsqrt(jnp.sum(post * post, axis=-1, keepdims=True) + 1e-06)


def forward_kernel(
    heads, key, value,
    pre_ref, ab_ref, meta_ref, segrow_ref, edge_ref, taps_ref, params_ref,
    out_ref, through_ref, states_ref, inverse_ref, end_ref,
    ext, state,
):
    step = pl.program_id(0)
    size = pre_ref.shape[0]
    wide = value + key
    kfirst, vfirst = heads * key, 2 * heads * key

    @pl.when(step == 0)
    def _():
        ext[0:8, :] = edge_ref[...].astype(full)
        rows, cols = iotas(key)
        eye = (rows == cols).astype(full)
        for h in range(heads):
            state[h, :, :value] = jnp.zeros((key, value), full)
            state[h, :, value:] = eye

    @pl.when(step > 0)
    def _():
        ext[0:8, :] = ext[size : size + 8, :]

    ext[8:, :] = pre_ref[...].astype(full)
    meta = meta_ref[...]
    log_decay, beta = gates(ab_ref[...], params_ref, heads)
    rows, cols, same_low, strict_low = masks(meta, segrow_ref)
    cum = exact((rows >= cols).astype(full), log_decay)
    cum_t = cum.T
    qs, ks, vs, lowers, stricts, fs, es, cs = [], [], [], [], [], [], [], []
    for h in range(heads):
        u = conv_sum(ext, taps_ref, meta, h * key, key, size)
        post = u * sigmoid(u)
        q = (post * unit(post)).astype(low)
        u = conv_sum(ext, taps_ref, meta, kfirst + h * key, key, size)
        post = u * sigmoid(u)
        k = (post * unit(post)).astype(low)
        u = conv_sum(ext, taps_ref, meta, vfirst + h * value, value, size)
        v = u * sigmoid(u)
        lower, strict, f, e, c = decay_parts(cum, cum_t, h, same_low, strict_low, meta)
        bcol = beta[:, heads + h : heads + h + 1]
        gram = mm_nt(jnp.concatenate([k, q], axis=0), k)
        qs.append(q), ks.append(k), vs.append(v), fs.append(f), es.append(e), cs.append(c)
        stricts.append(bcol * strict * gram[:size])
        lowers.append(lower * gram[size:])
    ts = inverses(stricts, rows, cols)
    for h in range(heads):
        bcol = beta[:, heads + h : heads + h + 1]
        s = state[h]
        states_ref[0, h] = s.astype(low)
        t = ts[h].astype(low)
        inverse_ref[0, h] = t
        ks_s = mm(ks[h], s)
        fb = fs[h] * bcol
        target = jnp.concatenate(
            [bcol * vs[h] - fb * ks_s[:, :value], -fb * ks_s[:, value:]], axis=1
        )
        delta = mm(t, target).astype(low)
        left = jnp.concatenate([(fs[h] * qs[h].astype(full)).astype(low), lowers[h].astype(low)], axis=1)
        out = mm(left, jnp.concatenate([s.astype(low), delta], axis=0))
        out_ref[:, h * value : (h + 1) * value] = out[:, :value]
        through_ref[:, h * key : (h + 1) * key] = out[:, value:].astype(low)
        ke = es[h] * ks[h].astype(full)
        s = cs[h] * s + mm_tn(ke, delta)
        state[h] = s
        end_ref[h] = s.astype(low)


def forward_chain(pre, ab, meta, segrow, edge, taps, params, heads, key, value):
    length = pre.shape[0]
    blocks = length // BLOCK
    width = pre.shape[1]
    wide = value + key
    return pl.pallas_call(
        partial(forward_kernel, heads, key, value),
        grid=(blocks,),
        in_specs=[
            pl.BlockSpec((BLOCK, width), lambda n: (n, 0)),
            pl.BlockSpec((BLOCK, LANES), lambda n: (n, 0)),
            pl.BlockSpec((BLOCK, LANES), lambda n: (n, 0)),
            pl.BlockSpec((8, BLOCK), lambda n: (0, n)),
            pl.BlockSpec((8, width), lambda n: (0, 0)),
            pl.BlockSpec(taps.shape, lambda n: (0, 0)),
            pl.BlockSpec((8, LANES), lambda n: (0, 0)),
        ],
        out_specs=[
            pl.BlockSpec((BLOCK, heads * value), lambda n: (n, 0)),
            pl.BlockSpec((BLOCK, heads * key), lambda n: (n, 0)),
            pl.BlockSpec((1, heads, key, wide), lambda n: (n, 0, 0, 0)),
            pl.BlockSpec((1, heads, BLOCK, BLOCK), lambda n: (n, 0, 0, 0)),
            pl.BlockSpec((heads, key, wide), lambda n: (0, 0, 0)),
        ],
        out_shape=[
            jax.ShapeDtypeStruct((length, heads * value), full),
            jax.ShapeDtypeStruct((length, heads * key), low),
            jax.ShapeDtypeStruct((blocks, heads, key, wide), low),
            jax.ShapeDtypeStruct((blocks, heads, BLOCK, BLOCK), low),
            jax.ShapeDtypeStruct((heads, key, wide), low),
        ],
        scratch_shapes=[
            pltpu.VMEM((BLOCK + 8, width), full),
            pltpu.VMEM((heads, key, wide), full),
        ],
        compiler_params=pltpu.CompilerParams(vmem_limit_bytes=48 * MIB),
        name="chain_forward",
    )(pre, ab, meta, segrow, edge, taps, params)


def output_kernel(heads, key, value, place_ref, ends_ref, local_ref, through_ref, gate_ref, gain_ref,
                  y_ref, mixed_ref, state_ref):
    @pl.when(pl.program_id(0) == 0)
    def _():
        state_ref[...] = jnp.zeros_like(state_ref)

        def one(j, carry):
            for h in range(heads):
                part = ends_ref[j, h]
                state_ref[h] = (
                    mm(part[:, value:], state_ref[h]) + part[:, :value].astype(full)
                )
            return carry

        lax.fori_loop(0, place_ref[0], one, 0)

    for h in range(heads):
        cols = slice(h * value, (h + 1) * value)
        o = local_ref[:, cols] + mm(through_ref[:, h * key : (h + 1) * key], state_ref[h])
        mixed_ref[:, cols] = o.astype(mixed_ref.dtype)
        s3 = lax.rsqrt(jnp.mean(o * o, axis=-1, keepdims=True) + 1e-05)
        gz = gate_ref[:, cols]
        y_ref[:, cols] = (o * s3 * gain_ref[0:1, :] * (gz * sigmoid(gz))).astype(low)


def chain_output(place, ends, local, through, gate, gain, heads, key, value, rows=256):
    length, wide = local.shape
    return pl.pallas_call(
        partial(output_kernel, heads, key, value),
        grid=(length // rows,),
        in_specs=[
            pl.BlockSpec(memory_space=pltpu.SMEM),
            pl.BlockSpec(ends.shape, lambda n: (0, 0, 0, 0), pipeline_mode=pl.Buffered(1)),
            pl.BlockSpec((rows, wide), lambda n: (n, 0)),
            pl.BlockSpec((rows, heads * key), lambda n: (n, 0)),
            pl.BlockSpec((rows, wide), lambda n: (n, 0)),
            pl.BlockSpec((1, value), lambda n: (0, 0)),
        ],
        out_specs=[
            pl.BlockSpec((rows, wide), lambda n: (n, 0)),
            pl.BlockSpec((rows, wide), lambda n: (n, 0)),
            pl.BlockSpec((heads, key, value), lambda n: (0, 0, 0)),
        ],
        out_shape=[
            jax.ShapeDtypeStruct((length, wide), low),
            jax.ShapeDtypeStruct((length, wide), full),
            jax.ShapeDtypeStruct((heads, key, value), full),
        ],
        compiler_params=pltpu.CompilerParams(vmem_limit_bytes=48 * MIB),
        name="chain_output",
    )(place, ends, local, through, gate, gain)


def gate_back_kernel(heads, key, value, dy_ref, mixed_ref, gate_ref, gain_ref, through_ref,
                     dgz_ref, do_ref, gain_grad_ref, adjoint_ref):
    @pl.when(pl.program_id(0) == 0)
    def _():
        gain_grad_ref[...] = jnp.zeros_like(gain_grad_ref)
        adjoint_ref[...] = jnp.zeros_like(adjoint_ref)

    rows = dy_ref.shape[0]
    gain = gain_ref[0:1, :]
    for h in range(heads):
        cols = slice(h * value, (h + 1) * value)
        o = mixed_ref[:, cols].astype(full)
        s3 = lax.rsqrt(jnp.mean(o * o, axis=-1, keepdims=True) + 1e-05)
        n3 = o * s3
        gz = gate_ref[:, cols]
        sig = sigmoid(gz)
        sg = gz * sig
        dy = dy_ref[:, cols]
        dyn = dy * n3
        part = dyn * sg
        gain_grad_ref[...] += jnp.sum(part.reshape(rows // 8, 8, value), axis=0)
        dgz_ref[:, cols] = (dyn * gain * (sig * (1.0 + gz * (1.0 - sig)))).astype(low)
        dn3 = dy * gain * sg
        do = s3 * (dn3 - n3 * jnp.mean(dn3 * n3, axis=-1, keepdims=True))
        do = do.astype(low)
        do_ref[:, cols] = do
        adjoint_ref[h] += mm_tn(through_ref[:, h * key : (h + 1) * key], do)


def gate_back(dy, mixed, gate, gain, through, heads, key, value, rows=256):
    length, wide = dy.shape
    return pl.pallas_call(
        partial(gate_back_kernel, heads, key, value),
        grid=(length // rows,),
        in_specs=[
            pl.BlockSpec((rows, wide), lambda n: (n, 0)),
            pl.BlockSpec((rows, wide), lambda n: (n, 0)),
            pl.BlockSpec((rows, wide), lambda n: (n, 0)),
            pl.BlockSpec((1, value), lambda n: (0, 0)),
            pl.BlockSpec((rows, heads * key), lambda n: (n, 0)),
        ],
        out_specs=[
            pl.BlockSpec((rows, wide), lambda n: (n, 0)),
            pl.BlockSpec((rows, wide), lambda n: (n, 0)),
            pl.BlockSpec((8, value), lambda n: (0, 0)),
            pl.BlockSpec((heads, key, value), lambda n: (0, 0, 0)),
        ],
        out_shape=[
            jax.ShapeDtypeStruct((length, wide), low),
            jax.ShapeDtypeStruct((length, wide), low),
            jax.ShapeDtypeStruct((8, value), full),
            jax.ShapeDtypeStruct((heads, key, value), full),
        ],
        compiler_params=pltpu.CompilerParams(vmem_limit_bytes=48 * MIB),
        name="gate_back",
    )(dy, mixed, gate, gain, through)


def lane_sum(array):
    return jnp.sum(array, axis=-1, keepdims=True)


def backward_kernel(
    heads, key, value, devices,
    place_ref, pre_ref, tail_ref, ab_ref, meta_ref, segrow_ref, edge_ref, edge_meta_ref, taps_ref, params_ref,
    states_ref, inverse_ref, state_in_ref, do_ref, ends_ref, adjoints_ref,
    dpre_ref, dab_ref, halo_ref, taps_grad_ref, params_grad_ref,
    ext, du, adjoint,
):
    step = pl.program_id(0)
    steps = pl.num_programs(0)
    size = pre_ref.shape[0]
    kfirst, vfirst = heads * key, 2 * heads * key

    @pl.when(step == 0)
    def _():
        adjoint[...] = jnp.zeros_like(adjoint)

        def one(k, carry):
            j = devices - 1 - k
            for h in range(heads):
                adjoint[h] = (
                    mm_tn(ends_ref[j, h, :, value:], adjoint[h]) + adjoints_ref[j, h].astype(full)
                )
            return carry

        lax.fori_loop(0, devices - 1 - place_ref[0], one, 0)
        du[8 + size :, :] = jnp.zeros((8, du.shape[1]), full)
        taps_grad_ref[...] = jnp.zeros_like(taps_grad_ref)
        params_grad_ref[...] = jnp.zeros_like(params_grad_ref)

    @pl.when(step > 0)
    def _():
        du[8 + size :, :] = du[8:16, :]

    du[0:8, :] = jnp.zeros((8, du.shape[1]), full)

    @pl.when(step < steps - 1)
    def _():
        ext[0:8, :] = tail_ref[8:16, :].astype(full)

    @pl.when(step == steps - 1)
    def _():
        ext[0:8, :] = edge_ref[...].astype(full)

    ext[8:, :] = pre_ref[...].astype(full)
    meta = meta_ref[...]
    ab = ab_ref[...]
    log_decay, beta = gates(ab, params_ref, heads)
    rows, cols, same_low, strict_low = masks(meta, segrow_ref)
    cum = exact((rows >= cols).astype(full), log_decay)
    cum_t = cum.T
    lane = lax.broadcasted_iota(jnp.int32, (size, LANES), 1)
    row8 = lax.broadcasted_iota(jnp.int32, (8, size), 0)
    dcum = jnp.zeros((size, LANES), full)
    dcum_rows = jnp.zeros((8, size), full)
    dcum_last = jnp.zeros((1, LANES), full)
    dbeta = jnp.zeros((size, LANES), full)
    lane1 = lax.broadcasted_iota(jnp.int32, (1, LANES), 1)

    for h in range(heads):
        qcols = slice(h * key, (h + 1) * key)
        kcols = slice(kfirst + h * key, kfirst + (h + 1) * key)
        vcols = slice(vfirst + h * value, vfirst + (h + 1) * value)
        uq = conv_sum(ext, taps_ref, meta, h * key, key, size)
        sq = sigmoid(uq)
        pq = uq * sq
        rq = unit(pq)
        qf = pq * rq
        q = qf.astype(low)
        uk = conv_sum(ext, taps_ref, meta, kfirst + h * key, key, size)
        sk = sigmoid(uk)
        pk = uk * sk
        rk = unit(pk)
        kf = pk * rk
        k = kf.astype(low)
        uv = conv_sum(ext, taps_ref, meta, vfirst + h * value, value, size)
        sv = sigmoid(uv)
        v = uv * sv
        lower, strict, f, e, c = decay_parts(cum, cum_t, h, same_low, strict_low, meta)
        b = beta[:, heads + h : heads + h + 1]
        kq = jnp.concatenate([k, q], axis=0)
        gram = mm_nt(kq, k)
        kk, qk = gram[:size], gram[size:]
        stored = states_ref[0, h]
        s = stored[:, :value].astype(full) + mm(stored[:, value:], state_in_ref[h])
        slow = s.astype(low)
        kqs = mm(kq, slow)
        ks, qs = kqs[:size], kqs[size:]
        rest = v - f * ks
        t = inverse_ref[0, h]
        delta = mm(t, b * rest).astype(low)
        do = do_ref[:, h * value : (h + 1) * value]
        dof = do.astype(full)
        ds = adjoint[h]
        dslow = ds.astype(low)
        ke = (e * kf).astype(low)
        p = lower * qk
        left = jnp.concatenate([p.T.astype(low), ke], axis=1)
        ddelta = mm(left, jnp.concatenate([do, dslow], axis=0))
        dtarget = mm_tn(t, ddelta)
        outer = mm_nt(jnp.concatenate([do, dtarget.astype(low)], axis=0), delta)
        dp, dan = outer[:size], outer[size:]
        eg = lower * dp
        hn = -strict * dan
        hg = b * hn
        x = eg * qk
        hk = hn * kk
        g1 = (b * f) * dtarget
        fdo = f * dof
        pair = jnp.concatenate([fdo.astype(low), (-g1).astype(low)], axis=0)
        both = mm_nt(pair, slow)
        dq = both[:size] + mm(eg, k)
        dsk = e * mm_nt(delta, dslow)
        left = jnp.concatenate([(hg + hg.T).astype(low), eg.T.astype(low)], axis=1)
        dk = both[size:] + dsk + mm(left, kq)
        dv = b * dtarget
        z = lane_sum(kf * dsk)
        dfrom = lane_sum(dof * qs) - b * lane_sum(dtarget * ks)
        hrow = lane_sum(hk)
        db = hrow + lane_sum(dtarget * rest)
        dbeta = dbeta + jnp.where(lane == heads + h, db, 0.0)
        dcum = dcum + jnp.where(lane == h, lane_sum(x) + b * hrow + f * dfrom - z, 0.0)
        drow = jnp.sum(x + b * hk, axis=0, keepdims=True)
        dcum_rows = dcum_rows + jnp.where(row8 == h, drow, 0.0)
        dlast = jnp.sum(z, axis=0, keepdims=True) + c * jnp.sum(
            lane_sum(ds * s), axis=0, keepdims=True
        )
        dcum_last = dcum_last + jnp.where(lane1 == h, dlast, 0.0)
        adjoint[h] = c * ds + mm_tn(jnp.concatenate([q, k], axis=0), pair)

        dpq = rq * (dq - qf * lane_sum(dq * qf))
        du[8 : 8 + size, qcols] = dpq * (sq * (1.0 + uq * (1.0 - sq)))
        dpk = rk * (dk - kf * lane_sum(dk * kf))
        du[8 : 8 + size, kcols] = dpk * (sk * (1.0 + uk * (1.0 - sk)))
        du[8 : 8 + size, vcols] = dv * (sv * (1.0 + uv * (1.0 - sv)))

    padded = jnp.concatenate([dcum_rows, jnp.zeros((LANES - 8, size), full)], axis=0)
    rowi = lax.broadcasted_iota(jnp.int32, (size, LANES), 0)
    dcum = dcum - padded.T + jnp.where(rowi == size - 1, dcum_last, 0.0)
    dlog = exact((rows <= cols).astype(full), dcum)
    dga = dlog * params_ref[0:1, :] * sigmoid(ab + params_ref[1:2, :])
    is_decay = lane < heads
    dga = jnp.where(is_decay, dga, 0.0)
    params_grad_ref[0:8, :] += jnp.sum(dga.reshape(size // 8, 8, LANES), axis=0)
    decay_part = jnp.where(is_decay, dlog * log_decay, 0.0)
    params_grad_ref[8:16, :] += jnp.sum(decay_part.reshape(size // 8, 8, LANES), axis=0)
    dab_ref[...] = jnp.where(is_decay, dga, dbeta * beta * (1.0 - beta)).astype(low)

    width = du.shape[1]
    for first in range(0, width, 512):
        cs = slice(first, first + 512)
        own = du[8 : 8 + size, cs]
        total = taps_ref[3:4, cs] * own
        taps_grad_ref[24:32, cs] += jnp.sum(
            (own * ext[8 : 8 + size, cs]).reshape(size // 8, 8, 512), axis=0
        )
        for lag in (1, 2, 3):
            total += taps_ref[3 - lag : 4 - lag, cs] * meta[:, 5 + lag : 6 + lag] * du[
                8 + lag : 8 + lag + size, cs
            ]
            taps_grad_ref[8 * (3 - lag) : 8 * (4 - lag), cs] += jnp.sum(
                (own * meta[:, lag : lag + 1] * ext[8 - lag : 8 - lag + size, cs]).reshape(
                    size // 8, 8, 512
                ),
                axis=0,
            )
        dpre_ref[:, cs] = total.astype(low)

    @pl.when(step == steps - 1)
    def _():
        edge_meta = edge_meta_ref[...]
        halo = jnp.zeros(halo_ref.shape, full)
        for lag in (1, 2, 3):
            halo += taps_ref[3 - lag : 4 - lag, :] * edge_meta[:, 5 + lag : 6 + lag] * du[
                lag : 8 + lag, :
            ]
        halo_ref[...] = halo


def backward_chain(place, pre, ab, meta, segrow, edge, edge_meta, taps, params, states, inverse,
                   state_in, do, ends, adjoints, heads, key, value):
    length, width = pre.shape
    blocks = length // BLOCK
    wide = value + key
    once = dict(pipeline_mode=pl.Buffered(1))
    last = blocks - 1
    return pl.pallas_call(
        partial(backward_kernel, heads, key, value, ends.shape[0]),
        grid=(blocks,),
        in_specs=[
            pl.BlockSpec(memory_space=pltpu.SMEM),
            pl.BlockSpec((BLOCK, width), lambda n: (last - n, 0)),
            pl.BlockSpec((16, width), lambda n: (jnp.maximum((last - n) * (BLOCK // 16) - 1, 0), 0)),
            pl.BlockSpec((BLOCK, LANES), lambda n: (last - n, 0)),
            pl.BlockSpec((BLOCK, LANES), lambda n: (last - n, 0)),
            pl.BlockSpec((8, BLOCK), lambda n: (0, last - n)),
            pl.BlockSpec((8, width), lambda n: (0, 0)),
            pl.BlockSpec((8, LANES), lambda n: (0, 0)),
            pl.BlockSpec(taps.shape, lambda n: (0, 0)),
            pl.BlockSpec((8, LANES), lambda n: (0, 0)),
            pl.BlockSpec((1, heads, key, wide), lambda n: (last - n, 0, 0, 0)),
            pl.BlockSpec((1, heads, BLOCK, BLOCK), lambda n: (last - n, 0, 0, 0)),
            pl.BlockSpec((heads, key, value), lambda n: (0, 0, 0)),
            pl.BlockSpec((BLOCK, heads * value), lambda n: (last - n, 0)),
            pl.BlockSpec(ends.shape, lambda n: (0, 0, 0, 0), **once),
            pl.BlockSpec(adjoints.shape, lambda n: (0, 0, 0, 0), **once),
        ],
        out_specs=[
            pl.BlockSpec((BLOCK, width), lambda n: (last - n, 0)),
            pl.BlockSpec((BLOCK, LANES), lambda n: (last - n, 0)),
            pl.BlockSpec((8, width), lambda n: (0, 0)),
            pl.BlockSpec((32, width), lambda n: (0, 0)),
            pl.BlockSpec((16, LANES), lambda n: (0, 0)),
        ],
        out_shape=[
            jax.ShapeDtypeStruct((length, width), low),
            jax.ShapeDtypeStruct((length, LANES), low),
            jax.ShapeDtypeStruct((8, width), full),
            jax.ShapeDtypeStruct((32, width), full),
            jax.ShapeDtypeStruct((16, LANES), full),
        ],
        scratch_shapes=[
            pltpu.VMEM((BLOCK + 8, width), full),
            pltpu.VMEM((BLOCK + 16, width), full),
            pltpu.VMEM((heads, key, value), full),
        ],
        compiler_params=pltpu.CompilerParams(vmem_limit_bytes=56 * MIB),
        name="chain_backward",
    )(place, pre, pre, ab, meta, segrow, edge, edge_meta, taps, params, states, inverse, state_in, do,
      ends, adjoints)


def segment_tables(doc_lengths, shard, length):
    starts = jnp.cumsum(doc_lengths, dtype=jnp.int32) - doc_lengths
    positions = shard * length + jnp.arange(-16, length + 8, dtype=jnp.int32)
    seg = jnp.sum((starts[None, :] <= positions[:, None]).astype(jnp.int32), axis=1)
    own = seg[16 : 16 + length]

    def lanes(first, count):
        base = seg[first : first + count]
        back = [seg[first - l : first - l + count] == base for l in (1, 2, 3)]
        ahead = [seg[first + l : first + l + count] == base for l in (1, 2, 3)]
        return base, back, ahead

    base, back, ahead = lanes(16, length)
    blocks = own.reshape(-1, BLOCK)
    before = seg[15 : 15 + length : BLOCK]
    alive = (blocks == before[:, None]).reshape(-1)
    to_last = (blocks == blocks[:, -1:]).reshape(-1)
    columns = [base, *back, alive, to_last, *ahead]
    meta = jnp.stack([a.astype(full) for a in columns], axis=1)
    meta = jnp.pad(meta, ((0, 0), (0, LANES - meta.shape[1])))
    base, back, ahead = lanes(8, 8)
    columns = [base, *back, base, base, *ahead]
    edge_meta = jnp.stack([a.astype(full) for a in columns], axis=1)
    edge_meta = jnp.pad(edge_meta, ((0, 0), (0, LANES - edge_meta.shape[1])))
    segrow = jnp.broadcast_to(own.astype(full)[None, :], (8, length))
    return meta, edge_meta, segrow


def rms_scale(array, epsilon):
    return lax.rsqrt(jnp.mean(array * array, axis=-1, keepdims=True) + epsilon)


def gather(parts):
    return lax.all_gather(jnp.concatenate(parts, axis=1), "seq", axis=0, tiled=True)


def scatter(grad):
    return lax.psum_scatter(grad.astype(low), "seq", scatter_dimension=0, tiled=True).astype(full)


def passed_along(block, axis, distance):
    devices = range(lax.axis_size(axis))
    route = [(i - distance, i) for i in devices if i - distance in devices]
    return lax.ppermute(block, axis, route)


def shards(
    tokens,
    doc_lengths,
    mixer_gain,
    query_weight,
    key_weight,
    value_weight,
    gate_weight,
    alpha_weight,
    beta_weight,
    decay_log,
    decay_bias,
    query_taps,
    key_taps,
    value_taps,
    head_gain,
    output_weight,
    ffn_gain,
    ffn_gate,
    ffn_up,
    ffn_down,
    cotangent,
):
    length = tokens.shape[0]
    heads = decay_log.shape[0]
    key = query_weight.shape[1] // heads
    value = head_gain.shape[0]
    keys, vals = heads * key, heads * value
    hidden_size = ffn_gate.shape[1]
    shard = lax.axis_index("seq")
    place = jnp.full((1,), shard, jnp.int32)
    meta, edge_meta, segrow = segment_tables(doc_lengths, shard, length)

    small = jnp.concatenate(
        [alpha_weight, beta_weight, jnp.zeros((alpha_weight.shape[0], LANES - 2 * heads), full)],
        axis=1,
    )
    w_in = gather([a.astype(low) for a in (query_weight, key_weight, value_weight)])
    w_small = lax.all_gather(small.astype(low), "seq", axis=0, tiled=True)
    w_gate = lax.all_gather(gate_weight.astype(low), "seq", axis=0, tiled=True)
    w_out = lax.all_gather(output_weight.T.astype(low), "seq", axis=0, tiled=True)
    w_widen = lax.all_gather(ffn_gate.astype(low), "seq", axis=0, tiled=True)
    w_lift = lax.all_gather(ffn_up.astype(low), "seq", axis=0, tiled=True)
    w_narrow = lax.all_gather(ffn_down.T.astype(low), "seq", axis=0, tiled=True)

    stream = tokens.astype(full)
    first_scale = rms_scale(stream, 1e-06)
    first_norm = stream * first_scale
    first_in = (first_norm * mixer_gain).astype(low)
    pre = mm(first_in, w_in).astype(low)
    ab = mm(first_in, w_small)
    edge = passed_along(pre[length - 8 :], "seq", 1)
    gate_pre = mm(first_in, w_gate)

    taps = jnp.concatenate([query_taps, key_taps, value_taps], axis=1)
    params = jnp.stack([-jnp.exp(decay_log), decay_bias])
    params = jnp.pad(params, ((0, 6), (0, LANES - heads)))
    local, through, states, inverse, end = forward_chain(
        pre, ab, meta, segrow, edge, taps, params, heads, key, value
    )
    ends = lax.all_gather(end, "seq")
    gain = head_gain[None, :]
    mix_out, mixed, state_in = chain_output(
        place, ends, local, through, gate_pre, gain, heads, key, value
    )
    middle = stream + lax.psum(mm_nt(mix_out, w_out).astype(low), "head").astype(full)
    second_scale = rms_scale(middle, 1e-06)
    second_norm = middle * second_scale
    second_in = (second_norm * ffn_gain).astype(low)
    gate_act = mm(second_in, w_widen)
    lift_act = mm(second_in, w_lift)
    sigma = jax.nn.sigmoid(gate_act)
    swish = gate_act * sigma
    hidden = (swish * lift_act).astype(low)
    result = (
        middle + lax.psum(mm_nt(hidden, w_narrow).astype(low), "head").astype(full)
    ).astype(low)

    grad_out = cotangent.astype(full)
    hidden_grad = mm(cotangent, w_narrow)
    gate_grad = (hidden_grad * lift_act * sigma * (1.0 + gate_act * (1.0 - sigma))).astype(low)
    lift_grad = (hidden_grad * swish).astype(low)
    second_grad = lax.psum(
        (mm_nt(gate_grad, w_widen) + mm_nt(lift_grad, w_lift)).astype(low), "head"
    ).astype(full)
    narrow_wgrad = scatter(mm_tn(cotangent, hidden)).T
    widen_wgrad = scatter(mm_tn(second_in, gate_grad))
    lift_wgrad = scatter(mm_tn(second_in, lift_grad))
    second_weighted = second_grad * ffn_gain
    ffn_gain_part = jnp.sum(second_grad * second_norm, axis=0)
    middle_grad = grad_out + second_scale * (
        second_weighted
        - second_norm * jnp.mean(second_weighted * second_norm, axis=-1, keepdims=True)
    )
    middle_low = middle_grad.astype(low)
    mix_grad = mm(middle_low, w_out)
    gate_pgrad, mixed_grad, head_gain_part, adjoint = gate_back(
        mix_grad, mixed, gate_pre, gain, through, heads, key, value
    )
    adjoints = lax.all_gather(adjoint.astype(low), "seq")
    output_wgrad = scatter(mm_tn(middle_low, mix_out)).T
    gate_wgrad = scatter(mm_tn(first_in, gate_pgrad))
    pre_grad, ab_grad, halo, taps_part, params_part = backward_chain(
        place, pre, ab, meta, segrow, edge, edge_meta, taps, params, states, inverse, state_in,
        mixed_grad, ends, adjoints, heads, key, value,
    )
    halo = passed_along(halo, "seq", -1)
    last = pre_grad[length - 8 :].astype(full) + halo
    pre_grad = lax.dynamic_update_slice(pre_grad, last.astype(low), (length - 8, 0))
    first_grad = lax.psum(
        (
            mm_nt(pre_grad, w_in) + mm_nt(gate_pgrad, w_gate) + mm_nt(ab_grad, w_small)
        ).astype(low),
        "head",
    ).astype(full)
    in_wgrad = scatter(mm_tn(first_in, pre_grad))
    small_wgrad = scatter(mm_tn(first_in, ab_grad))
    first_weighted = first_grad * mixer_gain
    mixer_gain_part = jnp.sum(first_grad * first_norm, axis=0)
    tokens_grad = middle_grad + first_scale * (
        first_weighted - first_norm * jnp.mean(first_weighted * first_norm, axis=-1, keepdims=True)
    )
    taps_part = jnp.sum(taps_part.reshape(4, 8, -1), axis=1)
    params_part = jnp.sum(params_part.reshape(2, 8, LANES), axis=1)
    mixer_gain_grad, ffn_gain_grad, taps_grad, params_grad = lax.psum(
        (
            mixer_gain_part.astype(low),
            ffn_gain_part.astype(low),
            taps_part.astype(low),
            params_part.astype(low),
        ),
        "seq",
    )
    head_gain_grad = lax.psum(jnp.sum(head_gain_part, axis=0), ("seq", "head"))
    taps_grad = taps_grad.astype(full)
    params_grad = params_grad.astype(full)
    return (
        result,
        tokens_grad,
        mixer_gain_grad.astype(full),
        in_wgrad[:, :keys],
        in_wgrad[:, keys : 2 * keys],
        in_wgrad[:, 2 * keys :],
        gate_wgrad,
        small_wgrad[:, :heads],
        small_wgrad[:, heads : 2 * heads],
        params_grad[1, :heads],
        params_grad[0, :heads],
        taps_grad[:, :keys],
        taps_grad[:, keys : 2 * keys],
        taps_grad[:, 2 * keys :],
        head_gain_grad,
        output_wgrad,
        ffn_gain_grad.astype(full),
        widen_wgrad,
        lift_wgrad,
        narrow_wgrad,
    )


def solution(mesh):
    rows, both = P("seq", None), P("seq", "head")
    in_specs = (
        rows, P(), P(), both, both, both, both, both, both, P("head"), P("head"),
        P(None, "head"), P(None, "head"), P(None, "head"), P(), P("head", "seq"), P(),
        both, both, P("head", "seq"), rows,
    )
    out_specs = (
        rows, rows, P(), both, both, both, both, both, both, P("head"), P("head"),
        P(None, "head"), P(None, "head"), P(None, "head"), P(), P("head", "seq"), P(),
        both, both, P("head", "seq"),
    )
    return jax.shard_map(shards, mesh=mesh, in_specs=in_specs, out_specs=out_specs, check_vma=False)
```

```python
from functools import partial

import jax
import jax.numpy as jnp
from jax import lax
from jax.experimental import pallas as pl
from jax.experimental.pallas import tpu as pltpu
from jax.sharding import PartitionSpec as P

BLOCK = 128
LANES = 128
low = jnp.bfloat16
full = jnp.float32
MIB = 1 << 20


def mm(a, b):
    return jnp.dot(a.astype(low), b.astype(low), preferred_element_type=full)


def mm_nt(a, b):
    return lax.dot_general(
        a.astype(low), b.astype(low), (((1,), (1,)), ((), ())), preferred_element_type=full
    )


def mm_tn(a, b):
    return lax.dot_general(
        a.astype(low), b.astype(low), (((0,), (0,)), ((), ())), preferred_element_type=full
    )


def exact(a, b):
    return jnp.dot(a, b, precision=lax.Precision.HIGHEST, preferred_element_type=full)


def sigmoid(t):
    return 1.0 / (1.0 + jnp.exp(-t))


def softplus(t):
    return jnp.maximum(t, 0.0) + jnp.log(1.0 + jnp.exp(-jnp.abs(t)))


def iotas(size):
    return (
        lax.broadcasted_iota(jnp.int32, (size, size), 0),
        lax.broadcasted_iota(jnp.int32, (size, size), 1),
    )


def conv_sum(ext, taps, meta, first, width, rows):
    total = taps[3:4, first : first + width] * ext[8 : 8 + rows, first : first + width]
    for lag in (1, 2, 3):
        total += (
            taps[3 - lag : 4 - lag, first : first + width]
            * meta[:, lag : lag + 1]
            * ext[8 - lag : 8 - lag + rows, first : first + width]
        )
    return total


def gates(ab, params, heads):
    log_decay = params[0:1, :] * softplus(ab + params[1:2, :])
    beta = sigmoid(ab)
    return log_decay, beta


def decay_parts(cum, cum_t, h, same_low, strict_low, meta):
    size = cum.shape[0]
    col = cum[:, h : h + 1]
    row = cum_t[h : h + 1, :]
    lower = jnp.where(same_low, jnp.exp(jnp.minimum(col - row, 0.0)), 0.0)
    strict = jnp.where(strict_low, lower, 0.0)
    last = cum[size - 1 : size, h : h + 1]
    from_start = jnp.exp(col) * meta[:, 4:5]
    to_end = jnp.exp(last - col) * meta[:, 5:6]
    carried = jnp.exp(last) * meta[size - 1 : size, 4:5]
    return lower, strict, from_start, to_end, carried


def unit_lower_inverse(strict, rows, cols):
    size = strict.shape[0]
    power = jnp.where((rows >> 3) == (cols >> 3), -strict, 0.0)
    inverse = jnp.where(rows == cols, 1.0, power)
    power = mm(power, power)
    inverse = inverse + mm(inverse, power)
    power = mm(power, power)
    inverse = inverse + mm(inverse, power)
    shift = 3
    while (1 << shift) < size:
        off = jnp.where(
            ((rows >> (shift + 1)) == (cols >> (shift + 1))) & ((rows >> shift) != (cols >> shift)),
            strict,
            0.0,
        )
        inverse = inverse - mm(inverse, mm(off, inverse))
        shift += 1
    return inverse


def inverses(stricts, rows, cols):
    size = stricts[0].shape[0]
    near = (rows >> 3) == (cols >> 3)
    powers = [jnp.where(near, -a, 0.0) for a in stricts]
    result = [jnp.where(rows == cols, 1.0, p) for p in powers]
    for _ in range(2):
        powers = [mm(p, p) for p in powers]
        result = [t + mm(t, p) for t, p in zip(result, powers)]
    shift = 3
    while (1 << shift) < size:
        pick = ((rows >> (shift + 1)) == (cols >> (shift + 1))) & (
            (rows >> shift) != (cols >> shift)
        )
        offs = [mm(jnp.where(pick, a, 0.0), t) for a, t in zip(stricts, result)]
        result = [t - mm(t, o) for t, o in zip(result, offs)]
        shift += 1
    return result


def masks(meta, segrow):
    size = meta.shape[0]
    rows, cols = iotas(size)
    same = meta[:, 0:1] == segrow[0:1, :]
    return rows, cols, same & (rows >= cols), same & (rows > cols)


def unit(post):
    return lax.rsqrt(jnp.sum(post * post, axis=-1, keepdims=True) + 1e-06)


def forward_kernel(
    heads, key, value,
    pre_ref, ab_ref, meta_ref, segrow_ref, edge_ref, taps_ref, params_ref,
    out_ref, through_ref, states_ref, inverse_ref, end_ref,
    ext, state,
):
    step = pl.program_id(0)
    size = pre_ref.shape[0]
    wide = value + key
    kfirst, vfirst = heads * key, 2 * heads * key

    @pl.when(step == 0)
    def _():
        ext[0:8, :] = edge_ref[...].astype(full)
        rows, cols = iotas(key)
        eye = (rows == cols).astype(full)
        for h in range(heads):
            state[h, :, :value] = jnp.zeros((key, value), full)
            state[h, :, value:] = eye

    @pl.when(step > 0)
    def _():
        ext[0:8, :] = ext[size : size + 8, :]

    ext[8:, :] = pre_ref[...].astype(full)
    meta = meta_ref[...]
    log_decay, beta = gates(ab_ref[...], params_ref, heads)
    rows, cols, same_low, strict_low = masks(meta, segrow_ref)
    cum = exact((rows >= cols).astype(full), log_decay)
    cum_t = cum.T
    qs, ks, vs, lowers, stricts, fs, es, cs = [], [], [], [], [], [], [], []
    for h in range(heads):
        u = conv_sum(ext, taps_ref, meta, h * key, key, size)
        post = u * sigmoid(u)
        q = (post * unit(post)).astype(low)
        u = conv_sum(ext, taps_ref, meta, kfirst + h * key, key, size)
        post = u * sigmoid(u)
        k = (post * unit(post)).astype(low)
        u = conv_sum(ext, taps_ref, meta, vfirst + h * value, value, size)
        v = u * sigmoid(u)
        lower, strict, f, e, c = decay_parts(cum, cum_t, h, same_low, strict_low, meta)
        bcol = beta[:, heads + h : heads + h + 1]
        gram = mm_nt(jnp.concatenate([k, q], axis=0), k)
        qs.append(q), ks.append(k), vs.append(v), fs.append(f), es.append(e), cs.append(c)
        stricts.append(bcol * strict * gram[:size])
        lowers.append(lower * gram[size:])
    ts = inverses(stricts, rows, cols)
    for h in range(heads):
        bcol = beta[:, heads + h : heads + h + 1]
        s = state[h]
        states_ref[0, h] = s.astype(low)
        t = ts[h].astype(low)
        inverse_ref[0, h] = t
        ks_s = mm(ks[h], s)
        fb = fs[h] * bcol
        target = jnp.concatenate(
            [bcol * vs[h] - fb * ks_s[:, :value], -fb * ks_s[:, value:]], axis=1
        )
        delta = mm(t, target).astype(low)
        left = jnp.concatenate([(fs[h] * qs[h].astype(full)).astype(low), lowers[h].astype(low)], axis=1)
        out = mm(left, jnp.concatenate([s.astype(low), delta], axis=0))
        out_ref[:, h * value : (h + 1) * value] = out[:, :value]
        through_ref[:, h * key : (h + 1) * key] = out[:, value:].astype(low)
        ke = es[h] * ks[h].astype(full)
        s = cs[h] * s + mm_tn(ke, delta)
        state[h] = s
        end_ref[h] = s.astype(low)


def forward_chain(pre, ab, meta, segrow, edge, taps, params, heads, key, value):
    length = pre.shape[0]
    blocks = length // BLOCK
    width = pre.shape[1]
    wide = value + key
    return pl.pallas_call(
        partial(forward_kernel, heads, key, value),
        grid=(blocks,),
        in_specs=[
            pl.BlockSpec((BLOCK, width), lambda n: (n, 0)),
            pl.BlockSpec((BLOCK, LANES), lambda n: (n, 0)),
            pl.BlockSpec((BLOCK, LANES), lambda n: (n, 0)),
            pl.BlockSpec((8, BLOCK), lambda n: (0, n)),
            pl.BlockSpec((8, width), lambda n: (0, 0)),
            pl.BlockSpec(taps.shape, lambda n: (0, 0)),
            pl.BlockSpec((8, LANES), lambda n: (0, 0)),
        ],
        out_specs=[
            pl.BlockSpec((BLOCK, heads * value), lambda n: (n, 0)),
            pl.BlockSpec((BLOCK, heads * key), lambda n: (n, 0)),
            pl.BlockSpec((1, heads, key, wide), lambda n: (n, 0, 0, 0)),
            pl.BlockSpec((1, heads, BLOCK, BLOCK), lambda n: (n, 0, 0, 0)),
            pl.BlockSpec((heads, key, wide), lambda n: (0, 0, 0)),
        ],
        out_shape=[
            jax.ShapeDtypeStruct((length, heads * value), full),
            jax.ShapeDtypeStruct((length, heads * key), low),
            jax.ShapeDtypeStruct((blocks, heads, key, wide), low),
            jax.ShapeDtypeStruct((blocks, heads, BLOCK, BLOCK), low),
            jax.ShapeDtypeStruct((heads, key, wide), low),
        ],
        scratch_shapes=[
            pltpu.VMEM((BLOCK + 8, width), full),
            pltpu.VMEM((heads, key, wide), full),
        ],
        compiler_params=pltpu.CompilerParams(vmem_limit_bytes=48 * MIB),
        name="chain_forward",
    )(pre, ab, meta, segrow, edge, taps, params)


def output_kernel(heads, key, value, place_ref, ends_ref, local_ref, through_ref, gate_ref, gain_ref,
                  y_ref, mixed_ref, state_ref):
    @pl.when(pl.program_id(0) == 0)
    def _():
        state_ref[...] = jnp.zeros_like(state_ref)

        def one(j, carry):
            for h in range(heads):
                part = ends_ref[j, h]
                state_ref[h] = (
                    mm(part[:, value:], state_ref[h]) + part[:, :value].astype(full)
                )
            return carry

        lax.fori_loop(0, place_ref[0], one, 0)

    for h in range(heads):
        cols = slice(h * value, (h + 1) * value)
        o = local_ref[:, cols] + mm(through_ref[:, h * key : (h + 1) * key], state_ref[h])
        mixed_ref[:, cols] = o.astype(mixed_ref.dtype)
        s3 = lax.rsqrt(jnp.mean(o * o, axis=-1, keepdims=True) + 1e-05)
        gz = gate_ref[:, cols]
        y_ref[:, cols] = (o * s3 * gain_ref[0:1, :] * (gz * sigmoid(gz))).astype(low)


def chain_output(place, ends, local, through, gate, gain, heads, key, value, rows=256):
    length, wide = local.shape
    return pl.pallas_call(
        partial(output_kernel, heads, key, value),
        grid=(length // rows,),
        in_specs=[
            pl.BlockSpec(memory_space=pltpu.SMEM),
            pl.BlockSpec(ends.shape, lambda n: (0, 0, 0, 0), pipeline_mode=pl.Buffered(1)),
            pl.BlockSpec((rows, wide), lambda n: (n, 0)),
            pl.BlockSpec((rows, heads * key), lambda n: (n, 0)),
            pl.BlockSpec((rows, wide), lambda n: (n, 0)),
            pl.BlockSpec((1, value), lambda n: (0, 0)),
        ],
        out_specs=[
            pl.BlockSpec((rows, wide), lambda n: (n, 0)),
            pl.BlockSpec((rows, wide), lambda n: (n, 0)),
            pl.BlockSpec((heads, key, value), lambda n: (0, 0, 0)),
        ],
        out_shape=[
            jax.ShapeDtypeStruct((length, wide), low),
            jax.ShapeDtypeStruct((length, wide), full),
            jax.ShapeDtypeStruct((heads, key, value), full),
        ],
        compiler_params=pltpu.CompilerParams(vmem_limit_bytes=48 * MIB),
        name="chain_output",
    )(place, ends, local, through, gate, gain)


def gate_back_kernel(heads, key, value, dy_ref, mixed_ref, gate_ref, gain_ref, through_ref,
                     dgz_ref, do_ref, gain_grad_ref, adjoint_ref):
    @pl.when(pl.program_id(0) == 0)
    def _():
        gain_grad_ref[...] = jnp.zeros_like(gain_grad_ref)
        adjoint_ref[...] = jnp.zeros_like(adjoint_ref)

    rows = dy_ref.shape[0]
    gain = gain_ref[0:1, :]
    for h in range(heads):
        cols = slice(h * value, (h + 1) * value)
        o = mixed_ref[:, cols].astype(full)
        s3 = lax.rsqrt(jnp.mean(o * o, axis=-1, keepdims=True) + 1e-05)
        n3 = o * s3
        gz = gate_ref[:, cols]
        sig = sigmoid(gz)
        sg = gz * sig
        dy = dy_ref[:, cols]
        dyn = dy * n3
        part = dyn * sg
        gain_grad_ref[...] += jnp.sum(part.reshape(rows // 8, 8, value), axis=0)
        dgz_ref[:, cols] = (dyn * gain * (sig * (1.0 + gz * (1.0 - sig)))).astype(low)
        dn3 = dy * gain * sg
        do = s3 * (dn3 - n3 * jnp.mean(dn3 * n3, axis=-1, keepdims=True))
        do = do.astype(low)
        do_ref[:, cols] = do
        adjoint_ref[h] += mm_tn(through_ref[:, h * key : (h + 1) * key], do)


def gate_back(dy, mixed, gate, gain, through, heads, key, value, rows=256):
    length, wide = dy.shape
    return pl.pallas_call(
        partial(gate_back_kernel, heads, key, value),
        grid=(length // rows,),
        in_specs=[
            pl.BlockSpec((rows, wide), lambda n: (n, 0)),
            pl.BlockSpec((rows, wide), lambda n: (n, 0)),
            pl.BlockSpec((rows, wide), lambda n: (n, 0)),
            pl.BlockSpec((1, value), lambda n: (0, 0)),
            pl.BlockSpec((rows, heads * key), lambda n: (n, 0)),
        ],
        out_specs=[
            pl.BlockSpec((rows, wide), lambda n: (n, 0)),
            pl.BlockSpec((rows, wide), lambda n: (n, 0)),
            pl.BlockSpec((8, value), lambda n: (0, 0)),
            pl.BlockSpec((heads, key, value), lambda n: (0, 0, 0)),
        ],
        out_shape=[
            jax.ShapeDtypeStruct((length, wide), low),
            jax.ShapeDtypeStruct((length, wide), low),
            jax.ShapeDtypeStruct((8, value), full),
            jax.ShapeDtypeStruct((heads, key, value), full),
        ],
        compiler_params=pltpu.CompilerParams(vmem_limit_bytes=48 * MIB),
        name="gate_back",
    )(dy, mixed, gate, gain, through)


def lane_sum(array):
    return jnp.sum(array, axis=-1, keepdims=True)


def backward_kernel(
    heads, key, value, devices,
    place_ref, pre_ref, tail_ref, ab_ref, meta_ref, segrow_ref, edge_ref, edge_meta_ref, taps_ref, params_ref,
    states_ref, inverse_ref, state_in_ref, do_ref, ends_ref, adjoints_ref,
    dpre_ref, dab_ref, halo_ref, taps_grad_ref, params_grad_ref,
    ext, du, adjoint,
):
    step = pl.program_id(0)
    steps = pl.num_programs(0)
    size = pre_ref.shape[0]
    kfirst, vfirst = heads * key, 2 * heads * key

    @pl.when(step == 0)
    def _():
        adjoint[...] = jnp.zeros_like(adjoint)

        def one(k, carry):
            j = devices - 1 - k
            for h in range(heads):
                adjoint[h] = (
                    mm_tn(ends_ref[j, h, :, value:], adjoint[h]) + adjoints_ref[j, h].astype(full)
                )
            return carry

        lax.fori_loop(0, devices - 1 - place_ref[0], one, 0)
        du[8 + size :, :] = jnp.zeros((8, du.shape[1]), full)
        taps_grad_ref[...] = jnp.zeros_like(taps_grad_ref)
        params_grad_ref[...] = jnp.zeros_like(params_grad_ref)

    @pl.when(step > 0)
    def _():
        du[8 + size :, :] = du[8:16, :]

    du[0:8, :] = jnp.zeros((8, du.shape[1]), full)

    @pl.when(step < steps - 1)
    def _():
        ext[0:8, :] = tail_ref[8:16, :].astype(full)

    @pl.when(step == steps - 1)
    def _():
        ext[0:8, :] = edge_ref[...].astype(full)

    ext[8:, :] = pre_ref[...].astype(full)
    meta = meta_ref[...]
    ab = ab_ref[...]
    log_decay, beta = gates(ab, params_ref, heads)
    rows, cols, same_low, strict_low = masks(meta, segrow_ref)
    cum = exact((rows >= cols).astype(full), log_decay)
    cum_t = cum.T
    lane = lax.broadcasted_iota(jnp.int32, (size, LANES), 1)
    row8 = lax.broadcasted_iota(jnp.int32, (8, size), 0)
    dcum = jnp.zeros((size, LANES), full)
    dcum_rows = jnp.zeros((8, size), full)
    dcum_last = jnp.zeros((1, LANES), full)
    dbeta = jnp.zeros((size, LANES), full)
    lane1 = lax.broadcasted_iota(jnp.int32, (1, LANES), 1)

    for h in range(heads):
        qcols = slice(h * key, (h + 1) * key)
        kcols = slice(kfirst + h * key, kfirst + (h + 1) * key)
        vcols = slice(vfirst + h * value, vfirst + (h + 1) * value)
        uq = conv_sum(ext, taps_ref, meta, h * key, key, size)
        sq = sigmoid(uq)
        pq = uq * sq
        rq = unit(pq)
        qf = pq * rq
        q = qf.astype(low)
        uk = conv_sum(ext, taps_ref, meta, kfirst + h * key, key, size)
        sk = sigmoid(uk)
        pk = uk * sk
        rk = unit(pk)
        kf = pk * rk
        k = kf.astype(low)
        uv = conv_sum(ext, taps_ref, meta, vfirst + h * value, value, size)
        sv = sigmoid(uv)
        v = uv * sv
        lower, strict, f, e, c = decay_parts(cum, cum_t, h, same_low, strict_low, meta)
        b = beta[:, heads + h : heads + h + 1]
        kq = jnp.concatenate([k, q], axis=0)
        gram = mm_nt(kq, k)
        kk, qk = gram[:size], gram[size:]
        stored = states_ref[0, h]
        s = stored[:, :value].astype(full) + mm(stored[:, value:], state_in_ref[h])
        slow = s.astype(low)
        kqs = mm(kq, slow)
        ks, qs = kqs[:size], kqs[size:]
        rest = v - f * ks
        t = inverse_ref[0, h]
        delta = mm(t, b * rest).astype(low)
        do = do_ref[:, h * value : (h + 1) * value]
        dof = do.astype(full)
        ds = adjoint[h]
        dslow = ds.astype(low)
        ke = (e * kf).astype(low)
        p = lower * qk
        left = jnp.concatenate([p.T.astype(low), ke], axis=1)
        ddelta = mm(left, jnp.concatenate([do, dslow], axis=0))
        dtarget = mm_tn(t, ddelta)
        outer = mm_nt(jnp.concatenate([do, dtarget.astype(low)], axis=0), delta)
        dp, dan = outer[:size], outer[size:]
        eg = lower * dp
        hn = -strict * dan
        hg = b * hn
        x = eg * qk
        hk = hn * kk
        g1 = (b * f) * dtarget
        fdo = f * dof
        pair = jnp.concatenate([fdo.astype(low), (-g1).astype(low)], axis=0)
        both = mm_nt(pair, slow)
        dq = both[:size] + mm(eg, k)
        dsk = e * mm_nt(delta, dslow)
        left = jnp.concatenate([(hg + hg.T).astype(low), eg.T.astype(low)], axis=1)
        dk = both[size:] + dsk + mm(left, kq)
        dv = b * dtarget
        z = lane_sum(kf * dsk)
        dfrom = lane_sum(dof * qs) - b * lane_sum(dtarget * ks)
        hrow = lane_sum(hk)
        db = hrow + lane_sum(dtarget * rest)
        dbeta = dbeta + jnp.where(lane == heads + h, db, 0.0)
        dcum = dcum + jnp.where(lane == h, lane_sum(x) + b * hrow + f * dfrom - z, 0.0)
        drow = jnp.sum(x + b * hk, axis=0, keepdims=True)
        dcum_rows = dcum_rows + jnp.where(row8 == h, drow, 0.0)
        dlast = jnp.sum(z, axis=0, keepdims=True) + c * jnp.sum(
            lane_sum(ds * s), axis=0, keepdims=True
        )
        dcum_last = dcum_last + jnp.where(lane1 == h, dlast, 0.0)
        adjoint[h] = c * ds + mm_tn(jnp.concatenate([q, k], axis=0), pair)

        dpq = rq * (dq - qf * lane_sum(dq * qf))
        du[8 : 8 + size, qcols] = dpq * (sq * (1.0 + uq * (1.0 - sq)))
        dpk = rk * (dk - kf * lane_sum(dk * kf))
        du[8 : 8 + size, kcols] = dpk * (sk * (1.0 + uk * (1.0 - sk)))
        du[8 : 8 + size, vcols] = dv * (sv * (1.0 + uv * (1.0 - sv)))

    padded = jnp.concatenate([dcum_rows, jnp.zeros((LANES - 8, size), full)], axis=0)
    rowi = lax.broadcasted_iota(jnp.int32, (size, LANES), 0)
    dcum = dcum - padded.T + jnp.where(rowi == size - 1, dcum_last, 0.0)
    dlog = exact((rows <= cols).astype(full), dcum)
    dga = dlog * params_ref[0:1, :] * sigmoid(ab + params_ref[1:2, :])
    is_decay = lane < heads
    dga = jnp.where(is_decay, dga, 0.0)
    params_grad_ref[0:8, :] += jnp.sum(dga.reshape(size // 8, 8, LANES), axis=0)
    decay_part = jnp.where(is_decay, dlog * log_decay, 0.0)
    params_grad_ref[8:16, :] += jnp.sum(decay_part.reshape(size // 8, 8, LANES), axis=0)
    dab_ref[...] = jnp.where(is_decay, dga, dbeta * beta * (1.0 - beta)).astype(low)

    width = du.shape[1]
    for first in range(0, width, 512):
        cs = slice(first, first + 512)
        own = du[8 : 8 + size, cs]
        total = taps_ref[3:4, cs] * own
        taps_grad_ref[24:32, cs] += jnp.sum(
            (own * ext[8 : 8 + size, cs]).reshape(size // 8, 8, 512), axis=0
        )
        for lag in (1, 2, 3):
            total += taps_ref[3 - lag : 4 - lag, cs] * meta[:, 5 + lag : 6 + lag] * du[
                8 + lag : 8 + lag + size, cs
            ]
            taps_grad_ref[8 * (3 - lag) : 8 * (4 - lag), cs] += jnp.sum(
                (own * meta[:, lag : lag + 1] * ext[8 - lag : 8 - lag + size, cs]).reshape(
                    size // 8, 8, 512
                ),
                axis=0,
            )
        dpre_ref[:, cs] = total.astype(low)

    @pl.when(step == steps - 1)
    def _():
        edge_meta = edge_meta_ref[...]
        halo = jnp.zeros(halo_ref.shape, full)
        for lag in (1, 2, 3):
            halo += taps_ref[3 - lag : 4 - lag, :] * edge_meta[:, 5 + lag : 6 + lag] * du[
                lag : 8 + lag, :
            ]
        halo_ref[...] = halo


def backward_chain(place, pre, ab, meta, segrow, edge, edge_meta, taps, params, states, inverse,
                   state_in, do, ends, adjoints, heads, key, value):
    length, width = pre.shape
    blocks = length // BLOCK
    wide = value + key
    once = dict(pipeline_mode=pl.Buffered(1))
    last = blocks - 1
    return pl.pallas_call(
        partial(backward_kernel, heads, key, value, ends.shape[0]),
        grid=(blocks,),
        in_specs=[
            pl.BlockSpec(memory_space=pltpu.SMEM),
            pl.BlockSpec((BLOCK, width), lambda n: (last - n, 0)),
            pl.BlockSpec((16, width), lambda n: (jnp.maximum((last - n) * (BLOCK // 16) - 1, 0), 0)),
            pl.BlockSpec((BLOCK, LANES), lambda n: (last - n, 0)),
            pl.BlockSpec((BLOCK, LANES), lambda n: (last - n, 0)),
            pl.BlockSpec((8, BLOCK), lambda n: (0, last - n)),
            pl.BlockSpec((8, width), lambda n: (0, 0)),
            pl.BlockSpec((8, LANES), lambda n: (0, 0)),
            pl.BlockSpec(taps.shape, lambda n: (0, 0)),
            pl.BlockSpec((8, LANES), lambda n: (0, 0)),
            pl.BlockSpec((1, heads, key, wide), lambda n: (last - n, 0, 0, 0)),
            pl.BlockSpec((1, heads, BLOCK, BLOCK), lambda n: (last - n, 0, 0, 0)),
            pl.BlockSpec((heads, key, value), lambda n: (0, 0, 0)),
            pl.BlockSpec((BLOCK, heads * value), lambda n: (last - n, 0)),
            pl.BlockSpec(ends.shape, lambda n: (0, 0, 0, 0), **once),
            pl.BlockSpec(adjoints.shape, lambda n: (0, 0, 0, 0), **once),
        ],
        out_specs=[
            pl.BlockSpec((BLOCK, width), lambda n: (last - n, 0)),
            pl.BlockSpec((BLOCK, LANES), lambda n: (last - n, 0)),
            pl.BlockSpec((8, width), lambda n: (0, 0)),
            pl.BlockSpec((32, width), lambda n: (0, 0)),
            pl.BlockSpec((16, LANES), lambda n: (0, 0)),
        ],
        out_shape=[
            jax.ShapeDtypeStruct((length, width), low),
            jax.ShapeDtypeStruct((length, LANES), low),
            jax.ShapeDtypeStruct((8, width), full),
            jax.ShapeDtypeStruct((32, width), full),
            jax.ShapeDtypeStruct((16, LANES), full),
        ],
        scratch_shapes=[
            pltpu.VMEM((BLOCK + 8, width), full),
            pltpu.VMEM((BLOCK + 16, width), full),
            pltpu.VMEM((heads, key, value), full),
        ],
        compiler_params=pltpu.CompilerParams(vmem_limit_bytes=56 * MIB),
        name="chain_backward",
    )(place, pre, pre, ab, meta, segrow, edge, edge_meta, taps, params, states, inverse, state_in, do,
      ends, adjoints)


def segment_tables(doc_lengths, shard, length):
    starts = jnp.cumsum(doc_lengths, dtype=jnp.int32) - doc_lengths
    positions = shard * length + jnp.arange(-16, length + 8, dtype=jnp.int32)
    seg = jnp.sum((starts[None, :] <= positions[:, None]).astype(jnp.int32), axis=1)
    own = seg[16 : 16 + length]

    def lanes(first, count):
        base = seg[first : first + count]
        back = [seg[first - l : first - l + count] == base for l in (1, 2, 3)]
        ahead = [seg[first + l : first + l + count] == base for l in (1, 2, 3)]
        return base, back, ahead

    base, back, ahead = lanes(16, length)
    blocks = own.reshape(-1, BLOCK)
    before = seg[15 : 15 + length : BLOCK]
    alive = (blocks == before[:, None]).reshape(-1)
    to_last = (blocks == blocks[:, -1:]).reshape(-1)
    columns = [base, *back, alive, to_last, *ahead]
    meta = jnp.stack([a.astype(full) for a in columns], axis=1)
    meta = jnp.pad(meta, ((0, 0), (0, LANES - meta.shape[1])))
    base, back, ahead = lanes(8, 8)
    columns = [base, *back, base, base, *ahead]
    edge_meta = jnp.stack([a.astype(full) for a in columns], axis=1)
    edge_meta = jnp.pad(edge_meta, ((0, 0), (0, LANES - edge_meta.shape[1])))
    segrow = jnp.broadcast_to(own.astype(full)[None, :], (8, length))
    return meta, edge_meta, segrow


ROWS = 128
PIECE = 32
HOP = 2
AHEAD = 2
RING = AHEAD + 1


def line_scratch(length, width):
    pieces = length // PIECE
    return [
        pltpu.VMEM((RING, ROWS, width), low),
        pltpu.VMEM((length, width), low),
        pltpu.VMEM((length, width), low),
        pltpu.VMEM((length, width), low),
        pltpu.VMEM((length, width), low),
        pltpu.SemaphoreType.DMA((pieces,)),
        pltpu.SemaphoreType.DMA((pieces,)),
        pltpu.SemaphoreType.DMA((pieces,)),
        pltpu.SemaphoreType.DMA((pieces,)),
    ]


def line_sum(step, last, compute, finish, scratch):
    own, from_left, from_right, to_right, to_left, got_left, got_right, sent_right, sent_left = scratch
    place = lax.axis_index("head")
    length, width = from_left.shape
    blocks, pieces, each = length // ROWS, length // PIECE, ROWS // PIECE
    left_there, right_there = place > 0, place < last

    def rows(piece):
        return pl.ds(pl.multiple_of(piece * PIECE, PIECE), PIECE)

    def hop(piece, rightwards):
        src, dst, sent, got, to = (
            (to_right, from_left, sent_right, got_left, place + 1)
            if rightwards
            else (to_left, from_right, sent_left, got_right, place - 1)
        )
        return pltpu.make_async_remote_copy(
            src_ref=src.at[rows(piece)],
            dst_ref=dst.at[rows(piece)],
            send_sem=sent.at[piece],
            recv_sem=got.at[piece],
            device_id={"head": to},
            device_id_type=pl.DeviceIdType.MESH,
        )

    def own_piece(piece):
        slot = lax.rem(piece // each, RING)
        first = pl.multiple_of(lax.rem(piece, each) * PIECE, PIECE)
        return own[slot, pl.ds(first, PIECE), :].astype(full)

    @pl.when(step == 0)
    def _():
        barrier = pltpu.get_barrier_semaphore()
        for there, to in ((left_there, place - 1), (right_there, place + 1)):

            @pl.when(there)
            def _(to=to):
                pl.semaphore_signal(
                    barrier, inc=1, device_id={"head": to}, device_id_type=pl.DeviceIdType.MESH
                )

        pl.semaphore_wait(barrier, jnp.minimum(place, 1) + jnp.minimum(last - place, 1))

        @pl.when(place == 0)
        def _():
            from_left[...] = jnp.zeros_like(from_left)

        @pl.when(place == last)
        def _():
            from_right[...] = jnp.zeros_like(from_right)

    @pl.when(step < blocks)
    def _():
        own[lax.rem(step, RING)] = compute().astype(low)

    def one(q, carry):
        now = step * each + q
        for rightwards in (True, False):
            came, more = (left_there, right_there) if rightwards else (right_there, left_there)
            source = from_left if rightwards else from_right
            target = to_right if rightwards else to_left
            piece = now - HOP * (place if rightwards else last - place)

            @pl.when((piece >= 0) & (piece < pieces))
            def _():
                @pl.when(came)
                def _():
                    hop(piece, rightwards).wait_recv()

                @pl.when(more)
                def _():
                    target[rows(piece), :] = (
                        own_piece(piece) + source[rows(piece), :].astype(full)
                    ).astype(low)
                    hop(piece, rightwards).start()

        return carry

    lax.fori_loop(0, each, one, 0)

    @pl.when(step >= AHEAD)
    def _():
        block = step - AHEAD
        span = pl.ds(pl.multiple_of(block * ROWS, ROWS), ROWS)
        finish(
            own[lax.rem(block, RING)].astype(full)
            + from_left[span, :].astype(full)
            + from_right[span, :].astype(full)
        )

    @pl.when(step == blocks + AHEAD - 1)
    def _():
        def settle(piece, carry):
            @pl.when(right_there)
            def _():
                hop(piece, True).wait_send()

            @pl.when(left_there)
            def _():
                hop(piece, False).wait_send()

            return carry

        lax.fori_loop(0, pieces, settle, 0)


def line_call(kernel, name, collective, length, width, resident, entering, leaving, outs, flops):
    blocks = length // ROWS

    def spec(array, stage):
        if stage == "first":
            return pl.BlockSpec((ROWS, array.shape[1]), lambda g: (jnp.minimum(g, blocks - 1), 0))
        if stage == "second":
            return pl.BlockSpec((ROWS, array.shape[1]), lambda g: (jnp.maximum(g - AHEAD, 0), 0))
        rank = len(array.shape)
        return pl.BlockSpec(array.shape, lambda g: (0,) * rank, pipeline_mode=pl.Buffered(1))

    in_specs = [
        pl.BlockSpec(memory_space=pltpu.SMEM) if a.dtype == jnp.int32 else spec(a, "all")
        for a in resident
    ]
    in_specs += [spec(a, "first") for a in entering] + [spec(a, "second") for a in leaving]
    shapes = [jax.ShapeDtypeStruct(shape, dtype) for shape, dtype, _ in outs]
    return pl.pallas_call(
        kernel,
        grid=(blocks + AHEAD,),
        in_specs=in_specs,
        out_specs=[
            spec(s, stage) if stage != "all" else pl.BlockSpec(s.shape, lambda g, r=len(s.shape): (0,) * r)
            for s, (_, _, stage) in zip(shapes, outs)
        ],
        out_shape=shapes,
        scratch_shapes=line_scratch(length, width),
        compiler_params=pltpu.CompilerParams(
            collective_id=collective, has_side_effects=True, vmem_limit_bytes=60 * MIB
        ),
        cost_estimate=pl.CostEstimate(flops=flops, bytes_accessed=40 * MIB, transcendentals=0),
        name=name,
    )(*resident, *entering, *leaving)


def mixer_out_kernel(heads, key, value, last, place_ref, ends_ref, w_out_ref, head_gain_ref, gain_ref,
                     local_ref, through_ref, gate_ref, tokens_ref,
                     y_ref, mixed_ref, state_ref, middle_ref, second_ref, *scratch):
    step = pl.program_id(0)

    @pl.when(step == 0)
    def _():
        state_ref[...] = jnp.zeros_like(state_ref)

        def one(j, carry):
            for h in range(heads):
                part = ends_ref[j, h]
                state_ref[h] = mm(part[:, value:], state_ref[h]) + part[:, :value].astype(full)
            return carry

        lax.fori_loop(0, lax.axis_index("seq"), one, 0)

    def compute():
        for h in range(heads):
            cols = slice(h * value, (h + 1) * value)
            o = local_ref[:, cols] + mm(through_ref[:, h * key : (h + 1) * key], state_ref[h])
            mixed_ref[:, cols] = o
            s3 = lax.rsqrt(jnp.mean(o * o, axis=-1, keepdims=True) + 1e-05)
            gz = gate_ref[:, cols]
            y_ref[:, cols] = (o * s3 * head_gain_ref[0:1, :] * (gz * sigmoid(gz))).astype(low)
        return mm_nt(y_ref[...], w_out_ref[...])

    def finish(total):
        middle = tokens_ref[...].astype(full) + total
        middle_ref[...] = middle
        scale = lax.rsqrt(jnp.mean(middle * middle, axis=-1, keepdims=True) + 1e-06)
        second_ref[...] = (middle * scale * gain_ref[0:1, :]).astype(low)

    line_sum(step, last, compute, finish, scratch)


def ffn_kernel(last, w_gate_ref, w_up_ref, w_down_ref, gain_ref,
               second_ref, cot_ref, middle_ref, cot_late_ref,
               hidden_ref, dgate_ref, dup_ref, partial_ref, dmiddle_ref, dlow_ref, gain_grad_ref,
               *scratch):
    step = pl.program_id(0)

    @pl.when(step == 0)
    def _():
        gain_grad_ref[...] = jnp.zeros_like(gain_grad_ref)

    def compute():
        h2 = second_ref[...]
        fg = mm(h2, w_gate_ref[...])
        fu = mm(h2, w_up_ref[...])
        sig = sigmoid(fg)
        swish = fg * sig
        hidden = (swish * fu).astype(low)
        hidden_ref[...] = hidden
        partial_ref[...] = mm_nt(hidden, w_down_ref[...]).astype(low)
        dhid = mm(cot_ref[...], w_down_ref[...])
        dfg = (dhid * fu * (sig * (1.0 + fg * (1.0 - sig)))).astype(low)
        dfu = (dhid * swish).astype(low)
        dgate_ref[...] = dfg
        dup_ref[...] = dfu
        return mm_nt(dfg, w_gate_ref[...]) + mm_nt(dfu, w_up_ref[...])

    def finish(grad):
        middle = middle_ref[...]
        scale = lax.rsqrt(jnp.mean(middle * middle, axis=-1, keepdims=True) + 1e-06)
        norm = middle * scale
        gain_grad_ref[...] += jnp.sum((grad * norm).reshape(ROWS // 8, 8, -1), axis=0)
        weighted = grad * gain_ref[0:1, :]
        dm = cot_late_ref[...].astype(full) + scale * (
            weighted - norm * jnp.mean(weighted * norm, axis=-1, keepdims=True)
        )
        dmiddle_ref[...] = dm
        dlow_ref[...] = dm.astype(low)

    line_sum(step, last, compute, finish, scratch)


def input_grad_kernel(last, w_in_ref, w_gate_ref, w_small_ref, gain_ref,
                      dpre_ref, dgz_ref, dab_ref, tokens_ref, dmiddle_ref,
                      dtokens_ref, gain_grad_ref, *scratch):
    step = pl.program_id(0)

    @pl.when(step == 0)
    def _():
        gain_grad_ref[...] = jnp.zeros_like(gain_grad_ref)

    def compute():
        return (
            mm_nt(dpre_ref[...], w_in_ref[...])
            + mm_nt(dgz_ref[...], w_gate_ref[...])
            + mm_nt(dab_ref[...], w_small_ref[...])
        )

    def finish(grad):
        stream = tokens_ref[...].astype(full)
        scale = lax.rsqrt(jnp.mean(stream * stream, axis=-1, keepdims=True) + 1e-06)
        norm = stream * scale
        gain_grad_ref[...] += jnp.sum((grad * norm).reshape(ROWS // 8, 8, -1), axis=0)
        weighted = grad * gain_ref[0:1, :]
        dtokens_ref[...] = dmiddle_ref[...] + scale * (
            weighted - norm * jnp.mean(weighted * norm, axis=-1, keepdims=True)
        )

    line_sum(step, last, compute, finish, scratch)


def rms_scale(array, epsilon):
    return lax.rsqrt(jnp.mean(array * array, axis=-1, keepdims=True) + epsilon)


def gather(parts):
    return lax.all_gather(jnp.concatenate(parts, axis=1), "seq", axis=0, tiled=True)


def scatter(grad):
    return lax.psum_scatter(grad.astype(low), "seq", scatter_dimension=0, tiled=True).astype(full)


def passed_along(block, axis, distance):
    devices = range(lax.axis_size(axis))
    route = [(i - distance, i) for i in devices if i - distance in devices]
    return lax.ppermute(block, axis, route)


def shards(
    tokens,
    doc_lengths,
    mixer_gain,
    query_weight,
    key_weight,
    value_weight,
    gate_weight,
    alpha_weight,
    beta_weight,
    decay_log,
    decay_bias,
    query_taps,
    key_taps,
    value_taps,
    head_gain,
    output_weight,
    ffn_gain,
    ffn_gate,
    ffn_up,
    ffn_down,
    cotangent,
):
    length = tokens.shape[0]
    heads = decay_log.shape[0]
    key = query_weight.shape[1] // heads
    value = head_gain.shape[0]
    keys, vals = heads * key, heads * value
    hidden_size = ffn_gate.shape[1]
    shard = lax.axis_index("seq")
    place = jnp.full((1,), shard, jnp.int32)
    meta, edge_meta, segrow = segment_tables(doc_lengths, shard, length)

    small = jnp.concatenate(
        [alpha_weight, beta_weight, jnp.zeros((alpha_weight.shape[0], LANES - 2 * heads), full)],
        axis=1,
    )
    w_in = gather([a.astype(low) for a in (query_weight, key_weight, value_weight)])
    w_small = lax.all_gather(small.astype(low), "seq", axis=0, tiled=True)
    w_gate = lax.all_gather(gate_weight.astype(low), "seq", axis=0, tiled=True)
    w_out = lax.all_gather(output_weight.T.astype(low), "seq", axis=0, tiled=True)
    w_widen = lax.all_gather(ffn_gate.astype(low), "seq", axis=0, tiled=True)
    w_lift = lax.all_gather(ffn_up.astype(low), "seq", axis=0, tiled=True)
    w_narrow = lax.all_gather(ffn_down.T.astype(low), "seq", axis=0, tiled=True)

    stream = tokens.astype(full)
    first_scale = rms_scale(stream, 1e-06)
    first_norm = stream * first_scale
    first_in = (first_norm * mixer_gain).astype(low)
    pre = mm(first_in, w_in).astype(low)
    ab = mm(first_in, w_small)
    edge = passed_along(pre[length - 8 :], "seq", 1)
    gate_pre = mm(first_in, w_gate)

    taps = jnp.concatenate([query_taps, key_taps, value_taps], axis=1)
    params = jnp.stack([-jnp.exp(decay_log), decay_bias])
    params = jnp.pad(params, ((0, 6), (0, LANES - heads)))
    local, through, states, inverse, end = forward_chain(
        pre, ab, meta, segrow, edge, taps, params, heads, key, value
    )
    ends = lax.all_gather(end, "seq")
    gain = head_gain[None, :]
    last = lax.axis_size("head") - 1
    width = tokens.shape[1]
    mix_out, mixed, state_in, middle, second_in = line_call(
        partial(mixer_out_kernel, heads, key, value, last), "mixer_out", 0, length, width,
        [place, ends, w_out, gain, ffn_gain[None, :]], [local, through, gate_pre], [tokens],
        [((length, vals), low, "first"), ((length, vals), full, "first"),
         ((heads, key, value), full, "all"), ((length, width), full, "second"),
         ((length, width), low, "second")],
        2 * length * vals * width,
    )
    hidden, gate_grad, lift_grad, narrow_part, middle_grad, middle_low, ffn_gain_part = line_call(
        partial(ffn_kernel, last), "ffn", 1, length, width,
        [w_widen, w_lift, w_narrow, ffn_gain[None, :]], [second_in, cotangent], [middle, cotangent],
        [((length, hidden_size), low, "first")] * 3
        + [((length, width), low, "first"), ((length, width), full, "second"),
           ((length, width), low, "second"), ((8, width), full, "all")],
        12 * length * width * hidden_size,
    )
    result = (middle + lax.psum(narrow_part, "head").astype(full)).astype(low)
    narrow_wgrad = scatter(mm_tn(cotangent, hidden)).T
    widen_wgrad = scatter(mm_tn(second_in, gate_grad))
    lift_wgrad = scatter(mm_tn(second_in, lift_grad))
    mix_grad = mm(middle_low, w_out)
    gate_pgrad, mixed_grad, head_gain_part, adjoint = gate_back(
        mix_grad, mixed, gate_pre, gain, through, heads, key, value
    )
    adjoints = lax.all_gather(adjoint.astype(low), "seq")
    output_wgrad = scatter(mm_tn(middle_low, mix_out)).T
    gate_wgrad = scatter(mm_tn(first_in, gate_pgrad))
    pre_grad, ab_grad, halo, taps_part, params_part = backward_chain(
        place, pre, ab, meta, segrow, edge, edge_meta, taps, params, states, inverse, state_in,
        mixed_grad, ends, adjoints, heads, key, value,
    )
    halo = passed_along(halo, "seq", -1)
    tail = pre_grad[length - 8 :].astype(full) + halo
    pre_grad = lax.dynamic_update_slice(pre_grad, tail.astype(low), (length - 8, 0))
    tokens_grad, mixer_gain_part = line_call(
        partial(input_grad_kernel, last), "input_grad", 2, length, width,
        [w_in, w_gate, w_small, mixer_gain[None, :]], [pre_grad, gate_pgrad, ab_grad],
        [tokens, middle_grad],
        [((length, width), full, "second"), ((8, width), full, "all")],
        2 * length * width * (2 * keys + 2 * vals + LANES),
    )
    in_wgrad = scatter(mm_tn(first_in, pre_grad))
    small_wgrad = scatter(mm_tn(first_in, ab_grad))
    taps_part = jnp.sum(taps_part.reshape(4, 8, -1), axis=1)
    params_part = jnp.sum(params_part.reshape(2, 8, LANES), axis=1)
    mixer_gain_grad, ffn_gain_grad, taps_grad, params_grad = lax.psum(
        (
            jnp.sum(mixer_gain_part, axis=0).astype(low),
            jnp.sum(ffn_gain_part, axis=0).astype(low),
            taps_part.astype(low),
            params_part.astype(low),
        ),
        "seq",
    )
    head_gain_grad = lax.psum(jnp.sum(head_gain_part, axis=0), ("seq", "head"))
    taps_grad = taps_grad.astype(full)
    params_grad = params_grad.astype(full)
    return (
        result,
        tokens_grad,
        mixer_gain_grad.astype(full),
        in_wgrad[:, :keys],
        in_wgrad[:, keys : 2 * keys],
        in_wgrad[:, 2 * keys :],
        gate_wgrad,
        small_wgrad[:, :heads],
        small_wgrad[:, heads : 2 * heads],
        params_grad[1, :heads],
        params_grad[0, :heads],
        taps_grad[:, :keys],
        taps_grad[:, keys : 2 * keys],
        taps_grad[:, 2 * keys :],
        head_gain_grad,
        output_wgrad,
        ffn_gain_grad.astype(full),
        widen_wgrad,
        lift_wgrad,
        narrow_wgrad,
    )


def solution(mesh):
    rows, both = P("seq", None), P("seq", "head")
    in_specs = (
        rows, P(), P(), both, both, both, both, both, both, P("head"), P("head"),
        P(None, "head"), P(None, "head"), P(None, "head"), P(), P("head", "seq"), P(),
        both, both, P("head", "seq"), rows,
    )
    out_specs = (
        rows, rows, P(), both, both, both, both, both, both, P("head"), P("head"),
        P(None, "head"), P(None, "head"), P(None, "head"), P(), P("head", "seq"), P(),
        both, both, P("head", "seq"),
    )
    return jax.shard_map(shards, mesh=mesh, in_specs=in_specs, out_specs=out_specs, check_vma=False)
```

```python
from functools import partial

import jax
import jax.numpy as jnp
from jax import lax
from jax.experimental import pallas as pl
from jax.experimental.pallas import tpu as pltpu
from jax.sharding import PartitionSpec as P

BLOCK = 128
LANES = 128
low = jnp.bfloat16
full = jnp.float32
MIB = 1 << 20


NEAR = 8
ONE = dict(pipeline_mode=pl.Buffered(1))
ANY = dict(memory_space=pl.ANY)
MESH = pl.DeviceIdType.MESH


def partner(mask):
    index = lax.axis_index("seq")
    bits = (lax.rem(index, 2), lax.rem(index // 2, 2), index // 4)
    return sum((1 << i) * ((1 - b) if mask >> i & 1 else b) for i, b in enumerate(bits))


def greet(masks, last=None):
    barrier = pltpu.get_barrier_semaphore()
    for mask in masks:
        pl.semaphore_signal(barrier, inc=1, device_id={"seq": partner(mask)}, device_id_type=MESH)
    count = len(masks)
    if last is not None:
        place = lax.axis_index("head")
        for there, to in ((place > 0, place - 1), (place < last, place + 1)):

            @pl.when(there)
            def _(to=to):
                pl.semaphore_signal(barrier, inc=1, device_id={"head": to}, device_id_type=MESH)

        count += jnp.minimum(place, 1) + jnp.minimum(last - place, 1)
    pl.semaphore_wait(barrier, count)


class Gather:
    masks = (1, 2, 4)
    semaphores = [pltpu.SemaphoreType.DMA((8,)), pltpu.SemaphoreType.DMA((8,)), pltpu.SemaphoreType.DMA((1,))]

    def __init__(self, shard, whole, sent, got, home):
        self.shard, self.whole, self.sent, self.got, self.home = shard, whole, sent, got, home
        self.size = shard.shape[0]

    def rows(self, mask, first=0, count=None):
        start = pl.multiple_of(partner(mask) * self.size + first, self.size // 2)
        return self.whole.at[pl.ds(start, self.size if count is None else count), :]

    def push(self, slot):
        half = self.size // 2
        mask, src, dst = (
            (2, self.shard, self.rows(0)),
            (4, self.shard, self.rows(0)),
            (2, self.rows(4, 0, half), self.rows(4, 0, half)),
            (4, self.rows(2, half, half), self.rows(2, half, half)),
            (1, self.shard, self.rows(0)),
            (1, self.rows(2), self.rows(2)),
            (1, self.rows(4), self.rows(4)),
            (1, self.rows(6), self.rows(6)),
        )[slot]
        return pltpu.make_async_remote_copy(
            src_ref=src, dst_ref=dst, send_sem=self.sent.at[slot], recv_sem=self.got.at[slot],
            device_id={"seq": partner(mask)}, device_id_type=MESH,
        )

    def local(self):
        return pltpu.make_async_copy(self.shard, self.rows(0), self.home.at[0])

    def start(self):
        self.local().start()
        for slot in (0, 1, 4):
            self.push(slot).start()

    def middle(self):
        for slot in (0, 1):
            self.push(slot).wait_recv()
        for slot in (2, 3, 5, 6):
            self.push(slot).start()

    def late(self):
        for slot in (2, 3):
            self.push(slot).wait_recv()
        self.push(7).start()

    def traded(self, slots):
        for slot in slots:
            self.push(slot).wait_recv()

    def settle(self):
        for slot in range(8):
            self.push(slot).wait_send()

    def end(self):
        self.traded((4, 5, 6, 7))
        self.settle()
        self.local().wait()


class Scatter:
    masks = (2, 4, 6)
    semaphores = [pltpu.SemaphoreType.DMA((3,)), pltpu.SemaphoreType.DMA((3,))]

    def __init__(self, parts, got, sent, came):
        self.parts, self.got, self.sent, self.came = parts, got, sent, came

    def push(self, k):
        return pltpu.make_async_remote_copy(
            src_ref=self.parts.at[k + 1], dst_ref=self.got.at[k], send_sem=self.sent.at[k],
            recv_sem=self.came.at[k], device_id={"seq": partner(2 * k + 2)}, device_id_type=MESH,
        )

    def start(self):
        for k in range(3):
            self.push(k).start()

    def end(self):
        for k in range(3):
            self.push(k).wait()


def load(step, pairs, sems):
    @pl.when(step == 0)
    def _():
        copies = [pltpu.make_async_copy(a, b, sems.at[n]) for n, (a, b) in enumerate(pairs)]
        for copy in copies:
            copy.start()
        for copy in copies:
            copy.wait()


def mm(a, b):
    return jnp.dot(a.astype(low), b.astype(low), preferred_element_type=full)


def mm_nt(a, b):
    return lax.dot_general(
        a.astype(low), b.astype(low), (((1,), (1,)), ((), ())), preferred_element_type=full
    )


def mm_tn(a, b):
    return lax.dot_general(
        a.astype(low), b.astype(low), (((0,), (0,)), ((), ())), preferred_element_type=full
    )


def exact(a, b):
    return jnp.dot(a, b, precision=lax.Precision.HIGHEST, preferred_element_type=full)


def sigmoid(t):
    return 1.0 / (1.0 + jnp.exp(-t))


def softplus(t):
    return jnp.maximum(t, 0.0) + jnp.log(1.0 + jnp.exp(-jnp.abs(t)))


def iotas(size):
    return (
        lax.broadcasted_iota(jnp.int32, (size, size), 0),
        lax.broadcasted_iota(jnp.int32, (size, size), 1),
    )


def conv_sum(ext, taps, meta, first, width, rows):
    total = taps[3:4, first : first + width] * ext[8 : 8 + rows, first : first + width]
    for lag in (1, 2, 3):
        total += (
            taps[3 - lag : 4 - lag, first : first + width]
            * meta[:, lag : lag + 1]
            * ext[8 - lag : 8 - lag + rows, first : first + width]
        )
    return total


def gates(ab, params, heads):
    log_decay = params[0:1, :] * softplus(ab + params[1:2, :])
    beta = sigmoid(ab)
    return log_decay, beta


def decay_parts(cum, cum_t, h, same_low, strict_low, meta):
    size = cum.shape[0]
    col = cum[:, h : h + 1]
    row = cum_t[h : h + 1, :]
    lower = jnp.where(same_low, jnp.exp(jnp.minimum(col - row, 0.0)), 0.0)
    strict = jnp.where(strict_low, lower, 0.0)
    last = cum[size - 1 : size, h : h + 1]
    from_start = jnp.exp(col) * meta[:, 4:5]
    to_end = jnp.exp(last - col) * meta[:, 5:6]
    carried = jnp.exp(last) * meta[size - 1 : size, 4:5]
    return lower, strict, from_start, to_end, carried


def unit_lower_inverse(strict, rows, cols):
    size = strict.shape[0]
    power = jnp.where((rows >> 3) == (cols >> 3), -strict, 0.0)
    inverse = jnp.where(rows == cols, 1.0, power)
    power = mm(power, power)
    inverse = inverse + mm(inverse, power)
    power = mm(power, power)
    inverse = inverse + mm(inverse, power)
    shift = 3
    while (1 << shift) < size:
        off = jnp.where(
            ((rows >> (shift + 1)) == (cols >> (shift + 1))) & ((rows >> shift) != (cols >> shift)),
            strict,
            0.0,
        )
        inverse = inverse - mm(inverse, mm(off, inverse))
        shift += 1
    return inverse


def inverses(stricts, rows, cols):
    size = stricts[0].shape[0]
    near = (rows >> 3) == (cols >> 3)
    powers = [jnp.where(near, -a, 0.0) for a in stricts]
    result = [jnp.where(rows == cols, 1.0, p) for p in powers]
    for _ in range(2):
        powers = [mm(p, p) for p in powers]
        result = [t + mm(t, p) for t, p in zip(result, powers)]
    shift = 3
    while (1 << shift) < size:
        pick = ((rows >> (shift + 1)) == (cols >> (shift + 1))) & (
            (rows >> shift) != (cols >> shift)
        )
        offs = [mm(jnp.where(pick, a, 0.0), t) for a, t in zip(stricts, result)]
        result = [t - mm(t, o) for t, o in zip(result, offs)]
        shift += 1
    return result


def masks(meta, segrow):
    size = meta.shape[0]
    rows, cols = iotas(size)
    same = meta[:, 0:1] == segrow[0:1, :]
    return rows, cols, same & (rows >= cols), same & (rows > cols)


def unit(post):
    return lax.rsqrt(jnp.sum(post * post, axis=-1, keepdims=True) + 1e-06)


def forward_kernel(
    heads, key, value, gathering,
    pre_ref, ab_ref, meta_ref, segrow_ref, edge_ref, taps_ref, params_ref, *refs
):
    step = pl.program_id(0)
    steps = pl.num_programs(0)
    if gathering:
        shard_ref, out_ref, through_ref, states_ref, inverse_ref, end_ref, whole_ref, ext, state, *sems = refs
        moving = Gather(shard_ref, whole_ref, *sems)

        @pl.when(step == 0)
        def _():
            greet(Gather.masks)
            moving.start()

        @pl.when(step == steps - 2)
        def _():
            moving.middle()

    else:
        out_ref, through_ref, states_ref, inverse_ref, end_ref, ext, state = refs
    size = pre_ref.shape[0]
    wide = value + key
    kfirst, vfirst = heads * key, 2 * heads * key

    @pl.when(step == 0)
    def _():
        ext[0:8, :] = edge_ref[...].astype(full)
        rows, cols = iotas(key)
        eye = (rows == cols).astype(full)
        for h in range(heads):
            state[h, :, :value] = jnp.zeros((key, value), full)
            state[h, :, value:] = eye

    @pl.when(step > 0)
    def _():
        ext[0:8, :] = ext[size : size + 8, :]

    ext[8:, :] = pre_ref[...].astype(full)
    meta = meta_ref[...]
    log_decay, beta = gates(ab_ref[...], params_ref, heads)
    rows, cols, same_low, strict_low = masks(meta, segrow_ref)
    cum = exact((rows >= cols).astype(full), log_decay)
    cum_t = cum.T
    qs, ks, vs, lowers, stricts, fs, es, cs = [], [], [], [], [], [], [], []
    for h in range(heads):
        u = conv_sum(ext, taps_ref, meta, h * key, key, size)
        post = u * sigmoid(u)
        q = (post * unit(post)).astype(low)
        u = conv_sum(ext, taps_ref, meta, kfirst + h * key, key, size)
        post = u * sigmoid(u)
        k = (post * unit(post)).astype(low)
        u = conv_sum(ext, taps_ref, meta, vfirst + h * value, value, size)
        v = u * sigmoid(u)
        lower, strict, f, e, c = decay_parts(cum, cum_t, h, same_low, strict_low, meta)
        bcol = beta[:, heads + h : heads + h + 1]
        gram = mm_nt(jnp.concatenate([k, q], axis=0), k)
        qs.append(q), ks.append(k), vs.append(v), fs.append(f), es.append(e), cs.append(c)
        stricts.append(bcol * strict * gram[:size])
        lowers.append(lower * gram[size:])
    ts = inverses(stricts, rows, cols)
    for h in range(heads):
        bcol = beta[:, heads + h : heads + h + 1]
        s = state[h]
        states_ref[0, h] = s.astype(low)
        t = ts[h].astype(low)
        inverse_ref[0, h] = t
        ks_s = mm(ks[h], s)
        fb = fs[h] * bcol
        target = jnp.concatenate(
            [bcol * vs[h] - fb * ks_s[:, :value], -fb * ks_s[:, value:]], axis=1
        )
        delta = mm(t, target).astype(low)
        left = jnp.concatenate([(fs[h] * qs[h].astype(full)).astype(low), lowers[h].astype(low)], axis=1)
        out = mm(left, jnp.concatenate([s.astype(low), delta], axis=0))
        out_ref[:, h * value : (h + 1) * value] = out[:, :value]
        through_ref[:, h * key : (h + 1) * key] = out[:, value:].astype(low)
        ke = es[h] * ks[h].astype(full)
        s = cs[h] * s + mm_tn(ke, delta)
        state[h] = s
        end_ref[h] = s.astype(low)

    if gathering:

        @pl.when(step == steps - 1)
        def _():
            moving.late()
            moving.end()


def forward_chain(pre, ab, meta, segrow, edge, taps, params, heads, key, value, shard=None):
    gathering = shard is not None
    moved = [jax.ShapeDtypeStruct((shard.shape[0] * NEAR, shard.shape[1]), low)] if gathering else []
    extra = dict(collective_id=5, has_side_effects=True) if gathering else {}
    length = pre.shape[0]
    blocks = length // BLOCK
    width = pre.shape[1]
    wide = value + key
    return pl.pallas_call(
        partial(forward_kernel, heads, key, value, gathering),
        grid=(blocks,),
        in_specs=[
            pl.BlockSpec((BLOCK, width), lambda n: (n, 0)),
            pl.BlockSpec((BLOCK, LANES), lambda n: (n, 0)),
            pl.BlockSpec((BLOCK, LANES), lambda n: (n, 0)),
            pl.BlockSpec((8, BLOCK), lambda n: (0, n)),
            pl.BlockSpec((8, width), lambda n: (0, 0)),
            pl.BlockSpec(taps.shape, lambda n: (0, 0)),
            pl.BlockSpec((8, LANES), lambda n: (0, 0)),
        ]
        + [pl.BlockSpec(**ANY) for _ in moved],
        out_specs=[
            pl.BlockSpec((BLOCK, heads * value), lambda n: (n, 0)),
            pl.BlockSpec((BLOCK, heads * key), lambda n: (n, 0)),
            pl.BlockSpec((1, heads, key, wide), lambda n: (n, 0, 0, 0)),
            pl.BlockSpec((1, heads, BLOCK, BLOCK), lambda n: (n, 0, 0, 0)),
            pl.BlockSpec((heads, key, wide), lambda n: (0, 0, 0)),
        ]
        + [pl.BlockSpec(**ANY) for _ in moved],
        out_shape=[
            jax.ShapeDtypeStruct((length, heads * value), full),
            jax.ShapeDtypeStruct((length, heads * key), low),
            jax.ShapeDtypeStruct((blocks, heads, key, wide), low),
            jax.ShapeDtypeStruct((blocks, heads, BLOCK, BLOCK), low),
            jax.ShapeDtypeStruct((heads, key, wide), low),
        ]
        + moved,
        scratch_shapes=[
            pltpu.VMEM((BLOCK + 8, width), full),
            pltpu.VMEM((heads, key, wide), full),
        ]
        + (Gather.semaphores if gathering else []),
        compiler_params=pltpu.CompilerParams(vmem_limit_bytes=48 * MIB, **extra),
        name="chain_forward",
    )(pre, ab, meta, segrow, edge, taps, params, *([shard] if gathering else []))


def gate_back_kernel(heads, key, value, dz_ref, mixed_ref, gate_ref, gain_ref, through_ref, whole_ref,
                     dgz_ref, do_ref, gain_grad_ref, adjoint_ref, weights, dy_ref, sems):
    load(pl.program_id(0), [(whole_ref.at[:, heads * value :], weights)], sems)

    @pl.when(pl.program_id(0) == 0)
    def _():
        gain_grad_ref[...] = jnp.zeros_like(gain_grad_ref)
        adjoint_ref[...] = jnp.zeros_like(adjoint_ref)

    rows = dz_ref.shape[0]
    gain = gain_ref[0:1, :]
    dy_ref[...] = mm(dz_ref[...], weights[...])
    for h in range(heads):
        cols = slice(h * value, (h + 1) * value)
        o = mixed_ref[:, cols].astype(full)
        s3 = lax.rsqrt(jnp.mean(o * o, axis=-1, keepdims=True) + 1e-05)
        n3 = o * s3
        gz = gate_ref[:, cols]
        sig = sigmoid(gz)
        sg = gz * sig
        dy = dy_ref[:, cols]
        dyn = dy * n3
        part = dyn * sg
        gain_grad_ref[...] += jnp.sum(part.reshape(rows // 8, 8, value), axis=0)
        dgz_ref[:, cols] = (dyn * gain * (sig * (1.0 + gz * (1.0 - sig)))).astype(low)
        dn3 = dy * gain * sg
        do = s3 * (dn3 - n3 * jnp.mean(dn3 * n3, axis=-1, keepdims=True))
        do = do.astype(low)
        do_ref[:, cols] = do
        adjoint_ref[h] += mm_tn(through_ref[:, h * key : (h + 1) * key], do)


def gate_back(dz, w_mix, mixed, gate, gain, through, heads, key, value, rows=256):
    length, width = dz.shape
    wide = heads * value
    return pl.pallas_call(
        partial(gate_back_kernel, heads, key, value),
        grid=(length // rows,),
        in_specs=[
            pl.BlockSpec((rows, width), lambda n: (n, 0)),
            pl.BlockSpec((rows, wide), lambda n: (n, 0)),
            pl.BlockSpec((rows, wide), lambda n: (n, 0)),
            pl.BlockSpec((1, value), lambda n: (0, 0)),
            pl.BlockSpec((rows, heads * key), lambda n: (n, 0)),
        ]
        + [pl.BlockSpec(**ANY)],
        out_specs=[
            pl.BlockSpec((rows, wide), lambda n: (n, 0)),
            pl.BlockSpec((rows, wide), lambda n: (n, 0)),
            pl.BlockSpec((8, value), lambda n: (0, 0)),
            pl.BlockSpec((heads, key, value), lambda n: (0, 0, 0)),
        ],
        out_shape=[
            jax.ShapeDtypeStruct((length, wide), low),
            jax.ShapeDtypeStruct((length, wide), low),
            jax.ShapeDtypeStruct((8, value), full),
            jax.ShapeDtypeStruct((heads, key, value), full),
        ],
        scratch_shapes=[
            pltpu.VMEM((width, wide), low),
            pltpu.VMEM((rows, wide), full),
            pltpu.SemaphoreType.DMA((1,)),
        ],
        compiler_params=pltpu.CompilerParams(vmem_limit_bytes=48 * MIB),
        name="gate_back",
    )(dz, mixed, gate, gain, through, w_mix)


def lane_sum(array):
    return jnp.sum(array, axis=-1, keepdims=True)


def backward_kernel(
    heads, key, value, devices, masks_of, scattering,
    pre_ref, tail_ref, ab_ref, meta_ref, segrow_ref, edge_ref, edge_meta_ref, taps_ref, params_ref,
    states_ref, inverse_ref, state_in_ref, do_ref, ends_ref, *refs
):
    step = pl.program_id(0)
    steps = pl.num_programs(0)
    pieces, refs = refs[: len(masks_of)], list(refs[len(masks_of) :])
    parts_ref = refs.pop(0) if scattering else None
    dpre_ref, dab_ref, halo_ref, taps_grad_ref, params_grad_ref = refs[:5]
    refs = refs[5:]
    got_ref = refs.pop(0) if scattering else None
    ext, du, adjoint, adjoints, home, *sems = refs
    if scattering:
        moving = Scatter(parts_ref, got_ref, *sems)

        @pl.when(step == 0)
        def _():
            greet(Scatter.masks)
            moving.start()

    size = pre_ref.shape[0]
    kfirst, vfirst = heads * key, 2 * heads * key

    @pl.when(step == 0)
    def _():
        adjoint[...] = jnp.zeros_like(adjoint)
        tall = heads * key
        copies = []
        for n, (mask, ref) in enumerate(zip(masks_of, pieces)):
            first = 0 if mask is None else pl.multiple_of(partner(mask) * tall, tall)
            target = adjoints.at[pl.ds(first, ref.shape[0]), :]
            copies.append(pltpu.make_async_copy(ref, target, home.at[n]))
        for copy in copies:
            copy.start()
        for copy in copies:
            copy.wait()

        def one(k, carry):
            j = devices - 1 - k
            for h in range(heads):
                rows = pl.ds(pl.multiple_of(j * tall + h * key, key), key)
                adjoint[h] = (
                    mm_tn(ends_ref[j, h, :, value:], adjoint[h]) + adjoints[rows, :].astype(full)
                )
            return carry

        lax.fori_loop(0, devices - 1 - lax.axis_index("seq"), one, 0)
        du[8 + size :, :] = jnp.zeros((8, du.shape[1]), full)
        taps_grad_ref[...] = jnp.zeros_like(taps_grad_ref)
        params_grad_ref[...] = jnp.zeros_like(params_grad_ref)

    @pl.when(step > 0)
    def _():
        du[8 + size :, :] = du[8:16, :]

    du[0:8, :] = jnp.zeros((8, du.shape[1]), full)

    @pl.when(step < steps - 1)
    def _():
        ext[0:8, :] = tail_ref[8:16, :].astype(full)

    @pl.when(step == steps - 1)
    def _():
        ext[0:8, :] = edge_ref[...].astype(full)

    ext[8:, :] = pre_ref[...].astype(full)
    meta = meta_ref[...]
    ab = ab_ref[...]
    log_decay, beta = gates(ab, params_ref, heads)
    rows, cols, same_low, strict_low = masks(meta, segrow_ref)
    cum = exact((rows >= cols).astype(full), log_decay)
    cum_t = cum.T
    lane = lax.broadcasted_iota(jnp.int32, (size, LANES), 1)
    row8 = lax.broadcasted_iota(jnp.int32, (8, size), 0)
    dcum = jnp.zeros((size, LANES), full)
    dcum_rows = jnp.zeros((8, size), full)
    dcum_last = jnp.zeros((1, LANES), full)
    dbeta = jnp.zeros((size, LANES), full)
    lane1 = lax.broadcasted_iota(jnp.int32, (1, LANES), 1)

    for h in range(heads):
        qcols = slice(h * key, (h + 1) * key)
        kcols = slice(kfirst + h * key, kfirst + (h + 1) * key)
        vcols = slice(vfirst + h * value, vfirst + (h + 1) * value)
        uq = conv_sum(ext, taps_ref, meta, h * key, key, size)
        sq = sigmoid(uq)
        pq = uq * sq
        rq = unit(pq)
        qf = pq * rq
        q = qf.astype(low)
        uk = conv_sum(ext, taps_ref, meta, kfirst + h * key, key, size)
        sk = sigmoid(uk)
        pk = uk * sk
        rk = unit(pk)
        kf = pk * rk
        k = kf.astype(low)
        uv = conv_sum(ext, taps_ref, meta, vfirst + h * value, value, size)
        sv = sigmoid(uv)
        v = uv * sv
        lower, strict, f, e, c = decay_parts(cum, cum_t, h, same_low, strict_low, meta)
        b = beta[:, heads + h : heads + h + 1]
        kq = jnp.concatenate([k, q], axis=0)
        gram = mm_nt(kq, k)
        kk, qk = gram[:size], gram[size:]
        stored = states_ref[0, h]
        s = stored[:, :value].astype(full) + mm(stored[:, value:], state_in_ref[h])
        slow = s.astype(low)
        kqs = mm(kq, slow)
        ks, qs = kqs[:size], kqs[size:]
        rest = v - f * ks
        t = inverse_ref[0, h]
        delta = mm(t, b * rest).astype(low)
        do = do_ref[:, h * value : (h + 1) * value]
        dof = do.astype(full)
        ds = adjoint[h]
        dslow = ds.astype(low)
        ke = (e * kf).astype(low)
        p = lower * qk
        left = jnp.concatenate([p.T.astype(low), ke], axis=1)
        ddelta = mm(left, jnp.concatenate([do, dslow], axis=0))
        dtarget = mm_tn(t, ddelta)
        outer = mm_nt(jnp.concatenate([do, dtarget.astype(low)], axis=0), delta)
        dp, dan = outer[:size], outer[size:]
        eg = lower * dp
        hn = -strict * dan
        hg = b * hn
        x = eg * qk
        hk = hn * kk
        g1 = (b * f) * dtarget
        fdo = f * dof
        pair = jnp.concatenate([fdo.astype(low), (-g1).astype(low)], axis=0)
        both = mm_nt(pair, slow)
        dq = both[:size] + mm(eg, k)
        dsk = e * mm_nt(delta, dslow)
        left = jnp.concatenate([(hg + hg.T).astype(low), eg.T.astype(low)], axis=1)
        dk = both[size:] + dsk + mm(left, kq)
        dv = b * dtarget
        z = lane_sum(kf * dsk)
        dfrom = lane_sum(dof * qs) - b * lane_sum(dtarget * ks)
        hrow = lane_sum(hk)
        db = hrow + lane_sum(dtarget * rest)
        dbeta = dbeta + jnp.where(lane == heads + h, db, 0.0)
        dcum = dcum + jnp.where(lane == h, lane_sum(x) + b * hrow + f * dfrom - z, 0.0)
        drow = jnp.sum(x + b * hk, axis=0, keepdims=True)
        dcum_rows = dcum_rows + jnp.where(row8 == h, drow, 0.0)
        dlast = jnp.sum(z, axis=0, keepdims=True) + c * jnp.sum(
            lane_sum(ds * s), axis=0, keepdims=True
        )
        dcum_last = dcum_last + jnp.where(lane1 == h, dlast, 0.0)
        adjoint[h] = c * ds + mm_tn(jnp.concatenate([q, k], axis=0), pair)

        dpq = rq * (dq - qf * lane_sum(dq * qf))
        du[8 : 8 + size, qcols] = dpq * (sq * (1.0 + uq * (1.0 - sq)))
        dpk = rk * (dk - kf * lane_sum(dk * kf))
        du[8 : 8 + size, kcols] = dpk * (sk * (1.0 + uk * (1.0 - sk)))
        du[8 : 8 + size, vcols] = dv * (sv * (1.0 + uv * (1.0 - sv)))

    padded = jnp.concatenate([dcum_rows, jnp.zeros((LANES - 8, size), full)], axis=0)
    rowi = lax.broadcasted_iota(jnp.int32, (size, LANES), 0)
    dcum = dcum - padded.T + jnp.where(rowi == size - 1, dcum_last, 0.0)
    dlog = exact((rows <= cols).astype(full), dcum)
    dga = dlog * params_ref[0:1, :] * sigmoid(ab + params_ref[1:2, :])
    is_decay = lane < heads
    dga = jnp.where(is_decay, dga, 0.0)
    params_grad_ref[0:8, :] += jnp.sum(dga.reshape(size // 8, 8, LANES), axis=0)
    decay_part = jnp.where(is_decay, dlog * log_decay, 0.0)
    params_grad_ref[8:16, :] += jnp.sum(decay_part.reshape(size // 8, 8, LANES), axis=0)
    dab_ref[...] = jnp.where(is_decay, dga, dbeta * beta * (1.0 - beta)).astype(low)

    width = du.shape[1]
    for first in range(0, width, 512):
        cs = slice(first, first + 512)
        own = du[8 : 8 + size, cs]
        total = taps_ref[3:4, cs] * own
        taps_grad_ref[24:32, cs] += jnp.sum(
            (own * ext[8 : 8 + size, cs]).reshape(size // 8, 8, 512), axis=0
        )
        for lag in (1, 2, 3):
            total += taps_ref[3 - lag : 4 - lag, cs] * meta[:, 5 + lag : 6 + lag] * du[
                8 + lag : 8 + lag + size, cs
            ]
            taps_grad_ref[8 * (3 - lag) : 8 * (4 - lag), cs] += jnp.sum(
                (own * meta[:, lag : lag + 1] * ext[8 - lag : 8 - lag + size, cs]).reshape(
                    size // 8, 8, 512
                ),
                axis=0,
            )
        dpre_ref[:, cs] = total.astype(low)

    @pl.when(step == steps - 1)
    def _():
        edge_meta = edge_meta_ref[...]
        halo = jnp.zeros(halo_ref.shape, full)
        for lag in (1, 2, 3):
            halo += taps_ref[3 - lag : 4 - lag, :] * edge_meta[:, 5 + lag : 6 + lag] * du[
                lag : 8 + lag, :
            ]
        halo_ref[...] = halo
        if scattering:
            moving.end()


def backward_chain(pre, ab, meta, segrow, edge, edge_meta, taps, params, states, inverse,
                   state_in, do, ends, adjoints, heads, key, value, parts=None):
    scattering = parts is not None
    moved = [jax.ShapeDtypeStruct((3,) + parts.shape[1:], low)] if scattering else []
    extra = dict(collective_id=6, has_side_effects=True) if scattering else {}
    masks_of = [mask for mask, _ in adjoints]
    devices = ends.shape[0]
    length, width = pre.shape
    blocks = length // BLOCK
    wide = value + key
    once = dict(pipeline_mode=pl.Buffered(1))
    last = blocks - 1
    return pl.pallas_call(
        partial(backward_kernel, heads, key, value, devices, masks_of, scattering),
        grid=(blocks,),
        in_specs=[
            pl.BlockSpec((BLOCK, width), lambda n: (last - n, 0)),
            pl.BlockSpec((16, width), lambda n: (jnp.maximum((last - n) * (BLOCK // 16) - 1, 0), 0)),
            pl.BlockSpec((BLOCK, LANES), lambda n: (last - n, 0)),
            pl.BlockSpec((BLOCK, LANES), lambda n: (last - n, 0)),
            pl.BlockSpec((8, BLOCK), lambda n: (0, last - n)),
            pl.BlockSpec((8, width), lambda n: (0, 0)),
            pl.BlockSpec((8, LANES), lambda n: (0, 0)),
            pl.BlockSpec(taps.shape, lambda n: (0, 0)),
            pl.BlockSpec((8, LANES), lambda n: (0, 0)),
            pl.BlockSpec((1, heads, key, wide), lambda n: (last - n, 0, 0, 0)),
            pl.BlockSpec((1, heads, BLOCK, BLOCK), lambda n: (last - n, 0, 0, 0)),
            pl.BlockSpec((heads, key, value), lambda n: (0, 0, 0)),
            pl.BlockSpec((BLOCK, heads * value), lambda n: (last - n, 0)),
            pl.BlockSpec(ends.shape, lambda n: (0, 0, 0, 0), **once),
        ]
        + [pl.BlockSpec(**ANY) for _ in (*adjoints, *moved)],
        out_specs=[
            pl.BlockSpec((BLOCK, width), lambda n: (last - n, 0)),
            pl.BlockSpec((BLOCK, LANES), lambda n: (last - n, 0)),
            pl.BlockSpec((8, width), lambda n: (0, 0)),
            pl.BlockSpec((32, width), lambda n: (0, 0)),
            pl.BlockSpec((16, LANES), lambda n: (0, 0)),
        ]
        + [pl.BlockSpec(**ANY) for _ in moved],
        out_shape=[
            jax.ShapeDtypeStruct((length, width), low),
            jax.ShapeDtypeStruct((length, LANES), low),
            jax.ShapeDtypeStruct((8, width), full),
            jax.ShapeDtypeStruct((32, width), full),
            jax.ShapeDtypeStruct((16, LANES), full),
        ]
        + moved,
        scratch_shapes=[
            pltpu.VMEM((BLOCK + 8, width), full),
            pltpu.VMEM((BLOCK + 16, width), full),
            pltpu.VMEM((heads, key, value), full),
            pltpu.VMEM((devices * heads * key, value), low),
            pltpu.SemaphoreType.DMA((len(adjoints),)),
        ]
        + (Scatter.semaphores if scattering else []),
        compiler_params=pltpu.CompilerParams(vmem_limit_bytes=56 * MIB, **extra),
        name="chain_backward",
    )(pre, pre, ab, meta, segrow, edge, edge_meta, taps, params, states, inverse, state_in, do, ends,
      *[a for _, a in adjoints], *([parts] if scattering else []))


def segment_tables(doc_lengths, shard, length):
    starts = jnp.cumsum(doc_lengths, dtype=jnp.int32) - doc_lengths
    positions = shard * length + jnp.arange(-16, length + 8, dtype=jnp.int32)
    seg = jnp.sum((starts[None, :] <= positions[:, None]).astype(jnp.int32), axis=1)
    own = seg[16 : 16 + length]

    def lanes(first, count):
        base = seg[first : first + count]
        back = [seg[first - l : first - l + count] == base for l in (1, 2, 3)]
        ahead = [seg[first + l : first + l + count] == base for l in (1, 2, 3)]
        return base, back, ahead

    base, back, ahead = lanes(16, length)
    blocks = own.reshape(-1, BLOCK)
    before = seg[15 : 15 + length : BLOCK]
    alive = (blocks == before[:, None]).reshape(-1)
    to_last = (blocks == blocks[:, -1:]).reshape(-1)
    columns = [base, *back, alive, to_last, *ahead]
    meta = jnp.stack([a.astype(full) for a in columns], axis=1)
    meta = jnp.pad(meta, ((0, 0), (0, LANES - meta.shape[1])))
    base, back, ahead = lanes(8, 8)
    columns = [base, *back, base, base, *ahead]
    edge_meta = jnp.stack([a.astype(full) for a in columns], axis=1)
    edge_meta = jnp.pad(edge_meta, ((0, 0), (0, LANES - edge_meta.shape[1])))
    segrow = jnp.broadcast_to(own.astype(full)[None, :], (8, length))
    return meta, edge_meta, segrow


ROWS = 256
PIECE = 32
HOP = 2
EACH = ROWS // PIECE
AHEAD = 1 + (EACH - 1 + 3 * HOP) // EACH
RING = AHEAD + 1


def exchanged(block, mask):
    return lax.ppermute(block, "seq", [(i, i ^ mask) for i in range(lax.axis_size("seq"))])


def spread(shard):
    if lax.axis_size("seq") != NEAR:
        return [(None, lax.all_gather(shard, "seq", axis=0, tiled=True))]
    own = [(0, shard)] + [(mask, exchanged(shard, mask)) for mask in (2, 4, 6)]
    return own + [(mask + 1, exchanged(a, 1)) for mask, a in own]


def line_scratch(length, width):
    pieces = length // PIECE
    return [
        pltpu.VMEM((RING, ROWS, width), low),
        pltpu.VMEM((length, width), low),
        pltpu.VMEM((length, width), low),
        pltpu.SemaphoreType.DMA((pieces,)),
        pltpu.SemaphoreType.DMA((pieces,)),
        pltpu.SemaphoreType.DMA((pieces,)),
        pltpu.SemaphoreType.DMA((pieces,)),
    ]


def line_sum(step, last, stages, finish, scratch):
    own, from_left, from_right, got_left, got_right, sent_right, sent_left = scratch
    place = lax.axis_index("head")
    length, width = from_left.shape
    blocks, pieces = length // ROWS, length // PIECE
    left_there, right_there = place > 0, place < last

    def rows(piece):
        return pl.ds(pl.multiple_of(piece * PIECE, PIECE), PIECE)

    def hop(piece, rightwards):
        kept, sent, got, to = (
            (from_left, sent_right, got_left, place + 1)
            if rightwards
            else (from_right, sent_left, got_right, place - 1)
        )
        return pltpu.make_async_remote_copy(
            src_ref=kept.at[rows(piece)],
            dst_ref=kept.at[rows(piece)],
            send_sem=sent.at[piece],
            recv_sem=got.at[piece],
            device_id={"head": to},
            device_id_type=MESH,
        )

    def own_piece(piece):
        slot = lax.rem(piece // EACH, RING)
        first = pl.multiple_of(lax.rem(piece, EACH) * PIECE, PIECE)
        return own[slot, pl.ds(first, PIECE), :].astype(full)

    @pl.when(step == 0)
    def _():
        @pl.when(place == 0)
        def _():
            from_left[...] = jnp.zeros_like(from_left)

        @pl.when(place == last)
        def _():
            from_right[...] = jnp.zeros_like(from_right)

    def one(q, carry):
        now = (step - 1) * EACH + q
        for rightwards in (True, False):
            came, more = (left_there, right_there) if rightwards else (right_there, left_there)
            kept = from_left if rightwards else from_right
            piece = now - HOP * (place if rightwards else last - place)

            @pl.when((piece >= 0) & (piece < pieces))
            def _():
                @pl.when(came)
                def _():
                    hop(piece, rightwards).wait_recv()

                @pl.when(more)
                def _():
                    kept[rows(piece), :] = (
                        own_piece(piece) + kept[rows(piece), :].astype(full)
                    ).astype(low)
                    hop(piece, rightwards).start()

        return carry

    done = 0
    for n, stage in enumerate(stages):

        @pl.when(step < blocks)
        def _(n=n, stage=stage):
            value = stage()
            if n == len(stages) - 1:
                own[lax.rem(step, RING)] = value.astype(low)

        until = EACH * (n + 1) // len(stages)
        lax.fori_loop(done, until, one, 0)
        done = until

    @pl.when(step >= AHEAD)
    def _():
        block = step - AHEAD
        span = pl.ds(pl.multiple_of(block * ROWS, ROWS), ROWS)
        total = from_left[span, :].astype(full) + from_right[span, :].astype(full)
        twice = jnp.where(left_there & right_there, 1.0, 0.0)
        finish(total - twice * own[lax.rem(block, RING)].astype(full))

    @pl.when(step == blocks + AHEAD - 1)
    def _():
        def settle(piece, carry):
            @pl.when(right_there)
            def _():
                hop(piece, True).wait_send()

            @pl.when(left_there)
            def _():
                hop(piece, False).wait_send()

            return carry

        lax.fori_loop(0, pieces, settle, 0)


def union(kinds):
    return sorted({mask for kind in kinds for mask in kind.masks})


def line_call(kernel, name, collective, length, width, last, resident, weights, entering, leaving, outs,
              scratch, gathers=(), scatters=()):
    blocks = length // ROWS
    steps = blocks + AHEAD

    def spec(array, stage):
        if stage == "first":
            return pl.BlockSpec((ROWS, array.shape[1]), lambda g: (jnp.minimum(g, blocks - 1), 0))
        if stage == "second":
            return pl.BlockSpec((ROWS, array.shape[1]), lambda g: (jnp.maximum(g - AHEAD, 0), 0))
        rank = len(array.shape)
        return pl.BlockSpec(array.shape, lambda g: (0,) * rank, **ONE)

    in_specs = [spec(a, "all") for a in resident]
    in_specs += [pl.BlockSpec(**ANY) for _ in (*weights, *gathers, *scatters)]
    in_specs += [spec(a, "first") for a in entering] + [spec(a, "second") for a in leaving]
    shapes = [jax.ShapeDtypeStruct(shape, dtype) for shape, dtype, _ in outs]
    out_specs = [
        spec(s, stage) if stage != "all" else pl.BlockSpec(s.shape, lambda g, r=len(s.shape): (0,) * r)
        for s, (_, _, stage) in zip(shapes, outs)
    ]
    moved = [jax.ShapeDtypeStruct((a.shape[0] * NEAR, a.shape[1]), low) for a in gathers]
    moved += [jax.ShapeDtypeStruct((3,) + a.shape[1:], low) for a in scatters]
    kinds = [Gather] * len(gathers) + [Scatter] * len(scatters)
    held = [pltpu.VMEM(a.shape, low) for a in weights] + [pltpu.SemaphoreType.DMA((len(weights),))]
    held += [s for kind in kinds for s in kind.semaphores]

    def body(*refs):
        refs = list(refs)

        def take(n):
            head, refs[:] = refs[:n], refs[n:]
            return head

        own_in, heavy = take(len(resident)), take(len(weights))
        sources = take(len(kinds))
        chunks = take(len(entering) + len(leaving))
        own_out, targets = take(len(outs)), take(len(moved))
        own_scratch = take(len(scratch) + 7)
        matrices, (sems,) = take(len(weights)), take(1)
        carried = [kind(a, b, *take(len(kind.semaphores))) for kind, a, b in zip(kinds, sources, targets)]
        step = pl.program_id(0)

        @pl.when(step == 0)
        def _():
            greet(union(kinds), last)
            for c in carried:
                c.start()

        load(step, list(zip(heavy, matrices)), sems)
        for at, turn in ((steps - 3, "middle"), (steps - 1, "late")):

            @pl.when(step == at)
            def _(turn=turn):
                for c in carried:
                    if isinstance(c, Gather):
                        getattr(c, turn)()

        kernel(matrices, *own_in, *chunks, *own_out, *own_scratch)

        @pl.when(step == steps - 1)
        def _():
            for c in carried:
                c.end()

    return pl.pallas_call(
        body,
        grid=(steps,),
        in_specs=in_specs,
        out_specs=out_specs + [pl.BlockSpec(**ANY) for _ in moved],
        out_shape=shapes + moved,
        scratch_shapes=scratch + line_scratch(length, width) + held,
        compiler_params=pltpu.CompilerParams(
            collective_id=collective, has_side_effects=True, vmem_limit_bytes=60 * MIB
        ),
        name=name,
    )(*resident, *weights, *gathers, *scatters, *entering, *leaving)


def mixer_out_kernel(heads, key, value, last, matrices,
                     ends_ref, head_gain_ref, gain_ref,
                     first_ref, local_ref, through_ref, tokens_ref,
                     y_ref, mixed_ref, gate_ref, state_ref, middle_ref, second_ref, *scratch):
    step = pl.program_id(0)
    (weights,) = matrices
    vals = heads * value

    @pl.when(step == 0)
    def _():
        state_ref[...] = jnp.zeros_like(state_ref)

        def one(j, carry):
            for h in range(heads):
                part = ends_ref[j, h]
                state_ref[h] = mm(part[:, value:], state_ref[h]) + part[:, :value].astype(full)
            return carry

        lax.fori_loop(0, lax.axis_index("seq"), one, 0)

    def gate():
        gate_ref[...] = mm(first_ref[...], weights[:, :vals])

    def mix():
        for h in range(heads):
            cols = slice(h * value, (h + 1) * value)
            o = local_ref[:, cols] + mm(through_ref[:, h * key : (h + 1) * key], state_ref[h])
            mixed_ref[:, cols] = o
            s3 = lax.rsqrt(jnp.mean(o * o, axis=-1, keepdims=True) + 1e-05)
            gz = gate_ref[:, cols]
            y_ref[:, cols] = (o * s3 * head_gain_ref[0:1, :] * (gz * sigmoid(gz))).astype(low)

    def project():
        return mm_nt(y_ref[...], weights[:, vals:])

    def finish(total):
        middle = tokens_ref[...].astype(full) + total
        middle_ref[...] = middle
        scale = lax.rsqrt(jnp.mean(middle * middle, axis=-1, keepdims=True) + 1e-06)
        second_ref[...] = (middle * scale * gain_ref[0:1, :]).astype(low)

    line_sum(step, last, [gate, mix, project], finish, scratch)


def ffn_kernel(last, size, matrices, gain_ref,
               second_ref, cot_ref, middle_ref, cot_late_ref,
               hidden_ref, dgate_ref, dup_ref, partial_ref, dmiddle_ref, dlow_ref, gain_grad_ref,
               fg, fu, *scratch):
    step = pl.program_id(0)
    (weights,) = matrices
    w_gate, w_up, w_down = (slice(n * size, (n + 1) * size) for n in range(3))

    @pl.when(step == 0)
    def _():
        gain_grad_ref[...] = jnp.zeros_like(gain_grad_ref)

    def one():
        fg[...] = mm(second_ref[...], weights[:, w_gate])

    def two():
        fu[...] = mm(second_ref[...], weights[:, w_up])

    def three():
        g = fg[...]
        hidden = (g * sigmoid(g) * fu[...]).astype(low)
        hidden_ref[...] = hidden
        partial_ref[...] = mm_nt(hidden, weights[:, w_down]).astype(low)

    def four():
        dhid = mm(cot_ref[...], weights[:, w_down])
        g = fg[...]
        sig = sigmoid(g)
        dgate_ref[...] = (dhid * fu[...] * (sig * (1.0 + g * (1.0 - sig)))).astype(low)
        dup_ref[...] = (dhid * (g * sig)).astype(low)

    def five():
        return mm_nt(dgate_ref[...], weights[:, w_gate]) + mm_nt(dup_ref[...], weights[:, w_up])

    def finish(grad):
        middle = middle_ref[...]
        scale = lax.rsqrt(jnp.mean(middle * middle, axis=-1, keepdims=True) + 1e-06)
        norm = middle * scale
        gain_grad_ref[...] += jnp.sum((grad * norm).reshape(ROWS // 8, 8, -1), axis=0)
        weighted = grad * gain_ref[0:1, :]
        dm = cot_late_ref[...].astype(full) + scale * (
            weighted - norm * jnp.mean(weighted * norm, axis=-1, keepdims=True)
        )
        dmiddle_ref[...] = dm
        dlow_ref[...] = dm.astype(low)

    line_sum(step, last, [one, two, three, four, five], finish, scratch)


def input_grad_kernel(last, keys, vals, matrices, gain_ref,
                      dpre_ref, dgz_ref, dab_ref, tokens_ref, dmiddle_ref,
                      dtokens_ref, gain_grad_ref, part, *scratch):
    step = pl.program_id(0)
    w_in, w_mix = matrices
    wide = 2 * keys + vals

    @pl.when(step == 0)
    def _():
        gain_grad_ref[...] = jnp.zeros_like(gain_grad_ref)

    def one():
        part[...] = mm_nt(dpre_ref[...], w_in[:, :wide])

    def two():
        return (
            part[...]
            + mm_nt(dgz_ref[...], w_mix[:, :vals])
            + mm_nt(dab_ref[...], w_in[:, wide:])
        )

    def finish(grad):
        stream = tokens_ref[...].astype(full)
        scale = lax.rsqrt(jnp.mean(stream * stream, axis=-1, keepdims=True) + 1e-06)
        norm = stream * scale
        gain_grad_ref[...] += jnp.sum((grad * norm).reshape(ROWS // 8, 8, -1), axis=0)
        weighted = grad * gain_ref[0:1, :]
        dtokens_ref[...] = dmiddle_ref[...] + scale * (
            weighted - norm * jnp.mean(weighted * norm, axis=-1, keepdims=True)
        )

    line_sum(step, last, [one, two], finish, scratch)


def input_kernel(wide, last, gathering, gain_ref, tokens_ref, before_ref, shard_ref,
                 first_ref, pre_ref, ab_ref, edge_ref, whole_ref, weights, total, home, *sems):
    rows = 256
    length, width = tokens_ref.shape
    half = width // 4
    back = pltpu.make_async_copy(weights, whole_ref, home.at[0])
    if gathering:
        greet(Gather.masks)
        moving = Gather(shard_ref, weights, *sems)
        moving.start()
    else:
        copy = pltpu.make_async_copy(shard_ref, weights, home.at[1])
        copy.start()

    def normed(block):
        x = block.astype(full)
        return (x * lax.rsqrt(jnp.mean(x * x, axis=-1, keepdims=True) + 1e-06) * gain_ref[0:1, :]).astype(low)

    def norm(n, carry):
        span = pl.ds(pl.multiple_of(n * rows, rows), rows)
        first_ref[span, :] = normed(tokens_ref[span, :])
        return carry

    lax.fori_loop(0, length // rows, norm, 0)

    def add(chip, fresh, done):
        start = pl.multiple_of(chip * half, half)

        def one(n, carry):
            span = pl.ds(pl.multiple_of(n * rows, rows), rows)
            part = mm(first_ref[span, pl.ds(start, half)], weights[pl.ds(start, half), :])
            if not fresh:
                part += total[span, :]
            if done:
                pre_ref[span, :] = part[:, :wide].astype(low)
                ab_ref[span, :] = part[:, wide:]
            else:
                total[span, :] = part
            return carry

        lax.fori_loop(0, length // rows, one, 0)

    if gathering:
        moving.local().wait()
        moving.traded((4,))
        add(partner(0) // 2, True, False)
        moving.middle()
        moving.traded((5, 6))
        add(partner(2) // 2, False, False)
        moving.late()
        add(partner(4) // 2, False, False)
        moving.traded((7,))
        back.start()
        add(partner(6) // 2, False, True)
    else:
        copy.wait()
        back.start()
        for chip in range(4):
            add(chip, chip == 0, chip == 3)
    edge_ref[...] = mm(normed(before_ref[...]), weights[:, :wide]).astype(low)
    if gathering:
        moving.settle()
    back.wait()


def input_projection(tokens, before, gain, shard, wide, last):
    length, width = tokens.shape
    gathering = lax.axis_size("seq") == NEAR
    if not gathering:
        shard = lax.all_gather(shard, "seq", axis=0, tiled=True)
    columns = shard.shape[1]
    here = pl.BlockSpec(memory_space=pltpu.VMEM)
    params = dict(collective_id=4, has_side_effects=True) if gathering else {}
    return pl.pallas_call(
        partial(input_kernel, wide, last, gathering),
        in_specs=[here, here, here, pl.BlockSpec(**ANY)],
        out_specs=[here, here, here, here, pl.BlockSpec(**ANY)],
        out_shape=[
            jax.ShapeDtypeStruct((length, width), low),
            jax.ShapeDtypeStruct((length, wide), low),
            jax.ShapeDtypeStruct((length, columns - wide), full),
            jax.ShapeDtypeStruct((before.shape[0], wide), low),
            jax.ShapeDtypeStruct((width, columns), low),
        ],
        scratch_shapes=[
            pltpu.VMEM((width, columns), low),
            pltpu.VMEM((length, columns), full),
            pltpu.SemaphoreType.DMA((2,)),
        ]
        + (Gather.semaphores if gathering else []),
        compiler_params=pltpu.CompilerParams(vmem_limit_bytes=56 * MIB, **params),
        name="input_projection",
    )(gain[None, :], tokens, before, shard)


def weight_kernel(groups, adding, counts, place_ref, *refs):
    lefts, rights = refs[: counts[0]], refs[counts[0] : counts[0] + counts[1]]
    rest = refs[counts[0] + counts[1] :]
    parts = []
    n = 0
    for g, many in enumerate(groups):
        left = lefts[g][...]
        for _ in range(many):
            parts.append(mm_tn(left, rights[n][...]))
            n += 1
    first = 0
    for part in parts:
        cols = slice(first, first + part.shape[1])
        first += part.shape[1]
        if adding:
            part += rest[0][0, :, cols].astype(full)
        rest[-1][0, :, cols] = part.astype(low)


def weight_call(place, pairs, odd, count, stride, added=None, width=256):
    lefts = [a for a, _ in pairs]
    rights = [b for _, bs in pairs for b in bs]
    length = lefts[0].shape[0]
    columns = sum(b.shape[1] for b in rights)

    def pick(k, place_ref):
        return (0, jnp.bitwise_xor(place_ref[0], stride * k + odd))

    in_specs = [pl.BlockSpec((length, width), pick) for _ in lefts]
    in_specs += [pl.BlockSpec(b.shape, lambda k, p: (0, 0), **ONE) for b in rights]
    if added is not None:
        in_specs += [pl.BlockSpec((1, width, columns), lambda k, p: (k, 0, 0))]
    out_specs = [pl.BlockSpec((1, width, columns), lambda k, p: (k, 0, 0))]
    out_shape = [jax.ShapeDtypeStruct((count, width, columns), low)]
    return pl.pallas_call(
        partial(
            weight_kernel, [len(bs) for _, bs in pairs], added is not None, (len(lefts), len(rights))
        ),
        grid_spec=pltpu.PrefetchScalarGridSpec(
            num_scalar_prefetch=1, grid=(count,), in_specs=in_specs, out_specs=out_specs
        ),
        out_shape=out_shape,
        compiler_params=pltpu.CompilerParams(vmem_limit_bytes=56 * MIB),
        name="weight_grads",
    )(place, *lefts, *rights, *(() if added is None else (added,)))


def pair_sums(place, pairs):
    (away,) = weight_call(place, pairs, 1, NEAR // 2, 2)
    (sums,) = weight_call(place, pairs, 0, NEAR // 2, 2, exchanged(away, 1))
    return sums


def far_sums(sums, got):
    return sum((got[k] for k in range(3)), start=sums[0].astype(full))


def plain_sums(place, pairs):
    width = pairs[0][0].shape[1]
    (grads,) = weight_call(jnp.zeros_like(place), pairs, 0, width // 256, 1)
    return lax.psum_scatter(grads.reshape(width, -1), "seq", scatter_dimension=0, tiled=True).astype(full)


def small_kernel(count, others, part_ref, out_ref, send, got, got_far, sent, came, sent_far, came_far):
    me, row = lax.axis_index("seq"), lax.axis_index("head")
    rows, far = part_ref.shape[0], got_far.shape[2]
    barrier = pltpu.get_barrier_semaphore()

    def greet(k, carry):
        pl.semaphore_signal(
            barrier, inc=1, device_id={"seq": lax.rem(me + k, count)},
            device_id_type=pl.DeviceIdType.MESH,
        )
        return carry

    lax.fori_loop(1, count, greet, 0)
    for k in range(1, others):
        pl.semaphore_signal(
            barrier, inc=1, device_id={"head": lax.rem(row + k, others)},
            device_id_type=pl.DeviceIdType.MESH,
        )
    pl.semaphore_wait(barrier, count + others - 2)

    def along(k):
        return pltpu.make_async_remote_copy(
            src_ref=part_ref, dst_ref=got.at[me], send_sem=sent.at[k], recv_sem=came.at[k],
            device_id={"seq": lax.rem(me + k, count)}, device_id_type=pl.DeviceIdType.MESH,
        )

    def across(k):
        return pltpu.make_async_remote_copy(
            src_ref=send, dst_ref=got_far.at[row], send_sem=sent_far.at[k], recv_sem=came_far.at[k],
            device_id={"head": lax.rem(row + k, others)}, device_id_type=pl.DeviceIdType.MESH,
        )

    def start(k, carry):
        along(k).start()
        return carry

    def wait(k, carry):
        along(k).wait()
        return carry

    lax.fori_loop(1, count, start, 0)
    got[me] = part_ref[...]
    lax.fori_loop(1, count, wait, 0)

    def add(k, carry):
        out_ref[...] += got[k]
        return carry

    out_ref[...] = got[0]
    lax.fori_loop(1, count, add, 0)
    send[...] = out_ref[:, :far]
    for k in range(1, others):
        across(k).start()
    got_far[row] = send[...]
    for k in range(1, others):
        across(k).wait()
    total = got_far[0]
    for k in range(1, others):
        total += got_far[k]
    out_ref[rows - 1 :, :far] = total[rows - 1 :, :]


def small_sums(part, far):
    count, others = lax.axis_size("seq"), lax.axis_size("head")
    return pl.pallas_call(
        partial(small_kernel, count, others),
        in_specs=[pl.BlockSpec(memory_space=pltpu.VMEM)],
        out_specs=pl.BlockSpec(memory_space=pltpu.VMEM),
        out_shape=jax.ShapeDtypeStruct(part.shape, full),
        scratch_shapes=[
            pltpu.VMEM((part.shape[0], far), full),
            pltpu.VMEM((count,) + part.shape, full),
            pltpu.VMEM((others, part.shape[0], far), full),
            pltpu.SemaphoreType.DMA((count,)),
            pltpu.SemaphoreType.DMA((count,)),
            pltpu.SemaphoreType.DMA((others,)),
            pltpu.SemaphoreType.DMA((others,)),
        ],
        compiler_params=pltpu.CompilerParams(collective_id=3, has_side_effects=True),
        name="small_sums",
    )(part)


def passed_along(block, axis, distance):
    devices = range(lax.axis_size(axis))
    route = [(i - distance, i) for i in devices if i - distance in devices]
    return lax.ppermute(block, axis, route)


def shards(
    tokens,
    doc_lengths,
    mixer_gain,
    query_weight,
    key_weight,
    value_weight,
    gate_weight,
    alpha_weight,
    beta_weight,
    decay_log,
    decay_bias,
    query_taps,
    key_taps,
    value_taps,
    head_gain,
    output_weight,
    ffn_gain,
    ffn_gate,
    ffn_up,
    ffn_down,
    cotangent,
):
    length, width = tokens.shape
    heads = decay_log.shape[0]
    key = query_weight.shape[1] // heads
    value = head_gain.shape[0]
    keys, vals = heads * key, heads * value
    wide = 2 * keys + vals
    size = ffn_gate.shape[1]
    last = lax.axis_size("head") - 1
    near = lax.axis_size("seq") == NEAR
    shard = lax.axis_index("seq")
    place = jnp.full((1,), shard, jnp.int32)

    small = jnp.zeros((alpha_weight.shape[0], LANES - 2 * heads), full)
    shard_in = jnp.concatenate(
        [query_weight, key_weight, value_weight, alpha_weight, beta_weight, small], axis=1
    ).astype(low)
    before = passed_along(tokens[length - 16 :], "seq", 1)
    shard_mix = jnp.concatenate([gate_weight.astype(low), output_weight.T.astype(low)], axis=1)
    shard_ffn = jnp.concatenate(
        [ffn_gate.astype(low), ffn_up.astype(low), ffn_down.T.astype(low)], axis=1
    )
    meta, edge_meta, segrow = segment_tables(doc_lengths, shard, length)
    taps = jnp.concatenate([query_taps, key_taps, value_taps], axis=1)
    params = jnp.stack([-jnp.exp(decay_log), decay_bias])
    params = jnp.pad(params, ((0, 6), (0, LANES - heads)))
    gain = head_gain[None, :]

    first_in, pre, ab, edge, w_in = input_projection(tokens, before, mixer_gain, shard_in, wide, last)
    edge = edge[8:]
    local, through, states, inverse, end, *moved = forward_chain(
        pre, ab, meta, segrow, edge, taps, params, heads, key, value, shard_mix if near else None
    )
    w_mix = moved[0] if near else lax.all_gather(shard_mix, "seq", axis=0, tiled=True)
    ends = lax.all_gather(end, "seq")
    mix_out, mixed, gate_pre, state_in, middle, second_in, *moved = line_call(
        partial(mixer_out_kernel, heads, key, value, last), "mixer_out", 0, length, width, last,
        [ends, gain, ffn_gain[None, :]], [w_mix], [first_in, local, through], [tokens],
        [((length, vals), low, "first"), ((length, vals), full, "first"),
         ((length, vals), full, "first"), ((heads, key, value), full, "all"),
         ((length, width), full, "second"), ((length, width), low, "second")],
        [], gathers=[shard_ffn] if near else [],
    )
    w_ffn = moved[0] if near else lax.all_gather(shard_ffn, "seq", axis=0, tiled=True)
    hidden, gate_grad, lift_grad, narrow_part, middle_grad, middle_low, ffn_gain_part = line_call(
        partial(ffn_kernel, last, size), "ffn", 1, length, width, last,
        [ffn_gain[None, :]], [w_ffn], [second_in, cotangent], [middle, cotangent],
        [((length, size), low, "first")] * 3
        + [((length, width), low, "first"), ((length, width), full, "second"),
           ((length, width), low, "second"), ((8, width), full, "all")],
        [pltpu.VMEM((ROWS, size), full)] * 2,
    )
    result = (middle + lax.psum(narrow_part, "head").astype(full)).astype(low)
    gate_pgrad, mixed_grad, head_gain_part, adjoint = gate_back(
        middle_low, w_mix, mixed, gate_pre, gain, through, heads, key, value
    )
    adjoints = spread(adjoint.astype(low).reshape(keys, value))
    pairs_up = [(second_in, [gate_grad, lift_grad])]
    pairs_rest = [(cotangent, [hidden]), (first_in, [gate_pgrad]), (middle_low, [mix_out])]
    sums_up = pair_sums(place, pairs_up) if near else None
    sums_rest = pair_sums(place, pairs_rest) if near else None
    pre_grad, ab_grad, halo, taps_part, params_part, *moved = backward_chain(
        pre, ab, meta, segrow, edge, edge_meta, taps, params, states, inverse, state_in,
        mixed_grad, ends, adjoints, heads, key, value, sums_up,
    )
    up_wgrad = far_sums(sums_up, moved[0]) if near else plain_sums(place, pairs_up)
    halo = passed_along(halo, "seq", -1)
    tail = pre_grad[length - 8 :].astype(full) + halo
    pre_grad = lax.dynamic_update_slice(pre_grad, tail.astype(low), (length - 8, 0))
    pairs_in = [(first_in, [pre_grad, ab_grad])]
    sums_in = pair_sums(place, pairs_in) if near else None
    tokens_grad, mixer_gain_part, *moved = line_call(
        partial(input_grad_kernel, last, keys, vals), "input_grad", 2, length, width, last,
        [mixer_gain[None, :]], [w_in, w_mix], [pre_grad, gate_pgrad, ab_grad],
        [tokens, middle_grad],
        [((length, width), full, "second"), ((8, width), full, "all")],
        [pltpu.VMEM((ROWS, width), full)], scatters=[sums_rest, sums_in] if near else [],
    )
    rest_wgrad = far_sums(sums_rest, moved[0]) if near else plain_sums(place, pairs_rest)
    in_wgrad = far_sums(sums_in, moved[1]) if near else plain_sums(place, pairs_in)
    params_part = jnp.sum(params_part.reshape(2, 8, LANES), axis=1).reshape(1, -1)
    lines = [
        jnp.sum(mixer_gain_part, axis=0, keepdims=True),
        jnp.sum(ffn_gain_part, axis=0, keepdims=True),
        jnp.sum(taps_part.reshape(4, 8, -1), axis=1),
        jnp.pad(params_part, ((0, 0), (0, width - params_part.shape[1]))),
        jnp.pad(jnp.sum(head_gain_part, axis=0)[None], ((0, 0), (0, width - value))),
    ]
    sums = small_sums(jnp.concatenate(lines, axis=0), value)
    taps_grad = sums[2:6]
    return (
        result,
        tokens_grad,
        sums[0],
        in_wgrad[:, :keys],
        in_wgrad[:, keys : 2 * keys],
        in_wgrad[:, 2 * keys : wide],
        rest_wgrad[:, size : size + vals],
        in_wgrad[:, wide : wide + heads],
        in_wgrad[:, wide + heads : wide + 2 * heads],
        sums[6, LANES : LANES + heads],
        sums[6, :heads],
        taps_grad[:, :keys],
        taps_grad[:, keys : 2 * keys],
        taps_grad[:, 2 * keys :],
        sums[7, :value],
        rest_wgrad[:, size + vals :].T,
        sums[1],
        up_wgrad[:, :size],
        up_wgrad[:, size:],
        rest_wgrad[:, :size].T,
    )


def solution(mesh):
    rows, both = P("seq", None), P("seq", "head")
    in_specs = (
        rows, P(), P(), both, both, both, both, both, both, P("head"), P("head"),
        P(None, "head"), P(None, "head"), P(None, "head"), P(), P("head", "seq"), P(),
        both, both, P("head", "seq"), rows,
    )
    out_specs = (
        rows, rows, P(), both, both, both, both, both, both, P("head"), P("head"),
        P(None, "head"), P(None, "head"), P(None, "head"), P(), P("head", "seq"), P(),
        both, both, P("head", "seq"),
    )
    return jax.shard_map(shards, mesh=mesh, in_specs=in_specs, out_specs=out_specs, check_vma=False)
```

```python
from functools import partial

import jax
import jax.numpy as jnp
from jax import lax
from jax.experimental import pallas as pl
from jax.experimental.pallas import tpu as pltpu
from jax.sharding import PartitionSpec as P

BLOCK = 128
LANES = 128
low = jnp.bfloat16
full = jnp.float32
MIB = 1 << 20


NEAR = 8
ONE = dict(pipeline_mode=pl.Buffered(1))
ANY = dict(memory_space=pl.ANY)
FREE = pl.CostEstimate(flops=1, bytes_accessed=1, transcendentals=0)
MESH = pl.DeviceIdType.MESH


def partner(mask):
    index = lax.axis_index("seq")
    bits = (lax.rem(index, 2), lax.rem(index // 2, 2), index // 4)
    return sum((1 << i) * ((1 - b) if mask >> i & 1 else b) for i, b in enumerate(bits))


def greet(masks, last=None):
    barrier = pltpu.get_barrier_semaphore()
    for mask in masks:
        pl.semaphore_signal(barrier, inc=1, device_id={"seq": partner(mask)}, device_id_type=MESH)
    count = len(masks)
    if last is not None:
        place = lax.axis_index("head")
        for there, to in ((place > 0, place - 1), (place < last, place + 1)):

            @pl.when(there)
            def _(to=to):
                pl.semaphore_signal(barrier, inc=1, device_id={"head": to}, device_id_type=MESH)

        count += jnp.minimum(place, 1) + jnp.minimum(last - place, 1)
    pl.semaphore_wait(barrier, count)


class Gather:
    masks = (1, 2, 4)
    semaphores = [pltpu.SemaphoreType.DMA((8,)), pltpu.SemaphoreType.DMA((8,)), pltpu.SemaphoreType.DMA((1,))]

    def __init__(self, shard, whole, sent, got, home):
        self.shard, self.whole, self.sent, self.got, self.home = shard, whole, sent, got, home
        self.size = shard.shape[0]

    def rows(self, mask, first=0, count=None):
        start = pl.multiple_of(partner(mask) * self.size + first, self.size // 2)
        return self.whole.at[pl.ds(start, self.size if count is None else count), :]

    def push(self, slot):
        half = self.size // 2
        mask, src, dst = (
            (2, self.shard, self.rows(0)),
            (4, self.shard, self.rows(0)),
            (2, self.rows(4, 0, half), self.rows(4, 0, half)),
            (4, self.rows(2, half, half), self.rows(2, half, half)),
            (1, self.shard, self.rows(0)),
            (1, self.rows(2), self.rows(2)),
            (1, self.rows(4), self.rows(4)),
            (1, self.rows(6), self.rows(6)),
        )[slot]
        return pltpu.make_async_remote_copy(
            src_ref=src, dst_ref=dst, send_sem=self.sent.at[slot], recv_sem=self.got.at[slot],
            device_id={"seq": partner(mask)}, device_id_type=MESH,
        )

    def local(self):
        return pltpu.make_async_copy(self.shard, self.rows(0), self.home.at[0])

    def start(self):
        self.local().start()
        for slot in (0, 1, 4):
            self.push(slot).start()

    def middle(self):
        for slot in (0, 1):
            self.push(slot).wait_recv()
        for slot in (2, 3, 5, 6):
            self.push(slot).start()

    def late(self):
        for slot in (2, 3):
            self.push(slot).wait_recv()
        self.push(7).start()

    def traded(self, slots):
        for slot in slots:
            self.push(slot).wait_recv()

    def settle(self):
        for slot in range(8):
            self.push(slot).wait_send()

    def end(self):
        self.traded((4, 5, 6, 7))
        self.settle()
        self.local().wait()


class Scatter:
    masks = (2, 4, 6)
    semaphores = [pltpu.SemaphoreType.DMA((3,)), pltpu.SemaphoreType.DMA((3,))]

    def __init__(self, parts, got, sent, came):
        self.parts, self.got, self.sent, self.came = parts, got, sent, came

    def push(self, k):
        return pltpu.make_async_remote_copy(
            src_ref=self.parts.at[k + 1], dst_ref=self.got.at[k], send_sem=self.sent.at[k],
            recv_sem=self.came.at[k], device_id={"seq": partner(2 * k + 2)}, device_id_type=MESH,
        )

    def start(self):
        for k in range(3):
            self.push(k).start()

    def end(self):
        for k in range(3):
            self.push(k).wait()


def load(step, pairs, sems):
    @pl.when(step == 0)
    def _():
        copies = [pltpu.make_async_copy(a, b, sems.at[n]) for n, (a, b) in enumerate(pairs)]
        for copy in copies:
            copy.start()
        for copy in copies:
            copy.wait()


def mm(a, b):
    return jnp.dot(a.astype(low), b.astype(low), preferred_element_type=full)


def mm_nt(a, b):
    return lax.dot_general(
        a.astype(low), b.astype(low), (((1,), (1,)), ((), ())), preferred_element_type=full
    )


def mm_tn(a, b):
    return lax.dot_general(
        a.astype(low), b.astype(low), (((0,), (0,)), ((), ())), preferred_element_type=full
    )


def exact(a, b):
    return jnp.dot(a, b, precision=lax.Precision.HIGHEST, preferred_element_type=full)


def sigmoid(t):
    return 1.0 / (1.0 + jnp.exp(-t))


def softplus(t):
    return jnp.maximum(t, 0.0) + jnp.log(1.0 + jnp.exp(-jnp.abs(t)))


def iotas(size):
    return (
        lax.broadcasted_iota(jnp.int32, (size, size), 0),
        lax.broadcasted_iota(jnp.int32, (size, size), 1),
    )


def conv_sum(ext, taps, meta, first, width, rows):
    total = taps[3:4, first : first + width] * ext[8 : 8 + rows, first : first + width]
    for lag in (1, 2, 3):
        total += (
            taps[3 - lag : 4 - lag, first : first + width]
            * meta[:, lag : lag + 1]
            * ext[8 - lag : 8 - lag + rows, first : first + width]
        )
    return total


def gates(ab, params, heads):
    log_decay = params[0:1, :] * softplus(ab + params[1:2, :])
    beta = sigmoid(ab)
    return log_decay, beta


def decay_parts(cum, cum_t, h, same_low, strict_low, meta):
    size = cum.shape[0]
    col = cum[:, h : h + 1]
    row = cum_t[h : h + 1, :]
    lower = jnp.where(same_low, jnp.exp(jnp.minimum(col - row, 0.0)), 0.0)
    strict = jnp.where(strict_low, lower, 0.0)
    last = cum[size - 1 : size, h : h + 1]
    from_start = jnp.exp(col) * meta[:, 4:5]
    to_end = jnp.exp(last - col) * meta[:, 5:6]
    carried = jnp.exp(last) * meta[size - 1 : size, 4:5]
    return lower, strict, from_start, to_end, carried


def unit_lower_inverse(strict, rows, cols):
    size = strict.shape[0]
    power = jnp.where((rows >> 3) == (cols >> 3), -strict, 0.0)
    inverse = jnp.where(rows == cols, 1.0, power)
    power = mm(power, power)
    inverse = inverse + mm(inverse, power)
    power = mm(power, power)
    inverse = inverse + mm(inverse, power)
    shift = 3
    while (1 << shift) < size:
        off = jnp.where(
            ((rows >> (shift + 1)) == (cols >> (shift + 1))) & ((rows >> shift) != (cols >> shift)),
            strict,
            0.0,
        )
        inverse = inverse - mm(inverse, mm(off, inverse))
        shift += 1
    return inverse


def inverses(stricts, rows, cols):
    size = stricts[0].shape[0]
    near = (rows >> 3) == (cols >> 3)
    powers = [jnp.where(near, -a, 0.0) for a in stricts]
    result = [jnp.where(rows == cols, 1.0, p) for p in powers]
    for _ in range(2):
        powers = [mm(p, p) for p in powers]
        result = [t + mm(t, p) for t, p in zip(result, powers)]
    shift = 3
    while (1 << shift) < size:
        pick = ((rows >> (shift + 1)) == (cols >> (shift + 1))) & (
            (rows >> shift) != (cols >> shift)
        )
        offs = [mm(jnp.where(pick, a, 0.0), t) for a, t in zip(stricts, result)]
        result = [t - mm(t, o) for t, o in zip(result, offs)]
        shift += 1
    return result


def masks(meta, segrow):
    size = meta.shape[0]
    rows, cols = iotas(size)
    same = meta[:, 0:1] == segrow[0:1, :]
    return rows, cols, same & (rows >= cols), same & (rows > cols)


def unit(post):
    return lax.rsqrt(jnp.sum(post * post, axis=-1, keepdims=True) + 1e-06)


def forward_kernel(
    heads, key, value, gathering,
    pre_ref, ab_ref, meta_ref, segrow_ref, edge_ref, taps_ref, params_ref, *refs
):
    step = pl.program_id(0)
    steps = pl.num_programs(0)
    if gathering:
        shard_ref, out_ref, through_ref, states_ref, inverse_ref, end_ref, whole_ref, ext, state, *sems = refs
        moving = Gather(shard_ref, whole_ref, *sems)

        @pl.when(step == 0)
        def _():
            greet(Gather.masks)
            moving.start()

        @pl.when(step == steps - 2)
        def _():
            moving.middle()

    else:
        out_ref, through_ref, states_ref, inverse_ref, end_ref, ext, state = refs
    size = pre_ref.shape[0]
    wide = value + key
    kfirst, vfirst = heads * key, 2 * heads * key

    @pl.when(step == 0)
    def _():
        ext[0:8, :] = edge_ref[...].astype(full)
        rows, cols = iotas(key)
        eye = (rows == cols).astype(full)
        for h in range(heads):
            state[h, :, :value] = jnp.zeros((key, value), full)
            state[h, :, value:] = eye

    @pl.when(step > 0)
    def _():
        ext[0:8, :] = ext[size : size + 8, :]

    ext[8:, :] = pre_ref[...].astype(full)
    meta = meta_ref[...]
    log_decay, beta = gates(ab_ref[...], params_ref, heads)
    rows, cols, same_low, strict_low = masks(meta, segrow_ref)
    cum = exact((rows >= cols).astype(full), log_decay)
    cum_t = cum.T
    qs, ks, vs, lowers, stricts, fs, es, cs = [], [], [], [], [], [], [], []
    for h in range(heads):
        u = conv_sum(ext, taps_ref, meta, h * key, key, size)
        post = u * sigmoid(u)
        q = (post * unit(post)).astype(low)
        u = conv_sum(ext, taps_ref, meta, kfirst + h * key, key, size)
        post = u * sigmoid(u)
        k = (post * unit(post)).astype(low)
        u = conv_sum(ext, taps_ref, meta, vfirst + h * value, value, size)
        v = u * sigmoid(u)
        lower, strict, f, e, c = decay_parts(cum, cum_t, h, same_low, strict_low, meta)
        bcol = beta[:, heads + h : heads + h + 1]
        gram = mm_nt(jnp.concatenate([k, q], axis=0), k)
        qs.append(q), ks.append(k), vs.append(v), fs.append(f), es.append(e), cs.append(c)
        stricts.append(bcol * strict * gram[:size])
        lowers.append(lower * gram[size:])
    ts = inverses(stricts, rows, cols)
    for h in range(heads):
        bcol = beta[:, heads + h : heads + h + 1]
        s = state[h]
        states_ref[0, h] = s.astype(low)
        t = ts[h].astype(low)
        inverse_ref[0, h] = t
        ks_s = mm(ks[h], s)
        fb = fs[h] * bcol
        target = jnp.concatenate(
            [bcol * vs[h] - fb * ks_s[:, :value], -fb * ks_s[:, value:]], axis=1
        )
        delta = mm(t, target).astype(low)
        left = jnp.concatenate([(fs[h] * qs[h].astype(full)).astype(low), lowers[h].astype(low)], axis=1)
        out = mm(left, jnp.concatenate([s.astype(low), delta], axis=0))
        out_ref[:, h * value : (h + 1) * value] = out[:, :value]
        through_ref[:, h * key : (h + 1) * key] = out[:, value:].astype(low)
        ke = es[h] * ks[h].astype(full)
        s = cs[h] * s + mm_tn(ke, delta)
        state[h] = s
        end_ref[h] = s.astype(low)

    if gathering:

        @pl.when(step == steps - 1)
        def _():
            moving.late()
            moving.end()


def forward_chain(pre, ab, meta, segrow, edge, taps, params, heads, key, value, shard=None):
    gathering = shard is not None
    moved = [jax.ShapeDtypeStruct((shard.shape[0] * NEAR, shard.shape[1]), low)] if gathering else []
    extra = dict(collective_id=5, has_side_effects=True) if gathering else {}
    length = pre.shape[0]
    blocks = length // BLOCK
    width = pre.shape[1]
    wide = value + key
    return pl.pallas_call(
        partial(forward_kernel, heads, key, value, gathering),
        grid=(blocks,),
        in_specs=[
            pl.BlockSpec((BLOCK, width), lambda n: (n, 0)),
            pl.BlockSpec((BLOCK, LANES), lambda n: (n, 0)),
            pl.BlockSpec((BLOCK, LANES), lambda n: (n, 0)),
            pl.BlockSpec((8, BLOCK), lambda n: (0, n)),
            pl.BlockSpec((8, width), lambda n: (0, 0)),
            pl.BlockSpec(taps.shape, lambda n: (0, 0)),
            pl.BlockSpec((8, LANES), lambda n: (0, 0)),
        ]
        + [pl.BlockSpec(**ANY) for _ in moved],
        out_specs=[
            pl.BlockSpec((BLOCK, heads * value), lambda n: (n, 0)),
            pl.BlockSpec((BLOCK, heads * key), lambda n: (n, 0)),
            pl.BlockSpec((1, heads, key, wide), lambda n: (n, 0, 0, 0)),
            pl.BlockSpec((1, heads, BLOCK, BLOCK), lambda n: (n, 0, 0, 0)),
            pl.BlockSpec((heads, key, wide), lambda n: (0, 0, 0)),
        ]
        + [pl.BlockSpec(**ANY) for _ in moved],
        out_shape=[
            jax.ShapeDtypeStruct((length, heads * value), full),
            jax.ShapeDtypeStruct((length, heads * key), low),
            jax.ShapeDtypeStruct((blocks, heads, key, wide), low),
            jax.ShapeDtypeStruct((blocks, heads, BLOCK, BLOCK), low),
            jax.ShapeDtypeStruct((heads, key, wide), low),
        ]
        + moved,
        scratch_shapes=[
            pltpu.VMEM((BLOCK + 8, width), full),
            pltpu.VMEM((heads, key, wide), full),
        ]
        + (Gather.semaphores if gathering else []),
        compiler_params=pltpu.CompilerParams(vmem_limit_bytes=48 * MIB, **extra),
        cost_estimate=FREE,
        name="chain_forward",
    )(pre, ab, meta, segrow, edge, taps, params, *([shard] if gathering else []))


def gate_back_kernel(heads, key, value, dz_ref, mixed_ref, gate_ref, gain_ref, through_ref, whole_ref,
                     dgz_ref, do_ref, gain_grad_ref, adjoint_ref, weights, dy_ref, sems):
    load(pl.program_id(0), [(whole_ref.at[:, heads * value :], weights)], sems)

    @pl.when(pl.program_id(0) == 0)
    def _():
        gain_grad_ref[...] = jnp.zeros_like(gain_grad_ref)
        adjoint_ref[...] = jnp.zeros_like(adjoint_ref)

    rows = dz_ref.shape[0]
    gain = gain_ref[0:1, :]
    dy_ref[...] = mm(dz_ref[...], weights[...])
    for h in range(heads):
        cols = slice(h * value, (h + 1) * value)
        o = mixed_ref[:, cols].astype(full)
        s3 = lax.rsqrt(jnp.mean(o * o, axis=-1, keepdims=True) + 1e-05)
        n3 = o * s3
        gz = gate_ref[:, cols]
        sig = sigmoid(gz)
        sg = gz * sig
        dy = dy_ref[:, cols]
        dyn = dy * n3
        part = dyn * sg
        gain_grad_ref[...] += jnp.sum(part.reshape(rows // 8, 8, value), axis=0)
        dgz_ref[:, cols] = (dyn * gain * (sig * (1.0 + gz * (1.0 - sig)))).astype(low)
        dn3 = dy * gain * sg
        do = s3 * (dn3 - n3 * jnp.mean(dn3 * n3, axis=-1, keepdims=True))
        do = do.astype(low)
        do_ref[:, cols] = do
        adjoint_ref[h] += mm_tn(through_ref[:, h * key : (h + 1) * key], do)


def gate_back(dz, w_mix, mixed, gate, gain, through, heads, key, value, rows=256):
    length, width = dz.shape
    wide = heads * value
    return pl.pallas_call(
        partial(gate_back_kernel, heads, key, value),
        grid=(length // rows,),
        in_specs=[
            pl.BlockSpec((rows, width), lambda n: (n, 0)),
            pl.BlockSpec((rows, wide), lambda n: (n, 0)),
            pl.BlockSpec((rows, wide), lambda n: (n, 0)),
            pl.BlockSpec((1, value), lambda n: (0, 0)),
            pl.BlockSpec((rows, heads * key), lambda n: (n, 0)),
        ]
        + [pl.BlockSpec(**ANY)],
        out_specs=[
            pl.BlockSpec((rows, wide), lambda n: (n, 0)),
            pl.BlockSpec((rows, wide), lambda n: (n, 0)),
            pl.BlockSpec((8, value), lambda n: (0, 0)),
            pl.BlockSpec((heads, key, value), lambda n: (0, 0, 0)),
        ],
        out_shape=[
            jax.ShapeDtypeStruct((length, wide), low),
            jax.ShapeDtypeStruct((length, wide), low),
            jax.ShapeDtypeStruct((8, value), full),
            jax.ShapeDtypeStruct((heads, key, value), full),
        ],
        scratch_shapes=[
            pltpu.VMEM((width, wide), low),
            pltpu.VMEM((rows, wide), full),
            pltpu.SemaphoreType.DMA((1,)),
        ],
        compiler_params=pltpu.CompilerParams(vmem_limit_bytes=48 * MIB),
        cost_estimate=FREE,
        name="gate_back",
    )(dz, mixed, gate, gain, through, w_mix)


def lane_sum(array):
    return jnp.sum(array, axis=-1, keepdims=True)


def backward_kernel(
    heads, key, value, devices, masks_of, scattering,
    pre_ref, tail_ref, ab_ref, meta_ref, segrow_ref, edge_ref, edge_meta_ref, taps_ref, params_ref,
    states_ref, inverse_ref, state_in_ref, do_ref, ends_ref, *refs
):
    step = pl.program_id(0)
    steps = pl.num_programs(0)
    pieces, refs = refs[: len(masks_of)], list(refs[len(masks_of) :])
    parts_ref = refs.pop(0) if scattering else None
    dpre_ref, dab_ref, halo_ref, taps_grad_ref, params_grad_ref = refs[:5]
    refs = refs[5:]
    got_ref = refs.pop(0) if scattering else None
    ext, du, adjoint, adjoints, home, *sems = refs
    if scattering:
        moving = Scatter(parts_ref, got_ref, *sems)

        @pl.when(step == 0)
        def _():
            greet(Scatter.masks)
            moving.start()

    size = pre_ref.shape[0]
    kfirst, vfirst = heads * key, 2 * heads * key

    @pl.when(step == 0)
    def _():
        adjoint[...] = jnp.zeros_like(adjoint)
        tall = heads * key
        copies = []
        for n, (mask, ref) in enumerate(zip(masks_of, pieces)):
            first = 0 if mask is None else pl.multiple_of(partner(mask) * tall, tall)
            target = adjoints.at[pl.ds(first, ref.shape[0]), :]
            copies.append(pltpu.make_async_copy(ref, target, home.at[n]))
        for copy in copies:
            copy.start()
        for copy in copies:
            copy.wait()

        def one(k, carry):
            j = devices - 1 - k
            for h in range(heads):
                rows = pl.ds(pl.multiple_of(j * tall + h * key, key), key)
                adjoint[h] = (
                    mm_tn(ends_ref[rows, value:], adjoint[h]) + adjoints[rows, :].astype(full)
                )
            return carry

        lax.fori_loop(0, devices - 1 - lax.axis_index("seq"), one, 0)
        du[8 + size :, :] = jnp.zeros((8, du.shape[1]), full)
        taps_grad_ref[...] = jnp.zeros_like(taps_grad_ref)
        params_grad_ref[...] = jnp.zeros_like(params_grad_ref)

    @pl.when(step > 0)
    def _():
        du[8 + size :, :] = du[8:16, :]

    du[0:8, :] = jnp.zeros((8, du.shape[1]), full)

    @pl.when(step < steps - 1)
    def _():
        ext[0:8, :] = tail_ref[8:16, :].astype(full)

    @pl.when(step == steps - 1)
    def _():
        ext[0:8, :] = edge_ref[...].astype(full)

    ext[8:, :] = pre_ref[...].astype(full)
    meta = meta_ref[...]
    ab = ab_ref[...]
    log_decay, beta = gates(ab, params_ref, heads)
    rows, cols, same_low, strict_low = masks(meta, segrow_ref)
    cum = exact((rows >= cols).astype(full), log_decay)
    cum_t = cum.T
    lane = lax.broadcasted_iota(jnp.int32, (size, LANES), 1)
    row8 = lax.broadcasted_iota(jnp.int32, (8, size), 0)
    dcum = jnp.zeros((size, LANES), full)
    dcum_rows = jnp.zeros((8, size), full)
    dcum_last = jnp.zeros((1, LANES), full)
    dbeta = jnp.zeros((size, LANES), full)
    lane1 = lax.broadcasted_iota(jnp.int32, (1, LANES), 1)

    for h in range(heads):
        qcols = slice(h * key, (h + 1) * key)
        kcols = slice(kfirst + h * key, kfirst + (h + 1) * key)
        vcols = slice(vfirst + h * value, vfirst + (h + 1) * value)
        uq = conv_sum(ext, taps_ref, meta, h * key, key, size)
        sq = sigmoid(uq)
        pq = uq * sq
        rq = unit(pq)
        qf = pq * rq
        q = qf.astype(low)
        uk = conv_sum(ext, taps_ref, meta, kfirst + h * key, key, size)
        sk = sigmoid(uk)
        pk = uk * sk
        rk = unit(pk)
        kf = pk * rk
        k = kf.astype(low)
        uv = conv_sum(ext, taps_ref, meta, vfirst + h * value, value, size)
        sv = sigmoid(uv)
        v = uv * sv
        lower, strict, f, e, c = decay_parts(cum, cum_t, h, same_low, strict_low, meta)
        b = beta[:, heads + h : heads + h + 1]
        kq = jnp.concatenate([k, q], axis=0)
        gram = mm_nt(kq, k)
        kk, qk = gram[:size], gram[size:]
        stored = states_ref[0, h]
        s = stored[:, :value].astype(full) + mm(stored[:, value:], state_in_ref[h])
        slow = s.astype(low)
        kqs = mm(kq, slow)
        ks, qs = kqs[:size], kqs[size:]
        rest = v - f * ks
        t = inverse_ref[0, h]
        delta = mm(t, b * rest).astype(low)
        do = do_ref[:, h * value : (h + 1) * value]
        dof = do.astype(full)
        ds = adjoint[h]
        dslow = ds.astype(low)
        ke = (e * kf).astype(low)
        p = lower * qk
        left = jnp.concatenate([p.T.astype(low), ke], axis=1)
        ddelta = mm(left, jnp.concatenate([do, dslow], axis=0))
        dtarget = mm_tn(t, ddelta)
        outer = mm_nt(jnp.concatenate([do, dtarget.astype(low)], axis=0), delta)
        dp, dan = outer[:size], outer[size:]
        eg = lower * dp
        hn = -strict * dan
        hg = b * hn
        x = eg * qk
        hk = hn * kk
        g1 = (b * f) * dtarget
        fdo = f * dof
        pair = jnp.concatenate([fdo.astype(low), (-g1).astype(low)], axis=0)
        both = mm_nt(pair, slow)
        dq = both[:size] + mm(eg, k)
        dsk = e * mm_nt(delta, dslow)
        left = jnp.concatenate([(hg + hg.T).astype(low), eg.T.astype(low)], axis=1)
        dk = both[size:] + dsk + mm(left, kq)
        dv = b * dtarget
        z = lane_sum(kf * dsk)
        dfrom = lane_sum(dof * qs) - b * lane_sum(dtarget * ks)
        hrow = lane_sum(hk)
        db = hrow + lane_sum(dtarget * rest)
        dbeta = dbeta + jnp.where(lane == heads + h, db, 0.0)
        dcum = dcum + jnp.where(lane == h, lane_sum(x) + b * hrow + f * dfrom - z, 0.0)
        drow = jnp.sum(x + b * hk, axis=0, keepdims=True)
        dcum_rows = dcum_rows + jnp.where(row8 == h, drow, 0.0)
        dlast = jnp.sum(z, axis=0, keepdims=True) + c * jnp.sum(
            lane_sum(ds * s), axis=0, keepdims=True
        )
        dcum_last = dcum_last + jnp.where(lane1 == h, dlast, 0.0)
        adjoint[h] = c * ds + mm_tn(jnp.concatenate([q, k], axis=0), pair)

        dpq = rq * (dq - qf * lane_sum(dq * qf))
        du[8 : 8 + size, qcols] = dpq * (sq * (1.0 + uq * (1.0 - sq)))
        dpk = rk * (dk - kf * lane_sum(dk * kf))
        du[8 : 8 + size, kcols] = dpk * (sk * (1.0 + uk * (1.0 - sk)))
        du[8 : 8 + size, vcols] = dv * (sv * (1.0 + uv * (1.0 - sv)))

    padded = jnp.concatenate([dcum_rows, jnp.zeros((LANES - 8, size), full)], axis=0)
    rowi = lax.broadcasted_iota(jnp.int32, (size, LANES), 0)
    dcum = dcum - padded.T + jnp.where(rowi == size - 1, dcum_last, 0.0)
    dlog = exact((rows <= cols).astype(full), dcum)
    dga = dlog * params_ref[0:1, :] * sigmoid(ab + params_ref[1:2, :])
    is_decay = lane < heads
    dga = jnp.where(is_decay, dga, 0.0)
    params_grad_ref[0:8, :] += jnp.sum(dga.reshape(size // 8, 8, LANES), axis=0)
    decay_part = jnp.where(is_decay, dlog * log_decay, 0.0)
    params_grad_ref[8:16, :] += jnp.sum(decay_part.reshape(size // 8, 8, LANES), axis=0)
    dab_ref[...] = jnp.where(is_decay, dga, dbeta * beta * (1.0 - beta)).astype(low)

    width = du.shape[1]
    for first in range(0, width, 512):
        cs = slice(first, first + 512)
        own = du[8 : 8 + size, cs]
        total = taps_ref[3:4, cs] * own
        taps_grad_ref[24:32, cs] += jnp.sum(
            (own * ext[8 : 8 + size, cs]).reshape(size // 8, 8, 512), axis=0
        )
        for lag in (1, 2, 3):
            total += taps_ref[3 - lag : 4 - lag, cs] * meta[:, 5 + lag : 6 + lag] * du[
                8 + lag : 8 + lag + size, cs
            ]
            taps_grad_ref[8 * (3 - lag) : 8 * (4 - lag), cs] += jnp.sum(
                (own * meta[:, lag : lag + 1] * ext[8 - lag : 8 - lag + size, cs]).reshape(
                    size // 8, 8, 512
                ),
                axis=0,
            )
        dpre_ref[:, cs] = total.astype(low)

    @pl.when(step == steps - 1)
    def _():
        edge_meta = edge_meta_ref[...]
        halo = jnp.zeros(halo_ref.shape, full)
        for lag in (1, 2, 3):
            halo += taps_ref[3 - lag : 4 - lag, :] * edge_meta[:, 5 + lag : 6 + lag] * du[
                lag : 8 + lag, :
            ]
        halo_ref[...] = halo
        if scattering:
            moving.end()


def backward_chain(pre, ab, meta, segrow, edge, edge_meta, taps, params, states, inverse,
                   state_in, do, ends, adjoints, heads, key, value, parts=None):
    scattering = parts is not None
    moved = [jax.ShapeDtypeStruct((3,) + parts.shape[1:], low)] if scattering else []
    extra = dict(collective_id=6, has_side_effects=True) if scattering else {}
    masks_of = [mask for mask, _ in adjoints]
    devices = ends.shape[0] // (heads * key)
    length, width = pre.shape
    blocks = length // BLOCK
    wide = value + key
    once = dict(pipeline_mode=pl.Buffered(1))
    last = blocks - 1
    return pl.pallas_call(
        partial(backward_kernel, heads, key, value, devices, masks_of, scattering),
        grid=(blocks,),
        in_specs=[
            pl.BlockSpec((BLOCK, width), lambda n: (last - n, 0)),
            pl.BlockSpec((16, width), lambda n: (jnp.maximum((last - n) * (BLOCK // 16) - 1, 0), 0)),
            pl.BlockSpec((BLOCK, LANES), lambda n: (last - n, 0)),
            pl.BlockSpec((BLOCK, LANES), lambda n: (last - n, 0)),
            pl.BlockSpec((8, BLOCK), lambda n: (0, last - n)),
            pl.BlockSpec((8, width), lambda n: (0, 0)),
            pl.BlockSpec((8, LANES), lambda n: (0, 0)),
            pl.BlockSpec(taps.shape, lambda n: (0, 0)),
            pl.BlockSpec((8, LANES), lambda n: (0, 0)),
            pl.BlockSpec((1, heads, key, wide), lambda n: (last - n, 0, 0, 0)),
            pl.BlockSpec((1, heads, BLOCK, BLOCK), lambda n: (last - n, 0, 0, 0)),
            pl.BlockSpec((heads, key, value), lambda n: (0, 0, 0)),
            pl.BlockSpec((BLOCK, heads * value), lambda n: (last - n, 0)),
            pl.BlockSpec(ends.shape, lambda n: (0, 0), **once),
        ]
        + [pl.BlockSpec(**ANY) for _ in (*adjoints, *moved)],
        out_specs=[
            pl.BlockSpec((BLOCK, width), lambda n: (last - n, 0)),
            pl.BlockSpec((BLOCK, LANES), lambda n: (last - n, 0)),
            pl.BlockSpec((8, width), lambda n: (0, 0)),
            pl.BlockSpec((32, width), lambda n: (0, 0)),
            pl.BlockSpec((16, LANES), lambda n: (0, 0)),
        ]
        + [pl.BlockSpec(**ANY) for _ in moved],
        out_shape=[
            jax.ShapeDtypeStruct((length, width), low),
            jax.ShapeDtypeStruct((length, LANES), low),
            jax.ShapeDtypeStruct((8, width), full),
            jax.ShapeDtypeStruct((32, width), full),
            jax.ShapeDtypeStruct((16, LANES), full),
        ]
        + moved,
        scratch_shapes=[
            pltpu.VMEM((BLOCK + 8, width), full),
            pltpu.VMEM((BLOCK + 16, width), full),
            pltpu.VMEM((heads, key, value), full),
            pltpu.VMEM((devices * heads * key, value), low),
            pltpu.SemaphoreType.DMA((len(adjoints),)),
        ]
        + (Scatter.semaphores if scattering else []),
        compiler_params=pltpu.CompilerParams(vmem_limit_bytes=56 * MIB, **extra),
        cost_estimate=FREE,
        name="chain_backward",
    )(pre, pre, ab, meta, segrow, edge, edge_meta, taps, params, states, inverse, state_in, do, ends,
      *[a for _, a in adjoints], *([parts] if scattering else []))


def segment_tables(doc_lengths, shard, length):
    starts = jnp.cumsum(doc_lengths, dtype=jnp.int32) - doc_lengths
    positions = shard * length + jnp.arange(-16, length + 8, dtype=jnp.int32)
    seg = jnp.sum((starts[None, :] <= positions[:, None]).astype(jnp.int32), axis=1)
    own = seg[16 : 16 + length]

    def lanes(first, count):
        base = seg[first : first + count]
        back = [seg[first - l : first - l + count] == base for l in (1, 2, 3)]
        ahead = [seg[first + l : first + l + count] == base for l in (1, 2, 3)]
        return base, back, ahead

    base, back, ahead = lanes(16, length)
    blocks = own.reshape(-1, BLOCK)
    before = seg[15 : 15 + length : BLOCK]
    alive = (blocks == before[:, None]).reshape(-1)
    to_last = (blocks == blocks[:, -1:]).reshape(-1)
    columns = [base, *back, alive, to_last, *ahead]
    meta = jnp.stack([a.astype(full) for a in columns], axis=1)
    meta = jnp.pad(meta, ((0, 0), (0, LANES - meta.shape[1])))
    base, back, ahead = lanes(8, 8)
    columns = [base, *back, base, base, *ahead]
    edge_meta = jnp.stack([a.astype(full) for a in columns], axis=1)
    edge_meta = jnp.pad(edge_meta, ((0, 0), (0, LANES - edge_meta.shape[1])))
    segrow = jnp.broadcast_to(own.astype(full)[None, :], (8, length))
    return meta, edge_meta, segrow


ROWS = 256
PIECE = 32
HOP = 2
EACH = ROWS // PIECE
AHEAD = 1 + (EACH - 1 + 3 * HOP) // EACH
RING = AHEAD + 1


def exchanged(block, mask):
    return lax.ppermute(block, "seq", [(i, i ^ mask) for i in range(lax.axis_size("seq"))])


def spread(shard):
    if lax.axis_size("seq") != NEAR:
        return [(None, lax.all_gather(shard, "seq", axis=0, tiled=True))]
    own = [(0, shard)] + [(mask, exchanged(shard, mask)) for mask in (2, 4, 6)]
    return own + [(mask + 1, exchanged(a, 1)) for mask, a in own]


def line_scratch(length, width):
    pieces = length // PIECE
    return [
        pltpu.VMEM((RING, ROWS, width), low),
        pltpu.VMEM((length, width), low),
        pltpu.VMEM((length, width), low),
        pltpu.SemaphoreType.DMA((pieces,)),
        pltpu.SemaphoreType.DMA((pieces,)),
        pltpu.SemaphoreType.DMA((pieces,)),
        pltpu.SemaphoreType.DMA((pieces,)),
    ]


def line_sum(step, last, stages, finish, scratch):
    own, from_left, from_right, got_left, got_right, sent_right, sent_left = scratch
    place = lax.axis_index("head")
    length, width = from_left.shape
    blocks, pieces = length // ROWS, length // PIECE
    left_there, right_there = place > 0, place < last

    def rows(piece):
        return pl.ds(pl.multiple_of(piece * PIECE, PIECE), PIECE)

    def hop(piece, rightwards):
        kept, sent, got, to = (
            (from_left, sent_right, got_left, place + 1)
            if rightwards
            else (from_right, sent_left, got_right, place - 1)
        )
        return pltpu.make_async_remote_copy(
            src_ref=kept.at[rows(piece)],
            dst_ref=kept.at[rows(piece)],
            send_sem=sent.at[piece],
            recv_sem=got.at[piece],
            device_id={"head": to},
            device_id_type=MESH,
        )

    def own_piece(piece):
        slot = lax.rem(piece // EACH, RING)
        first = pl.multiple_of(lax.rem(piece, EACH) * PIECE, PIECE)
        return own[slot, pl.ds(first, PIECE), :].astype(full)

    @pl.when(step == 0)
    def _():
        @pl.when(place == 0)
        def _():
            from_left[...] = jnp.zeros_like(from_left)

        @pl.when(place == last)
        def _():
            from_right[...] = jnp.zeros_like(from_right)

    def one(q, carry):
        now = (step - 1) * EACH + q
        for rightwards in (True, False):
            came, more = (left_there, right_there) if rightwards else (right_there, left_there)
            kept = from_left if rightwards else from_right
            piece = now - HOP * (place if rightwards else last - place)

            @pl.when((piece >= 0) & (piece < pieces))
            def _():
                @pl.when(came)
                def _():
                    hop(piece, rightwards).wait_recv()

                @pl.when(more)
                def _():
                    kept[rows(piece), :] = (
                        own_piece(piece) + kept[rows(piece), :].astype(full)
                    ).astype(low)
                    hop(piece, rightwards).start()

        return carry

    done = 0
    for n, stage in enumerate(stages):

        @pl.when(step < blocks)
        def _(n=n, stage=stage):
            value = stage()
            if n == len(stages) - 1:
                own[lax.rem(step, RING)] = value.astype(low)

        until = EACH * (n + 1) // len(stages)
        lax.fori_loop(done, until, one, 0)
        done = until

    @pl.when(step >= AHEAD)
    def _():
        block = step - AHEAD
        span = pl.ds(pl.multiple_of(block * ROWS, ROWS), ROWS)
        total = from_left[span, :].astype(full) + from_right[span, :].astype(full)
        twice = jnp.where(left_there & right_there, 1.0, 0.0)
        finish(total - twice * own[lax.rem(block, RING)].astype(full))

    @pl.when(step == blocks + AHEAD - 1)
    def _():
        def settle(piece, carry):
            @pl.when(right_there)
            def _():
                hop(piece, True).wait_send()

            @pl.when(left_there)
            def _():
                hop(piece, False).wait_send()

            return carry

        lax.fori_loop(0, pieces, settle, 0)


def union(kinds):
    return sorted({mask for kind in kinds for mask in kind.masks})


def line_call(kernel, name, collective, length, width, last, resident, weights, entering, leaving, outs,
              scratch, gathers=(), scatters=(), early=None):
    blocks = length // ROWS
    steps = blocks + AHEAD

    def spec(array, stage):
        if stage == "first":
            return pl.BlockSpec((ROWS, array.shape[1]), lambda g: (jnp.minimum(g, blocks - 1), 0))
        if stage == "second":
            return pl.BlockSpec((ROWS, array.shape[1]), lambda g: (jnp.maximum(g - AHEAD, 0), 0))
        rank = len(array.shape)
        return pl.BlockSpec(array.shape, lambda g: (0,) * rank, **ONE)

    in_specs = [spec(a, "all") for a in resident]
    first_one = [] if early is None else [early]
    in_specs += [pl.BlockSpec(**ANY) for _ in (*weights, *first_one, *gathers, *scatters)]
    in_specs += [spec(a, "first") for a in entering] + [spec(a, "second") for a in leaving]
    shapes = [jax.ShapeDtypeStruct(shape, dtype) for shape, dtype, _ in outs]
    out_specs = [
        spec(s, stage) if stage != "all" else pl.BlockSpec(s.shape, lambda g, r=len(s.shape): (0,) * r)
        for s, (_, _, stage) in zip(shapes, outs)
    ]
    moved = [jax.ShapeDtypeStruct((a.shape[0] * NEAR, a.shape[1]), low) for a in (*first_one, *gathers)]
    moved += [jax.ShapeDtypeStruct((3,) + a.shape[1:], low) for a in scatters]
    kinds = [Gather] * len(gathers) + [Scatter] * len(scatters)
    whole_first = [pltpu.VMEM(s.shape, low) for s in moved[: len(first_one)]]
    held = [pltpu.VMEM(a.shape, low) for a in weights] + [pltpu.SemaphoreType.DMA((len(weights),))]
    held += whole_first + [s for _ in first_one for s in Gather.semaphores]
    held += [s for kind in kinds for s in kind.semaphores]

    def body(*refs):
        refs = list(refs)

        def take(n):
            head, refs[:] = refs[:n], refs[n:]
            return head

        own_in, heavy = take(len(resident)), take(len(weights))
        ahead, sources = take(len(first_one)), take(len(kinds))
        chunks = take(len(entering) + len(leaving))
        own_out, handed, targets = take(len(outs)), take(len(first_one)), take(len(kinds))
        own_scratch = take(len(scratch) + 7)
        matrices, (sems,) = take(len(weights)), take(1)
        if first_one:
            (table,), signals = take(1), take(3)
            lead = Gather(ahead[0], table, *signals)
            back = pltpu.make_async_copy(table, handed[0], signals[2].at[0])
            matrices.append(table)
        carried = [kind(a, b, *take(len(kind.semaphores))) for kind, a, b in zip(kinds, sources, targets)]
        step = pl.program_id(0)

        @pl.when(step == 0)
        def _():
            greet(union(kinds + [Gather] * len(first_one)), last)
            for c in [lead] if first_one else carried:
                c.start()

        load(step, list(zip(heavy, matrices)), sems)
        if first_one:

            @pl.when(step == 0)
            def _():
                lead.middle()
                lead.late()
                for c in carried:
                    c.start()
                lead.end()
                back.start()

        for at, turn in ((steps - 3, "middle"), (steps - 1, "late")):

            @pl.when(step == at)
            def _(turn=turn):
                for c in carried:
                    if isinstance(c, Gather):
                        getattr(c, turn)()

        kernel(matrices, *own_in, *chunks, *own_out, *own_scratch)

        @pl.when(step == steps - 1)
        def _():
            for c in carried:
                c.end()
            if first_one:
                back.wait()

    return pl.pallas_call(
        body,
        grid=(steps,),
        in_specs=in_specs,
        out_specs=out_specs + [pl.BlockSpec(**ANY) for _ in moved],
        out_shape=shapes + moved,
        scratch_shapes=scratch + line_scratch(length, width) + held,
        compiler_params=pltpu.CompilerParams(
            collective_id=collective, has_side_effects=True, vmem_limit_bytes=60 * MIB
        ),
        cost_estimate=FREE,
        name=name,
    )(*resident, *weights, *first_one, *gathers, *scatters, *entering, *leaving)


def mixer_out_kernel(heads, key, value, last, matrices,
                     head_gain_ref, gain_ref,
                     first_ref, local_ref, through_ref, tokens_ref,
                     y_ref, mixed_ref, gate_ref, state_ref, middle_ref, second_ref, *scratch):
    step = pl.program_id(0)
    weights, ends = matrices
    vals = heads * value

    @pl.when(step == 0)
    def _():
        state_ref[...] = jnp.zeros_like(state_ref)

        def one(j, carry):
            for h in range(heads):
                rows = pl.ds(pl.multiple_of((j * heads + h) * key, key), key)
                part = ends[rows, :]
                state_ref[h] = mm(part[:, value:], state_ref[h]) + part[:, :value].astype(full)
            return carry

        lax.fori_loop(0, lax.axis_index("seq"), one, 0)

    def gate():
        gate_ref[...] = mm(first_ref[...], weights[:, :vals])

    def mix():
        for h in range(heads):
            cols = slice(h * value, (h + 1) * value)
            o = local_ref[:, cols] + mm(through_ref[:, h * key : (h + 1) * key], state_ref[h])
            mixed_ref[:, cols] = o
            s3 = lax.rsqrt(jnp.mean(o * o, axis=-1, keepdims=True) + 1e-05)
            gz = gate_ref[:, cols]
            y_ref[:, cols] = (o * s3 * head_gain_ref[0:1, :] * (gz * sigmoid(gz))).astype(low)

    def project():
        return mm_nt(y_ref[...], weights[:, vals:])

    def finish(total):
        middle = tokens_ref[...].astype(full) + total
        middle_ref[...] = middle
        scale = lax.rsqrt(jnp.mean(middle * middle, axis=-1, keepdims=True) + 1e-06)
        second_ref[...] = (middle * scale * gain_ref[0:1, :]).astype(low)

    line_sum(step, last, [gate, mix, project], finish, scratch)


def ffn_kernel(last, size, matrices, gain_ref,
               second_ref, cot_ref, middle_ref, cot_late_ref,
               hidden_ref, dgate_ref, dup_ref, partial_ref, dmiddle_ref, dlow_ref, gain_grad_ref,
               fg, fu, *scratch):
    step = pl.program_id(0)
    (weights,) = matrices
    w_gate, w_up, w_down = (slice(n * size, (n + 1) * size) for n in range(3))

    @pl.when(step == 0)
    def _():
        gain_grad_ref[...] = jnp.zeros_like(gain_grad_ref)

    def one():
        fg[...] = mm(second_ref[...], weights[:, w_gate])

    def two():
        fu[...] = mm(second_ref[...], weights[:, w_up])

    def three():
        g = fg[...]
        hidden = (g * sigmoid(g) * fu[...]).astype(low)
        hidden_ref[...] = hidden
        partial_ref[...] = mm_nt(hidden, weights[:, w_down]).astype(low)

    def four():
        dhid = mm(cot_ref[...], weights[:, w_down])
        g = fg[...]
        sig = sigmoid(g)
        dgate_ref[...] = (dhid * fu[...] * (sig * (1.0 + g * (1.0 - sig)))).astype(low)
        dup_ref[...] = (dhid * (g * sig)).astype(low)

    def five():
        return mm_nt(dgate_ref[...], weights[:, w_gate]) + mm_nt(dup_ref[...], weights[:, w_up])

    def finish(grad):
        middle = middle_ref[...]
        scale = lax.rsqrt(jnp.mean(middle * middle, axis=-1, keepdims=True) + 1e-06)
        norm = middle * scale
        gain_grad_ref[...] += jnp.sum((grad * norm).reshape(ROWS // 8, 8, -1), axis=0)
        weighted = grad * gain_ref[0:1, :]
        dm = cot_late_ref[...].astype(full) + scale * (
            weighted - norm * jnp.mean(weighted * norm, axis=-1, keepdims=True)
        )
        dmiddle_ref[...] = dm
        dlow_ref[...] = dm.astype(low)

    line_sum(step, last, [one, two, three, four, five], finish, scratch)


def input_grad_kernel(last, keys, vals, matrices, gain_ref,
                      dpre_ref, dgz_ref, dab_ref, tokens_ref,
                      term_ref, gain_grad_ref, part, *scratch):
    step = pl.program_id(0)
    w_in, w_mix = matrices
    wide = 2 * keys + vals

    @pl.when(step == 0)
    def _():
        gain_grad_ref[...] = jnp.zeros_like(gain_grad_ref)

    def one():
        part[...] = mm_nt(dpre_ref[...], w_in[:, :wide])

    def two():
        return (
            part[...]
            + mm_nt(dgz_ref[...], w_mix[:, :vals])
            + mm_nt(dab_ref[...], w_in[:, wide:])
        )

    def finish(grad):
        stream = tokens_ref[...].astype(full)
        scale = lax.rsqrt(jnp.mean(stream * stream, axis=-1, keepdims=True) + 1e-06)
        norm = stream * scale
        gain_grad_ref[...] += jnp.sum((grad * norm).reshape(ROWS // 8, 8, -1), axis=0)
        weighted = grad * gain_ref[0:1, :]
        term_ref[...] = (
            scale * (weighted - norm * jnp.mean(weighted * norm, axis=-1, keepdims=True))
        ).astype(low)

    line_sum(step, last, [one, two], finish, scratch)


def input_kernel(wide, gathering, gain_ref, *refs):
    rows = 256
    if gathering:
        heavy, (before_hbm, tokens_hbm), refs = refs[:9], refs[9:11], refs[11:]
        small_ref, sources = heavy[3], heavy[4:]
    else:
        (shard_ref, before_hbm, tokens_hbm), refs = refs[:3], refs[3:]
    first_ref, pre_ref, ab_ref, edge_ref, whole_ref = refs[:5]
    refs = refs[5:]
    if gathering:
        (mix_ref, ffn_ref), refs = refs[:2], refs[2:]
    weights, total, tokens_ref, before, home, *refs = refs
    length, width = tokens_ref.shape
    half = width // 4
    back = pltpu.make_async_copy(weights, whole_ref, home.at[0])
    here = pltpu.make_async_copy(tokens_hbm, tokens_ref, home.at[1])
    here.start()
    if gathering:
        shard, *buffers = refs[:6]
        sems = refs[6:]
        pairs = [(before_hbm, before), *zip(sources, buffers)]
        copies = [pltpu.make_async_copy(a, b, home.at[2 + n]) for n, (a, b) in enumerate(pairs)]
        for copy in copies:
            copy.start()
        first = 0
        for ref in heavy[:3]:
            shard[:, first : first + ref.shape[1]] = ref[...].astype(low)
            first += ref.shape[1]
        shard[:, first:] = small_ref[...].astype(low)
        greet(Gather.masks)
        moving = Gather(shard, weights, *sems)
        moving.start()
    else:
        copies = [
            pltpu.make_async_copy(shard_ref, weights, home.at[2]),
            pltpu.make_async_copy(before_hbm, before, home.at[3]),
        ]
        for copy in copies:
            copy.start()

    def normed(block):
        x = block.astype(full)
        return (x * lax.rsqrt(jnp.mean(x * x, axis=-1, keepdims=True) + 1e-06) * gain_ref[0:1, :]).astype(low)

    def norm(n, carry):
        span = pl.ds(pl.multiple_of(n * rows, rows), rows)
        first_ref[span, :] = normed(tokens_ref[span, :])
        return carry

    here.wait()
    lax.fori_loop(0, length // rows, norm, 0)

    def add(chip, fresh, done):
        start = pl.multiple_of(chip * half, half)

        def one(n, carry):
            span = pl.ds(pl.multiple_of(n * rows, rows), rows)
            part = mm(first_ref[span, pl.ds(start, half)], weights[pl.ds(start, half), :])
            if not fresh:
                part += total[span, :]
            if done:
                pre_ref[span, :] = part[:, :wide].astype(low)
                ab_ref[span, :] = part[:, wide:]
            else:
                total[span, :] = part
            return carry

        lax.fori_loop(0, length // rows, one, 0)

    if gathering:
        moving.local().wait()
        moving.traded((4,))
        add(partner(0) // 2, True, False)
        for copy in copies:
            copy.wait()
        gate, out, up, lift, down = buffers
        vals, size = gate.shape[1], up.shape[1]
        mix_ref[:, :vals] = gate[...].astype(low)
        for first in range(0, vals, 128):
            mix_ref[:, vals + first : vals + first + 128] = out[first : first + 128, :].T.astype(low)
        ffn_ref[:, :size] = up[...].astype(low)
        ffn_ref[:, size : 2 * size] = lift[...].astype(low)
        for first in range(0, size, 128):
            cols = slice(2 * size + first, 2 * size + first + 128)
            ffn_ref[:, cols] = down[first : first + 128, :].T.astype(low)
        moving.middle()
        moving.traded((5, 6))
        add(partner(2) // 2, False, False)
        moving.late()
        add(partner(4) // 2, False, False)
        moving.traded((7,))
        back.start()
        add(partner(6) // 2, False, True)
    else:
        for copy in copies:
            copy.wait()
        back.start()
        for chip in range(4):
            add(chip, chip == 0, chip == 3)
    edge_ref[...] = mm(normed(before[...]), weights[:, :wide]).astype(low)
    if gathering:
        moving.settle()
    back.wait()


def input_projection(tokens, before, gain, heavy, wide):
    length, width = tokens.shape
    gathering = len(heavy) > 1
    here = pl.BlockSpec(memory_space=pltpu.VMEM)
    away = pl.BlockSpec(**ANY)
    if gathering:
        operands = [*heavy, before, tokens]
        in_specs = [here] * 4 + [away] * 7
        rows = heavy[0].shape[0]
        columns = sum(a.shape[1] for a in heavy[:4])
        shards_out = [
            jax.ShapeDtypeStruct((rows, 2 * heavy[4].shape[1]), low),
            jax.ShapeDtypeStruct((rows, 3 * heavy[6].shape[1]), low),
        ]
        more = [pltpu.VMEM((rows, columns), low)] + [pltpu.VMEM(a.shape, full) for a in heavy[4:]]
        more += Gather.semaphores
        params = dict(collective_id=4, has_side_effects=True)
    else:
        operands = [*heavy, before, tokens]
        in_specs = [away] * 3
        columns = heavy[0].shape[1]
        shards_out, more, params = [], [], {}
    return pl.pallas_call(
        partial(input_kernel, wide, gathering),
        in_specs=[here] + in_specs,
        out_specs=[here] * 4 + [away] + [here] * len(shards_out),
        out_shape=[
            jax.ShapeDtypeStruct((length, width), low),
            jax.ShapeDtypeStruct((length, wide), low),
            jax.ShapeDtypeStruct((length, columns - wide), full),
            jax.ShapeDtypeStruct((16, wide), low),
            jax.ShapeDtypeStruct((width, columns), low),
        ]
        + shards_out,
        scratch_shapes=[
            pltpu.VMEM((width, columns), low),
            pltpu.VMEM((length, columns), full),
            pltpu.VMEM((length, width), low),
            pltpu.VMEM((16, width), low),
            pltpu.SemaphoreType.DMA((8,)),
        ]
        + more,
        compiler_params=pltpu.CompilerParams(vmem_limit_bytes=60 * MIB, **params),
        cost_estimate=FREE,
        name="input_projection",
    )(gain[None, :], *operands)


def weight_kernel(groups, adding, counts, place_ref, *refs):
    lefts, rights = refs[: counts[0]], refs[counts[0] : counts[0] + counts[1]]
    rest = refs[counts[0] + counts[1] :]
    parts = []
    n = 0
    for g, many in enumerate(groups):
        left = lefts[g][...]
        for _ in range(many):
            parts.append(mm_tn(left, rights[n][...]))
            n += 1
    first = 0
    for part in parts:
        cols = slice(first, first + part.shape[1])
        first += part.shape[1]
        if adding:
            part += rest[0][0, :, cols].astype(full)
        rest[-1][0, :, cols] = part.astype(low)


def weight_call(place, pairs, odd, count, stride, added=None, width=256):
    lefts = [a for a, _ in pairs]
    rights = [b for _, bs in pairs for b in bs]
    length = lefts[0].shape[0]
    columns = sum(b.shape[1] for b in rights)

    def pick(k, place_ref):
        return (0, jnp.bitwise_xor(place_ref[0], stride * k + odd))

    in_specs = [pl.BlockSpec((length, width), pick) for _ in lefts]
    in_specs += [pl.BlockSpec(b.shape, lambda k, p: (0, 0), **ONE) for b in rights]
    if added is not None:
        in_specs += [pl.BlockSpec((1, width, columns), lambda k, p: (k, 0, 0))]
    out_specs = [pl.BlockSpec((1, width, columns), lambda k, p: (k, 0, 0))]
    out_shape = [jax.ShapeDtypeStruct((count, width, columns), low)]
    return pl.pallas_call(
        partial(
            weight_kernel, [len(bs) for _, bs in pairs], added is not None, (len(lefts), len(rights))
        ),
        grid_spec=pltpu.PrefetchScalarGridSpec(
            num_scalar_prefetch=1, grid=(count,), in_specs=in_specs, out_specs=out_specs
        ),
        out_shape=out_shape,
        compiler_params=pltpu.CompilerParams(vmem_limit_bytes=56 * MIB),
        cost_estimate=FREE,
        name="weight_grads",
    )(place, *lefts, *rights, *(() if added is None else (added,)))


def pair_sums(place, pairs):
    (away,) = weight_call(place, pairs, 1, NEAR // 2, 2)
    (sums,) = weight_call(place, pairs, 0, NEAR // 2, 2, exchanged(away, 1))
    return sums


def plain_sums(place, pairs):
    width = pairs[0][0].shape[1]
    (grads,) = weight_call(jnp.zeros_like(place), pairs, 0, width // 256, 1)
    return lax.psum_scatter(grads.reshape(width, -1), "seq", scatter_dimension=0, tiled=True).astype(full)


def final_kernel(heads, keys, vals, size, dmiddle_ref, term_ref, in_own, in_got, up_own, up_got, down_own, down_got,
                 gate_own, gate_got, out_own, out_got,
                 dtokens_ref, q_ref, k_ref, v_ref, a_ref, b_ref, up_ref, lift_ref, down_ref, gate_ref, out_ref):
    def total(own, got, cols=slice(None)):
        return own[0, :, cols].astype(full) + sum(got[k, :, cols].astype(full) for k in range(3))

    @pl.when(pl.program_id(0) < 8)
    def _():
        dtokens_ref[...] = dmiddle_ref[...] + term_ref[...].astype(full)
        wide = 2 * keys + vals
        q_ref[...] = total(in_own, in_got, slice(0, keys))
        k_ref[...] = total(in_own, in_got, slice(keys, 2 * keys))
        v_ref[...] = total(in_own, in_got, slice(2 * keys, wide))
        small = total(in_own, in_got, slice(wide, wide + LANES))
        a_ref[...] = small[:, :heads]
        b_ref[...] = small[:, heads : 2 * heads]
        up_ref[...] = total(up_own, up_got, slice(0, size))
        lift_ref[...] = total(up_own, up_got, slice(size, 2 * size))
        gate_ref[...] = total(gate_own, gate_got)
        out_ref[...] = total(out_own, out_got).T

    down_ref[...] = total(down_own, down_got).T


def final_sums(dmiddle, term, sums_in, got_in, sums_up, got_up, sums_rest, got_rest, heads, keys, vals, size):
    length, width = dmiddle.shape
    rows = sums_in.shape[1]
    eight = lambda n: jnp.minimum(n, 7)
    many, few = length // 8, rows // 8

    def both(array, block, index):
        return [pl.BlockSpec((1,) + block, index), pl.BlockSpec((3,) + block, index)]

    wide_in, wide_up = sums_in.shape[2], sums_up.shape[2]
    at_gate, at_out = size // LANES, (size + vals) // LANES
    in_specs = [pl.BlockSpec((many, width), lambda n: (eight(n), 0))] * 2
    in_specs += both(sums_in, (few, wide_in), lambda n: (0, eight(n), 0))
    in_specs += both(sums_up, (few, wide_up), lambda n: (0, eight(n), 0))
    in_specs += both(sums_rest, (rows, LANES), lambda n: (0, 0, n))
    in_specs += both(sums_rest, (rows, LANES), lambda n: (0, 0, at_gate + eight(n)))
    in_specs += both(sums_rest, (rows, LANES), lambda n: (0, 0, at_out + eight(n)))
    byrow = lambda columns: pl.BlockSpec((few, columns), lambda n: (eight(n), 0))
    return pl.pallas_call(
        partial(final_kernel, heads, keys, vals, size),
        grid=(size // LANES,),
        in_specs=in_specs,
        out_specs=[
            pl.BlockSpec((many, width), lambda n: (eight(n), 0)),
            byrow(keys), byrow(keys), byrow(vals), byrow(heads), byrow(heads), byrow(size), byrow(size),
            pl.BlockSpec((LANES, rows), lambda n: (n, 0)),
            pl.BlockSpec((rows, LANES), lambda n: (0, eight(n))),
            pl.BlockSpec((LANES, rows), lambda n: (eight(n), 0)),
        ],
        out_shape=[
            jax.ShapeDtypeStruct(shape, full)
            for shape in (
                (length, width), (rows, keys), (rows, keys), (rows, vals), (rows, heads), (rows, heads),
                (rows, size), (rows, size), (size, rows), (rows, vals), (vals, rows),
            )
        ],
        compiler_params=pltpu.CompilerParams(vmem_limit_bytes=48 * MIB),
        cost_estimate=FREE,
        name="final_sums",
    )(dmiddle, term, sums_in, got_in, sums_up, got_up, sums_rest, got_rest, sums_rest, got_rest,
      sums_rest, got_rest)


def small_kernel(count, others, part_ref, out_ref, send, got, got_far, sent, came, sent_far, came_far):
    me, row = lax.axis_index("seq"), lax.axis_index("head")
    rows, far = part_ref.shape[0], got_far.shape[2]
    barrier = pltpu.get_barrier_semaphore()

    def greet(k, carry):
        pl.semaphore_signal(
            barrier, inc=1, device_id={"seq": lax.rem(me + k, count)},
            device_id_type=pl.DeviceIdType.MESH,
        )
        return carry

    lax.fori_loop(1, count, greet, 0)
    for k in range(1, others):
        pl.semaphore_signal(
            barrier, inc=1, device_id={"head": lax.rem(row + k, others)},
            device_id_type=pl.DeviceIdType.MESH,
        )
    pl.semaphore_wait(barrier, count + others - 2)

    def along(k):
        return pltpu.make_async_remote_copy(
            src_ref=part_ref, dst_ref=got.at[me], send_sem=sent.at[k], recv_sem=came.at[k],
            device_id={"seq": lax.rem(me + k, count)}, device_id_type=pl.DeviceIdType.MESH,
        )

    def across(k):
        return pltpu.make_async_remote_copy(
            src_ref=send, dst_ref=got_far.at[row], send_sem=sent_far.at[k], recv_sem=came_far.at[k],
            device_id={"head": lax.rem(row + k, others)}, device_id_type=pl.DeviceIdType.MESH,
        )

    def start(k, carry):
        along(k).start()
        return carry

    def wait(k, carry):
        along(k).wait()
        return carry

    lax.fori_loop(1, count, start, 0)
    got[me] = part_ref[...]
    lax.fori_loop(1, count, wait, 0)

    def add(k, carry):
        out_ref[...] += got[k]
        return carry

    out_ref[...] = got[0]
    lax.fori_loop(1, count, add, 0)
    send[...] = out_ref[:, :far]
    for k in range(1, others):
        across(k).start()
    got_far[row] = send[...]
    for k in range(1, others):
        across(k).wait()
    total = got_far[0]
    for k in range(1, others):
        total += got_far[k]
    out_ref[rows - 1 :, :far] = total[rows - 1 :, :]


def small_sums(part, far):
    count, others = lax.axis_size("seq"), lax.axis_size("head")
    return pl.pallas_call(
        partial(small_kernel, count, others),
        in_specs=[pl.BlockSpec(memory_space=pltpu.VMEM)],
        out_specs=pl.BlockSpec(memory_space=pltpu.VMEM),
        out_shape=jax.ShapeDtypeStruct(part.shape, full),
        scratch_shapes=[
            pltpu.VMEM((part.shape[0], far), full),
            pltpu.VMEM((count,) + part.shape, full),
            pltpu.VMEM((others, part.shape[0], far), full),
            pltpu.SemaphoreType.DMA((count,)),
            pltpu.SemaphoreType.DMA((count,)),
            pltpu.SemaphoreType.DMA((others,)),
            pltpu.SemaphoreType.DMA((others,)),
        ],
        compiler_params=pltpu.CompilerParams(collective_id=3, has_side_effects=True),
        name="small_sums",
    )(part)


def passed_along(block, axis, distance):
    devices = range(lax.axis_size(axis))
    route = [(i - distance, i) for i in devices if i - distance in devices]
    return lax.ppermute(block, axis, route)


def shards(
    tokens,
    doc_lengths,
    mixer_gain,
    query_weight,
    key_weight,
    value_weight,
    gate_weight,
    alpha_weight,
    beta_weight,
    decay_log,
    decay_bias,
    query_taps,
    key_taps,
    value_taps,
    head_gain,
    output_weight,
    ffn_gain,
    ffn_gate,
    ffn_up,
    ffn_down,
    cotangent,
):
    length, width = tokens.shape
    heads = decay_log.shape[0]
    key = query_weight.shape[1] // heads
    value = head_gain.shape[0]
    keys, vals = heads * key, heads * value
    wide = 2 * keys + vals
    size = ffn_gate.shape[1]
    last = lax.axis_size("head") - 1
    near = lax.axis_size("seq") == NEAR
    shard = lax.axis_index("seq")
    place = jnp.full((1,), shard, jnp.int32)

    small = jnp.concatenate(
        [alpha_weight, beta_weight, jnp.zeros((alpha_weight.shape[0], LANES - 2 * heads), full)], axis=1
    )
    taps = jnp.concatenate([query_taps, key_taps, value_taps], axis=1)
    params = jnp.stack([-jnp.exp(decay_log), decay_bias])
    params = jnp.pad(params, ((0, 6), (0, LANES - heads)))
    gain = head_gain[None, :]

    if near:
        heavy = [query_weight, key_weight, value_weight, small, gate_weight, output_weight]
        heavy += [ffn_gate, ffn_up, ffn_down]
    else:
        shard_in = jnp.concatenate([query_weight, key_weight, value_weight, small], axis=1)
        heavy = [lax.all_gather(shard_in.astype(low), "seq", axis=0, tiled=True)]
    meta, edge_meta, segrow = segment_tables(doc_lengths, shard, length)
    first_in, pre, ab, edge, w_in, *laid = input_projection(
        tokens, passed_along(tokens[length - 16 :], "seq", 1), mixer_gain, heavy, wide
    )
    if near:
        shard_mix, shard_ffn = laid
    else:
        shard_mix = jnp.concatenate([gate_weight, output_weight.T], axis=1).astype(low)
        shard_ffn = jnp.concatenate([ffn_gate, ffn_up, ffn_down.T], axis=1).astype(low)
    edge = edge[8:]
    local, through, states, inverse, end, *moved = forward_chain(
        pre, ab, meta, segrow, edge, taps, params, heads, key, value, shard_mix if near else None
    )
    end = end.reshape(keys, value + key)
    if near:
        held, moving = [moved[0]], dict(early=end, gathers=[shard_ffn])
        (w_mix,) = held
    else:
        w_mix = lax.all_gather(shard_mix, "seq", axis=0, tiled=True)
        ends = lax.all_gather(end, "seq", axis=0, tiled=True)
        held, moving = [w_mix, ends], {}
    mix_out, mixed, gate_pre, state_in, middle, second_in, *moved = line_call(
        partial(mixer_out_kernel, heads, key, value, last), "mixer_out", 0, length, width, last,
        [gain, ffn_gain[None, :]], held, [first_in, local, through], [tokens],
        [((length, vals), low, "first"), ((length, vals), full, "first"),
         ((length, vals), full, "first"), ((heads, key, value), full, "all"),
         ((length, width), full, "second"), ((length, width), low, "second")],
        [], **moving,
    )
    if near:
        ends, w_ffn = moved
    else:
        w_ffn = lax.all_gather(shard_ffn, "seq", axis=0, tiled=True)
    hidden, gate_grad, lift_grad, narrow_part, middle_grad, middle_low, ffn_gain_part = line_call(
        partial(ffn_kernel, last, size), "ffn", 1, length, width, last,
        [ffn_gain[None, :]], [w_ffn], [second_in, cotangent], [middle, cotangent],
        [((length, size), low, "first")] * 3
        + [((length, width), low, "first"), ((length, width), full, "second"),
           ((length, width), low, "second"), ((8, width), full, "all")],
        [pltpu.VMEM((ROWS, size), full)] * 2,
    )
    narrow_sum = lax.psum_scatter(narrow_part, "head", scatter_dimension=0, tiled=True)
    gate_pgrad, mixed_grad, head_gain_part, adjoint = gate_back(
        middle_low, w_mix, mixed, gate_pre, gain, through, heads, key, value
    )
    adjoints = spread(adjoint.astype(low).reshape(keys, value))
    pairs_up = [(second_in, [gate_grad, lift_grad])]
    pairs_rest = [(cotangent, [hidden]), (first_in, [gate_pgrad]), (middle_low, [mix_out])]
    sums_up = pair_sums(place, pairs_up) if near else None
    sums_rest = pair_sums(place, pairs_rest) if near else None
    if near:
        narrow_sum, sums_up = lax.optimization_barrier((narrow_sum, sums_up))
    narrow_sum = lax.all_gather(narrow_sum, "head", axis=0, tiled=True)
    result = (middle + narrow_sum.astype(full)).astype(low)
    pre_grad, ab_grad, halo, taps_part, params_part, *moved = backward_chain(
        pre, ab, meta, segrow, edge, edge_meta, taps, params, states, inverse, state_in,
        mixed_grad, ends, adjoints, heads, key, value, sums_up,
    )
    got_up = moved
    halo = passed_along(halo, "seq", -1)
    tail = pre_grad[length - 8 :].astype(full) + halo
    pre_grad = lax.dynamic_update_slice(pre_grad, tail.astype(low), (length - 8, 0))
    pairs_in = [(first_in, [pre_grad, ab_grad])]
    sums_in = pair_sums(place, pairs_in) if near else None
    term, mixer_gain_part, *moved = line_call(
        partial(input_grad_kernel, last, keys, vals), "input_grad", 2, length, width, last,
        [mixer_gain[None, :]], [w_in, w_mix], [pre_grad, gate_pgrad, ab_grad],
        [tokens],
        [((length, width), low, "second"), ((8, width), full, "all")],
        [pltpu.VMEM((ROWS, width), full)], scatters=[sums_rest, sums_in] if near else [],
    )
    if near:
        (tokens_grad, query_grad, key_grad, value_grad, alpha_grad, beta_grad, up_grad, lift_grad,
         down_grad, gate_grad, out_grad) = final_sums(
            middle_grad, term, sums_in, moved[1], sums_up, got_up[0], sums_rest, moved[0],
            heads, keys, vals, size,
        )
    else:
        up, rest, into = (plain_sums(place, pairs) for pairs in (pairs_up, pairs_rest, pairs_in))
        tokens_grad = middle_grad + term.astype(full)
        query_grad, key_grad, value_grad = into[:, :keys], into[:, keys : 2 * keys], into[:, 2 * keys : wide]
        alpha_grad, beta_grad = into[:, wide : wide + heads], into[:, wide + heads : wide + 2 * heads]
        up_grad, lift_grad = up[:, :size], up[:, size:]
        down_grad, gate_grad, out_grad = (
            rest[:, :size].T, rest[:, size : size + vals], rest[:, size + vals :].T
        )
    params_part = jnp.sum(params_part.reshape(2, 8, LANES), axis=1).reshape(1, -1)
    lines = [
        jnp.sum(mixer_gain_part, axis=0, keepdims=True),
        jnp.sum(ffn_gain_part, axis=0, keepdims=True),
        jnp.sum(taps_part.reshape(4, 8, -1), axis=1),
        jnp.pad(params_part, ((0, 0), (0, width - params_part.shape[1]))),
        jnp.pad(jnp.sum(head_gain_part, axis=0)[None], ((0, 0), (0, width - value))),
    ]
    sums = small_sums(jnp.concatenate(lines, axis=0), value)
    taps_grad = sums[2:6]
    return (
        result,
        tokens_grad,
        sums[0],
        query_grad,
        key_grad,
        value_grad,
        gate_grad,
        alpha_grad,
        beta_grad,
        sums[6, LANES : LANES + heads],
        sums[6, :heads],
        taps_grad[:, :keys],
        taps_grad[:, keys : 2 * keys],
        taps_grad[:, 2 * keys :],
        sums[7, :value],
        out_grad,
        sums[1],
        up_grad,
        lift_grad,
        down_grad,
    )


def solution(mesh):
    rows, both = P("seq", None), P("seq", "head")
    in_specs = (
        rows, P(), P(), both, both, both, both, both, both, P("head"), P("head"),
        P(None, "head"), P(None, "head"), P(None, "head"), P(), P("head", "seq"), P(),
        both, both, P("head", "seq"), rows,
    )
    out_specs = (
        rows, rows, P(), both, both, both, both, both, both, P("head"), P("head"),
        P(None, "head"), P(None, "head"), P(None, "head"), P(), P("head", "seq"), P(),
        both, both, P("head", "seq"),
    )
    return jax.shard_map(shards, mesh=mesh, in_specs=in_specs, out_specs=out_specs, check_vma=False)
```

```python
from functools import partial

import jax
import jax.numpy as jnp
from jax import lax
from jax.experimental import pallas as pl
from jax.experimental.pallas import tpu as pltpu
from jax.sharding import PartitionSpec as P

BLOCK = 128
LANES = 128
low = jnp.bfloat16
full = jnp.float32
MIB = 1 << 20


NEAR = 8
ONE = dict(pipeline_mode=pl.Buffered(1))
ANY = dict(memory_space=pl.ANY)
FREE = pl.CostEstimate(flops=1, bytes_accessed=1, transcendentals=0)
MESH = pl.DeviceIdType.MESH


def partner(mask):
    index = lax.axis_index("seq")
    bits = (lax.rem(index, 2), lax.rem(index // 2, 2), index // 4)
    return sum((1 << i) * ((1 - b) if mask >> i & 1 else b) for i, b in enumerate(bits))


def greet(masks, last=None):
    barrier = pltpu.get_barrier_semaphore()
    for mask in masks:
        pl.semaphore_signal(barrier, inc=1, device_id={"seq": partner(mask)}, device_id_type=MESH)
    count = len(masks)
    if last is not None:
        place = lax.axis_index("head")
        for there, to in ((place > 0, place - 1), (place < last, place + 1)):

            @pl.when(there)
            def _(to=to):
                pl.semaphore_signal(barrier, inc=1, device_id={"head": to}, device_id_type=MESH)

        count += jnp.minimum(place, 1) + jnp.minimum(last - place, 1)
    pl.semaphore_wait(barrier, count)


class Gather:
    masks = (1, 2, 4)
    semaphores = [pltpu.SemaphoreType.DMA((8,)), pltpu.SemaphoreType.DMA((8,)), pltpu.SemaphoreType.DMA((1,))]

    def __init__(self, shard, whole, sent, got, home):
        self.shard, self.whole, self.sent, self.got, self.home = shard, whole, sent, got, home
        self.size = shard.shape[0]

    def rows(self, mask, first=0, count=None):
        start = pl.multiple_of(partner(mask) * self.size + first, self.size // 2)
        return self.whole.at[pl.ds(start, self.size if count is None else count), :]

    def push(self, slot):
        half = self.size // 2
        mask, src, dst = (
            (2, self.shard, self.rows(0)),
            (4, self.shard, self.rows(0)),
            (2, self.rows(4, 0, half), self.rows(4, 0, half)),
            (4, self.rows(2, half, half), self.rows(2, half, half)),
            (1, self.shard, self.rows(0)),
            (1, self.rows(2), self.rows(2)),
            (1, self.rows(4), self.rows(4)),
            (1, self.rows(6), self.rows(6)),
        )[slot]
        return pltpu.make_async_remote_copy(
            src_ref=src, dst_ref=dst, send_sem=self.sent.at[slot], recv_sem=self.got.at[slot],
            device_id={"seq": partner(mask)}, device_id_type=MESH,
        )

    def local(self):
        return pltpu.make_async_copy(self.shard, self.rows(0), self.home.at[0])

    def start(self):
        self.local().start()
        for slot in (0, 1, 4):
            self.push(slot).start()

    def middle(self):
        for slot in (0, 1):
            self.push(slot).wait_recv()
        for slot in (2, 3, 5, 6):
            self.push(slot).start()

    def late(self):
        for slot in (2, 3):
            self.push(slot).wait_recv()
        self.push(7).start()

    def traded(self, slots):
        for slot in slots:
            self.push(slot).wait_recv()

    def settle(self):
        for slot in range(8):
            self.push(slot).wait_send()

    def end(self):
        self.traded((4, 5, 6, 7))
        self.settle()
        self.local().wait()


class Scatter:
    masks = (2, 4, 6)
    semaphores = [pltpu.SemaphoreType.DMA((3,)), pltpu.SemaphoreType.DMA((3,))]

    def __init__(self, parts, got, sent, came):
        self.parts, self.got, self.sent, self.came = parts, got, sent, came

    def push(self, k):
        return pltpu.make_async_remote_copy(
            src_ref=self.parts.at[k + 1], dst_ref=self.got.at[k], send_sem=self.sent.at[k],
            recv_sem=self.came.at[k], device_id={"seq": partner(2 * k + 2)}, device_id_type=MESH,
        )

    def start(self):
        for k in range(3):
            self.push(k).start()

    def end(self):
        for k in range(3):
            self.push(k).wait()


def load(step, pairs, sems):
    @pl.when(step == 0)
    def _():
        copies = [pltpu.make_async_copy(a, b, sems.at[n]) for n, (a, b) in enumerate(pairs)]
        for copy in copies:
            copy.start()
        for copy in copies:
            copy.wait()


def mm(a, b):
    return jnp.dot(a.astype(low), b.astype(low), preferred_element_type=full)


def mm_nt(a, b):
    return lax.dot_general(
        a.astype(low), b.astype(low), (((1,), (1,)), ((), ())), preferred_element_type=full
    )


def mm_tn(a, b):
    return lax.dot_general(
        a.astype(low), b.astype(low), (((0,), (0,)), ((), ())), preferred_element_type=full
    )


def exact(a, b):
    return jnp.dot(a, b, precision=lax.Precision.HIGHEST, preferred_element_type=full)


def sigmoid(t):
    return 1.0 / (1.0 + jnp.exp(-t))


def softplus(t):
    return jnp.maximum(t, 0.0) + jnp.log(1.0 + jnp.exp(-jnp.abs(t)))


def iotas(size):
    return (
        lax.broadcasted_iota(jnp.int32, (size, size), 0),
        lax.broadcasted_iota(jnp.int32, (size, size), 1),
    )


def conv_sum(ext, taps, meta, first, width, rows):
    total = taps[3:4, first : first + width] * ext[8 : 8 + rows, first : first + width]
    for lag in (1, 2, 3):
        total += (
            taps[3 - lag : 4 - lag, first : first + width]
            * meta[:, lag : lag + 1]
            * ext[8 - lag : 8 - lag + rows, first : first + width]
        )
    return total


def gates(ab, params, heads):
    log_decay = params[0:1, :] * softplus(ab + params[1:2, :])
    beta = sigmoid(ab)
    return log_decay, beta


def decay_parts(cum, cum_t, h, same_low, strict_low, meta):
    size = cum.shape[0]
    col = cum[:, h : h + 1]
    row = cum_t[h : h + 1, :]
    lower = jnp.where(same_low, jnp.exp(jnp.minimum(col - row, 0.0)), 0.0)
    strict = jnp.where(strict_low, lower, 0.0)
    last = cum[size - 1 : size, h : h + 1]
    from_start = jnp.exp(col) * meta[:, 4:5]
    to_end = jnp.exp(last - col) * meta[:, 5:6]
    carried = jnp.exp(last) * meta[size - 1 : size, 4:5]
    return lower, strict, from_start, to_end, carried


def unit_lower_inverse(strict, rows, cols):
    size = strict.shape[0]
    power = jnp.where((rows >> 3) == (cols >> 3), -strict, 0.0)
    inverse = jnp.where(rows == cols, 1.0, power)
    power = mm(power, power)
    inverse = inverse + mm(inverse, power)
    power = mm(power, power)
    inverse = inverse + mm(inverse, power)
    shift = 3
    while (1 << shift) < size:
        off = jnp.where(
            ((rows >> (shift + 1)) == (cols >> (shift + 1))) & ((rows >> shift) != (cols >> shift)),
            strict,
            0.0,
        )
        inverse = inverse - mm(inverse, mm(off, inverse))
        shift += 1
    return inverse


def inverses(stricts, rows, cols):
    size = stricts[0].shape[0]
    near = (rows >> 3) == (cols >> 3)
    powers = [jnp.where(near, -a, 0.0) for a in stricts]
    result = [jnp.where(rows == cols, 1.0, p) for p in powers]
    for _ in range(2):
        powers = [mm(p, p) for p in powers]
        result = [t + mm(t, p) for t, p in zip(result, powers)]
    shift = 3
    while (1 << shift) < size:
        pick = ((rows >> (shift + 1)) == (cols >> (shift + 1))) & (
            (rows >> shift) != (cols >> shift)
        )
        offs = [mm(jnp.where(pick, a, 0.0), t) for a, t in zip(stricts, result)]
        result = [t - mm(t, o) for t, o in zip(result, offs)]
        shift += 1
    return result


def masks(meta, segrow):
    size = meta.shape[0]
    rows, cols = iotas(size)
    same = meta[:, 0:1] == segrow[0:1, :]
    return rows, cols, same & (rows >= cols), same & (rows > cols)


def unit(post):
    return lax.rsqrt(jnp.sum(post * post, axis=-1, keepdims=True) + 1e-06)


def forward_kernel(
    heads, key, value, gathering,
    pre_ref, ab_ref, meta_ref, segrow_ref, edge_ref, taps_ref, params_ref, *refs
):
    step = pl.program_id(0)
    steps = pl.num_programs(0)
    if gathering:
        shard_ref, out_ref, through_ref, states_ref, inverse_ref, end_ref, whole_ref, ext, state, *sems = refs
        moving = Gather(shard_ref, whole_ref, *sems)

        @pl.when(step == 0)
        def _():
            greet(Gather.masks)
            moving.start()

        @pl.when(step == steps - 2)
        def _():
            moving.middle()

    else:
        out_ref, through_ref, states_ref, inverse_ref, end_ref, ext, state = refs
    size = pre_ref.shape[0]
    wide = value + key
    kfirst, vfirst = heads * key, 2 * heads * key

    @pl.when(step == 0)
    def _():
        ext[0:8, :] = edge_ref[...].astype(full)
        rows, cols = iotas(key)
        eye = (rows == cols).astype(full)
        for h in range(heads):
            state[h, :, :value] = jnp.zeros((key, value), full)
            state[h, :, value:] = eye

    @pl.when(step > 0)
    def _():
        ext[0:8, :] = ext[size : size + 8, :]

    ext[8:, :] = pre_ref[...].astype(full)
    meta = meta_ref[...]
    log_decay, beta = gates(ab_ref[...], params_ref, heads)
    rows, cols, same_low, strict_low = masks(meta, segrow_ref)
    cum = exact((rows >= cols).astype(full), log_decay)
    cum_t = cum.T
    qs, ks, vs, lowers, stricts, fs, es, cs = [], [], [], [], [], [], [], []
    for h in range(heads):
        u = conv_sum(ext, taps_ref, meta, h * key, key, size)
        post = u * sigmoid(u)
        q = (post * unit(post)).astype(low)
        u = conv_sum(ext, taps_ref, meta, kfirst + h * key, key, size)
        post = u * sigmoid(u)
        k = (post * unit(post)).astype(low)
        u = conv_sum(ext, taps_ref, meta, vfirst + h * value, value, size)
        v = u * sigmoid(u)
        lower, strict, f, e, c = decay_parts(cum, cum_t, h, same_low, strict_low, meta)
        bcol = beta[:, heads + h : heads + h + 1]
        gram = mm_nt(jnp.concatenate([k, q], axis=0), k)
        qs.append(q), ks.append(k), vs.append(v), fs.append(f), es.append(e), cs.append(c)
        stricts.append(bcol * strict * gram[:size])
        lowers.append(lower * gram[size:])
    ts = inverses(stricts, rows, cols)
    for h in range(heads):
        bcol = beta[:, heads + h : heads + h + 1]
        s = state[h]
        states_ref[0, h] = s.astype(low)
        t = ts[h].astype(low)
        inverse_ref[0, h] = t
        ks_s = mm(ks[h], s)
        fb = fs[h] * bcol
        target = jnp.concatenate(
            [bcol * vs[h] - fb * ks_s[:, :value], -fb * ks_s[:, value:]], axis=1
        )
        delta = mm(t, target).astype(low)
        left = jnp.concatenate([(fs[h] * qs[h].astype(full)).astype(low), lowers[h].astype(low)], axis=1)
        out = mm(left, jnp.concatenate([s.astype(low), delta], axis=0))
        out_ref[:, h * value : (h + 1) * value] = out[:, :value]
        through_ref[:, h * key : (h + 1) * key] = out[:, value:].astype(low)
        ke = es[h] * ks[h].astype(full)
        s = cs[h] * s + mm_tn(ke, delta)
        state[h] = s
        end_ref[h] = s.astype(low)

    if gathering:

        @pl.when(step == steps - 1)
        def _():
            moving.late()
            moving.end()


def forward_chain(pre, ab, meta, segrow, edge, taps, params, heads, key, value, shard=None):
    gathering = shard is not None
    moved = [jax.ShapeDtypeStruct((shard.shape[0] * NEAR, shard.shape[1]), low)] if gathering else []
    extra = dict(collective_id=5, has_side_effects=True) if gathering else {}
    length = pre.shape[0]
    blocks = length // BLOCK
    width = pre.shape[1]
    wide = value + key
    return pl.pallas_call(
        partial(forward_kernel, heads, key, value, gathering),
        grid=(blocks,),
        in_specs=[
            pl.BlockSpec((BLOCK, width), lambda n: (n, 0)),
            pl.BlockSpec((BLOCK, LANES), lambda n: (n, 0)),
            pl.BlockSpec((BLOCK, LANES), lambda n: (n, 0)),
            pl.BlockSpec((8, BLOCK), lambda n: (0, n)),
            pl.BlockSpec((8, width), lambda n: (0, 0)),
            pl.BlockSpec(taps.shape, lambda n: (0, 0)),
            pl.BlockSpec((8, LANES), lambda n: (0, 0)),
        ]
        + [pl.BlockSpec(**ANY) for _ in moved],
        out_specs=[
            pl.BlockSpec((BLOCK, heads * value), lambda n: (n, 0)),
            pl.BlockSpec((BLOCK, heads * key), lambda n: (n, 0)),
            pl.BlockSpec((1, heads, key, wide), lambda n: (n, 0, 0, 0)),
            pl.BlockSpec((1, heads, BLOCK, BLOCK), lambda n: (n, 0, 0, 0)),
            pl.BlockSpec((heads, key, wide), lambda n: (0, 0, 0)),
        ]
        + [pl.BlockSpec(**ANY) for _ in moved],
        out_shape=[
            jax.ShapeDtypeStruct((length, heads * value), full),
            jax.ShapeDtypeStruct((length, heads * key), low),
            jax.ShapeDtypeStruct((blocks, heads, key, wide), low),
            jax.ShapeDtypeStruct((blocks, heads, BLOCK, BLOCK), low),
            jax.ShapeDtypeStruct((heads, key, wide), low),
        ]
        + moved,
        scratch_shapes=[
            pltpu.VMEM((BLOCK + 8, width), full),
            pltpu.VMEM((heads, key, wide), full),
        ]
        + (Gather.semaphores if gathering else []),
        compiler_params=pltpu.CompilerParams(vmem_limit_bytes=48 * MIB, **extra),
        cost_estimate=FREE,
        name="chain_forward",
    )(pre, ab, meta, segrow, edge, taps, params, *([shard] if gathering else []))


def gate_back_kernel(heads, key, value, dz_ref, mixed_ref, gate_ref, gain_ref, through_ref, whole_ref,
                     dgz_ref, do_ref, gain_grad_ref, adjoint_ref, weights, dy_ref, sems):
    load(pl.program_id(0), [(whole_ref.at[:, heads * value :], weights)], sems)

    @pl.when(pl.program_id(0) == 0)
    def _():
        gain_grad_ref[...] = jnp.zeros_like(gain_grad_ref)
        adjoint_ref[...] = jnp.zeros_like(adjoint_ref)

    rows = dz_ref.shape[0]
    gain = gain_ref[0:1, :]
    dy_ref[...] = mm(dz_ref[...], weights[...])
    for h in range(heads):
        cols = slice(h * value, (h + 1) * value)
        o = mixed_ref[:, cols].astype(full)
        s3 = lax.rsqrt(jnp.mean(o * o, axis=-1, keepdims=True) + 1e-05)
        n3 = o * s3
        gz = gate_ref[:, cols]
        sig = sigmoid(gz)
        sg = gz * sig
        dy = dy_ref[:, cols]
        dyn = dy * n3
        part = dyn * sg
        gain_grad_ref[...] += jnp.sum(part.reshape(rows // 8, 8, value), axis=0)
        dgz_ref[:, cols] = (dyn * gain * (sig * (1.0 + gz * (1.0 - sig)))).astype(low)
        dn3 = dy * gain * sg
        do = s3 * (dn3 - n3 * jnp.mean(dn3 * n3, axis=-1, keepdims=True))
        do = do.astype(low)
        do_ref[:, cols] = do
        adjoint_ref[h] += mm_tn(through_ref[:, h * key : (h + 1) * key], do)


def gate_back(dz, w_mix, mixed, gate, gain, through, heads, key, value, rows=256):
    length, width = dz.shape
    wide = heads * value
    return pl.pallas_call(
        partial(gate_back_kernel, heads, key, value),
        grid=(length // rows,),
        in_specs=[
            pl.BlockSpec((rows, width), lambda n: (n, 0)),
            pl.BlockSpec((rows, wide), lambda n: (n, 0)),
            pl.BlockSpec((rows, wide), lambda n: (n, 0)),
            pl.BlockSpec((1, value), lambda n: (0, 0)),
            pl.BlockSpec((rows, heads * key), lambda n: (n, 0)),
        ]
        + [pl.BlockSpec(**ANY)],
        out_specs=[
            pl.BlockSpec((rows, wide), lambda n: (n, 0)),
            pl.BlockSpec((rows, wide), lambda n: (n, 0)),
            pl.BlockSpec((8, value), lambda n: (0, 0)),
            pl.BlockSpec((heads, key, value), lambda n: (0, 0, 0)),
        ],
        out_shape=[
            jax.ShapeDtypeStruct((length, wide), low),
            jax.ShapeDtypeStruct((length, wide), low),
            jax.ShapeDtypeStruct((8, value), full),
            jax.ShapeDtypeStruct((heads, key, value), full),
        ],
        scratch_shapes=[
            pltpu.VMEM((width, wide), low),
            pltpu.VMEM((rows, wide), full),
            pltpu.SemaphoreType.DMA((1,)),
        ],
        compiler_params=pltpu.CompilerParams(vmem_limit_bytes=48 * MIB),
        cost_estimate=FREE,
        name="gate_back",
    )(dz, mixed, gate, gain, through, w_mix)


def lane_sum(array):
    return jnp.sum(array, axis=-1, keepdims=True)


def backward_kernel(
    heads, key, value, devices, masks_of, scattering,
    pre_ref, tail_ref, ab_ref, meta_ref, segrow_ref, edge_ref, edge_meta_ref, taps_ref, params_ref,
    states_ref, inverse_ref, state_in_ref, do_ref, ends_ref, *refs
):
    step = pl.program_id(0)
    steps = pl.num_programs(0)
    pieces, refs = refs[: len(masks_of)], list(refs[len(masks_of) :])
    parts_ref = refs.pop(0) if scattering else None
    dpre_ref, dab_ref, halo_ref, taps_grad_ref, params_grad_ref = refs[:5]
    refs = refs[5:]
    got_ref = refs.pop(0) if scattering else None
    ext, du, adjoint, adjoints, home, *sems = refs
    if scattering:
        moving = Scatter(parts_ref, got_ref, *sems)

        @pl.when(step == 0)
        def _():
            greet(Scatter.masks)
            moving.start()

    size = pre_ref.shape[0]
    kfirst, vfirst = heads * key, 2 * heads * key

    @pl.when(step == 0)
    def _():
        adjoint[...] = jnp.zeros_like(adjoint)
        tall = heads * key
        copies = []
        for n, (mask, ref) in enumerate(zip(masks_of, pieces)):
            first = 0 if mask is None else pl.multiple_of(partner(mask) * tall, tall)
            target = adjoints.at[pl.ds(first, ref.shape[0]), :]
            copies.append(pltpu.make_async_copy(ref, target, home.at[n]))
        for copy in copies:
            copy.start()
        for copy in copies:
            copy.wait()

        def one(k, carry):
            j = devices - 1 - k
            for h in range(heads):
                rows = pl.ds(pl.multiple_of(j * tall + h * key, key), key)
                adjoint[h] = (
                    mm_tn(ends_ref[rows, value:], adjoint[h]) + adjoints[rows, :].astype(full)
                )
            return carry

        lax.fori_loop(0, devices - 1 - lax.axis_index("seq"), one, 0)
        du[8 + size :, :] = jnp.zeros((8, du.shape[1]), full)
        taps_grad_ref[...] = jnp.zeros_like(taps_grad_ref)
        params_grad_ref[...] = jnp.zeros_like(params_grad_ref)

    @pl.when(step > 0)
    def _():
        du[8 + size :, :] = du[8:16, :]

    du[0:8, :] = jnp.zeros((8, du.shape[1]), full)

    @pl.when(step < steps - 1)
    def _():
        ext[0:8, :] = tail_ref[8:16, :].astype(full)

    @pl.when(step == steps - 1)
    def _():
        ext[0:8, :] = edge_ref[...].astype(full)

    ext[8:, :] = pre_ref[...].astype(full)
    meta = meta_ref[...]
    ab = ab_ref[...]
    log_decay, beta = gates(ab, params_ref, heads)
    rows, cols, same_low, strict_low = masks(meta, segrow_ref)
    cum = exact((rows >= cols).astype(full), log_decay)
    cum_t = cum.T
    lane = lax.broadcasted_iota(jnp.int32, (size, LANES), 1)
    row8 = lax.broadcasted_iota(jnp.int32, (8, size), 0)
    dcum = jnp.zeros((size, LANES), full)
    dcum_rows = jnp.zeros((8, size), full)
    dcum_last = jnp.zeros((1, LANES), full)
    dbeta = jnp.zeros((size, LANES), full)
    lane1 = lax.broadcasted_iota(jnp.int32, (1, LANES), 1)

    for h in range(heads):
        qcols = slice(h * key, (h + 1) * key)
        kcols = slice(kfirst + h * key, kfirst + (h + 1) * key)
        vcols = slice(vfirst + h * value, vfirst + (h + 1) * value)
        uq = conv_sum(ext, taps_ref, meta, h * key, key, size)
        sq = sigmoid(uq)
        pq = uq * sq
        rq = unit(pq)
        qf = pq * rq
        q = qf.astype(low)
        uk = conv_sum(ext, taps_ref, meta, kfirst + h * key, key, size)
        sk = sigmoid(uk)
        pk = uk * sk
        rk = unit(pk)
        kf = pk * rk
        k = kf.astype(low)
        uv = conv_sum(ext, taps_ref, meta, vfirst + h * value, value, size)
        sv = sigmoid(uv)
        v = uv * sv
        lower, strict, f, e, c = decay_parts(cum, cum_t, h, same_low, strict_low, meta)
        b = beta[:, heads + h : heads + h + 1]
        kq = jnp.concatenate([k, q], axis=0)
        gram = mm_nt(kq, k)
        kk, qk = gram[:size], gram[size:]
        stored = states_ref[0, h]
        s = stored[:, :value].astype(full) + mm(stored[:, value:], state_in_ref[h])
        slow = s.astype(low)
        kqs = mm(kq, slow)
        ks, qs = kqs[:size], kqs[size:]
        rest = v - f * ks
        t = inverse_ref[0, h]
        delta = mm(t, b * rest).astype(low)
        do = do_ref[:, h * value : (h + 1) * value]
        dof = do.astype(full)
        ds = adjoint[h]
        dslow = ds.astype(low)
        ke = (e * kf).astype(low)
        p = lower * qk
        left = jnp.concatenate([p.T.astype(low), ke], axis=1)
        ddelta = mm(left, jnp.concatenate([do, dslow], axis=0))
        dtarget = mm_tn(t, ddelta)
        outer = mm_nt(jnp.concatenate([do, dtarget.astype(low)], axis=0), delta)
        dp, dan = outer[:size], outer[size:]
        eg = lower * dp
        hn = -strict * dan
        hg = b * hn
        x = eg * qk
        hk = hn * kk
        g1 = (b * f) * dtarget
        fdo = f * dof
        pair = jnp.concatenate([fdo.astype(low), (-g1).astype(low)], axis=0)
        both = mm_nt(pair, slow)
        dq = both[:size] + mm(eg, k)
        dsk = e * mm_nt(delta, dslow)
        left = jnp.concatenate([(hg + hg.T).astype(low), eg.T.astype(low)], axis=1)
        dk = both[size:] + dsk + mm(left, kq)
        dv = b * dtarget
        z = lane_sum(kf * dsk)
        dfrom = lane_sum(dof * qs) - b * lane_sum(dtarget * ks)
        hrow = lane_sum(hk)
        db = hrow + lane_sum(dtarget * rest)
        dbeta = dbeta + jnp.where(lane == heads + h, db, 0.0)
        dcum = dcum + jnp.where(lane == h, lane_sum(x) + b * hrow + f * dfrom - z, 0.0)
        drow = jnp.sum(x + b * hk, axis=0, keepdims=True)
        dcum_rows = dcum_rows + jnp.where(row8 == h, drow, 0.0)
        dlast = jnp.sum(z, axis=0, keepdims=True) + c * jnp.sum(
            lane_sum(ds * s), axis=0, keepdims=True
        )
        dcum_last = dcum_last + jnp.where(lane1 == h, dlast, 0.0)
        adjoint[h] = c * ds + mm_tn(jnp.concatenate([q, k], axis=0), pair)

        dpq = rq * (dq - qf * lane_sum(dq * qf))
        du[8 : 8 + size, qcols] = dpq * (sq * (1.0 + uq * (1.0 - sq)))
        dpk = rk * (dk - kf * lane_sum(dk * kf))
        du[8 : 8 + size, kcols] = dpk * (sk * (1.0 + uk * (1.0 - sk)))
        du[8 : 8 + size, vcols] = dv * (sv * (1.0 + uv * (1.0 - sv)))

    padded = jnp.concatenate([dcum_rows, jnp.zeros((LANES - 8, size), full)], axis=0)
    rowi = lax.broadcasted_iota(jnp.int32, (size, LANES), 0)
    dcum = dcum - padded.T + jnp.where(rowi == size - 1, dcum_last, 0.0)
    dlog = exact((rows <= cols).astype(full), dcum)
    dga = dlog * params_ref[0:1, :] * sigmoid(ab + params_ref[1:2, :])
    is_decay = lane < heads
    dga = jnp.where(is_decay, dga, 0.0)
    params_grad_ref[0:8, :] += jnp.sum(dga.reshape(size // 8, 8, LANES), axis=0)
    decay_part = jnp.where(is_decay, dlog * log_decay, 0.0)
    params_grad_ref[8:16, :] += jnp.sum(decay_part.reshape(size // 8, 8, LANES), axis=0)
    dab_ref[...] = jnp.where(is_decay, dga, dbeta * beta * (1.0 - beta)).astype(low)

    width = du.shape[1]
    for first in range(0, width, 512):
        cs = slice(first, first + 512)
        own = du[8 : 8 + size, cs]
        total = taps_ref[3:4, cs] * own
        taps_grad_ref[24:32, cs] += jnp.sum(
            (own * ext[8 : 8 + size, cs]).reshape(size // 8, 8, 512), axis=0
        )
        for lag in (1, 2, 3):
            total += taps_ref[3 - lag : 4 - lag, cs] * meta[:, 5 + lag : 6 + lag] * du[
                8 + lag : 8 + lag + size, cs
            ]
            taps_grad_ref[8 * (3 - lag) : 8 * (4 - lag), cs] += jnp.sum(
                (own * meta[:, lag : lag + 1] * ext[8 - lag : 8 - lag + size, cs]).reshape(
                    size // 8, 8, 512
                ),
                axis=0,
            )
        dpre_ref[:, cs] = total.astype(low)

    @pl.when(step == steps - 1)
    def _():
        edge_meta = edge_meta_ref[...]
        halo = jnp.zeros(halo_ref.shape, full)
        for lag in (1, 2, 3):
            halo += taps_ref[3 - lag : 4 - lag, :] * edge_meta[:, 5 + lag : 6 + lag] * du[
                lag : 8 + lag, :
            ]
        halo_ref[...] = halo
        if scattering:
            moving.end()


def backward_chain(pre, ab, meta, segrow, edge, edge_meta, taps, params, states, inverse,
                   state_in, do, ends, adjoints, heads, key, value, parts=None):
    scattering = parts is not None
    moved = [jax.ShapeDtypeStruct((3,) + parts.shape[1:], low)] if scattering else []
    extra = dict(collective_id=6, has_side_effects=True) if scattering else {}
    masks_of = [mask for mask, _ in adjoints]
    devices = ends.shape[0] // (heads * key)
    length, width = pre.shape
    blocks = length // BLOCK
    wide = value + key
    once = dict(pipeline_mode=pl.Buffered(1))
    last = blocks - 1
    return pl.pallas_call(
        partial(backward_kernel, heads, key, value, devices, masks_of, scattering),
        grid=(blocks,),
        in_specs=[
            pl.BlockSpec((BLOCK, width), lambda n: (last - n, 0)),
            pl.BlockSpec((16, width), lambda n: (jnp.maximum((last - n) * (BLOCK // 16) - 1, 0), 0)),
            pl.BlockSpec((BLOCK, LANES), lambda n: (last - n, 0)),
            pl.BlockSpec((BLOCK, LANES), lambda n: (last - n, 0)),
            pl.BlockSpec((8, BLOCK), lambda n: (0, last - n)),
            pl.BlockSpec((8, width), lambda n: (0, 0)),
            pl.BlockSpec((8, LANES), lambda n: (0, 0)),
            pl.BlockSpec(taps.shape, lambda n: (0, 0)),
            pl.BlockSpec((8, LANES), lambda n: (0, 0)),
            pl.BlockSpec((1, heads, key, wide), lambda n: (last - n, 0, 0, 0)),
            pl.BlockSpec((1, heads, BLOCK, BLOCK), lambda n: (last - n, 0, 0, 0)),
            pl.BlockSpec((heads, key, value), lambda n: (0, 0, 0)),
            pl.BlockSpec((BLOCK, heads * value), lambda n: (last - n, 0)),
            pl.BlockSpec(ends.shape, lambda n: (0, 0), **once),
        ]
        + [pl.BlockSpec(**ANY) for _ in (*adjoints, *moved)],
        out_specs=[
            pl.BlockSpec((BLOCK, width), lambda n: (last - n, 0)),
            pl.BlockSpec((BLOCK, LANES), lambda n: (last - n, 0)),
            pl.BlockSpec((8, width), lambda n: (0, 0)),
            pl.BlockSpec((32, width), lambda n: (0, 0)),
            pl.BlockSpec((16, LANES), lambda n: (0, 0)),
        ]
        + [pl.BlockSpec(**ANY) for _ in moved],
        out_shape=[
            jax.ShapeDtypeStruct((length, width), low),
            jax.ShapeDtypeStruct((length, LANES), low),
            jax.ShapeDtypeStruct((8, width), full),
            jax.ShapeDtypeStruct((32, width), full),
            jax.ShapeDtypeStruct((16, LANES), full),
        ]
        + moved,
        scratch_shapes=[
            pltpu.VMEM((BLOCK + 8, width), full),
            pltpu.VMEM((BLOCK + 16, width), full),
            pltpu.VMEM((heads, key, value), full),
            pltpu.VMEM((devices * heads * key, value), low),
            pltpu.SemaphoreType.DMA((len(adjoints),)),
        ]
        + (Scatter.semaphores if scattering else []),
        compiler_params=pltpu.CompilerParams(vmem_limit_bytes=56 * MIB, **extra),
        cost_estimate=FREE,
        name="chain_backward",
    )(pre, pre, ab, meta, segrow, edge, edge_meta, taps, params, states, inverse, state_in, do, ends,
      *[a for _, a in adjoints], *([parts] if scattering else []))


def segment_tables(doc_lengths, shard, length):
    starts = jnp.cumsum(doc_lengths, dtype=jnp.int32) - doc_lengths
    positions = shard * length + jnp.arange(-16, length + 8, dtype=jnp.int32)
    seg = jnp.sum((starts[None, :] <= positions[:, None]).astype(jnp.int32), axis=1)
    own = seg[16 : 16 + length]

    def lanes(first, count):
        base = seg[first : first + count]
        back = [seg[first - l : first - l + count] == base for l in (1, 2, 3)]
        ahead = [seg[first + l : first + l + count] == base for l in (1, 2, 3)]
        return base, back, ahead

    base, back, ahead = lanes(16, length)
    blocks = own.reshape(-1, BLOCK)
    before = seg[15 : 15 + length : BLOCK]
    alive = (blocks == before[:, None]).reshape(-1)
    to_last = (blocks == blocks[:, -1:]).reshape(-1)
    columns = [base, *back, alive, to_last, *ahead]
    meta = jnp.stack([a.astype(full) for a in columns], axis=1)
    meta = jnp.pad(meta, ((0, 0), (0, LANES - meta.shape[1])))
    base, back, ahead = lanes(8, 8)
    columns = [base, *back, base, base, *ahead]
    edge_meta = jnp.stack([a.astype(full) for a in columns], axis=1)
    edge_meta = jnp.pad(edge_meta, ((0, 0), (0, LANES - edge_meta.shape[1])))
    segrow = jnp.broadcast_to(own.astype(full)[None, :], (8, length))
    return meta, edge_meta, segrow


ROWS = 256
PIECE = 32
HOP = 2
EACH = ROWS // PIECE
AHEAD = 1 + (EACH - 1 + 3 * HOP) // EACH
RING = AHEAD + 1


def exchanged(block, mask):
    return lax.ppermute(block, "seq", [(i, i ^ mask) for i in range(lax.axis_size("seq"))])


def spread(shard):
    if lax.axis_size("seq") != NEAR:
        return [(None, lax.all_gather(shard, "seq", axis=0, tiled=True))]
    own = [(0, shard)] + [(mask, exchanged(shard, mask)) for mask in (2, 4, 6)]
    return own + [(mask + 1, exchanged(a, 1)) for mask, a in own]


def line_scratch(length, width):
    pieces = length // PIECE
    return [
        pltpu.VMEM((RING, ROWS, width), low),
        pltpu.VMEM((length, width), low),
        pltpu.VMEM((length, width), low),
        pltpu.SemaphoreType.DMA((pieces,)),
        pltpu.SemaphoreType.DMA((pieces,)),
        pltpu.SemaphoreType.DMA((pieces,)),
        pltpu.SemaphoreType.DMA((pieces,)),
    ]


def line_sum(step, last, stages, finish, scratch):
    own, from_left, from_right, got_left, got_right, sent_right, sent_left = scratch
    place = lax.axis_index("head")
    length, width = from_left.shape
    blocks, pieces = length // ROWS, length // PIECE
    left_there, right_there = place > 0, place < last

    def rows(piece):
        return pl.ds(pl.multiple_of(piece * PIECE, PIECE), PIECE)

    def hop(piece, rightwards):
        kept, sent, got, to = (
            (from_left, sent_right, got_left, place + 1)
            if rightwards
            else (from_right, sent_left, got_right, place - 1)
        )
        return pltpu.make_async_remote_copy(
            src_ref=kept.at[rows(piece)],
            dst_ref=kept.at[rows(piece)],
            send_sem=sent.at[piece],
            recv_sem=got.at[piece],
            device_id={"head": to},
            device_id_type=MESH,
        )

    def own_piece(piece):
        slot = lax.rem(piece // EACH, RING)
        first = pl.multiple_of(lax.rem(piece, EACH) * PIECE, PIECE)
        return own[slot, pl.ds(first, PIECE), :].astype(full)

    @pl.when(step == 0)
    def _():
        @pl.when(place == 0)
        def _():
            from_left[...] = jnp.zeros_like(from_left)

        @pl.when(place == last)
        def _():
            from_right[...] = jnp.zeros_like(from_right)

    def one(q, carry):
        now = (step - 1) * EACH + q
        for rightwards in (True, False):
            came, more = (left_there, right_there) if rightwards else (right_there, left_there)
            kept = from_left if rightwards else from_right
            piece = now - HOP * (place if rightwards else last - place)

            @pl.when((piece >= 0) & (piece < pieces))
            def _():
                @pl.when(came)
                def _():
                    hop(piece, rightwards).wait_recv()

                @pl.when(more)
                def _():
                    kept[rows(piece), :] = (
                        own_piece(piece) + kept[rows(piece), :].astype(full)
                    ).astype(low)
                    hop(piece, rightwards).start()

        return carry

    done = 0
    for n, stage in enumerate(stages):

        @pl.when(step < blocks)
        def _(n=n, stage=stage):
            value = stage()
            if n == len(stages) - 1:
                own[lax.rem(step, RING)] = value.astype(low)

        until = EACH * (n + 1) // len(stages)
        lax.fori_loop(done, until, one, 0)
        done = until

    @pl.when(step >= AHEAD)
    def _():
        block = step - AHEAD
        span = pl.ds(pl.multiple_of(block * ROWS, ROWS), ROWS)
        total = from_left[span, :].astype(full) + from_right[span, :].astype(full)
        twice = jnp.where(left_there & right_there, 1.0, 0.0)
        finish(total - twice * own[lax.rem(block, RING)].astype(full))

    @pl.when(step == blocks + AHEAD - 1)
    def _():
        def settle(piece, carry):
            @pl.when(right_there)
            def _():
                hop(piece, True).wait_send()

            @pl.when(left_there)
            def _():
                hop(piece, False).wait_send()

            return carry

        lax.fori_loop(0, pieces, settle, 0)


def union(kinds):
    return sorted({mask for kind in kinds for mask in kind.masks})


def line_call(kernel, name, collective, length, width, last, resident, weights, entering, leaving, outs,
              scratch, gathers=(), scatters=(), early=None, masks=()):
    blocks = length // ROWS
    steps = blocks + AHEAD
    cuts, weights = [c for _, c in weights], [a for a, _ in weights]

    def spec(array, stage):
        if stage == "first":
            return pl.BlockSpec((ROWS, array.shape[1]), lambda g: (jnp.minimum(g, blocks - 1), 0))
        if stage == "second":
            return pl.BlockSpec((ROWS, array.shape[1]), lambda g: (jnp.maximum(g - AHEAD, 0), 0))
        rank = len(array.shape)
        return pl.BlockSpec(array.shape, lambda g: (0,) * rank, **ONE)

    in_specs = [spec(a, "all") for a in resident]
    first_one = [] if early is None else [early]
    in_specs += [pl.BlockSpec(**ANY) for _ in (*weights, *first_one, *gathers, *scatters)]
    in_specs += [spec(a, "first") for a in entering] + [spec(a, "second") for a in leaving]
    shapes = [jax.ShapeDtypeStruct(shape, dtype) for shape, dtype, _ in outs]
    out_specs = [
        spec(s, stage) if stage != "all" else pl.BlockSpec(s.shape, lambda g, r=len(s.shape): (0,) * r)
        for s, (_, _, stage) in zip(shapes, outs)
    ]
    moved = [jax.ShapeDtypeStruct((a.shape[0] * NEAR, a.shape[1]), low) for a in (*first_one, *gathers)]
    moved += [jax.ShapeDtypeStruct((3,) + a.shape[1:], low) for a in scatters]
    kinds = [Gather] * len(gathers) + [Scatter] * len(scatters)
    whole_first = [pltpu.VMEM(s.shape, low) for s in moved[: len(first_one)]]
    held = [pltpu.VMEM(a.shape, low) for a in weights] + [pltpu.SemaphoreType.DMA((sum(len(c) for c in cuts),))]
    held += whole_first + [s for _ in first_one for s in Gather.semaphores]
    held += [s for kind in kinds for s in kind.semaphores]

    def body(*refs):
        refs = list(refs)

        def take(n):
            head, refs[:] = refs[:n], refs[n:]
            return head

        own_in, heavy = take(len(resident)), take(len(weights))
        ahead, sources = take(len(first_one)), take(len(kinds))
        chunks = take(len(entering) + len(leaving))
        own_out, handed, targets = take(len(outs)), take(len(first_one)), take(len(kinds))
        own_scratch = take(len(scratch) + 7)
        matrices, (sems,) = take(len(weights)), take(1)
        if first_one:
            (table,), signals = take(1), take(3)
            lead = Gather(ahead[0], table, *signals)
            back = pltpu.make_async_copy(table, handed[0], signals[2].at[0])
            matrices.append(table)
        carried = [kind(a, b, *take(len(kind.semaphores))) for kind, a, b in zip(kinds, sources, targets)]
        step = pl.program_id(0)

        @pl.when(step == 0)
        def _():
            greet(sorted({*masks, *union(kinds + [Gather] * len(first_one))}), last)
            for c in [lead] if first_one else carried:
                c.start()

        waits = []
        for source, target, parts in zip(heavy, matrices, cuts):
            for first, count in parts:
                part = pl.ds(first, count)
                waits.append(
                    pltpu.make_async_copy(source.at[:, part], target.at[:, part], sems.at[len(waits)])
                )

        @pl.when(step == 0)
        def _():
            for copy in waits:
                copy.start()

        def ready(k):
            @pl.when(step == 0)
            def _():
                waits[k].wait()

        if first_one:

            @pl.when(step == 0)
            def _():
                lead.middle()
                lead.late()
                for c in carried:
                    c.start()
                lead.end()
                back.start()

        for at, turn in ((steps - 3, "middle"), (steps - 1, "late")):

            @pl.when(step == at)
            def _(turn=turn):
                for c in carried:
                    if isinstance(c, Gather):
                        getattr(c, turn)()

        kernel(ready, matrices, *own_in, *chunks, *own_out, *own_scratch)

        @pl.when(step == steps - 1)
        def _():
            for c in carried:
                c.end()
            if first_one:
                back.wait()

    return pl.pallas_call(
        body,
        grid=(steps,),
        in_specs=in_specs,
        out_specs=out_specs + [pl.BlockSpec(**ANY) for _ in moved],
        out_shape=shapes + moved,
        scratch_shapes=scratch + line_scratch(length, width) + held,
        compiler_params=pltpu.CompilerParams(
            collective_id=collective, has_side_effects=True, vmem_limit_bytes=60 * MIB
        ),
        cost_estimate=FREE,
        name=name,
    )(*resident, *weights, *first_one, *gathers, *scatters, *entering, *leaving)


def mixer_out_kernel(heads, key, value, last, handed, ready, matrices,
                     head_gain_ref, gain_ref,
                     first_ref, local_ref, through_ref, tokens_ref,
                     y_ref, mixed_ref, gate_ref, state_ref, middle_ref, second_ref, *scratch):
    step = pl.program_id(0)
    weights, ends = matrices
    vals = heads * value

    if handed is not None:
        ready(handed)

    @pl.when(step == 0)
    def _():
        state_ref[...] = jnp.zeros_like(state_ref)

        def one(j, carry):
            for h in range(heads):
                rows = pl.ds(pl.multiple_of((j * heads + h) * key, key), key)
                part = ends[rows, :]
                state_ref[h] = mm(part[:, value:], state_ref[h]) + part[:, :value].astype(full)
            return carry

        lax.fori_loop(0, lax.axis_index("seq"), one, 0)

    def gate():
        ready(0)
        gate_ref[...] = mm(first_ref[...], weights[:, :vals])

    def mix():
        for h in range(heads):
            cols = slice(h * value, (h + 1) * value)
            o = local_ref[:, cols] + mm(through_ref[:, h * key : (h + 1) * key], state_ref[h])
            mixed_ref[:, cols] = o
            s3 = lax.rsqrt(jnp.mean(o * o, axis=-1, keepdims=True) + 1e-05)
            gz = gate_ref[:, cols]
            y_ref[:, cols] = (o * s3 * head_gain_ref[0:1, :] * (gz * sigmoid(gz))).astype(low)

    def project():
        ready(1)
        return mm_nt(y_ref[...], weights[:, vals:])

    def finish(total):
        middle = tokens_ref[...].astype(full) + total
        middle_ref[...] = middle
        scale = lax.rsqrt(jnp.mean(middle * middle, axis=-1, keepdims=True) + 1e-06)
        second_ref[...] = (middle * scale * gain_ref[0:1, :]).astype(low)

    line_sum(step, last, [gate, mix, project], finish, scratch)


def ffn_kernel(last, size, ready, matrices, gain_ref,
               second_ref, cot_ref, middle_ref, cot_late_ref,
               hidden_ref, dgate_ref, dup_ref, partial_ref, dmiddle_ref, dlow_ref, gain_grad_ref,
               fg, fu, *scratch):
    step = pl.program_id(0)
    (weights,) = matrices
    w_gate, w_up, w_down = (slice(n * size, (n + 1) * size) for n in range(3))

    @pl.when(step == 0)
    def _():
        gain_grad_ref[...] = jnp.zeros_like(gain_grad_ref)

    def one():
        ready(0)
        fg[...] = mm(second_ref[...], weights[:, w_gate])

    def two():
        ready(1)
        fu[...] = mm(second_ref[...], weights[:, w_up])

    def three():
        ready(2)
        g = fg[...]
        hidden = (g * sigmoid(g) * fu[...]).astype(low)
        hidden_ref[...] = hidden
        partial_ref[...] = mm_nt(hidden, weights[:, w_down]).astype(low)

    def four():
        dhid = mm(cot_ref[...], weights[:, w_down])
        g = fg[...]
        sig = sigmoid(g)
        dgate_ref[...] = (dhid * fu[...] * (sig * (1.0 + g * (1.0 - sig)))).astype(low)
        dup_ref[...] = (dhid * (g * sig)).astype(low)

    def five():
        return mm_nt(dgate_ref[...], weights[:, w_gate]) + mm_nt(dup_ref[...], weights[:, w_up])

    def finish(grad):
        middle = middle_ref[...]
        scale = lax.rsqrt(jnp.mean(middle * middle, axis=-1, keepdims=True) + 1e-06)
        norm = middle * scale
        gain_grad_ref[...] += jnp.sum((grad * norm).reshape(ROWS // 8, 8, -1), axis=0)
        weighted = grad * gain_ref[0:1, :]
        dm = cot_late_ref[...].astype(full) + scale * (
            weighted - norm * jnp.mean(weighted * norm, axis=-1, keepdims=True)
        )
        dmiddle_ref[...] = dm
        dlow_ref[...] = dm.astype(low)

    line_sum(step, last, [one, two, three, four, five], finish, scratch)


def input_grad_kernel(last, keys, vals, near, ready, matrices, gain_ref, lines_ref,
                      dpre_ref, dgz_ref, dab_ref, tokens_ref,
                      term_ref, gains_ref, part, gain_grad, *scratch):
    step = pl.program_id(0)
    w_in, w_mix = matrices
    wide = 2 * keys + vals
    if near:
        (got, sent, came), scratch = scratch[:3], scratch[3:]

    @pl.when(step == 0)
    def _():
        gain_grad[...] = jnp.zeros_like(gain_grad)

    def one():
        ready(0)
        part[...] = mm_nt(dpre_ref[...], w_in[:, :wide])

    def two():
        ready(1)
        return (
            part[...]
            + mm_nt(dgz_ref[...], w_mix[:, :vals])
            + mm_nt(dab_ref[...], w_in[:, wide:])
        )

    def finish(grad):
        stream = tokens_ref[...].astype(full)
        scale = lax.rsqrt(jnp.mean(stream * stream, axis=-1, keepdims=True) + 1e-06)
        norm = stream * scale
        gain_grad[...] += jnp.sum((grad * norm).reshape(ROWS // 8, 8, -1), axis=0)
        weighted = grad * gain_ref[0:1, :]
        term_ref[...] = (
            scale * (weighted - norm * jnp.mean(weighted * norm, axis=-1, keepdims=True))
        ).astype(low)

    line_sum(step, last, [one, two], finish, scratch)

    @pl.when(step == pl.num_programs(0) - 1)
    def _():
        row = lax.broadcasted_iota(jnp.int32, gain_grad.shape, 0)
        first = jnp.sum(gain_grad[...], axis=0, keepdims=True)
        own = lines_ref[...] + jnp.where(row == 0, first, 0.0)
        if not near:
            gains_ref[...] = own
            return
        gain_grad[...] = own
        me = lax.axis_index("seq")

        def push(mask):
            return pltpu.make_async_remote_copy(
                src_ref=gain_grad, dst_ref=got.at[me], send_sem=sent.at[mask], recv_sem=came.at[mask],
                device_id={"seq": partner(mask)}, device_id_type=MESH,
            )

        for mask in range(1, NEAR):
            push(mask).start()
        got[me] = own
        for mask in range(1, NEAR):
            push(mask).wait()
        gains_ref[...] = sum((got[k] for k in range(1, NEAR)), start=got[0])


def input_kernel(wide, gathering, gain_ref, *refs):
    rows = 256
    if gathering:
        heavy, (before_hbm, tokens_hbm), refs = refs[:9], refs[9:11], refs[11:]
        small_ref, sources = heavy[3], heavy[4:]
    else:
        (shard_ref, before_hbm, tokens_hbm), refs = refs[:3], refs[3:]
    first_ref, pre_ref, ab_ref, edge_ref, whole_ref = refs[:5]
    refs = refs[5:]
    if gathering:
        (mix_ref, ffn_ref), refs = refs[:2], refs[2:]
    weights, total, tokens_ref, before, home, *refs = refs
    length, width = tokens_ref.shape
    half = width // 4
    back = pltpu.make_async_copy(weights, whole_ref, home.at[0])
    here = pltpu.make_async_copy(tokens_hbm, tokens_ref, home.at[1])
    here.start()
    if gathering:
        shard, *buffers = refs[:6]
        sems = refs[6:]
        pairs = [(before_hbm, before), *zip(sources, buffers)]
        copies = [pltpu.make_async_copy(a, b, home.at[2 + n]) for n, (a, b) in enumerate(pairs)]
        for copy in copies:
            copy.start()
        first = 0
        for ref in heavy[:3]:
            shard[:, first : first + ref.shape[1]] = ref[...].astype(low)
            first += ref.shape[1]
        shard[:, first:] = small_ref[...].astype(low)
        greet(Gather.masks)
        moving = Gather(shard, weights, *sems)
        moving.start()
    else:
        copies = [
            pltpu.make_async_copy(shard_ref, weights, home.at[2]),
            pltpu.make_async_copy(before_hbm, before, home.at[3]),
        ]
        for copy in copies:
            copy.start()

    def normed(block):
        x = block.astype(full)
        return (x * lax.rsqrt(jnp.mean(x * x, axis=-1, keepdims=True) + 1e-06) * gain_ref[0:1, :]).astype(low)

    def norm(n, carry):
        span = pl.ds(pl.multiple_of(n * rows, rows), rows)
        first_ref[span, :] = normed(tokens_ref[span, :])
        return carry

    here.wait()
    lax.fori_loop(0, length // rows, norm, 0)

    def add(chip, fresh, done):
        start = pl.multiple_of(chip * half, half)

        def one(n, carry):
            span = pl.ds(pl.multiple_of(n * rows, rows), rows)
            part = mm(first_ref[span, pl.ds(start, half)], weights[pl.ds(start, half), :])
            if not fresh:
                part += total[span, :]
            if done:
                pre_ref[span, :] = part[:, :wide].astype(low)
                ab_ref[span, :] = part[:, wide:]
            else:
                total[span, :] = part
            return carry

        lax.fori_loop(0, length // rows, one, 0)

    if gathering:
        moving.local().wait()
        moving.traded((4,))
        add(partner(0) // 2, True, False)
        for copy in copies:
            copy.wait()
        gate, out, up, lift, down = buffers
        vals, size = gate.shape[1], up.shape[1]
        mix_ref[:, :vals] = gate[...].astype(low)
        for first in range(0, vals, 128):
            mix_ref[:, vals + first : vals + first + 128] = out[first : first + 128, :].T.astype(low)
        ffn_ref[:, :size] = up[...].astype(low)
        ffn_ref[:, size : 2 * size] = lift[...].astype(low)
        for first in range(0, size, 128):
            cols = slice(2 * size + first, 2 * size + first + 128)
            ffn_ref[:, cols] = down[first : first + 128, :].T.astype(low)
        moving.middle()
        moving.traded((5, 6))
        add(partner(2) // 2, False, False)
        moving.late()
        add(partner(4) // 2, False, False)
        moving.traded((7,))
        back.start()
        add(partner(6) // 2, False, True)
    else:
        for copy in copies:
            copy.wait()
        back.start()
        for chip in range(4):
            add(chip, chip == 0, chip == 3)
    edge_ref[...] = mm(normed(before[...]), weights[:, :wide]).astype(low)
    if gathering:
        moving.settle()
    back.wait()


def input_projection(tokens, before, gain, heavy, wide):
    length, width = tokens.shape
    gathering = len(heavy) > 1
    here = pl.BlockSpec(memory_space=pltpu.VMEM)
    away = pl.BlockSpec(**ANY)
    if gathering:
        operands = [*heavy, before, tokens]
        in_specs = [here] * 4 + [away] * 7
        rows = heavy[0].shape[0]
        columns = sum(a.shape[1] for a in heavy[:4])
        shards_out = [
            jax.ShapeDtypeStruct((rows, 2 * heavy[4].shape[1]), low),
            jax.ShapeDtypeStruct((rows, 3 * heavy[6].shape[1]), low),
        ]
        more = [pltpu.VMEM((rows, columns), low)] + [pltpu.VMEM(a.shape, full) for a in heavy[4:]]
        more += Gather.semaphores
        params = dict(collective_id=4, has_side_effects=True)
    else:
        operands = [*heavy, before, tokens]
        in_specs = [away] * 3
        columns = heavy[0].shape[1]
        shards_out, more, params = [], [], {}
    return pl.pallas_call(
        partial(input_kernel, wide, gathering),
        in_specs=[here] + in_specs,
        out_specs=[here] * 4 + [away] + [here] * len(shards_out),
        out_shape=[
            jax.ShapeDtypeStruct((length, width), low),
            jax.ShapeDtypeStruct((length, wide), low),
            jax.ShapeDtypeStruct((length, columns - wide), full),
            jax.ShapeDtypeStruct((16, wide), low),
            jax.ShapeDtypeStruct((width, columns), low),
        ]
        + shards_out,
        scratch_shapes=[
            pltpu.VMEM((width, columns), low),
            pltpu.VMEM((length, columns), full),
            pltpu.VMEM((length, width), low),
            pltpu.VMEM((16, width), low),
            pltpu.SemaphoreType.DMA((8,)),
        ]
        + more,
        compiler_params=pltpu.CompilerParams(vmem_limit_bytes=60 * MIB, **params),
        cost_estimate=FREE,
        name="input_projection",
    )(gain[None, :], *operands)


def weight_kernel(groups, adding, counts, place_ref, *refs):
    lefts, rights = refs[: counts[0]], refs[counts[0] : counts[0] + counts[1]]
    rest = refs[counts[0] + counts[1] :]
    parts = []
    n = 0
    for g, many in enumerate(groups):
        left = lefts[g][...]
        for _ in range(many):
            parts.append(mm_tn(left, rights[n][...]))
            n += 1
    first = 0
    for part in parts:
        cols = slice(first, first + part.shape[1])
        first += part.shape[1]
        if adding:
            part += rest[0][0, :, cols].astype(full)
        rest[-1][0, :, cols] = part.astype(low)


def weight_call(place, pairs, odd, count, stride, added=None, width=256):
    lefts = [a for a, _ in pairs]
    rights = [b for _, bs in pairs for b in bs]
    length = lefts[0].shape[0]
    columns = sum(b.shape[1] for b in rights)

    def pick(k, place_ref):
        return (0, jnp.bitwise_xor(place_ref[0], stride * k + odd))

    in_specs = [pl.BlockSpec((length, width), pick) for _ in lefts]
    in_specs += [pl.BlockSpec(b.shape, lambda k, p: (0, 0), **ONE) for b in rights]
    if added is not None:
        in_specs += [pl.BlockSpec((1, width, columns), lambda k, p: (k, 0, 0))]
    out_specs = [pl.BlockSpec((1, width, columns), lambda k, p: (k, 0, 0))]
    out_shape = [jax.ShapeDtypeStruct((count, width, columns), low)]
    return pl.pallas_call(
        partial(
            weight_kernel, [len(bs) for _, bs in pairs], added is not None, (len(lefts), len(rights))
        ),
        grid_spec=pltpu.PrefetchScalarGridSpec(
            num_scalar_prefetch=1, grid=(count,), in_specs=in_specs, out_specs=out_specs
        ),
        out_shape=out_shape,
        compiler_params=pltpu.CompilerParams(vmem_limit_bytes=56 * MIB),
        cost_estimate=FREE,
        name="weight_grads",
    )(place, *lefts, *rights, *(() if added is None else (added,)))


def pair_sums(place, pairs):
    (away,) = weight_call(place, pairs, 1, NEAR // 2, 2)
    (sums,) = weight_call(place, pairs, 0, NEAR // 2, 2, exchanged(away, 1))
    return sums


def plain_sums(place, pairs):
    width = pairs[0][0].shape[1]
    (grads,) = weight_call(jnp.zeros_like(place), pairs, 0, width // 256, 1)
    return lax.psum_scatter(grads.reshape(width, -1), "seq", scatter_dimension=0, tiled=True).astype(full)


def final_kernel(heads, keys, vals, size, middle_ref, sum_ref, dmiddle_ref, term_ref, in_own, in_got,
                 up_own, up_got, down_own, down_got, gate_own, gate_got, out_own, out_got,
                 result_ref, dtokens_ref, q_ref, k_ref, v_ref, a_ref, b_ref, up_ref, lift_ref, down_ref,
                 gate_ref, out_ref):
    def total(own, got, cols=slice(None)):
        return own[0, :, cols].astype(full) + sum(got[k, :, cols].astype(full) for k in range(3))

    @pl.when(pl.program_id(0) < 8)
    def _():
        result_ref[...] = (middle_ref[...] + sum_ref[...].astype(full)).astype(low)
        dtokens_ref[...] = dmiddle_ref[...] + term_ref[...].astype(full)
        wide = 2 * keys + vals
        q_ref[...] = total(in_own, in_got, slice(0, keys))
        k_ref[...] = total(in_own, in_got, slice(keys, 2 * keys))
        v_ref[...] = total(in_own, in_got, slice(2 * keys, wide))
        small = total(in_own, in_got, slice(wide, wide + LANES))
        a_ref[...] = small[:, :heads]
        b_ref[...] = small[:, heads : 2 * heads]
        up_ref[...] = total(up_own, up_got, slice(0, size))
        lift_ref[...] = total(up_own, up_got, slice(size, 2 * size))
        gate_ref[...] = total(gate_own, gate_got)
        out_ref[...] = total(out_own, out_got).T

    down_ref[...] = total(down_own, down_got).T


def final_sums(middle, narrow_sum, dmiddle, term, sums_in, got_in, sums_up, got_up, sums_rest, got_rest, heads, keys, vals, size):
    length, width = dmiddle.shape
    rows = sums_in.shape[1]
    eight = lambda n: jnp.minimum(n, 7)
    many, few = length // 8, rows // 8

    def both(array, block, index):
        return [pl.BlockSpec((1,) + block, index), pl.BlockSpec((3,) + block, index)]

    wide_in, wide_up = sums_in.shape[2], sums_up.shape[2]
    at_gate, at_out = size // LANES, (size + vals) // LANES
    tall = pl.BlockSpec((many, width), lambda n: (eight(n), 0))
    in_specs = [tall] * 4
    in_specs += both(sums_in, (few, wide_in), lambda n: (0, eight(n), 0))
    in_specs += both(sums_up, (few, wide_up), lambda n: (0, eight(n), 0))
    in_specs += both(sums_rest, (rows, LANES), lambda n: (0, 0, n))
    in_specs += both(sums_rest, (rows, LANES), lambda n: (0, 0, at_gate + eight(n)))
    in_specs += both(sums_rest, (rows, LANES), lambda n: (0, 0, at_out + eight(n)))
    byrow = lambda columns: pl.BlockSpec((few, columns), lambda n: (eight(n), 0))
    outs = [
        ((length, width), low), ((length, width), full), ((rows, keys), full), ((rows, keys), full),
        ((rows, vals), full), ((rows, heads), full), ((rows, heads), full), ((rows, size), full),
        ((rows, size), full), ((size, rows), full), ((rows, vals), full), ((vals, rows), full),
    ]
    return pl.pallas_call(
        partial(final_kernel, heads, keys, vals, size),
        grid=(size // LANES,),
        in_specs=in_specs,
        out_specs=[
            tall, tall,
            byrow(keys), byrow(keys), byrow(vals), byrow(heads), byrow(heads), byrow(size), byrow(size),
            pl.BlockSpec((LANES, rows), lambda n: (n, 0)),
            pl.BlockSpec((rows, LANES), lambda n: (0, eight(n))),
            pl.BlockSpec((LANES, rows), lambda n: (eight(n), 0)),
        ],
        out_shape=[jax.ShapeDtypeStruct(shape, dtype) for shape, dtype in outs],
        compiler_params=pltpu.CompilerParams(vmem_limit_bytes=48 * MIB),
        cost_estimate=FREE,
        name="final_sums",
    )(middle, narrow_sum, dmiddle, term, sums_in, got_in, sums_up, got_up, sums_rest, got_rest, sums_rest,
      got_rest, sums_rest, got_rest)


def small_sums(part):
    return lax.psum(part, "seq")


def passed_along(block, axis, distance):
    devices = range(lax.axis_size(axis))
    route = [(i - distance, i) for i in devices if i - distance in devices]
    return lax.ppermute(block, axis, route)


def shards(
    tokens,
    doc_lengths,
    mixer_gain,
    query_weight,
    key_weight,
    value_weight,
    gate_weight,
    alpha_weight,
    beta_weight,
    decay_log,
    decay_bias,
    query_taps,
    key_taps,
    value_taps,
    head_gain,
    output_weight,
    ffn_gain,
    ffn_gate,
    ffn_up,
    ffn_down,
    cotangent,
):
    length, width = tokens.shape
    heads = decay_log.shape[0]
    key = query_weight.shape[1] // heads
    value = head_gain.shape[0]
    keys, vals = heads * key, heads * value
    wide = 2 * keys + vals
    size = ffn_gate.shape[1]
    last = lax.axis_size("head") - 1
    near = lax.axis_size("seq") == NEAR
    shard = lax.axis_index("seq")
    place = jnp.full((1,), shard, jnp.int32)

    small = jnp.concatenate(
        [alpha_weight, beta_weight, jnp.zeros((alpha_weight.shape[0], LANES - 2 * heads), full)], axis=1
    )
    taps = jnp.concatenate([query_taps, key_taps, value_taps], axis=1)
    params = jnp.stack([-jnp.exp(decay_log), decay_bias])
    params = jnp.pad(params, ((0, 6), (0, LANES - heads)))
    gain = head_gain[None, :]

    if near:
        heavy = [query_weight, key_weight, value_weight, small, gate_weight, output_weight]
        heavy += [ffn_gate, ffn_up, ffn_down]
    else:
        shard_in = jnp.concatenate([query_weight, key_weight, value_weight, small], axis=1)
        heavy = [lax.all_gather(shard_in.astype(low), "seq", axis=0, tiled=True)]
    meta, edge_meta, segrow = segment_tables(doc_lengths, shard, length)
    first_in, pre, ab, edge, w_in, *laid = input_projection(
        tokens, passed_along(tokens[length - 16 :], "seq", 1), mixer_gain, heavy, wide
    )
    if near:
        shard_mix, shard_ffn = laid
    else:
        shard_mix = jnp.concatenate([gate_weight, output_weight.T], axis=1).astype(low)
        shard_ffn = jnp.concatenate([ffn_gate, ffn_up, ffn_down.T], axis=1).astype(low)
    edge = edge[8:]
    local, through, states, inverse, end, *moved = forward_chain(
        pre, ab, meta, segrow, edge, taps, params, heads, key, value, shard_mix if near else None
    )
    end = end.reshape(keys, value + key)
    if near:
        w_mix = moved[0]
        held, moving = [(w_mix, [(0, vals), (vals, vals)])], dict(early=end, gathers=[shard_ffn])
    else:
        w_mix = lax.all_gather(shard_mix, "seq", axis=0, tiled=True)
        ends = lax.all_gather(end, "seq", axis=0, tiled=True)
        held, moving = [(w_mix, [(0, vals), (vals, vals)]), (ends, [(0, ends.shape[1])])], {}
    mix_out, mixed, gate_pre, state_in, middle, second_in, *moved = line_call(
        partial(mixer_out_kernel, heads, key, value, last, None if near else 2), "mixer_out", 0, length, width, last,
        [gain, ffn_gain[None, :]], held, [first_in, local, through], [tokens],
        [((length, vals), low, "first"), ((length, vals), full, "first"),
         ((length, vals), full, "first"), ((heads, key, value), full, "all"),
         ((length, width), full, "second"), ((length, width), low, "second")],
        [], **moving,
    )
    if near:
        ends, w_ffn = moved
    else:
        w_ffn = lax.all_gather(shard_ffn, "seq", axis=0, tiled=True)
    hidden, gate_grad, lift_grad, narrow_part, middle_grad, middle_low, ffn_gain_part = line_call(
        partial(ffn_kernel, last, size), "ffn", 1, length, width, last,
        [ffn_gain[None, :]], [(w_ffn, [(n * size, size) for n in range(3)])], [second_in, cotangent], [middle, cotangent],
        [((length, size), low, "first")] * 3
        + [((length, width), low, "first"), ((length, width), full, "second"),
           ((length, width), low, "second"), ((8, width), full, "all")],
        [pltpu.VMEM((ROWS, size), full)] * 2,
    )
    narrow_sum = lax.psum_scatter(narrow_part, "head", scatter_dimension=0, tiled=True)
    gate_pgrad, mixed_grad, head_gain_part, adjoint = gate_back(
        middle_low, w_mix, mixed, gate_pre, gain, through, heads, key, value
    )
    for mask in (1, 2):
        head_gain_part += lax.ppermute(
            head_gain_part, "head", [(i, i ^ mask) for i in range(last + 1)]
        )
    adjoints = spread(adjoint.astype(low).reshape(keys, value))
    pairs_up = [(second_in, [gate_grad, lift_grad])]
    pairs_rest = [(cotangent, [hidden]), (first_in, [gate_pgrad]), (middle_low, [mix_out])]
    sums_up = pair_sums(place, pairs_up) if near else None
    sums_rest = pair_sums(place, pairs_rest) if near else None
    if near:
        narrow_sum, sums_up, head_gain_part = lax.optimization_barrier(
            (narrow_sum, sums_up, head_gain_part)
        )
    narrow_sum = lax.all_gather(narrow_sum, "head", axis=0, tiled=True)
    pre_grad, ab_grad, halo, taps_part, params_part, *moved = backward_chain(
        pre, ab, meta, segrow, edge, edge_meta, taps, params, states, inverse, state_in,
        mixed_grad, ends, adjoints, heads, key, value, sums_up,
    )
    got_up = moved
    halo = passed_along(halo, "seq", -1)
    tail = pre_grad[length - 8 :].astype(full) + halo
    pre_grad = lax.dynamic_update_slice(pre_grad, tail.astype(low), (length - 8, 0))
    pairs_in = [(first_in, [pre_grad, ab_grad])]
    sums_in = pair_sums(place, pairs_in) if near else None
    params_part = jnp.sum(params_part.reshape(2, 8, LANES), axis=1).reshape(1, -1)
    lines = jnp.concatenate(
        [
            jnp.zeros((1, width), full),
            jnp.sum(ffn_gain_part, axis=0, keepdims=True),
            jnp.sum(taps_part.reshape(4, 8, -1), axis=1),
            jnp.pad(params_part, ((0, 0), (0, width - params_part.shape[1]))),
            jnp.pad(jnp.sum(head_gain_part, axis=0)[None], ((0, 0), (0, width - value))),
        ],
        axis=0,
    )
    term, gains, *moved = line_call(
        partial(input_grad_kernel, last, keys, vals, near), "input_grad", 2, length, width, last,
        [mixer_gain[None, :], lines], [(w_in, [(0, w_in.shape[1])]), (w_mix, [(0, vals)])],
        [pre_grad, gate_pgrad, ab_grad], [tokens],
        [((length, width), low, "second"), ((8, width), full, "all")],
        [pltpu.VMEM((ROWS, width), full), pltpu.VMEM((8, width), full)]
        + ([pltpu.VMEM((NEAR, 8, width), full), *[pltpu.SemaphoreType.DMA((NEAR,))] * 2] if near else []),
        scatters=[sums_rest, sums_in] if near else [], masks=range(1, NEAR) if near else (),
    )
    if near:
        (result, tokens_grad, query_grad, key_grad, value_grad, alpha_grad, beta_grad, up_grad, lift_grad,
         down_grad, gate_grad, out_grad) = final_sums(
            middle, narrow_sum, middle_grad, term, sums_in, moved[1], sums_up, got_up[0], sums_rest, moved[0],
            heads, keys, vals, size,
        )
    else:
        up, rest, into = (plain_sums(place, pairs) for pairs in (pairs_up, pairs_rest, pairs_in))
        tokens_grad = middle_grad + term.astype(full)
        query_grad, key_grad, value_grad = into[:, :keys], into[:, keys : 2 * keys], into[:, 2 * keys : wide]
        alpha_grad, beta_grad = into[:, wide : wide + heads], into[:, wide + heads : wide + 2 * heads]
        up_grad, lift_grad = up[:, :size], up[:, size:]
        down_grad, gate_grad, out_grad = (
            rest[:, :size].T, rest[:, size : size + vals], rest[:, size + vals :].T
        )
        result = (middle + narrow_sum.astype(full)).astype(low)
    sums = gains if near else small_sums(gains)
    taps_grad = sums[2:6]
    return (
        result,
        tokens_grad,
        sums[0],
        query_grad,
        key_grad,
        value_grad,
        gate_grad,
        alpha_grad,
        beta_grad,
        sums[6, LANES : LANES + heads],
        sums[6, :heads],
        taps_grad[:, :keys],
        taps_grad[:, keys : 2 * keys],
        taps_grad[:, 2 * keys :],
        sums[7, :value],
        out_grad,
        sums[1],
        up_grad,
        lift_grad,
        down_grad,
    )


def solution(mesh):
    rows, both = P("seq", None), P("seq", "head")
    in_specs = (
        rows, P(), P(), both, both, both, both, both, both, P("head"), P("head"),
        P(None, "head"), P(None, "head"), P(None, "head"), P(), P("head", "seq"), P(),
        both, both, P("head", "seq"), rows,
    )
    out_specs = (
        rows, rows, P(), both, both, both, both, both, both, P("head"), P("head"),
        P(None, "head"), P(None, "head"), P(None, "head"), P(), P("head", "seq"), P(),
        both, both, P("head", "seq"),
    )
    return jax.shard_map(shards, mesh=mesh, in_specs=in_specs, out_specs=out_specs, check_vma=False)
```

```python
from functools import partial

import jax
import jax.numpy as jnp
from jax import lax
from jax.experimental import pallas as pl
from jax.experimental.pallas import tpu as pltpu
from jax.sharding import PartitionSpec as P

BLOCK = 128
LANES = 128
low = jnp.bfloat16
full = jnp.float32
MIB = 1 << 20


NEAR = 8
ONE = dict(pipeline_mode=pl.Buffered(1))
ANY = dict(memory_space=pl.ANY)
FREE = pl.CostEstimate(flops=1, bytes_accessed=1, transcendentals=0)
MESH = pl.DeviceIdType.MESH


def partner(mask):
    index = lax.axis_index("seq")
    bits = (lax.rem(index, 2), lax.rem(index // 2, 2), index // 4)
    return sum((1 << i) * ((1 - b) if mask >> i & 1 else b) for i, b in enumerate(bits))


def greet(masks, last=None, all_heads=False):
    barrier = pltpu.get_barrier_semaphore()
    for mask in masks:
        pl.semaphore_signal(barrier, inc=1, device_id={"seq": partner(mask)}, device_id_type=MESH)
    count = len(masks)
    if all_heads:
        place = lax.axis_index("head")
        for k in range(1, last + 1):
            to = lax.rem(place + k, last + 1)
            pl.semaphore_signal(barrier, inc=1, device_id={"head": to}, device_id_type=MESH)
        count += last
    elif last is not None:
        place = lax.axis_index("head")
        for there, to in ((place > 0, place - 1), (place < last, place + 1)):

            @pl.when(there)
            def _(to=to):
                pl.semaphore_signal(barrier, inc=1, device_id={"head": to}, device_id_type=MESH)

        count += jnp.minimum(place, 1) + jnp.minimum(last - place, 1)
    pl.semaphore_wait(barrier, count)


class Gather:
    masks = (1, 2, 4)
    semaphores = [pltpu.SemaphoreType.DMA((8,)), pltpu.SemaphoreType.DMA((8,)), pltpu.SemaphoreType.DMA((1,))]

    def __init__(self, shard, whole, sent, got, home):
        self.shard, self.whole, self.sent, self.got, self.home = shard, whole, sent, got, home
        self.size = shard.shape[0]

    def rows(self, mask, first=0, count=None):
        start = pl.multiple_of(partner(mask) * self.size + first, self.size // 2)
        return self.whole.at[pl.ds(start, self.size if count is None else count), :]

    def push(self, slot):
        half = self.size // 2
        mask, src, dst = (
            (2, self.shard, self.rows(0)),
            (4, self.shard, self.rows(0)),
            (2, self.rows(4, 0, half), self.rows(4, 0, half)),
            (4, self.rows(2, half, half), self.rows(2, half, half)),
            (1, self.shard, self.rows(0)),
            (1, self.rows(2), self.rows(2)),
            (1, self.rows(4), self.rows(4)),
            (1, self.rows(6), self.rows(6)),
        )[slot]
        return pltpu.make_async_remote_copy(
            src_ref=src, dst_ref=dst, send_sem=self.sent.at[slot], recv_sem=self.got.at[slot],
            device_id={"seq": partner(mask)}, device_id_type=MESH,
        )

    def local(self):
        return pltpu.make_async_copy(self.shard, self.rows(0), self.home.at[0])

    def start(self):
        self.local().start()
        for slot in (0, 1, 4):
            self.push(slot).start()

    def middle(self):
        for slot in (0, 1):
            self.push(slot).wait_recv()
        for slot in (2, 3, 5, 6):
            self.push(slot).start()

    def late(self):
        for slot in (2, 3):
            self.push(slot).wait_recv()
        self.push(7).start()

    def traded(self, slots):
        for slot in slots:
            self.push(slot).wait_recv()

    def settle(self):
        for slot in range(8):
            self.push(slot).wait_send()

    def end(self):
        self.traded((4, 5, 6, 7))
        self.settle()
        self.local().wait()


class Scatter:
    masks = (2, 4, 6)
    semaphores = [pltpu.SemaphoreType.DMA((3,)), pltpu.SemaphoreType.DMA((3,))]

    def __init__(self, parts, got, sent, came):
        self.parts, self.got, self.sent, self.came = parts, got, sent, came

    def push(self, k):
        return pltpu.make_async_remote_copy(
            src_ref=self.parts.at[k + 1], dst_ref=self.got.at[k], send_sem=self.sent.at[k],
            recv_sem=self.came.at[k], device_id={"seq": partner(2 * k + 2)}, device_id_type=MESH,
        )

    def start(self):
        for k in range(3):
            self.push(k).start()

    def end(self):
        for k in range(3):
            self.push(k).wait()


def load(step, pairs, sems):
    @pl.when(step == 0)
    def _():
        copies = [pltpu.make_async_copy(a, b, sems.at[n]) for n, (a, b) in enumerate(pairs)]
        for copy in copies:
            copy.start()
        for copy in copies:
            copy.wait()


def mm(a, b):
    return jnp.dot(a.astype(low), b.astype(low), preferred_element_type=full)


def mm_nt(a, b):
    return lax.dot_general(
        a.astype(low), b.astype(low), (((1,), (1,)), ((), ())), preferred_element_type=full
    )


def mm_tn(a, b):
    return lax.dot_general(
        a.astype(low), b.astype(low), (((0,), (0,)), ((), ())), preferred_element_type=full
    )


def exact(a, b):
    return jnp.dot(a, b, precision=lax.Precision.HIGHEST, preferred_element_type=full)


def sigmoid(t):
    return 1.0 / (1.0 + jnp.exp(-t))


def softplus(t):
    return jnp.maximum(t, 0.0) + jnp.log(1.0 + jnp.exp(-jnp.abs(t)))


def iotas(size):
    return (
        lax.broadcasted_iota(jnp.int32, (size, size), 0),
        lax.broadcasted_iota(jnp.int32, (size, size), 1),
    )


def conv_sum(ext, taps, meta, first, width, rows):
    total = taps[3:4, first : first + width] * ext[8 : 8 + rows, first : first + width]
    for lag in (1, 2, 3):
        total += (
            taps[3 - lag : 4 - lag, first : first + width]
            * meta[:, lag : lag + 1]
            * ext[8 - lag : 8 - lag + rows, first : first + width]
        )
    return total


def gates(ab, params, heads):
    log_decay = params[0:1, :] * softplus(ab + params[1:2, :])
    beta = sigmoid(ab)
    return log_decay, beta


def decay_parts(cum, cum_t, h, same_low, strict_low, meta):
    size = cum.shape[0]
    col = cum[:, h : h + 1]
    row = cum_t[h : h + 1, :]
    lower = jnp.where(same_low, jnp.exp(jnp.minimum(col - row, 0.0)), 0.0)
    strict = jnp.where(strict_low, lower, 0.0)
    last = cum[size - 1 : size, h : h + 1]
    from_start = jnp.exp(col) * meta[:, 4:5]
    to_end = jnp.exp(last - col) * meta[:, 5:6]
    carried = jnp.exp(last) * meta[size - 1 : size, 4:5]
    return lower, strict, from_start, to_end, carried


def unit_lower_inverse(strict, rows, cols):
    size = strict.shape[0]
    power = jnp.where((rows >> 3) == (cols >> 3), -strict, 0.0)
    inverse = jnp.where(rows == cols, 1.0, power)
    power = mm(power, power)
    inverse = inverse + mm(inverse, power)
    power = mm(power, power)
    inverse = inverse + mm(inverse, power)
    shift = 3
    while (1 << shift) < size:
        off = jnp.where(
            ((rows >> (shift + 1)) == (cols >> (shift + 1))) & ((rows >> shift) != (cols >> shift)),
            strict,
            0.0,
        )
        inverse = inverse - mm(inverse, mm(off, inverse))
        shift += 1
    return inverse


def inverses(stricts, rows, cols):
    size = stricts[0].shape[0]
    near = (rows >> 3) == (cols >> 3)
    powers = [jnp.where(near, -a, 0.0) for a in stricts]
    result = [jnp.where(rows == cols, 1.0, p) for p in powers]
    for _ in range(2):
        powers = [mm(p, p) for p in powers]
        result = [t + mm(t, p) for t, p in zip(result, powers)]
    shift = 3
    while (1 << shift) < size:
        pick = ((rows >> (shift + 1)) == (cols >> (shift + 1))) & (
            (rows >> shift) != (cols >> shift)
        )
        offs = [mm(jnp.where(pick, a, 0.0), t) for a, t in zip(stricts, result)]
        result = [t - mm(t, o) for t, o in zip(result, offs)]
        shift += 1
    return result


def masks(meta, segrow):
    size = meta.shape[0]
    rows, cols = iotas(size)
    same = meta[:, 0:1] == segrow[0:1, :]
    return rows, cols, same & (rows >= cols), same & (rows > cols)


def unit(post):
    return lax.rsqrt(jnp.sum(post * post, axis=-1, keepdims=True) + 1e-06)


def forward_kernel(
    heads, key, value, gathering,
    pre_ref, ab_ref, meta_ref, segrow_ref, edge_ref, taps_ref, params_ref, *refs
):
    step = pl.program_id(0)
    steps = pl.num_programs(0)
    if gathering:
        shard_ref, out_ref, through_ref, states_ref, inverse_ref, end_ref, whole_ref, ext, state, *sems = refs
        moving = Gather(shard_ref, whole_ref, *sems)

        @pl.when(step == 0)
        def _():
            greet(Gather.masks)
            moving.start()

        @pl.when(step == steps - 2)
        def _():
            moving.middle()

    else:
        out_ref, through_ref, states_ref, inverse_ref, end_ref, ext, state = refs
    size = pre_ref.shape[0]
    wide = value + key
    kfirst, vfirst = heads * key, 2 * heads * key

    @pl.when(step == 0)
    def _():
        ext[0:8, :] = edge_ref[...].astype(full)
        rows, cols = iotas(key)
        eye = (rows == cols).astype(full)
        for h in range(heads):
            state[h, :, :value] = jnp.zeros((key, value), full)
            state[h, :, value:] = eye

    @pl.when(step > 0)
    def _():
        ext[0:8, :] = ext[size : size + 8, :]

    ext[8:, :] = pre_ref[...].astype(full)
    meta = meta_ref[...]
    log_decay, beta = gates(ab_ref[...], params_ref, heads)
    rows, cols, same_low, strict_low = masks(meta, segrow_ref)
    cum = exact((rows >= cols).astype(full), log_decay)
    cum_t = cum.T
    qs, ks, vs, lowers, stricts, fs, es, cs = [], [], [], [], [], [], [], []
    for h in range(heads):
        u = conv_sum(ext, taps_ref, meta, h * key, key, size)
        post = u * sigmoid(u)
        q = (post * unit(post)).astype(low)
        u = conv_sum(ext, taps_ref, meta, kfirst + h * key, key, size)
        post = u * sigmoid(u)
        k = (post * unit(post)).astype(low)
        u = conv_sum(ext, taps_ref, meta, vfirst + h * value, value, size)
        v = u * sigmoid(u)
        lower, strict, f, e, c = decay_parts(cum, cum_t, h, same_low, strict_low, meta)
        bcol = beta[:, heads + h : heads + h + 1]
        gram = mm_nt(jnp.concatenate([k, q], axis=0), k)
        qs.append(q), ks.append(k), vs.append(v), fs.append(f), es.append(e), cs.append(c)
        stricts.append(bcol * strict * gram[:size])
        lowers.append(lower * gram[size:])
    ts = inverses(stricts, rows, cols)
    for h in range(heads):
        bcol = beta[:, heads + h : heads + h + 1]
        s = state[h]
        states_ref[0, h] = s.astype(low)
        t = ts[h].astype(low)
        inverse_ref[0, h] = t
        ks_s = mm(ks[h], s)
        fb = fs[h] * bcol
        target = jnp.concatenate(
            [bcol * vs[h] - fb * ks_s[:, :value], -fb * ks_s[:, value:]], axis=1
        )
        delta = mm(t, target).astype(low)
        left = jnp.concatenate([(fs[h] * qs[h].astype(full)).astype(low), lowers[h].astype(low)], axis=1)
        out = mm(left, jnp.concatenate([s.astype(low), delta], axis=0))
        out_ref[:, h * value : (h + 1) * value] = out[:, :value]
        through_ref[:, h * key : (h + 1) * key] = out[:, value:].astype(low)
        ke = es[h] * ks[h].astype(full)
        s = cs[h] * s + mm_tn(ke, delta)
        state[h] = s
        end_ref[h] = s.astype(low)

    if gathering:

        @pl.when(step == steps - 1)
        def _():
            moving.late()
            moving.end()


def forward_chain(pre, ab, meta, segrow, edge, taps, params, heads, key, value, shard=None):
    gathering = shard is not None
    moved = [jax.ShapeDtypeStruct((shard.shape[0] * NEAR, shard.shape[1]), low)] if gathering else []
    extra = dict(collective_id=5, has_side_effects=True) if gathering else {}
    length = pre.shape[0]
    blocks = length // BLOCK
    width = pre.shape[1]
    wide = value + key
    return pl.pallas_call(
        partial(forward_kernel, heads, key, value, gathering),
        grid=(blocks,),
        in_specs=[
            pl.BlockSpec((BLOCK, width), lambda n: (n, 0)),
            pl.BlockSpec((BLOCK, LANES), lambda n: (n, 0)),
            pl.BlockSpec((BLOCK, LANES), lambda n: (n, 0)),
            pl.BlockSpec((8, BLOCK), lambda n: (0, n)),
            pl.BlockSpec((8, width), lambda n: (0, 0)),
            pl.BlockSpec(taps.shape, lambda n: (0, 0)),
            pl.BlockSpec((8, LANES), lambda n: (0, 0)),
        ]
        + [pl.BlockSpec(**ANY) for _ in moved],
        out_specs=[
            pl.BlockSpec((BLOCK, heads * value), lambda n: (n, 0)),
            pl.BlockSpec((BLOCK, heads * key), lambda n: (n, 0)),
            pl.BlockSpec((1, heads, key, wide), lambda n: (n, 0, 0, 0)),
            pl.BlockSpec((1, heads, BLOCK, BLOCK), lambda n: (n, 0, 0, 0)),
            pl.BlockSpec((heads, key, wide), lambda n: (0, 0, 0)),
        ]
        + [pl.BlockSpec(**ANY) for _ in moved],
        out_shape=[
            jax.ShapeDtypeStruct((length, heads * value), full),
            jax.ShapeDtypeStruct((length, heads * key), low),
            jax.ShapeDtypeStruct((blocks, heads, key, wide), low),
            jax.ShapeDtypeStruct((blocks, heads, BLOCK, BLOCK), low),
            jax.ShapeDtypeStruct((heads, key, wide), low),
        ]
        + moved,
        scratch_shapes=[
            pltpu.VMEM((BLOCK + 8, width), full),
            pltpu.VMEM((heads, key, wide), full),
        ]
        + (Gather.semaphores if gathering else []),
        compiler_params=pltpu.CompilerParams(vmem_limit_bytes=48 * MIB, **extra),
        cost_estimate=FREE,
        name="chain_forward",
    )(pre, ab, meta, segrow, edge, taps, params, *([shard] if gathering else []))


def gate_back_kernel(heads, key, value, dz_ref, mixed_ref, gate_ref, gain_ref, through_ref, whole_ref,
                     dgz_ref, do_ref, gain_grad_ref, adjoint_ref, weights, dy_ref, sems):
    load(pl.program_id(0), [(whole_ref.at[:, heads * value :], weights)], sems)

    @pl.when(pl.program_id(0) == 0)
    def _():
        gain_grad_ref[...] = jnp.zeros_like(gain_grad_ref)
        adjoint_ref[...] = jnp.zeros_like(adjoint_ref)

    rows = dz_ref.shape[0]
    gain = gain_ref[0:1, :]
    dy_ref[...] = mm(dz_ref[...], weights[...])
    for h in range(heads):
        cols = slice(h * value, (h + 1) * value)
        o = mixed_ref[:, cols].astype(full)
        s3 = lax.rsqrt(jnp.mean(o * o, axis=-1, keepdims=True) + 1e-05)
        n3 = o * s3
        gz = gate_ref[:, cols]
        sig = sigmoid(gz)
        sg = gz * sig
        dy = dy_ref[:, cols]
        dyn = dy * n3
        part = dyn * sg
        gain_grad_ref[...] += jnp.sum(part.reshape(rows // 8, 8, value), axis=0)
        dgz_ref[:, cols] = (dyn * gain * (sig * (1.0 + gz * (1.0 - sig)))).astype(low)
        dn3 = dy * gain * sg
        do = s3 * (dn3 - n3 * jnp.mean(dn3 * n3, axis=-1, keepdims=True))
        do = do.astype(low)
        do_ref[:, cols] = do
        adjoint_ref[h] += mm_tn(through_ref[:, h * key : (h + 1) * key], do)


def gate_back(dz, w_mix, mixed, gate, gain, through, heads, key, value, rows=256):
    length, width = dz.shape
    wide = heads * value
    return pl.pallas_call(
        partial(gate_back_kernel, heads, key, value),
        grid=(length // rows,),
        in_specs=[
            pl.BlockSpec((rows, width), lambda n: (n, 0)),
            pl.BlockSpec((rows, wide), lambda n: (n, 0)),
            pl.BlockSpec((rows, wide), lambda n: (n, 0)),
            pl.BlockSpec((1, value), lambda n: (0, 0)),
            pl.BlockSpec((rows, heads * key), lambda n: (n, 0)),
        ]
        + [pl.BlockSpec(**ANY)],
        out_specs=[
            pl.BlockSpec((rows, wide), lambda n: (n, 0)),
            pl.BlockSpec((rows, wide), lambda n: (n, 0)),
            pl.BlockSpec((8, value), lambda n: (0, 0)),
            pl.BlockSpec((heads, key, value), lambda n: (0, 0, 0)),
        ],
        out_shape=[
            jax.ShapeDtypeStruct((length, wide), low),
            jax.ShapeDtypeStruct((length, wide), low),
            jax.ShapeDtypeStruct((8, value), full),
            jax.ShapeDtypeStruct((heads, key, value), full),
        ],
        scratch_shapes=[
            pltpu.VMEM((width, wide), low),
            pltpu.VMEM((rows, wide), full),
            pltpu.SemaphoreType.DMA((1,)),
        ],
        compiler_params=pltpu.CompilerParams(vmem_limit_bytes=48 * MIB),
        cost_estimate=FREE,
        name="gate_back",
    )(dz, mixed, gate, gain, through, w_mix)


def lane_sum(array):
    return jnp.sum(array, axis=-1, keepdims=True)


def backward_kernel(
    heads, key, value, devices, scattering,
    pre_ref, tail_ref, ab_ref, meta_ref, segrow_ref, edge_ref, edge_meta_ref, taps_ref, params_ref,
    states_ref, inverse_ref, state_in_ref, do_ref, ends_ref, *refs
):
    step = pl.program_id(0)
    steps = pl.num_programs(0)
    piece, *refs = refs
    parts_ref = refs.pop(0) if scattering else None
    dpre_ref, dab_ref, halo_ref, taps_grad_ref, params_grad_ref = refs[:5]
    refs = refs[5:]
    got_ref = refs.pop(0) if scattering else None
    ext, du, adjoint, adjoints, home, *sems = refs
    if scattering:
        moving = Scatter(parts_ref, got_ref, *sems[:2])
        lead = Gather(piece, adjoints, *sems[2:])

        @pl.when(step == 0)
        def _():
            greet(sorted({*Scatter.masks, *Gather.masks}))
            lead.start()

    size = pre_ref.shape[0]
    kfirst, vfirst = heads * key, 2 * heads * key

    @pl.when(step == 0)
    def _():
        adjoint[...] = jnp.zeros_like(adjoint)
        tall = heads * key
        if scattering:
            lead.middle()
            lead.late()
            moving.start()
            lead.end()
        else:
            copy = pltpu.make_async_copy(piece, adjoints, home.at[0])
            copy.start()
            copy.wait()

        def one(k, carry):
            j = devices - 1 - k
            for h in range(heads):
                rows = pl.ds(pl.multiple_of(j * tall + h * key, key), key)
                adjoint[h] = (
                    mm_tn(ends_ref[rows, value:], adjoint[h]) + adjoints[rows, :].astype(full)
                )
            return carry

        lax.fori_loop(0, devices - 1 - lax.axis_index("seq"), one, 0)
        du[8 + size :, :] = jnp.zeros((8, du.shape[1]), full)
        taps_grad_ref[...] = jnp.zeros_like(taps_grad_ref)
        params_grad_ref[...] = jnp.zeros_like(params_grad_ref)

    @pl.when(step > 0)
    def _():
        du[8 + size :, :] = du[8:16, :]

    du[0:8, :] = jnp.zeros((8, du.shape[1]), full)

    @pl.when(step < steps - 1)
    def _():
        ext[0:8, :] = tail_ref[8:16, :].astype(full)

    @pl.when(step == steps - 1)
    def _():
        ext[0:8, :] = edge_ref[...].astype(full)

    ext[8:, :] = pre_ref[...].astype(full)
    meta = meta_ref[...]
    ab = ab_ref[...]
    log_decay, beta = gates(ab, params_ref, heads)
    rows, cols, same_low, strict_low = masks(meta, segrow_ref)
    cum = exact((rows >= cols).astype(full), log_decay)
    cum_t = cum.T
    lane = lax.broadcasted_iota(jnp.int32, (size, LANES), 1)
    row8 = lax.broadcasted_iota(jnp.int32, (8, size), 0)
    dcum = jnp.zeros((size, LANES), full)
    dcum_rows = jnp.zeros((8, size), full)
    dcum_last = jnp.zeros((1, LANES), full)
    dbeta = jnp.zeros((size, LANES), full)
    lane1 = lax.broadcasted_iota(jnp.int32, (1, LANES), 1)

    for h in range(heads):
        qcols = slice(h * key, (h + 1) * key)
        kcols = slice(kfirst + h * key, kfirst + (h + 1) * key)
        vcols = slice(vfirst + h * value, vfirst + (h + 1) * value)
        uq = conv_sum(ext, taps_ref, meta, h * key, key, size)
        sq = sigmoid(uq)
        pq = uq * sq
        rq = unit(pq)
        qf = pq * rq
        q = qf.astype(low)
        uk = conv_sum(ext, taps_ref, meta, kfirst + h * key, key, size)
        sk = sigmoid(uk)
        pk = uk * sk
        rk = unit(pk)
        kf = pk * rk
        k = kf.astype(low)
        uv = conv_sum(ext, taps_ref, meta, vfirst + h * value, value, size)
        sv = sigmoid(uv)
        v = uv * sv
        lower, strict, f, e, c = decay_parts(cum, cum_t, h, same_low, strict_low, meta)
        b = beta[:, heads + h : heads + h + 1]
        kq = jnp.concatenate([k, q], axis=0)
        gram = mm_nt(kq, k)
        kk, qk = gram[:size], gram[size:]
        stored = states_ref[0, h]
        s = stored[:, :value].astype(full) + mm(stored[:, value:], state_in_ref[h])
        slow = s.astype(low)
        kqs = mm(kq, slow)
        ks, qs = kqs[:size], kqs[size:]
        rest = v - f * ks
        t = inverse_ref[0, h]
        delta = mm(t, b * rest).astype(low)
        do = do_ref[:, h * value : (h + 1) * value]
        dof = do.astype(full)
        ds = adjoint[h]
        dslow = ds.astype(low)
        ke = (e * kf).astype(low)
        p = lower * qk
        left = jnp.concatenate([p.T.astype(low), ke], axis=1)
        ddelta = mm(left, jnp.concatenate([do, dslow], axis=0))
        dtarget = mm_tn(t, ddelta)
        outer = mm_nt(jnp.concatenate([do, dtarget.astype(low)], axis=0), delta)
        dp, dan = outer[:size], outer[size:]
        eg = lower * dp
        hn = -strict * dan
        hg = b * hn
        x = eg * qk
        hk = hn * kk
        g1 = (b * f) * dtarget
        fdo = f * dof
        pair = jnp.concatenate([fdo.astype(low), (-g1).astype(low)], axis=0)
        both = mm_nt(pair, slow)
        dq = both[:size] + mm(eg, k)
        dsk = e * mm_nt(delta, dslow)
        left = jnp.concatenate([(hg + hg.T).astype(low), eg.T.astype(low)], axis=1)
        dk = both[size:] + dsk + mm(left, kq)
        dv = b * dtarget
        z = lane_sum(kf * dsk)
        dfrom = lane_sum(dof * qs) - b * lane_sum(dtarget * ks)
        hrow = lane_sum(hk)
        db = hrow + lane_sum(dtarget * rest)
        dbeta = dbeta + jnp.where(lane == heads + h, db, 0.0)
        dcum = dcum + jnp.where(lane == h, lane_sum(x) + b * hrow + f * dfrom - z, 0.0)
        drow = jnp.sum(x + b * hk, axis=0, keepdims=True)
        dcum_rows = dcum_rows + jnp.where(row8 == h, drow, 0.0)
        dlast = jnp.sum(z, axis=0, keepdims=True) + c * jnp.sum(
            lane_sum(ds * s), axis=0, keepdims=True
        )
        dcum_last = dcum_last + jnp.where(lane1 == h, dlast, 0.0)
        adjoint[h] = c * ds + mm_tn(jnp.concatenate([q, k], axis=0), pair)

        dpq = rq * (dq - qf * lane_sum(dq * qf))
        du[8 : 8 + size, qcols] = dpq * (sq * (1.0 + uq * (1.0 - sq)))
        dpk = rk * (dk - kf * lane_sum(dk * kf))
        du[8 : 8 + size, kcols] = dpk * (sk * (1.0 + uk * (1.0 - sk)))
        du[8 : 8 + size, vcols] = dv * (sv * (1.0 + uv * (1.0 - sv)))

    padded = jnp.concatenate([dcum_rows, jnp.zeros((LANES - 8, size), full)], axis=0)
    rowi = lax.broadcasted_iota(jnp.int32, (size, LANES), 0)
    dcum = dcum - padded.T + jnp.where(rowi == size - 1, dcum_last, 0.0)
    dlog = exact((rows <= cols).astype(full), dcum)
    dga = dlog * params_ref[0:1, :] * sigmoid(ab + params_ref[1:2, :])
    is_decay = lane < heads
    dga = jnp.where(is_decay, dga, 0.0)
    params_grad_ref[0:8, :] += jnp.sum(dga.reshape(size // 8, 8, LANES), axis=0)
    decay_part = jnp.where(is_decay, dlog * log_decay, 0.0)
    params_grad_ref[8:16, :] += jnp.sum(decay_part.reshape(size // 8, 8, LANES), axis=0)
    dab_ref[...] = jnp.where(is_decay, dga, dbeta * beta * (1.0 - beta)).astype(low)

    width = du.shape[1]
    for first in range(0, width, 512):
        cs = slice(first, first + 512)
        own = du[8 : 8 + size, cs]
        total = taps_ref[3:4, cs] * own
        taps_grad_ref[24:32, cs] += jnp.sum(
            (own * ext[8 : 8 + size, cs]).reshape(size // 8, 8, 512), axis=0
        )
        for lag in (1, 2, 3):
            total += taps_ref[3 - lag : 4 - lag, cs] * meta[:, 5 + lag : 6 + lag] * du[
                8 + lag : 8 + lag + size, cs
            ]
            taps_grad_ref[8 * (3 - lag) : 8 * (4 - lag), cs] += jnp.sum(
                (own * meta[:, lag : lag + 1] * ext[8 - lag : 8 - lag + size, cs]).reshape(
                    size // 8, 8, 512
                ),
                axis=0,
            )
        dpre_ref[:, cs] = total.astype(low)

    @pl.when(step == steps - 1)
    def _():
        edge_meta = edge_meta_ref[...]
        halo = jnp.zeros(halo_ref.shape, full)
        for lag in (1, 2, 3):
            halo += taps_ref[3 - lag : 4 - lag, :] * edge_meta[:, 5 + lag : 6 + lag] * du[
                lag : 8 + lag, :
            ]
        halo_ref[...] = halo
        if scattering:
            moving.end()


def backward_chain(pre, ab, meta, segrow, edge, edge_meta, taps, params, states, inverse,
                   state_in, do, ends, adjoints, heads, key, value, parts=None):
    scattering = parts is not None
    moved = [jax.ShapeDtypeStruct((3,) + parts.shape[1:], low)] if scattering else []
    extra = dict(collective_id=6, has_side_effects=True) if scattering else {}
    devices = ends.shape[0] // (heads * key)
    length, width = pre.shape
    blocks = length // BLOCK
    wide = value + key
    once = dict(pipeline_mode=pl.Buffered(1))
    last = blocks - 1
    return pl.pallas_call(
        partial(backward_kernel, heads, key, value, devices, scattering),
        grid=(blocks,),
        in_specs=[
            pl.BlockSpec((BLOCK, width), lambda n: (last - n, 0)),
            pl.BlockSpec((16, width), lambda n: (jnp.maximum((last - n) * (BLOCK // 16) - 1, 0), 0)),
            pl.BlockSpec((BLOCK, LANES), lambda n: (last - n, 0)),
            pl.BlockSpec((BLOCK, LANES), lambda n: (last - n, 0)),
            pl.BlockSpec((8, BLOCK), lambda n: (0, last - n)),
            pl.BlockSpec((8, width), lambda n: (0, 0)),
            pl.BlockSpec((8, LANES), lambda n: (0, 0)),
            pl.BlockSpec(taps.shape, lambda n: (0, 0)),
            pl.BlockSpec((8, LANES), lambda n: (0, 0)),
            pl.BlockSpec((1, heads, key, wide), lambda n: (last - n, 0, 0, 0)),
            pl.BlockSpec((1, heads, BLOCK, BLOCK), lambda n: (last - n, 0, 0, 0)),
            pl.BlockSpec((heads, key, value), lambda n: (0, 0, 0)),
            pl.BlockSpec((BLOCK, heads * value), lambda n: (last - n, 0)),
            pl.BlockSpec(ends.shape, lambda n: (0, 0), **once),
        ]
        + [pl.BlockSpec(**ANY) for _ in (0, *moved)],
        out_specs=[
            pl.BlockSpec((BLOCK, width), lambda n: (last - n, 0)),
            pl.BlockSpec((BLOCK, LANES), lambda n: (last - n, 0)),
            pl.BlockSpec((8, width), lambda n: (0, 0)),
            pl.BlockSpec((32, width), lambda n: (0, 0)),
            pl.BlockSpec((16, LANES), lambda n: (0, 0)),
        ]
        + [pl.BlockSpec(**ANY) for _ in moved],
        out_shape=[
            jax.ShapeDtypeStruct((length, width), low),
            jax.ShapeDtypeStruct((length, LANES), low),
            jax.ShapeDtypeStruct((8, width), full),
            jax.ShapeDtypeStruct((32, width), full),
            jax.ShapeDtypeStruct((16, LANES), full),
        ]
        + moved,
        scratch_shapes=[
            pltpu.VMEM((BLOCK + 8, width), full),
            pltpu.VMEM((BLOCK + 16, width), full),
            pltpu.VMEM((heads, key, value), full),
            pltpu.VMEM((devices * heads * key, value), low),
            pltpu.SemaphoreType.DMA((1,)),
        ]
        + (Scatter.semaphores + Gather.semaphores if scattering else []),
        compiler_params=pltpu.CompilerParams(vmem_limit_bytes=56 * MIB, **extra),
        cost_estimate=FREE,
        name="chain_backward",
    )(pre, pre, ab, meta, segrow, edge, edge_meta, taps, params, states, inverse, state_in, do, ends,
      adjoints, *([parts] if scattering else []))


def segment_tables(doc_lengths, shard, length):
    starts = jnp.cumsum(doc_lengths, dtype=jnp.int32) - doc_lengths
    positions = shard * length + jnp.arange(-16, length + 8, dtype=jnp.int32)
    seg = jnp.sum((starts[None, :] <= positions[:, None]).astype(jnp.int32), axis=1)
    own = seg[16 : 16 + length]

    def lanes(first, count):
        base = seg[first : first + count]
        back = [seg[first - l : first - l + count] == base for l in (1, 2, 3)]
        ahead = [seg[first + l : first + l + count] == base for l in (1, 2, 3)]
        return base, back, ahead

    base, back, ahead = lanes(16, length)
    blocks = own.reshape(-1, BLOCK)
    before = seg[15 : 15 + length : BLOCK]
    alive = (blocks == before[:, None]).reshape(-1)
    to_last = (blocks == blocks[:, -1:]).reshape(-1)
    columns = [base, *back, alive, to_last, *ahead]
    meta = jnp.stack([a.astype(full) for a in columns], axis=1)
    meta = jnp.pad(meta, ((0, 0), (0, LANES - meta.shape[1])))
    base, back, ahead = lanes(8, 8)
    columns = [base, *back, base, base, *ahead]
    edge_meta = jnp.stack([a.astype(full) for a in columns], axis=1)
    edge_meta = jnp.pad(edge_meta, ((0, 0), (0, LANES - edge_meta.shape[1])))
    segrow = jnp.broadcast_to(own.astype(full)[None, :], (8, length))
    return meta, edge_meta, segrow


ROWS = 256
PIECE = 32
HOP = 2
EACH = ROWS // PIECE
AHEAD = 1 + (EACH - 1 + 3 * HOP) // EACH
RING = AHEAD + 1


def exchanged(block, mask):
    return lax.ppermute(block, "seq", [(i, i ^ mask) for i in range(lax.axis_size("seq"))])


def line_scratch(length, width):
    pieces = length // PIECE
    return [
        pltpu.VMEM((RING, ROWS, width), low),
        pltpu.VMEM((length, width), low),
        pltpu.VMEM((length, width), low),
        pltpu.SemaphoreType.DMA((pieces,)),
        pltpu.SemaphoreType.DMA((pieces,)),
        pltpu.SemaphoreType.DMA((pieces,)),
        pltpu.SemaphoreType.DMA((pieces,)),
    ]


def line_sum(step, last, stages, finish, scratch):
    own, from_left, from_right, got_left, got_right, sent_right, sent_left = scratch
    place = lax.axis_index("head")
    length, width = from_left.shape
    blocks, pieces = length // ROWS, length // PIECE
    left_there, right_there = place > 0, place < last

    def rows(piece):
        return pl.ds(pl.multiple_of(piece * PIECE, PIECE), PIECE)

    def hop(piece, rightwards):
        kept, sent, got, to = (
            (from_left, sent_right, got_left, place + 1)
            if rightwards
            else (from_right, sent_left, got_right, place - 1)
        )
        return pltpu.make_async_remote_copy(
            src_ref=kept.at[rows(piece)],
            dst_ref=kept.at[rows(piece)],
            send_sem=sent.at[piece],
            recv_sem=got.at[piece],
            device_id={"head": to},
            device_id_type=MESH,
        )

    def own_piece(piece):
        slot = lax.rem(piece // EACH, RING)
        first = pl.multiple_of(lax.rem(piece, EACH) * PIECE, PIECE)
        return own[slot, pl.ds(first, PIECE), :].astype(full)

    @pl.when(step == 0)
    def _():
        @pl.when(place == 0)
        def _():
            from_left[...] = jnp.zeros_like(from_left)

        @pl.when(place == last)
        def _():
            from_right[...] = jnp.zeros_like(from_right)

    def one(q, carry):
        now = (step - 1) * EACH + q
        for rightwards in (True, False):
            came, more = (left_there, right_there) if rightwards else (right_there, left_there)
            kept = from_left if rightwards else from_right
            piece = now - HOP * (place if rightwards else last - place)

            @pl.when((piece >= 0) & (piece < pieces))
            def _():
                @pl.when(came)
                def _():
                    hop(piece, rightwards).wait_recv()

                @pl.when(more)
                def _():
                    kept[rows(piece), :] = (
                        own_piece(piece) + kept[rows(piece), :].astype(full)
                    ).astype(low)
                    hop(piece, rightwards).start()

        return carry

    done = 0
    for n, stage in enumerate(stages):

        @pl.when(step < blocks)
        def _(n=n, stage=stage):
            value = stage()
            if n == len(stages) - 1:
                own[lax.rem(step, RING)] = value.astype(low)

        until = EACH * (n + 1) // len(stages)
        lax.fori_loop(done, until, one, 0)
        done = until

    @pl.when(step >= AHEAD)
    def _():
        block = step - AHEAD
        span = pl.ds(pl.multiple_of(block * ROWS, ROWS), ROWS)
        total = from_left[span, :].astype(full) + from_right[span, :].astype(full)
        twice = jnp.where(left_there & right_there, 1.0, 0.0)
        finish(total - twice * own[lax.rem(block, RING)].astype(full))

    @pl.when(step == blocks + AHEAD - 1)
    def _():
        def settle(piece, carry):
            @pl.when(right_there)
            def _():
                hop(piece, True).wait_send()

            @pl.when(left_there)
            def _():
                hop(piece, False).wait_send()

            return carry

        lax.fori_loop(0, pieces, settle, 0)


def union(kinds):
    return sorted({mask for kind in kinds for mask in kind.masks})


def line_call(kernel, name, collective, length, width, last, resident, weights, entering, leaving, outs,
              scratch, gathers=(), scatters=(), early=None, masks=()):
    blocks = length // ROWS
    steps = blocks + AHEAD
    cuts, weights = [c for _, c in weights], [a for a, _ in weights]

    def spec(array, stage):
        if stage == "first":
            return pl.BlockSpec((ROWS, array.shape[1]), lambda g: (jnp.minimum(g, blocks - 1), 0))
        if stage == "second":
            return pl.BlockSpec((ROWS, array.shape[1]), lambda g: (jnp.maximum(g - AHEAD, 0), 0))
        rank = len(array.shape)
        return pl.BlockSpec(array.shape, lambda g: (0,) * rank, **ONE)

    in_specs = [spec(a, "all") for a in resident]
    first_one = [] if early is None else [early]
    in_specs += [pl.BlockSpec(**ANY) for _ in (*weights, *first_one, *gathers, *scatters)]
    in_specs += [spec(a, "first") for a in entering] + [spec(a, "second") for a in leaving]
    shapes = [jax.ShapeDtypeStruct(shape, dtype) for shape, dtype, _ in outs]
    out_specs = [
        spec(s, stage) if stage != "all" else pl.BlockSpec(s.shape, lambda g, r=len(s.shape): (0,) * r)
        for s, (_, _, stage) in zip(shapes, outs)
    ]
    moved = [jax.ShapeDtypeStruct((a.shape[0] * NEAR, a.shape[1]), low) for a in (*first_one, *gathers)]
    moved += [jax.ShapeDtypeStruct((3,) + a.shape[1:], low) for a in scatters]
    kinds = [Gather] * len(gathers) + [Scatter] * len(scatters)
    whole_first = [pltpu.VMEM(s.shape, low) for s in moved[: len(first_one)]]
    held = [pltpu.VMEM(a.shape, low) for a in weights] + [pltpu.SemaphoreType.DMA((sum(len(c) for c in cuts),))]
    held += whole_first + [s for _ in first_one for s in Gather.semaphores]
    held += [s for kind in kinds for s in kind.semaphores]

    def body(*refs):
        refs = list(refs)

        def take(n):
            head, refs[:] = refs[:n], refs[n:]
            return head

        own_in, heavy = take(len(resident)), take(len(weights))
        ahead, sources = take(len(first_one)), take(len(kinds))
        chunks = take(len(entering) + len(leaving))
        own_out, handed, targets = take(len(outs)), take(len(first_one)), take(len(kinds))
        own_scratch = take(len(scratch) + 7)
        matrices, (sems,) = take(len(weights)), take(1)
        if first_one:
            (table,), signals = take(1), take(3)
            lead = Gather(ahead[0], table, *signals)
            back = pltpu.make_async_copy(table, handed[0], signals[2].at[0])
            matrices.append(table)
        carried = [kind(a, b, *take(len(kind.semaphores))) for kind, a, b in zip(kinds, sources, targets)]
        step = pl.program_id(0)

        @pl.when(step == 0)
        def _():
            greet(sorted({*masks, *union(kinds + [Gather] * len(first_one))}), last, bool(masks))
            for c in [lead] if first_one else carried:
                c.start()

        waits = []
        for source, target, parts in zip(heavy, matrices, cuts):
            for first, count in parts:
                part = pl.ds(first, count)
                waits.append(
                    pltpu.make_async_copy(source.at[:, part], target.at[:, part], sems.at[len(waits)])
                )

        @pl.when(step == 0)
        def _():
            for copy in waits:
                copy.start()

        def ready(k):
            @pl.when(step == 0)
            def _():
                waits[k].wait()

        if first_one:

            @pl.when(step == 0)
            def _():
                lead.middle()
                lead.late()
                for c in carried:
                    c.start()
                lead.end()
                back.start()

        for at, turn in ((steps - 3, "middle"), (steps - 1, "late")):

            @pl.when(step == at)
            def _(turn=turn):
                for c in carried:
                    if isinstance(c, Gather):
                        getattr(c, turn)()

        kernel(ready, matrices, *own_in, *chunks, *own_out, *own_scratch)

        @pl.when(step == steps - 1)
        def _():
            for c in carried:
                c.end()
            if first_one:
                back.wait()

    return pl.pallas_call(
        body,
        grid=(steps,),
        in_specs=in_specs,
        out_specs=out_specs + [pl.BlockSpec(**ANY) for _ in moved],
        out_shape=shapes + moved,
        scratch_shapes=scratch + line_scratch(length, width) + held,
        compiler_params=pltpu.CompilerParams(
            collective_id=collective, has_side_effects=True, vmem_limit_bytes=60 * MIB
        ),
        cost_estimate=FREE,
        name=name,
    )(*resident, *weights, *first_one, *gathers, *scatters, *entering, *leaving)


def mixer_out_kernel(heads, key, value, last, handed, ready, matrices,
                     head_gain_ref, gain_ref,
                     first_ref, local_ref, through_ref, tokens_ref,
                     y_ref, mixed_ref, gate_ref, state_ref, middle_ref, second_ref, *scratch):
    step = pl.program_id(0)
    weights, ends = matrices
    vals = heads * value

    if handed is not None:
        ready(handed)

    @pl.when(step == 0)
    def _():
        state_ref[...] = jnp.zeros_like(state_ref)

        def one(j, carry):
            for h in range(heads):
                rows = pl.ds(pl.multiple_of((j * heads + h) * key, key), key)
                part = ends[rows, :]
                state_ref[h] = mm(part[:, value:], state_ref[h]) + part[:, :value].astype(full)
            return carry

        lax.fori_loop(0, lax.axis_index("seq"), one, 0)

    def gate():
        ready(0)
        gate_ref[...] = mm(first_ref[...], weights[:, :vals])

    def mix():
        for h in range(heads):
            cols = slice(h * value, (h + 1) * value)
            o = local_ref[:, cols] + mm(through_ref[:, h * key : (h + 1) * key], state_ref[h])
            mixed_ref[:, cols] = o
            s3 = lax.rsqrt(jnp.mean(o * o, axis=-1, keepdims=True) + 1e-05)
            gz = gate_ref[:, cols]
            y_ref[:, cols] = (o * s3 * head_gain_ref[0:1, :] * (gz * sigmoid(gz))).astype(low)

    def project():
        ready(1)
        return mm_nt(y_ref[...], weights[:, vals:])

    def finish(total):
        middle = tokens_ref[...].astype(full) + total
        middle_ref[...] = middle
        scale = lax.rsqrt(jnp.mean(middle * middle, axis=-1, keepdims=True) + 1e-06)
        second_ref[...] = (middle * scale * gain_ref[0:1, :]).astype(low)

    line_sum(step, last, [gate, mix, project], finish, scratch)


def ffn_kernel(last, size, ready, matrices, gain_ref,
               second_ref, cot_ref, middle_ref, cot_late_ref,
               hidden_ref, dgate_ref, dup_ref, partial_ref, dmiddle_ref, dlow_ref, gain_grad_ref,
               fg, fu, *scratch):
    step = pl.program_id(0)
    (weights,) = matrices
    w_gate, w_up, w_down = (slice(n * size, (n + 1) * size) for n in range(3))

    @pl.when(step == 0)
    def _():
        gain_grad_ref[...] = jnp.zeros_like(gain_grad_ref)

    def one():
        ready(0)
        fg[...] = mm(second_ref[...], weights[:, w_gate])

    def two():
        ready(1)
        fu[...] = mm(second_ref[...], weights[:, w_up])

    def three():
        ready(2)
        g, lift = fg[...], fu[...]
        sig = sigmoid(g)
        swish = g * sig
        hidden = (swish * lift).astype(low)
        hidden_ref[...] = hidden
        fg[...] = lift * (sig * (1.0 + g * (1.0 - sig)))
        fu[...] = swish
        partial_ref[...] = mm_nt(hidden, weights[:, w_down]).astype(low)

    def four():
        dhid = mm(cot_ref[...], weights[:, w_down])
        dgate_ref[...] = (dhid * fg[...]).astype(low)
        dup_ref[...] = (dhid * fu[...]).astype(low)

    def five():
        return mm_nt(dgate_ref[...], weights[:, w_gate]) + mm_nt(dup_ref[...], weights[:, w_up])

    def finish(grad):
        middle = middle_ref[...]
        scale = lax.rsqrt(jnp.mean(middle * middle, axis=-1, keepdims=True) + 1e-06)
        norm = middle * scale
        gain_grad_ref[...] += jnp.sum((grad * norm).reshape(ROWS // 8, 8, -1), axis=0)
        weighted = grad * gain_ref[0:1, :]
        dm = cot_late_ref[...].astype(full) + scale * (
            weighted - norm * jnp.mean(weighted * norm, axis=-1, keepdims=True)
        )
        dmiddle_ref[...] = dm
        dlow_ref[...] = dm.astype(low)

    line_sum(step, last, [one, two, three, four, five], finish, scratch)


def input_grad_kernel(last, keys, vals, near, ready, matrices, gain_ref, lines_ref, head_ref,
                      dpre_ref, dgz_ref, dab_ref, tokens_ref,
                      term_ref, gains_ref, part, gain_grad, *scratch):
    step = pl.program_id(0)
    w_in, w_mix = matrices
    wide = 2 * keys + vals
    if near:
        (got, sent, came, got_head, sent_head, came_head), scratch = scratch[:6], scratch[6:]
        place = lax.axis_index("head")

        def across(k):
            return pltpu.make_async_remote_copy(
                src_ref=head_ref, dst_ref=got_head.at[place], send_sem=sent_head.at[k],
                recv_sem=came_head.at[k], device_id={"head": lax.rem(place + k, last + 1)},
                device_id_type=MESH,
            )

    @pl.when(step == 0)
    def _():
        gain_grad[...] = jnp.zeros_like(gain_grad)
        if near:
            for k in range(1, last + 1):
                across(k).start()
            got_head[place] = head_ref[...]

    def one():
        ready(0)
        part[...] = mm_nt(dpre_ref[...], w_in[:, :wide])

    def two():
        ready(1)
        return (
            part[...]
            + mm_nt(dgz_ref[...], w_mix[:, :vals])
            + mm_nt(dab_ref[...], w_in[:, wide:])
        )

    def finish(grad):
        stream = tokens_ref[...].astype(full)
        scale = lax.rsqrt(jnp.mean(stream * stream, axis=-1, keepdims=True) + 1e-06)
        norm = stream * scale
        gain_grad[...] += jnp.sum((grad * norm).reshape(ROWS // 8, 8, -1), axis=0)
        weighted = grad * gain_ref[0:1, :]
        term_ref[...] = (
            scale * (weighted - norm * jnp.mean(weighted * norm, axis=-1, keepdims=True))
        ).astype(low)

    line_sum(step, last, [one, two], finish, scratch)

    @pl.when(step == pl.num_programs(0) - 1)
    def _():
        row = lax.broadcasted_iota(jnp.int32, gain_grad.shape, 0)
        first = jnp.sum(gain_grad[...], axis=0, keepdims=True)
        own = lines_ref[...] + jnp.where(row == 0, first, 0.0)
        if not near:
            gains_ref[...] = own
            return
        for k in range(1, last + 1):
            across(k).wait()
        heads_sum = sum((got_head[k] for k in range(1, last + 1)), start=got_head[0])
        gain_grad[...] = own
        gain_grad[7:8, : head_ref.shape[1]] = jnp.sum(heads_sum, axis=0, keepdims=True)
        me = lax.axis_index("seq")

        def push(mask):
            return pltpu.make_async_remote_copy(
                src_ref=gain_grad, dst_ref=got.at[me], send_sem=sent.at[mask], recv_sem=came.at[mask],
                device_id={"seq": partner(mask)}, device_id_type=MESH,
            )

        for mask in range(1, NEAR):
            push(mask).start()
        got[me] = gain_grad[...]
        for mask in range(1, NEAR):
            push(mask).wait()
        gains_ref[...] = sum((got[k] for k in range(1, NEAR)), start=got[0])


def input_kernel(wide, gathering, gain_ref, *refs):
    rows = 256
    if gathering:
        heavy, (before_hbm, tokens_hbm), refs = refs[:9], refs[9:11], refs[11:]
        small_ref, sources = heavy[3], heavy[4:]
    else:
        (shard_ref, before_hbm, tokens_hbm), refs = refs[:3], refs[3:]
    first_ref, pre_ref, ab_ref, edge_ref, whole_ref = refs[:5]
    refs = refs[5:]
    if gathering:
        (mix_ref, ffn_ref), refs = refs[:2], refs[2:]
    weights, total, tokens_ref, before, home, *refs = refs
    length, width = tokens_ref.shape
    half = width // 4
    back = pltpu.make_async_copy(weights, whole_ref, home.at[0])
    here = pltpu.make_async_copy(tokens_hbm, tokens_ref, home.at[1])
    here.start()
    if gathering:
        shard, *buffers = refs[:6]
        sems = refs[6:]
        pairs = [(before_hbm, before), *zip(sources, buffers)]
        copies = [pltpu.make_async_copy(a, b, home.at[2 + n]) for n, (a, b) in enumerate(pairs)]
        for copy in copies:
            copy.start()
        first = 0
        for ref in heavy[:3]:
            shard[:, first : first + ref.shape[1]] = ref[...].astype(low)
            first += ref.shape[1]
        shard[:, first:] = small_ref[...].astype(low)
        greet(Gather.masks)
        moving = Gather(shard, weights, *sems)
        moving.start()
    else:
        copies = [
            pltpu.make_async_copy(shard_ref, weights, home.at[2]),
            pltpu.make_async_copy(before_hbm, before, home.at[3]),
        ]
        for copy in copies:
            copy.start()

    def normed(block):
        x = block.astype(full)
        return (x * lax.rsqrt(jnp.mean(x * x, axis=-1, keepdims=True) + 1e-06) * gain_ref[0:1, :]).astype(low)

    def norm(n, carry):
        span = pl.ds(pl.multiple_of(n * rows, rows), rows)
        first_ref[span, :] = normed(tokens_ref[span, :])
        return carry

    here.wait()
    lax.fori_loop(0, length // rows, norm, 0)

    def add(chip, fresh, done):
        start = pl.multiple_of(chip * half, half)

        def one(n, carry):
            span = pl.ds(pl.multiple_of(n * rows, rows), rows)
            part = mm(first_ref[span, pl.ds(start, half)], weights[pl.ds(start, half), :])
            if not fresh:
                part += total[span, :]
            if done:
                pre_ref[span, :] = part[:, :wide].astype(low)
                ab_ref[span, :] = part[:, wide:]
            else:
                total[span, :] = part
            return carry

        lax.fori_loop(0, length // rows, one, 0)

    if gathering:
        moving.local().wait()
        moving.traded((4,))
        add(partner(0) // 2, True, False)
        for copy in copies:
            copy.wait()
        gate, out, up, lift, down = buffers
        vals, size = gate.shape[1], up.shape[1]
        mix_ref[:, :vals] = gate[...].astype(low)
        for first in range(0, vals, 128):
            mix_ref[:, vals + first : vals + first + 128] = out[first : first + 128, :].T.astype(low)
        ffn_ref[:, :size] = up[...].astype(low)
        ffn_ref[:, size : 2 * size] = lift[...].astype(low)
        for first in range(0, size, 128):
            cols = slice(2 * size + first, 2 * size + first + 128)
            ffn_ref[:, cols] = down[first : first + 128, :].T.astype(low)
        moving.middle()
        moving.traded((5, 6))
        add(partner(2) // 2, False, False)
        moving.late()
        add(partner(4) // 2, False, False)
        moving.traded((7,))
        back.start()
        add(partner(6) // 2, False, True)
    else:
        for copy in copies:
            copy.wait()
        back.start()
        for chip in range(4):
            add(chip, chip == 0, chip == 3)
    edge_ref[...] = mm(normed(before[...]), weights[:, :wide]).astype(low)
    if gathering:
        moving.settle()
    back.wait()


def input_projection(tokens, before, gain, heavy, wide):
    length, width = tokens.shape
    gathering = len(heavy) > 1
    here = pl.BlockSpec(memory_space=pltpu.VMEM)
    away = pl.BlockSpec(**ANY)
    if gathering:
        operands = [*heavy, before, tokens]
        in_specs = [here] * 4 + [away] * 7
        rows = heavy[0].shape[0]
        columns = sum(a.shape[1] for a in heavy[:4])
        shards_out = [
            jax.ShapeDtypeStruct((rows, 2 * heavy[4].shape[1]), low),
            jax.ShapeDtypeStruct((rows, 3 * heavy[6].shape[1]), low),
        ]
        more = [pltpu.VMEM((rows, columns), low)] + [pltpu.VMEM(a.shape, full) for a in heavy[4:]]
        more += Gather.semaphores
        params = dict(collective_id=4, has_side_effects=True)
    else:
        operands = [*heavy, before, tokens]
        in_specs = [away] * 3
        columns = heavy[0].shape[1]
        shards_out, more, params = [], [], {}
    return pl.pallas_call(
        partial(input_kernel, wide, gathering),
        in_specs=[here] + in_specs,
        out_specs=[here] * 4 + [away] + [here] * len(shards_out),
        out_shape=[
            jax.ShapeDtypeStruct((length, width), low),
            jax.ShapeDtypeStruct((length, wide), low),
            jax.ShapeDtypeStruct((length, columns - wide), full),
            jax.ShapeDtypeStruct((16, wide), low),
            jax.ShapeDtypeStruct((width, columns), low),
        ]
        + shards_out,
        scratch_shapes=[
            pltpu.VMEM((width, columns), low),
            pltpu.VMEM((length, columns), full),
            pltpu.VMEM((length, width), low),
            pltpu.VMEM((16, width), low),
            pltpu.SemaphoreType.DMA((8,)),
        ]
        + more,
        compiler_params=pltpu.CompilerParams(vmem_limit_bytes=60 * MIB, **params),
        cost_estimate=FREE,
        name="input_projection",
    )(gain[None, :], *operands)


def weight_kernel(groups, adding, counts, place_ref, *refs):
    lefts, rights = refs[: counts[0]], refs[counts[0] : counts[0] + counts[1]]
    rest = refs[counts[0] + counts[1] :]
    parts = []
    n = 0
    for g, many in enumerate(groups):
        left = lefts[g][...]
        for _ in range(many):
            parts.append(mm_tn(left, rights[n][...]))
            n += 1
    first = 0
    for part in parts:
        cols = slice(first, first + part.shape[1])
        first += part.shape[1]
        if adding:
            part += rest[0][0, :, cols].astype(full)
        rest[-1][0, :, cols] = part.astype(low)


def weight_call(place, pairs, odd, count, stride, added=None, width=256):
    lefts = [a for a, _ in pairs]
    rights = [b for _, bs in pairs for b in bs]
    length = lefts[0].shape[0]
    columns = sum(b.shape[1] for b in rights)

    def pick(k, place_ref):
        return (0, jnp.bitwise_xor(place_ref[0], stride * k + odd))

    in_specs = [pl.BlockSpec((length, width), pick) for _ in lefts]
    in_specs += [pl.BlockSpec(b.shape, lambda k, p: (0, 0), **ONE) for b in rights]
    if added is not None:
        in_specs += [pl.BlockSpec((1, width, columns), lambda k, p: (k, 0, 0))]
    out_specs = [pl.BlockSpec((1, width, columns), lambda k, p: (k, 0, 0))]
    out_shape = [jax.ShapeDtypeStruct((count, width, columns), low)]
    return pl.pallas_call(
        partial(
            weight_kernel, [len(bs) for _, bs in pairs], added is not None, (len(lefts), len(rights))
        ),
        grid_spec=pltpu.PrefetchScalarGridSpec(
            num_scalar_prefetch=1, grid=(count,), in_specs=in_specs, out_specs=out_specs
        ),
        out_shape=out_shape,
        compiler_params=pltpu.CompilerParams(vmem_limit_bytes=56 * MIB),
        cost_estimate=FREE,
        name="weight_grads",
    )(place, *lefts, *rights, *(() if added is None else (added,)))


def pair_sums(place, pairs):
    (away,) = weight_call(place, pairs, 1, NEAR // 2, 2)
    (sums,) = weight_call(place, pairs, 0, NEAR // 2, 2, exchanged(away, 1))
    return sums


def plain_sums(place, pairs):
    width = pairs[0][0].shape[1]
    (grads,) = weight_call(jnp.zeros_like(place), pairs, 0, width // 256, 1)
    return lax.psum_scatter(grads.reshape(width, -1), "seq", scatter_dimension=0, tiled=True).astype(full)


def final_kernel(heads, keys, vals, size, middle_ref, sum_ref, dmiddle_ref, term_ref, in_own, in_got,
                 up_own, up_got, down_own, down_got, gate_own, gate_got, out_own, out_got, gains_ref,
                 tq_ref, tk_ref, tv_ref, result_ref, dtokens_ref, q_ref, k_ref, v_ref, a_ref, b_ref, up_ref, lift_ref, down_ref,
                 gate_ref, out_ref):
    def total(own, got, cols=slice(None)):
        return own[0, :, cols].astype(full) + sum(got[k, :, cols].astype(full) for k in range(3))

    @pl.when(pl.program_id(0) < 8)
    def _():
        result_ref[...] = (middle_ref[...] + sum_ref[...].astype(full)).astype(low)
        dtokens_ref[...] = dmiddle_ref[...] + term_ref[...].astype(full)
        wide = 2 * keys + vals
        q_ref[...] = total(in_own, in_got, slice(0, keys))
        k_ref[...] = total(in_own, in_got, slice(keys, 2 * keys))
        v_ref[...] = total(in_own, in_got, slice(2 * keys, wide))
        small = total(in_own, in_got, slice(wide, wide + LANES))
        a_ref[...] = small[:, :heads]
        b_ref[...] = small[:, heads : 2 * heads]
        up_ref[...] = total(up_own, up_got, slice(0, size))
        lift_ref[...] = total(up_own, up_got, slice(size, 2 * size))
        gate_ref[...] = total(gate_own, gate_got)
        out_ref[...] = total(out_own, out_got).T

    @pl.when(pl.program_id(0) == 0)
    def _():
        tq_ref[...] = gains_ref[2:6, :keys]
        tk_ref[...] = gains_ref[2:6, keys : 2 * keys]
        tv_ref[...] = gains_ref[2:6, 2 * keys :]

    down_ref[...] = total(down_own, down_got).T


def final_sums(middle, narrow_sum, dmiddle, term, sums_in, got_in, sums_up, got_up, sums_rest, got_rest, gains, heads, keys, vals,
               size):
    length, width = dmiddle.shape
    rows = sums_in.shape[1]
    eight = lambda n: jnp.minimum(n, 7)
    many, few = length // 8, rows // 8

    def both(array, block, index):
        return [pl.BlockSpec((1,) + block, index), pl.BlockSpec((3,) + block, index)]

    wide_in, wide_up = sums_in.shape[2], sums_up.shape[2]
    at_gate, at_out = size // LANES, (size + vals) // LANES
    tall = pl.BlockSpec((many, width), lambda n: (eight(n), 0))
    in_specs = [tall] * 4
    in_specs += both(sums_in, (few, wide_in), lambda n: (0, eight(n), 0))
    in_specs += both(sums_up, (few, wide_up), lambda n: (0, eight(n), 0))
    in_specs += both(sums_rest, (rows, LANES), lambda n: (0, 0, n))
    in_specs += both(sums_rest, (rows, LANES), lambda n: (0, 0, at_gate + eight(n)))
    in_specs += both(sums_rest, (rows, LANES), lambda n: (0, 0, at_out + eight(n)))
    once = lambda *shape: pl.BlockSpec(shape, lambda n: (0, 0))
    in_specs += [once(*gains.shape)]
    byrow = lambda columns: pl.BlockSpec((few, columns), lambda n: (eight(n), 0))
    outs = [
        ((4, keys), full), ((4, keys), full), ((4, vals), full), ((length, width), low), ((length, width), full), ((rows, keys), full), ((rows, keys), full),
        ((rows, vals), full), ((rows, heads), full), ((rows, heads), full), ((rows, size), full),
        ((rows, size), full), ((size, rows), full), ((rows, vals), full), ((vals, rows), full),
    ]
    return pl.pallas_call(
        partial(final_kernel, heads, keys, vals, size),
        grid=(size // LANES,),
        in_specs=in_specs,
        out_specs=[
            once(4, keys), once(4, keys), once(4, vals), tall, tall,
            byrow(keys), byrow(keys), byrow(vals), byrow(heads), byrow(heads), byrow(size), byrow(size),
            pl.BlockSpec((LANES, rows), lambda n: (n, 0)),
            pl.BlockSpec((rows, LANES), lambda n: (0, eight(n))),
            pl.BlockSpec((LANES, rows), lambda n: (eight(n), 0)),
        ],
        out_shape=[jax.ShapeDtypeStruct(shape, dtype) for shape, dtype in outs],
        compiler_params=pltpu.CompilerParams(vmem_limit_bytes=48 * MIB),
        cost_estimate=FREE,
        name="final_sums",
    )(middle, narrow_sum, dmiddle, term, sums_in, got_in, sums_up, got_up, sums_rest, got_rest, sums_rest,
      got_rest, sums_rest, got_rest, gains)


def small_sums(part):
    return lax.psum(part, "seq")


def passed_along(block, axis, distance):
    devices = range(lax.axis_size(axis))
    route = [(i - distance, i) for i in devices if i - distance in devices]
    return lax.ppermute(block, axis, route)


def shards(
    tokens,
    doc_lengths,
    mixer_gain,
    query_weight,
    key_weight,
    value_weight,
    gate_weight,
    alpha_weight,
    beta_weight,
    decay_log,
    decay_bias,
    query_taps,
    key_taps,
    value_taps,
    head_gain,
    output_weight,
    ffn_gain,
    ffn_gate,
    ffn_up,
    ffn_down,
    cotangent,
):
    length, width = tokens.shape
    heads = decay_log.shape[0]
    key = query_weight.shape[1] // heads
    value = head_gain.shape[0]
    keys, vals = heads * key, heads * value
    wide = 2 * keys + vals
    size = ffn_gate.shape[1]
    last = lax.axis_size("head") - 1
    near = lax.axis_size("seq") == NEAR
    shard = lax.axis_index("seq")
    place = jnp.full((1,), shard, jnp.int32)

    small = jnp.concatenate(
        [alpha_weight, beta_weight, jnp.zeros((alpha_weight.shape[0], LANES - 2 * heads), full)], axis=1
    )
    taps = jnp.concatenate([query_taps, key_taps, value_taps], axis=1)
    params = jnp.stack([-jnp.exp(decay_log), decay_bias])
    params = jnp.pad(params, ((0, 6), (0, LANES - heads)))
    gain = head_gain[None, :]

    if near:
        heavy = [query_weight, key_weight, value_weight, small, gate_weight, output_weight]
        heavy += [ffn_gate, ffn_up, ffn_down]
    else:
        shard_in = jnp.concatenate([query_weight, key_weight, value_weight, small], axis=1)
        heavy = [lax.all_gather(shard_in.astype(low), "seq", axis=0, tiled=True)]
    meta, edge_meta, segrow = segment_tables(doc_lengths, shard, length)
    first_in, pre, ab, edge, w_in, *laid = input_projection(
        tokens, passed_along(tokens[length - 16 :], "seq", 1), mixer_gain, heavy, wide
    )
    if near:
        shard_mix, shard_ffn = laid
    else:
        shard_mix = jnp.concatenate([gate_weight, output_weight.T], axis=1).astype(low)
        shard_ffn = jnp.concatenate([ffn_gate, ffn_up, ffn_down.T], axis=1).astype(low)
    edge = edge[8:]
    local, through, states, inverse, end, *moved = forward_chain(
        pre, ab, meta, segrow, edge, taps, params, heads, key, value, shard_mix if near else None
    )
    end = end.reshape(keys, value + key)
    if near:
        w_mix = moved[0]
        held, moving = [(w_mix, [(0, vals), (vals, vals)])], dict(early=end, gathers=[shard_ffn])
    else:
        w_mix = lax.all_gather(shard_mix, "seq", axis=0, tiled=True)
        ends = lax.all_gather(end, "seq", axis=0, tiled=True)
        held, moving = [(w_mix, [(0, vals), (vals, vals)]), (ends, [(0, ends.shape[1])])], {}
    mix_out, mixed, gate_pre, state_in, middle, second_in, *moved = line_call(
        partial(mixer_out_kernel, heads, key, value, last, None if near else 2), "mixer_out", 0, length, width, last,
        [gain, ffn_gain[None, :]], held, [first_in, local, through], [tokens],
        [((length, vals), low, "first"), ((length, vals), full, "first"),
         ((length, vals), full, "first"), ((heads, key, value), full, "all"),
         ((length, width), full, "second"), ((length, width), low, "second")],
        [], **moving,
    )
    if near:
        ends, w_ffn = moved
    else:
        w_ffn = lax.all_gather(shard_ffn, "seq", axis=0, tiled=True)
    hidden, gate_grad, lift_grad, narrow_part, middle_grad, middle_low, ffn_gain_part = line_call(
        partial(ffn_kernel, last, size), "ffn", 1, length, width, last,
        [ffn_gain[None, :]], [(w_ffn, [(n * size, size) for n in range(3)])], [second_in, cotangent], [middle, cotangent],
        [((length, size), low, "first")] * 3
        + [((length, width), low, "first"), ((length, width), full, "second"),
           ((length, width), low, "second"), ((8, width), full, "all")],
        [pltpu.VMEM((ROWS, size), full)] * 2,
    )
    narrow_sum = lax.psum_scatter(narrow_part, "head", scatter_dimension=0, tiled=True)
    gate_pgrad, mixed_grad, head_gain_part, adjoint = gate_back(
        middle_low, w_mix, mixed, gate_pre, gain, through, heads, key, value
    )
    if not near:
        head_gain_part = lax.psum(head_gain_part, "head")
    adjoint = adjoint.astype(low).reshape(keys, value)
    if not near:
        adjoint = lax.all_gather(adjoint, "seq", axis=0, tiled=True)
    pairs_up = [(second_in, [gate_grad, lift_grad])]
    pairs_rest = [(cotangent, [hidden]), (first_in, [gate_pgrad]), (middle_low, [mix_out])]
    sums_up = pair_sums(place, pairs_up) if near else None
    sums_rest = pair_sums(place, pairs_rest) if near else None
    pre_grad, ab_grad, halo, taps_part, params_part, *moved = backward_chain(
        pre, ab, meta, segrow, edge, edge_meta, taps, params, states, inverse, state_in,
        mixed_grad, ends, adjoint, heads, key, value, sums_up,
    )
    got_up = moved
    if near:
        narrow_sum, halo = lax.optimization_barrier((narrow_sum, halo))
    narrow_sum = lax.all_gather(narrow_sum, "head", axis=0, tiled=True)
    halo = passed_along(halo, "seq", -1)
    tail = pre_grad[length - 8 :].astype(full) + halo
    pre_grad = lax.dynamic_update_slice(pre_grad, tail.astype(low), (length - 8, 0))
    pairs_in = [(first_in, [pre_grad, ab_grad])]
    sums_in = pair_sums(place, pairs_in) if near else None
    params_part = jnp.sum(params_part.reshape(2, 8, LANES), axis=1).reshape(1, -1)
    lines = jnp.concatenate(
        [
            jnp.zeros((1, width), full),
            jnp.sum(ffn_gain_part, axis=0, keepdims=True),
            jnp.sum(taps_part.reshape(4, 8, -1), axis=1),
            jnp.pad(params_part, ((0, 0), (0, width - params_part.shape[1]))),
            jnp.zeros((1, width), full)
            if near
            else jnp.pad(jnp.sum(head_gain_part, axis=0)[None], ((0, 0), (0, width - value))),
        ],
        axis=0,
    )
    term, gains, *moved = line_call(
        partial(input_grad_kernel, last, keys, vals, near), "input_grad", 2, length, width, last,
        [mixer_gain[None, :], lines, head_gain_part], [(w_in, [(0, w_in.shape[1])]), (w_mix, [(0, vals)])],
        [pre_grad, gate_pgrad, ab_grad], [tokens],
        [((length, width), low, "second"), ((8, width), full, "all")],
        [pltpu.VMEM((ROWS, width), full), pltpu.VMEM((8, width), full)]
        + ([pltpu.VMEM((NEAR, 8, width), full), *[pltpu.SemaphoreType.DMA((NEAR,))] * 2] if near else [])
        + ([pltpu.VMEM((last + 1, 8, value), full), *[pltpu.SemaphoreType.DMA((last + 1,))] * 2] if near else []),
        scatters=[sums_rest, sums_in] if near else [], masks=range(1, NEAR) if near else (),
    )
    sums = gains if near else small_sums(gains)
    if near:
        (tq_grad, tk_grad, tv_grad, result, tokens_grad, query_grad, key_grad, value_grad, alpha_grad, beta_grad, up_grad, lift_grad,
         down_grad, gate_grad, out_grad) = final_sums(
            middle, narrow_sum, middle_grad, term, sums_in, moved[1], sums_up, got_up[0], sums_rest, moved[0],
            gains, heads, keys, vals, size,
        )
    else:
        up, rest, into = (plain_sums(place, pairs) for pairs in (pairs_up, pairs_rest, pairs_in))
        tokens_grad = middle_grad + term.astype(full)
        query_grad, key_grad, value_grad = into[:, :keys], into[:, keys : 2 * keys], into[:, 2 * keys : wide]
        alpha_grad, beta_grad = into[:, wide : wide + heads], into[:, wide + heads : wide + 2 * heads]
        up_grad, lift_grad = up[:, :size], up[:, size:]
        down_grad, gate_grad, out_grad = (
            rest[:, :size].T, rest[:, size : size + vals], rest[:, size + vals :].T
        )
        result = (middle + narrow_sum.astype(full)).astype(low)
        taps_grad = sums[2:6]
        tq_grad, tk_grad, tv_grad = (
            taps_grad[:, :keys], taps_grad[:, keys : 2 * keys], taps_grad[:, 2 * keys :]
        )
    return (
        result,
        tokens_grad,
        sums[0],
        query_grad,
        key_grad,
        value_grad,
        gate_grad,
        alpha_grad,
        beta_grad,
        sums[6, LANES : LANES + heads],
        sums[6, :heads],
        tq_grad,
        tk_grad,
        tv_grad,
        sums[7, :value],
        out_grad,
        sums[1],
        up_grad,
        lift_grad,
        down_grad,
    )


def solution(mesh):
    rows, both = P("seq", None), P("seq", "head")
    in_specs = (
        rows, P(), P(), both, both, both, both, both, both, P("head"), P("head"),
        P(None, "head"), P(None, "head"), P(None, "head"), P(), P("head", "seq"), P(),
        both, both, P("head", "seq"), rows,
    )
    out_specs = (
        rows, rows, P(), both, both, both, both, both, both, P("head"), P("head"),
        P(None, "head"), P(None, "head"), P(None, "head"), P(), P("head", "seq"), P(),
        both, both, P("head", "seq"),
    )
    return jax.shard_map(shards, mesh=mesh, in_specs=in_specs, out_specs=out_specs, check_vma=False)
```

```python
from functools import partial

import jax
import jax.numpy as jnp
from jax import lax
from jax.experimental import pallas as pl
from jax.experimental.pallas import tpu as pltpu
from jax.sharding import PartitionSpec as P

BLOCK = 128
LANES = 128
low = jnp.bfloat16
full = jnp.float32
MIB = 1 << 20


NEAR = 8
ONE = dict(pipeline_mode=pl.Buffered(1))
ANY = dict(memory_space=pl.ANY)
FREE = pl.CostEstimate(flops=1, bytes_accessed=1, transcendentals=0)
MESH = pl.DeviceIdType.MESH


def partner(mask):
    index = lax.axis_index("seq")
    bits = (lax.rem(index, 2), lax.rem(index // 2, 2), index // 4)
    return sum((1 << i) * ((1 - b) if mask >> i & 1 else b) for i, b in enumerate(bits))


def greet(masks, last=None, all_heads=False):
    barrier = pltpu.get_barrier_semaphore()
    for mask in masks:
        pl.semaphore_signal(barrier, inc=1, device_id={"seq": partner(mask)}, device_id_type=MESH)
    count = len(masks)
    if all_heads:
        place = lax.axis_index("head")
        for k in range(1, last + 1):
            to = lax.rem(place + k, last + 1)
            pl.semaphore_signal(barrier, inc=1, device_id={"head": to}, device_id_type=MESH)
        count += last
    elif last is not None:
        place = lax.axis_index("head")
        for there, to in ((place > 0, place - 1), (place < last, place + 1)):

            @pl.when(there)
            def _(to=to):
                pl.semaphore_signal(barrier, inc=1, device_id={"head": to}, device_id_type=MESH)

        count += jnp.minimum(place, 1) + jnp.minimum(last - place, 1)
    pl.semaphore_wait(barrier, count)


class Gather:
    masks = (1, 2, 4)
    semaphores = [pltpu.SemaphoreType.DMA((8,)), pltpu.SemaphoreType.DMA((8,)), pltpu.SemaphoreType.DMA((1,))]

    def __init__(self, shard, whole, sent, got, home):
        self.shard, self.whole, self.sent, self.got, self.home = shard, whole, sent, got, home
        self.size = shard.shape[0]

    def rows(self, mask, first=0, count=None):
        start = pl.multiple_of(partner(mask) * self.size + first, self.size // 2)
        return self.whole.at[pl.ds(start, self.size if count is None else count), :]

    def push(self, slot):
        half = self.size // 2
        mask, src, dst = (
            (2, self.shard, self.rows(0)),
            (4, self.shard, self.rows(0)),
            (2, self.rows(4, 0, half), self.rows(4, 0, half)),
            (4, self.rows(2, half, half), self.rows(2, half, half)),
            (1, self.shard, self.rows(0)),
            (1, self.rows(2), self.rows(2)),
            (1, self.rows(4), self.rows(4)),
            (1, self.rows(6), self.rows(6)),
        )[slot]
        return pltpu.make_async_remote_copy(
            src_ref=src, dst_ref=dst, send_sem=self.sent.at[slot], recv_sem=self.got.at[slot],
            device_id={"seq": partner(mask)}, device_id_type=MESH,
        )

    def local(self):
        return pltpu.make_async_copy(self.shard, self.rows(0), self.home.at[0])

    def start(self):
        self.local().start()
        for slot in (0, 1, 4):
            self.push(slot).start()

    def middle(self):
        for slot in (0, 1):
            self.push(slot).wait_recv()
        for slot in (2, 3, 5, 6):
            self.push(slot).start()

    def late(self):
        for slot in (2, 3):
            self.push(slot).wait_recv()
        self.push(7).start()

    def traded(self, slots):
        for slot in slots:
            self.push(slot).wait_recv()

    def settle(self):
        for slot in range(8):
            self.push(slot).wait_send()

    def end(self):
        self.traded((4, 5, 6, 7))
        self.settle()
        self.local().wait()


class Scatter:
    masks = (2, 4, 6)
    semaphores = [pltpu.SemaphoreType.DMA((3,)), pltpu.SemaphoreType.DMA((3,))]

    def __init__(self, parts, got, sent, came, first=0):
        self.parts, self.got, self.sent, self.came = parts, got, sent, came
        self.columns = pl.ds(first, got.shape[2])

    def push(self, k):
        return pltpu.make_async_remote_copy(
            src_ref=self.parts.at[k + 1, :, self.columns], dst_ref=self.got.at[k], send_sem=self.sent.at[k],
            recv_sem=self.came.at[k], device_id={"seq": partner(2 * k + 2)}, device_id_type=MESH,
        )

    def start(self):
        for k in range(3):
            self.push(k).start()

    def end(self):
        for k in range(3):
            self.push(k).wait()


def load(step, pairs, sems):
    @pl.when(step == 0)
    def _():
        copies = [pltpu.make_async_copy(a, b, sems.at[n]) for n, (a, b) in enumerate(pairs)]
        for copy in copies:
            copy.start()
        for copy in copies:
            copy.wait()


def mm(a, b):
    return jnp.dot(a.astype(low), b.astype(low), preferred_element_type=full)


def mm_nt(a, b):
    return lax.dot_general(
        a.astype(low), b.astype(low), (((1,), (1,)), ((), ())), preferred_element_type=full
    )


def mm_tn(a, b):
    return lax.dot_general(
        a.astype(low), b.astype(low), (((0,), (0,)), ((), ())), preferred_element_type=full
    )


def exact(a, b):
    return jnp.dot(a, b, precision=lax.Precision.HIGHEST, preferred_element_type=full)


def sigmoid(t):
    return 1.0 / (1.0 + jnp.exp(-t))


def softplus(t):
    return jnp.maximum(t, 0.0) + jnp.log(1.0 + jnp.exp(-jnp.abs(t)))


def iotas(size):
    return (
        lax.broadcasted_iota(jnp.int32, (size, size), 0),
        lax.broadcasted_iota(jnp.int32, (size, size), 1),
    )


def conv_sum(ext, taps, meta, first, width, rows):
    total = taps[3:4, first : first + width] * ext[8 : 8 + rows, first : first + width]
    for lag in (1, 2, 3):
        total += (
            taps[3 - lag : 4 - lag, first : first + width]
            * meta[:, lag : lag + 1]
            * ext[8 - lag : 8 - lag + rows, first : first + width]
        )
    return total


def gates(ab, params, heads):
    log_decay = params[0:1, :] * softplus(ab + params[1:2, :])
    beta = sigmoid(ab)
    return log_decay, beta


def decay_parts(cum, cum_t, h, same_low, strict_low, meta):
    size = cum.shape[0]
    col = cum[:, h : h + 1]
    row = cum_t[h : h + 1, :]
    lower = jnp.where(same_low, jnp.exp(jnp.minimum(col - row, 0.0)), 0.0)
    strict = jnp.where(strict_low, lower, 0.0)
    last = cum[size - 1 : size, h : h + 1]
    from_start = jnp.exp(col) * meta[:, 4:5]
    to_end = jnp.exp(last - col) * meta[:, 5:6]
    carried = jnp.exp(last) * meta[size - 1 : size, 4:5]
    return lower, strict, from_start, to_end, carried


def unit_lower_inverse(strict, rows, cols):
    size = strict.shape[0]
    power = jnp.where((rows >> 3) == (cols >> 3), -strict, 0.0)
    inverse = jnp.where(rows == cols, 1.0, power)
    power = mm(power, power)
    inverse = inverse + mm(inverse, power)
    power = mm(power, power)
    inverse = inverse + mm(inverse, power)
    shift = 3
    while (1 << shift) < size:
        off = jnp.where(
            ((rows >> (shift + 1)) == (cols >> (shift + 1))) & ((rows >> shift) != (cols >> shift)),
            strict,
            0.0,
        )
        inverse = inverse - mm(inverse, mm(off, inverse))
        shift += 1
    return inverse


def inverses(stricts, rows, cols):
    size = stricts[0].shape[0]
    near = (rows >> 3) == (cols >> 3)
    powers = [jnp.where(near, -a, 0.0) for a in stricts]
    result = [jnp.where(rows == cols, 1.0, p) for p in powers]
    for _ in range(2):
        powers = [mm(p, p) for p in powers]
        result = [t + mm(t, p) for t, p in zip(result, powers)]
    shift = 3
    while (1 << shift) < size:
        pick = ((rows >> (shift + 1)) == (cols >> (shift + 1))) & (
            (rows >> shift) != (cols >> shift)
        )
        offs = [mm(jnp.where(pick, a, 0.0), t) for a, t in zip(stricts, result)]
        result = [t - mm(t, o) for t, o in zip(result, offs)]
        shift += 1
    return result


def masks(meta, segrow):
    size = meta.shape[0]
    rows, cols = iotas(size)
    same = meta[:, 0:1] == segrow[0:1, :]
    return rows, cols, same & (rows >= cols), same & (rows > cols)


def unit(post):
    return lax.rsqrt(jnp.sum(post * post, axis=-1, keepdims=True) + 1e-06)


def forward_kernel(
    heads, key, value, gathering,
    pre_ref, ab_ref, meta_ref, segrow_ref, edge_ref, taps_ref, params_ref, *refs
):
    step = pl.program_id(0)
    steps = pl.num_programs(0)
    if gathering:
        shard_ref, out_ref, through_ref, states_ref, inverse_ref, end_ref, whole_ref, ext, state, *sems = refs
        moving = Gather(shard_ref, whole_ref, *sems)

        @pl.when(step == 0)
        def _():
            greet(Gather.masks)
            moving.start()

        @pl.when(step == steps - 2)
        def _():
            moving.middle()

    else:
        out_ref, through_ref, states_ref, inverse_ref, end_ref, ext, state = refs
    size = pre_ref.shape[0]
    wide = value + key
    kfirst, vfirst = heads * key, 2 * heads * key

    @pl.when(step == 0)
    def _():
        ext[0:8, :] = edge_ref[...].astype(full)
        rows, cols = iotas(key)
        eye = (rows == cols).astype(full)
        for h in range(heads):
            state[h, :, :value] = jnp.zeros((key, value), full)
            state[h, :, value:] = eye

    @pl.when(step > 0)
    def _():
        ext[0:8, :] = ext[size : size + 8, :]

    ext[8:, :] = pre_ref[...].astype(full)
    meta = meta_ref[...]
    log_decay, beta = gates(ab_ref[...], params_ref, heads)
    rows, cols, same_low, strict_low = masks(meta, segrow_ref)
    cum = exact((rows >= cols).astype(full), log_decay)
    cum_t = cum.T
    qs, ks, vs, lowers, stricts, fs, es, cs = [], [], [], [], [], [], [], []
    for h in range(heads):
        u = conv_sum(ext, taps_ref, meta, h * key, key, size)
        post = u * sigmoid(u)
        q = (post * unit(post)).astype(low)
        u = conv_sum(ext, taps_ref, meta, kfirst + h * key, key, size)
        post = u * sigmoid(u)
        k = (post * unit(post)).astype(low)
        u = conv_sum(ext, taps_ref, meta, vfirst + h * value, value, size)
        v = u * sigmoid(u)
        lower, strict, f, e, c = decay_parts(cum, cum_t, h, same_low, strict_low, meta)
        bcol = beta[:, heads + h : heads + h + 1]
        gram = mm_nt(jnp.concatenate([k, q], axis=0), k)
        qs.append(q), ks.append(k), vs.append(v), fs.append(f), es.append(e), cs.append(c)
        stricts.append(bcol * strict * gram[:size])
        lowers.append(lower * gram[size:])
    ts = inverses(stricts, rows, cols)
    for h in range(heads):
        bcol = beta[:, heads + h : heads + h + 1]
        s = state[h]
        states_ref[0, h] = s.astype(low)
        t = ts[h].astype(low)
        inverse_ref[0, h] = t
        ks_s = mm(ks[h], s)
        fb = fs[h] * bcol
        target = jnp.concatenate(
            [bcol * vs[h] - fb * ks_s[:, :value], -fb * ks_s[:, value:]], axis=1
        )
        delta = mm(t, target).astype(low)
        left = jnp.concatenate([(fs[h] * qs[h].astype(full)).astype(low), lowers[h].astype(low)], axis=1)
        out = mm(left, jnp.concatenate([s.astype(low), delta], axis=0))
        out_ref[:, h * value : (h + 1) * value] = out[:, :value]
        through_ref[:, h * key : (h + 1) * key] = out[:, value:].astype(low)
        ke = es[h] * ks[h].astype(full)
        s = cs[h] * s + mm_tn(ke, delta)
        state[h] = s
        end_ref[h] = s.astype(low)

    if gathering:

        @pl.when(step == steps - 1)
        def _():
            moving.late()
            moving.end()


def forward_chain(pre, ab, meta, segrow, edge, taps, params, heads, key, value, shard=None):
    gathering = shard is not None
    moved = [jax.ShapeDtypeStruct((shard.shape[0] * NEAR, shard.shape[1]), low)] if gathering else []
    extra = dict(collective_id=5, has_side_effects=True) if gathering else {}
    length = pre.shape[0]
    blocks = length // BLOCK
    width = pre.shape[1]
    wide = value + key
    return pl.pallas_call(
        partial(forward_kernel, heads, key, value, gathering),
        grid=(blocks,),
        in_specs=[
            pl.BlockSpec((BLOCK, width), lambda n: (n, 0)),
            pl.BlockSpec((BLOCK, LANES), lambda n: (n, 0)),
            pl.BlockSpec((BLOCK, LANES), lambda n: (n, 0)),
            pl.BlockSpec((8, BLOCK), lambda n: (0, n)),
            pl.BlockSpec((8, width), lambda n: (0, 0)),
            pl.BlockSpec(taps.shape, lambda n: (0, 0)),
            pl.BlockSpec((8, LANES), lambda n: (0, 0)),
        ]
        + [pl.BlockSpec(**ANY) for _ in moved],
        out_specs=[
            pl.BlockSpec((BLOCK, heads * value), lambda n: (n, 0)),
            pl.BlockSpec((BLOCK, heads * key), lambda n: (n, 0)),
            pl.BlockSpec((1, heads, key, wide), lambda n: (n, 0, 0, 0)),
            pl.BlockSpec((1, heads, BLOCK, BLOCK), lambda n: (n, 0, 0, 0)),
            pl.BlockSpec((heads, key, wide), lambda n: (0, 0, 0)),
        ]
        + [pl.BlockSpec(**ANY) for _ in moved],
        out_shape=[
            jax.ShapeDtypeStruct((length, heads * value), full),
            jax.ShapeDtypeStruct((length, heads * key), low),
            jax.ShapeDtypeStruct((blocks, heads, key, wide), low),
            jax.ShapeDtypeStruct((blocks, heads, BLOCK, BLOCK), low),
            jax.ShapeDtypeStruct((heads, key, wide), low),
        ]
        + moved,
        scratch_shapes=[
            pltpu.VMEM((BLOCK + 8, width), full),
            pltpu.VMEM((heads, key, wide), full),
        ]
        + (Gather.semaphores if gathering else []),
        compiler_params=pltpu.CompilerParams(vmem_limit_bytes=48 * MIB, **extra),
        cost_estimate=FREE,
        name="chain_forward",
    )(pre, ab, meta, segrow, edge, taps, params, *([shard] if gathering else []))


def gate_back_kernel(heads, key, value, dz_ref, mixed_ref, gate_ref, gain_ref, through_ref, whole_ref,
                     dgz_ref, do_ref, gain_grad_ref, adjoint_ref, weights, dy_ref, sems):
    load(pl.program_id(0), [(whole_ref.at[:, heads * value :], weights)], sems)

    @pl.when(pl.program_id(0) == 0)
    def _():
        gain_grad_ref[...] = jnp.zeros_like(gain_grad_ref)
        adjoint_ref[...] = jnp.zeros_like(adjoint_ref)

    rows = dz_ref.shape[0]
    gain = gain_ref[0:1, :]
    dy_ref[...] = mm(dz_ref[...], weights[...])
    for h in range(heads):
        cols = slice(h * value, (h + 1) * value)
        o = mixed_ref[:, cols].astype(full)
        s3 = lax.rsqrt(jnp.mean(o * o, axis=-1, keepdims=True) + 1e-05)
        n3 = o * s3
        gz = gate_ref[:, cols]
        sig = sigmoid(gz)
        sg = gz * sig
        dy = dy_ref[:, cols]
        dyn = dy * n3
        part = dyn * sg
        gain_grad_ref[...] += jnp.sum(part.reshape(rows // 8, 8, value), axis=0)
        dgz_ref[:, cols] = (dyn * gain * (sig * (1.0 + gz * (1.0 - sig)))).astype(low)
        dn3 = dy * gain * sg
        do = s3 * (dn3 - n3 * jnp.mean(dn3 * n3, axis=-1, keepdims=True))
        do = do.astype(low)
        do_ref[:, cols] = do
        adjoint_ref[h] += mm_tn(through_ref[:, h * key : (h + 1) * key], do)


def gate_back(dz, w_mix, mixed, gate, gain, through, heads, key, value, rows=256):
    length, width = dz.shape
    wide = heads * value
    return pl.pallas_call(
        partial(gate_back_kernel, heads, key, value),
        grid=(length // rows,),
        in_specs=[
            pl.BlockSpec((rows, width), lambda n: (n, 0)),
            pl.BlockSpec((rows, wide), lambda n: (n, 0)),
            pl.BlockSpec((rows, wide), lambda n: (n, 0)),
            pl.BlockSpec((1, value), lambda n: (0, 0)),
            pl.BlockSpec((rows, heads * key), lambda n: (n, 0)),
        ]
        + [pl.BlockSpec(**ANY)],
        out_specs=[
            pl.BlockSpec((rows, wide), lambda n: (n, 0)),
            pl.BlockSpec((rows, wide), lambda n: (n, 0)),
            pl.BlockSpec((8, value), lambda n: (0, 0)),
            pl.BlockSpec((heads, key, value), lambda n: (0, 0, 0)),
        ],
        out_shape=[
            jax.ShapeDtypeStruct((length, wide), low),
            jax.ShapeDtypeStruct((length, wide), low),
            jax.ShapeDtypeStruct((8, value), full),
            jax.ShapeDtypeStruct((heads, key, value), full),
        ],
        scratch_shapes=[
            pltpu.VMEM((width, wide), low),
            pltpu.VMEM((rows, wide), full),
            pltpu.SemaphoreType.DMA((1,)),
        ],
        compiler_params=pltpu.CompilerParams(vmem_limit_bytes=48 * MIB),
        cost_estimate=FREE,
        name="gate_back",
    )(dz, mixed, gate, gain, through, w_mix)


def lane_sum(array):
    return jnp.sum(array, axis=-1, keepdims=True)


def backward_kernel(
    heads, key, value, devices, scattering,
    pre_ref, tail_ref, ab_ref, meta_ref, segrow_ref, edge_ref, edge_meta_ref, taps_ref, params_ref,
    states_ref, inverse_ref, state_in_ref, do_ref, ends_ref, *refs
):
    step = pl.program_id(0)
    steps = pl.num_programs(0)
    piece, *refs = refs
    parts_ref = refs.pop(0) if scattering else None
    dpre_ref, dab_ref, halo_ref, taps_grad_ref, params_grad_ref = refs[:5]
    refs = refs[5:]
    got_ref = refs.pop(0) if scattering else None
    ext, du, adjoint, adjoints, home, *sems = refs
    if scattering:
        moving = Scatter(parts_ref, got_ref, *sems[:2])
        lead = Gather(piece, adjoints, *sems[2:])

        @pl.when(step == 0)
        def _():
            greet(sorted({*Scatter.masks, *Gather.masks}))
            lead.start()

    size = pre_ref.shape[0]
    kfirst, vfirst = heads * key, 2 * heads * key

    @pl.when(step == 0)
    def _():
        adjoint[...] = jnp.zeros_like(adjoint)
        tall = heads * key
        if scattering:
            lead.middle()
            lead.late()
            moving.start()
            lead.end()
        else:
            copy = pltpu.make_async_copy(piece, adjoints, home.at[0])
            copy.start()
            copy.wait()

        def one(k, carry):
            j = devices - 1 - k
            for h in range(heads):
                rows = pl.ds(pl.multiple_of(j * tall + h * key, key), key)
                adjoint[h] = (
                    mm_tn(ends_ref[rows, value:], adjoint[h]) + adjoints[rows, :].astype(full)
                )
            return carry

        lax.fori_loop(0, devices - 1 - lax.axis_index("seq"), one, 0)
        du[8 + size :, :] = jnp.zeros((8, du.shape[1]), full)
        taps_grad_ref[...] = jnp.zeros_like(taps_grad_ref)
        params_grad_ref[...] = jnp.zeros_like(params_grad_ref)

    @pl.when(step > 0)
    def _():
        du[8 + size :, :] = du[8:16, :]

    du[0:8, :] = jnp.zeros((8, du.shape[1]), full)

    @pl.when(step < steps - 1)
    def _():
        ext[0:8, :] = tail_ref[8:16, :].astype(full)

    @pl.when(step == steps - 1)
    def _():
        ext[0:8, :] = edge_ref[...].astype(full)

    ext[8:, :] = pre_ref[...].astype(full)
    meta = meta_ref[...]
    ab = ab_ref[...]
    log_decay, beta = gates(ab, params_ref, heads)
    rows, cols, same_low, strict_low = masks(meta, segrow_ref)
    cum = exact((rows >= cols).astype(full), log_decay)
    cum_t = cum.T
    lane = lax.broadcasted_iota(jnp.int32, (size, LANES), 1)
    row8 = lax.broadcasted_iota(jnp.int32, (8, size), 0)
    dcum = jnp.zeros((size, LANES), full)
    dcum_rows = jnp.zeros((8, size), full)
    dcum_last = jnp.zeros((1, LANES), full)
    dbeta = jnp.zeros((size, LANES), full)
    lane1 = lax.broadcasted_iota(jnp.int32, (1, LANES), 1)

    for h in range(heads):
        qcols = slice(h * key, (h + 1) * key)
        kcols = slice(kfirst + h * key, kfirst + (h + 1) * key)
        vcols = slice(vfirst + h * value, vfirst + (h + 1) * value)
        uq = conv_sum(ext, taps_ref, meta, h * key, key, size)
        sq = sigmoid(uq)
        pq = uq * sq
        rq = unit(pq)
        qf = pq * rq
        q = qf.astype(low)
        uk = conv_sum(ext, taps_ref, meta, kfirst + h * key, key, size)
        sk = sigmoid(uk)
        pk = uk * sk
        rk = unit(pk)
        kf = pk * rk
        k = kf.astype(low)
        uv = conv_sum(ext, taps_ref, meta, vfirst + h * value, value, size)
        sv = sigmoid(uv)
        v = uv * sv
        lower, strict, f, e, c = decay_parts(cum, cum_t, h, same_low, strict_low, meta)
        b = beta[:, heads + h : heads + h + 1]
        kq = jnp.concatenate([k, q], axis=0)
        gram = mm_nt(kq, k)
        kk, qk = gram[:size], gram[size:]
        stored = states_ref[0, h]
        s = stored[:, :value].astype(full) + mm(stored[:, value:], state_in_ref[h])
        slow = s.astype(low)
        kqs = mm(kq, slow)
        ks, qs = kqs[:size], kqs[size:]
        rest = v - f * ks
        t = inverse_ref[0, h]
        delta = mm(t, b * rest).astype(low)
        do = do_ref[:, h * value : (h + 1) * value]
        dof = do.astype(full)
        ds = adjoint[h]
        dslow = ds.astype(low)
        ke = (e * kf).astype(low)
        p = lower * qk
        left = jnp.concatenate([p.T.astype(low), ke], axis=1)
        ddelta = mm(left, jnp.concatenate([do, dslow], axis=0))
        dtarget = mm_tn(t, ddelta)
        outer = mm_nt(jnp.concatenate([do, dtarget.astype(low)], axis=0), delta)
        dp, dan = outer[:size], outer[size:]
        eg = lower * dp
        hn = -strict * dan
        hg = b * hn
        x = eg * qk
        hk = hn * kk
        g1 = (b * f) * dtarget
        fdo = f * dof
        pair = jnp.concatenate([fdo.astype(low), (-g1).astype(low)], axis=0)
        both = mm_nt(pair, slow)
        dq = both[:size] + mm(eg, k)
        dsk = e * mm_nt(delta, dslow)
        left = jnp.concatenate([(hg + hg.T).astype(low), eg.T.astype(low)], axis=1)
        dk = both[size:] + dsk + mm(left, kq)
        dv = b * dtarget
        z = lane_sum(kf * dsk)
        dfrom = lane_sum(dof * qs) - b * lane_sum(dtarget * ks)
        hrow = lane_sum(hk)
        db = hrow + lane_sum(dtarget * rest)
        dbeta = dbeta + jnp.where(lane == heads + h, db, 0.0)
        dcum = dcum + jnp.where(lane == h, lane_sum(x) + b * hrow + f * dfrom - z, 0.0)
        drow = jnp.sum(x + b * hk, axis=0, keepdims=True)
        dcum_rows = dcum_rows + jnp.where(row8 == h, drow, 0.0)
        dlast = jnp.sum(z, axis=0, keepdims=True) + c * jnp.sum(
            lane_sum(ds * s), axis=0, keepdims=True
        )
        dcum_last = dcum_last + jnp.where(lane1 == h, dlast, 0.0)
        adjoint[h] = c * ds + mm_tn(jnp.concatenate([q, k], axis=0), pair)

        dpq = rq * (dq - qf * lane_sum(dq * qf))
        du[8 : 8 + size, qcols] = dpq * (sq * (1.0 + uq * (1.0 - sq)))
        dpk = rk * (dk - kf * lane_sum(dk * kf))
        du[8 : 8 + size, kcols] = dpk * (sk * (1.0 + uk * (1.0 - sk)))
        du[8 : 8 + size, vcols] = dv * (sv * (1.0 + uv * (1.0 - sv)))

    padded = jnp.concatenate([dcum_rows, jnp.zeros((LANES - 8, size), full)], axis=0)
    rowi = lax.broadcasted_iota(jnp.int32, (size, LANES), 0)
    dcum = dcum - padded.T + jnp.where(rowi == size - 1, dcum_last, 0.0)
    dlog = exact((rows <= cols).astype(full), dcum)
    dga = dlog * params_ref[0:1, :] * sigmoid(ab + params_ref[1:2, :])
    is_decay = lane < heads
    dga = jnp.where(is_decay, dga, 0.0)
    params_grad_ref[0:8, :] += jnp.sum(dga.reshape(size // 8, 8, LANES), axis=0)
    decay_part = jnp.where(is_decay, dlog * log_decay, 0.0)
    params_grad_ref[8:16, :] += jnp.sum(decay_part.reshape(size // 8, 8, LANES), axis=0)
    dab_ref[...] = jnp.where(is_decay, dga, dbeta * beta * (1.0 - beta)).astype(low)

    width = du.shape[1]
    for first in range(0, width, 512):
        cs = slice(first, first + 512)
        own = du[8 : 8 + size, cs]
        total = taps_ref[3:4, cs] * own
        taps_grad_ref[24:32, cs] += jnp.sum(
            (own * ext[8 : 8 + size, cs]).reshape(size // 8, 8, 512), axis=0
        )
        for lag in (1, 2, 3):
            total += taps_ref[3 - lag : 4 - lag, cs] * meta[:, 5 + lag : 6 + lag] * du[
                8 + lag : 8 + lag + size, cs
            ]
            taps_grad_ref[8 * (3 - lag) : 8 * (4 - lag), cs] += jnp.sum(
                (own * meta[:, lag : lag + 1] * ext[8 - lag : 8 - lag + size, cs]).reshape(
                    size // 8, 8, 512
                ),
                axis=0,
            )
        dpre_ref[:, cs] = total.astype(low)

    @pl.when(step == steps - 1)
    def _():
        edge_meta = edge_meta_ref[...]
        halo = jnp.zeros(halo_ref.shape, full)
        for lag in (1, 2, 3):
            halo += taps_ref[3 - lag : 4 - lag, :] * edge_meta[:, 5 + lag : 6 + lag] * du[
                lag : 8 + lag, :
            ]
        halo_ref[...] = halo
        if scattering:
            moving.end()


def backward_chain(pre, ab, meta, segrow, edge, edge_meta, taps, params, states, inverse,
                   state_in, do, ends, adjoints, heads, key, value, parts=None, sent=0):
    scattering = parts is not None
    moved = [jax.ShapeDtypeStruct((3, parts.shape[1], sent), low)] if scattering else []
    extra = dict(collective_id=6, has_side_effects=True) if scattering else {}
    devices = ends.shape[0] // (heads * key)
    length, width = pre.shape
    blocks = length // BLOCK
    wide = value + key
    once = dict(pipeline_mode=pl.Buffered(1))
    last = blocks - 1
    return pl.pallas_call(
        partial(backward_kernel, heads, key, value, devices, scattering),
        grid=(blocks,),
        in_specs=[
            pl.BlockSpec((BLOCK, width), lambda n: (last - n, 0)),
            pl.BlockSpec((16, width), lambda n: (jnp.maximum((last - n) * (BLOCK // 16) - 1, 0), 0)),
            pl.BlockSpec((BLOCK, LANES), lambda n: (last - n, 0)),
            pl.BlockSpec((BLOCK, LANES), lambda n: (last - n, 0)),
            pl.BlockSpec((8, BLOCK), lambda n: (0, last - n)),
            pl.BlockSpec((8, width), lambda n: (0, 0)),
            pl.BlockSpec((8, LANES), lambda n: (0, 0)),
            pl.BlockSpec(taps.shape, lambda n: (0, 0)),
            pl.BlockSpec((8, LANES), lambda n: (0, 0)),
            pl.BlockSpec((1, heads, key, wide), lambda n: (last - n, 0, 0, 0)),
            pl.BlockSpec((1, heads, BLOCK, BLOCK), lambda n: (last - n, 0, 0, 0)),
            pl.BlockSpec((heads, key, value), lambda n: (0, 0, 0)),
            pl.BlockSpec((BLOCK, heads * value), lambda n: (last - n, 0)),
            pl.BlockSpec(ends.shape, lambda n: (0, 0), **once),
        ]
        + [pl.BlockSpec(**ANY) for _ in (0, *moved)],
        out_specs=[
            pl.BlockSpec((BLOCK, width), lambda n: (last - n, 0)),
            pl.BlockSpec((BLOCK, LANES), lambda n: (last - n, 0)),
            pl.BlockSpec((8, width), lambda n: (0, 0)),
            pl.BlockSpec((32, width), lambda n: (0, 0)),
            pl.BlockSpec((16, LANES), lambda n: (0, 0)),
        ]
        + [pl.BlockSpec(**ANY) for _ in moved],
        out_shape=[
            jax.ShapeDtypeStruct((length, width), low),
            jax.ShapeDtypeStruct((length, LANES), low),
            jax.ShapeDtypeStruct((8, width), full),
            jax.ShapeDtypeStruct((32, width), full),
            jax.ShapeDtypeStruct((16, LANES), full),
        ]
        + moved,
        scratch_shapes=[
            pltpu.VMEM((BLOCK + 8, width), full),
            pltpu.VMEM((BLOCK + 16, width), full),
            pltpu.VMEM((heads, key, value), full),
            pltpu.VMEM((devices * heads * key, value), low),
            pltpu.SemaphoreType.DMA((1,)),
        ]
        + (Scatter.semaphores + Gather.semaphores if scattering else []),
        compiler_params=pltpu.CompilerParams(vmem_limit_bytes=56 * MIB, **extra),
        cost_estimate=FREE,
        name="chain_backward",
    )(pre, pre, ab, meta, segrow, edge, edge_meta, taps, params, states, inverse, state_in, do, ends,
      adjoints, *([parts] if scattering else []))


def segment_tables(doc_lengths, shard, length):
    starts = jnp.cumsum(doc_lengths, dtype=jnp.int32) - doc_lengths
    positions = shard * length + jnp.arange(-16, length + 8, dtype=jnp.int32)
    seg = jnp.sum((starts[None, :] <= positions[:, None]).astype(jnp.int32), axis=1)
    own = seg[16 : 16 + length]

    def lanes(first, count):
        base = seg[first : first + count]
        back = [seg[first - l : first - l + count] == base for l in (1, 2, 3)]
        ahead = [seg[first + l : first + l + count] == base for l in (1, 2, 3)]
        return base, back, ahead

    base, back, ahead = lanes(16, length)
    blocks = own.reshape(-1, BLOCK)
    before = seg[15 : 15 + length : BLOCK]
    alive = (blocks == before[:, None]).reshape(-1)
    to_last = (blocks == blocks[:, -1:]).reshape(-1)
    columns = [base, *back, alive, to_last, *ahead]
    meta = jnp.stack([a.astype(full) for a in columns], axis=1)
    meta = jnp.pad(meta, ((0, 0), (0, LANES - meta.shape[1])))
    base, back, ahead = lanes(8, 8)
    columns = [base, *back, base, base, *ahead]
    edge_meta = jnp.stack([a.astype(full) for a in columns], axis=1)
    edge_meta = jnp.pad(edge_meta, ((0, 0), (0, LANES - edge_meta.shape[1])))
    segrow = jnp.broadcast_to(own.astype(full)[None, :], (8, length))
    return meta, edge_meta, segrow


ROWS = 256
PIECE = 32
HOP = 2
EACH = ROWS // PIECE
AHEAD = 1 + (EACH - 1 + 3 * HOP) // EACH
RING = AHEAD + 1


def exchanged(block, mask):
    return lax.ppermute(block, "seq", [(i, i ^ mask) for i in range(lax.axis_size("seq"))])


def line_scratch(length, width):
    pieces = length // PIECE
    return [
        pltpu.VMEM((RING, ROWS, width), low),
        pltpu.VMEM((length, width), low),
        pltpu.VMEM((length, width), low),
        pltpu.SemaphoreType.DMA((pieces,)),
        pltpu.SemaphoreType.DMA((pieces,)),
        pltpu.SemaphoreType.DMA((pieces,)),
        pltpu.SemaphoreType.DMA((pieces,)),
    ]


def line_sum(step, last, stages, finish, scratch):
    own, from_left, from_right, got_left, got_right, sent_right, sent_left = scratch
    place = lax.axis_index("head")
    length, width = from_left.shape
    blocks, pieces = length // ROWS, length // PIECE
    left_there, right_there = place > 0, place < last

    def rows(piece):
        return pl.ds(pl.multiple_of(piece * PIECE, PIECE), PIECE)

    def hop(piece, rightwards):
        kept, sent, got, to = (
            (from_left, sent_right, got_left, place + 1)
            if rightwards
            else (from_right, sent_left, got_right, place - 1)
        )
        return pltpu.make_async_remote_copy(
            src_ref=kept.at[rows(piece)],
            dst_ref=kept.at[rows(piece)],
            send_sem=sent.at[piece],
            recv_sem=got.at[piece],
            device_id={"head": to},
            device_id_type=MESH,
        )

    def own_piece(piece):
        slot = lax.rem(piece // EACH, RING)
        first = pl.multiple_of(lax.rem(piece, EACH) * PIECE, PIECE)
        return own[slot, pl.ds(first, PIECE), :].astype(full)

    @pl.when(step == 0)
    def _():
        @pl.when(place == 0)
        def _():
            from_left[...] = jnp.zeros_like(from_left)

        @pl.when(place == last)
        def _():
            from_right[...] = jnp.zeros_like(from_right)

    def one(q, carry):
        now = (step - 1) * EACH + q
        for rightwards in (True, False):
            came, more = (left_there, right_there) if rightwards else (right_there, left_there)
            kept = from_left if rightwards else from_right
            piece = now - HOP * (place if rightwards else last - place)

            @pl.when((piece >= 0) & (piece < pieces))
            def _():
                @pl.when(came)
                def _():
                    hop(piece, rightwards).wait_recv()

                @pl.when(more)
                def _():
                    kept[rows(piece), :] = (
                        own_piece(piece) + kept[rows(piece), :].astype(full)
                    ).astype(low)
                    hop(piece, rightwards).start()

        return carry

    done = 0
    for n, stage in enumerate(stages):

        @pl.when(step < blocks)
        def _(n=n, stage=stage):
            value = stage()
            if n == len(stages) - 1:
                own[lax.rem(step, RING)] = value.astype(low)

        until = EACH * (n + 1) // len(stages)
        lax.fori_loop(done, until, one, 0)
        done = until

    @pl.when(step >= AHEAD)
    def _():
        block = step - AHEAD
        span = pl.ds(pl.multiple_of(block * ROWS, ROWS), ROWS)
        total = from_left[span, :].astype(full) + from_right[span, :].astype(full)
        twice = jnp.where(left_there & right_there, 1.0, 0.0)
        finish(total - twice * own[lax.rem(block, RING)].astype(full))

    @pl.when(step == blocks + AHEAD - 1)
    def _():
        def settle(piece, carry):
            @pl.when(right_there)
            def _():
                hop(piece, True).wait_send()

            @pl.when(left_there)
            def _():
                hop(piece, False).wait_send()

            return carry

        lax.fori_loop(0, pieces, settle, 0)


def union(kinds):
    return sorted({mask for kind in kinds for mask in kind.masks})


def line_call(kernel, name, collective, length, width, last, resident, weights, entering, leaving, outs,
              scratch, gathers=(), scatters=(), early=None, masks=()):
    blocks = length // ROWS
    steps = blocks + AHEAD
    cuts, weights = [c for _, c in weights], [a for a, _ in weights]

    def spec(array, stage):
        if stage == "first":
            return pl.BlockSpec((ROWS, array.shape[1]), lambda g: (jnp.minimum(g, blocks - 1), 0))
        if stage == "second":
            return pl.BlockSpec((ROWS, array.shape[1]), lambda g: (jnp.maximum(g - AHEAD, 0), 0))
        rank = len(array.shape)
        return pl.BlockSpec(array.shape, lambda g: (0,) * rank, **ONE)

    in_specs = [spec(a, "all") for a in resident]
    first_one = [] if early is None else [early]
    in_specs += [pl.BlockSpec(**ANY) for _ in (*weights, *first_one, *gathers, *scatters)]
    in_specs += [spec(a, "first") for a in entering] + [spec(a, "second") for a in leaving]
    shapes = [jax.ShapeDtypeStruct(shape, dtype) for shape, dtype, _ in outs]
    out_specs = [
        spec(s, stage) if stage != "all" else pl.BlockSpec(s.shape, lambda g, r=len(s.shape): (0,) * r)
        for s, (_, _, stage) in zip(shapes, outs)
    ]
    moved = [jax.ShapeDtypeStruct((a.shape[0] * NEAR, a.shape[1]), low) for a in (*first_one, *gathers)]
    firsts, scatters = [f for _, f in scatters], [a for a, _ in scatters]
    moved += [jax.ShapeDtypeStruct((3, a.shape[1], a.shape[2] - f), low) for a, f in zip(scatters, firsts)]
    kinds = [Gather] * len(gathers) + [Scatter] * len(scatters)
    whole_first = [pltpu.VMEM(s.shape, low) for s in moved[: len(first_one)]]
    held = [pltpu.VMEM(a.shape, low) for a in weights] + [pltpu.SemaphoreType.DMA((sum(len(c) for c in cuts),))]
    held += whole_first + [s for _ in first_one for s in Gather.semaphores]
    held += [s for kind in kinds for s in kind.semaphores]

    def body(*refs):
        refs = list(refs)

        def take(n):
            head, refs[:] = refs[:n], refs[n:]
            return head

        own_in, heavy = take(len(resident)), take(len(weights))
        ahead, sources = take(len(first_one)), take(len(kinds))
        chunks = take(len(entering) + len(leaving))
        own_out, handed, targets = take(len(outs)), take(len(first_one)), take(len(kinds))
        own_scratch = take(len(scratch) + 7)
        matrices, (sems,) = take(len(weights)), take(1)
        if first_one:
            (table,), signals = take(1), take(3)
            lead = Gather(ahead[0], table, *signals)
            back = pltpu.make_async_copy(table, handed[0], signals[2].at[0])
            matrices.append(table)
        begins = [()] * len(gathers) + [(first,) for first in firsts]
        carried = [
            kind(a, b, *take(len(kind.semaphores)), *first)
            for kind, a, b, first in zip(kinds, sources, targets, begins)
        ]
        step = pl.program_id(0)

        @pl.when(step == 0)
        def _():
            greet(sorted({*masks, *union(kinds + [Gather] * len(first_one))}), last, bool(masks))
            for c in [lead] if first_one else carried:
                c.start()

        waits = []
        for source, target, parts in zip(heavy, matrices, cuts):
            for first, count in parts:
                part = pl.ds(first, count)
                waits.append(
                    pltpu.make_async_copy(source.at[:, part], target.at[:, part], sems.at[len(waits)])
                )

        @pl.when(step == 0)
        def _():
            for copy in waits:
                copy.start()

        def ready(k):
            @pl.when(step == 0)
            def _():
                waits[k].wait()

        if first_one:

            @pl.when(step == 0)
            def _():
                lead.middle()
                lead.late()
                for c in carried:
                    c.start()
                lead.end()
                back.start()

        for at, turn in ((steps - 3, "middle"), (steps - 1, "late")):

            @pl.when(step == at)
            def _(turn=turn):
                for c in carried:
                    if isinstance(c, Gather):
                        getattr(c, turn)()

        kernel(ready, matrices, *own_in, *chunks, *own_out, *own_scratch)

        @pl.when(step == steps - 1)
        def _():
            for c in carried:
                c.end()
            if first_one:
                back.wait()

    return pl.pallas_call(
        body,
        grid=(steps,),
        in_specs=in_specs,
        out_specs=out_specs + [pl.BlockSpec(**ANY) for _ in moved],
        out_shape=shapes + moved,
        scratch_shapes=scratch + line_scratch(length, width) + held,
        compiler_params=pltpu.CompilerParams(
            collective_id=collective, has_side_effects=True, vmem_limit_bytes=60 * MIB
        ),
        cost_estimate=FREE,
        name=name,
    )(*resident, *weights, *first_one, *gathers, *scatters, *entering, *leaving)


def mixer_out_kernel(heads, key, value, last, handed, ready, matrices,
                     head_gain_ref, gain_ref,
                     first_ref, local_ref, through_ref, tokens_ref,
                     y_ref, mixed_ref, gate_ref, state_ref, middle_ref, second_ref, *scratch):
    step = pl.program_id(0)
    weights, ends = matrices
    vals = heads * value

    if handed is not None:
        ready(handed)

    @pl.when(step == 0)
    def _():
        state_ref[...] = jnp.zeros_like(state_ref)

        def one(j, carry):
            for h in range(heads):
                rows = pl.ds(pl.multiple_of((j * heads + h) * key, key), key)
                part = ends[rows, :]
                state_ref[h] = mm(part[:, value:], state_ref[h]) + part[:, :value].astype(full)
            return carry

        lax.fori_loop(0, lax.axis_index("seq"), one, 0)

    def gate():
        ready(0)
        gate_ref[...] = mm(first_ref[...], weights[:, :vals])

    def mix():
        for h in range(heads):
            cols = slice(h * value, (h + 1) * value)
            o = local_ref[:, cols] + mm(through_ref[:, h * key : (h + 1) * key], state_ref[h])
            mixed_ref[:, cols] = o
            s3 = lax.rsqrt(jnp.mean(o * o, axis=-1, keepdims=True) + 1e-05)
            gz = gate_ref[:, cols]
            y_ref[:, cols] = (o * s3 * head_gain_ref[0:1, :] * (gz * sigmoid(gz))).astype(low)

    def project():
        ready(1)
        return mm_nt(y_ref[...], weights[:, vals:])

    def finish(total):
        middle = tokens_ref[...].astype(full) + total
        middle_ref[...] = middle
        scale = lax.rsqrt(jnp.mean(middle * middle, axis=-1, keepdims=True) + 1e-06)
        second_ref[...] = (middle * scale * gain_ref[0:1, :]).astype(low)

    line_sum(step, last, [gate, mix, project], finish, scratch)


def ffn_kernel(last, size, ready, matrices, gain_ref,
               second_ref, cot_ref, middle_ref, cot_late_ref,
               hidden_ref, dgate_ref, dup_ref, partial_ref, dmiddle_ref, dlow_ref, gain_grad_ref,
               fg, fu, *scratch):
    step = pl.program_id(0)
    (weights,) = matrices
    w_gate, w_up, w_down = (slice(n * size, (n + 1) * size) for n in range(3))

    @pl.when(step == 0)
    def _():
        gain_grad_ref[...] = jnp.zeros_like(gain_grad_ref)

    def one():
        ready(0)
        fg[...] = mm(second_ref[...], weights[:, w_gate])

    def two():
        ready(1)
        fu[...] = mm(second_ref[...], weights[:, w_up])

    def three():
        ready(2)
        g, lift = fg[...], fu[...]
        sig = sigmoid(g)
        swish = g * sig
        hidden = (swish * lift).astype(low)
        hidden_ref[...] = hidden
        fg[...] = lift * (sig * (1.0 + g * (1.0 - sig)))
        fu[...] = swish
        partial_ref[...] = mm_nt(hidden, weights[:, w_down]).astype(low)

    def four():
        dhid = mm(cot_ref[...], weights[:, w_down])
        dgate_ref[...] = (dhid * fg[...]).astype(low)
        dup_ref[...] = (dhid * fu[...]).astype(low)

    def five():
        return mm_nt(dgate_ref[...], weights[:, w_gate]) + mm_nt(dup_ref[...], weights[:, w_up])

    def finish(grad):
        middle = middle_ref[...]
        scale = lax.rsqrt(jnp.mean(middle * middle, axis=-1, keepdims=True) + 1e-06)
        norm = middle * scale
        gain_grad_ref[...] += jnp.sum((grad * norm).reshape(ROWS // 8, 8, -1), axis=0)
        weighted = grad * gain_ref[0:1, :]
        dm = cot_late_ref[...].astype(full) + scale * (
            weighted - norm * jnp.mean(weighted * norm, axis=-1, keepdims=True)
        )
        dmiddle_ref[...] = dm
        dlow_ref[...] = dm.astype(low)

    line_sum(step, last, [one, two, three, four, five], finish, scratch)


def input_grad_kernel(last, keys, vals, near, ready, matrices, gain_ref, lines_ref, head_ref,
                      dpre_ref, dgz_ref, dab_ref, tokens_ref,
                      term_ref, gains_ref, part, gain_grad, *scratch):
    step = pl.program_id(0)
    w_in, w_mix = matrices
    wide = 2 * keys + vals
    if near:
        (got, sent, came, got_head, sent_head, came_head), scratch = scratch[:6], scratch[6:]
        place = lax.axis_index("head")

        def across(k):
            return pltpu.make_async_remote_copy(
                src_ref=head_ref, dst_ref=got_head.at[place], send_sem=sent_head.at[k],
                recv_sem=came_head.at[k], device_id={"head": lax.rem(place + k, last + 1)},
                device_id_type=MESH,
            )

    @pl.when(step == 0)
    def _():
        gain_grad[...] = jnp.zeros_like(gain_grad)
        if near:
            for k in range(1, last + 1):
                across(k).start()
            got_head[place] = head_ref[...]

    def one():
        ready(0)
        part[...] = mm_nt(dpre_ref[...], w_in[:, :wide])

    def two():
        ready(1)
        return (
            part[...]
            + mm_nt(dgz_ref[...], w_mix[:, :vals])
            + mm_nt(dab_ref[...], w_in[:, wide:])
        )

    def finish(grad):
        stream = tokens_ref[...].astype(full)
        scale = lax.rsqrt(jnp.mean(stream * stream, axis=-1, keepdims=True) + 1e-06)
        norm = stream * scale
        gain_grad[...] += jnp.sum((grad * norm).reshape(ROWS // 8, 8, -1), axis=0)
        weighted = grad * gain_ref[0:1, :]
        term_ref[...] = (
            scale * (weighted - norm * jnp.mean(weighted * norm, axis=-1, keepdims=True))
        ).astype(low)

    line_sum(step, last, [one, two], finish, scratch)

    @pl.when(step == pl.num_programs(0) - 1)
    def _():
        row = lax.broadcasted_iota(jnp.int32, gain_grad.shape, 0)
        first = jnp.sum(gain_grad[...], axis=0, keepdims=True)
        own = lines_ref[...] + jnp.where(row == 0, first, 0.0)
        if not near:
            gains_ref[...] = own
            return
        for k in range(1, last + 1):
            across(k).wait()
        heads_sum = sum((got_head[k] for k in range(1, last + 1)), start=got_head[0])
        gain_grad[...] = own
        gain_grad[7:8, : head_ref.shape[1]] = jnp.sum(heads_sum, axis=0, keepdims=True)
        me = lax.axis_index("seq")

        def push(mask):
            return pltpu.make_async_remote_copy(
                src_ref=gain_grad, dst_ref=got.at[me], send_sem=sent.at[mask], recv_sem=came.at[mask],
                device_id={"seq": partner(mask)}, device_id_type=MESH,
            )

        for mask in range(1, NEAR):
            push(mask).start()
        got[me] = gain_grad[...]
        for mask in range(1, NEAR):
            push(mask).wait()
        gains_ref[...] = sum((got[k] for k in range(1, NEAR)), start=got[0])


def input_kernel(wide, gathering, gain_ref, *refs):
    rows = 256
    if gathering:
        heavy, (before_hbm, tokens_hbm), refs = refs[:9], refs[9:11], refs[11:]
        small_ref, sources = heavy[3], heavy[4:]
    else:
        (shard_ref, before_hbm, tokens_hbm), refs = refs[:3], refs[3:]
    first_ref, pre_ref, ab_ref, edge_ref, whole_ref = refs[:5]
    refs = refs[5:]
    if gathering:
        (mix_ref, ffn_ref), refs = refs[:2], refs[2:]
    weights, total, tokens_ref, before, home, *refs = refs
    length, width = tokens_ref.shape
    half = width // 4
    back = pltpu.make_async_copy(weights, whole_ref, home.at[0])
    here = pltpu.make_async_copy(tokens_hbm, tokens_ref, home.at[1])
    here.start()
    if gathering:
        shard, *buffers = refs[:6]
        sems = refs[6:]
        pairs = [(before_hbm, before), *zip(sources, buffers)]
        copies = [pltpu.make_async_copy(a, b, home.at[2 + n]) for n, (a, b) in enumerate(pairs)]
        for copy in copies:
            copy.start()
        first = 0
        for ref in heavy[:3]:
            shard[:, first : first + ref.shape[1]] = ref[...].astype(low)
            first += ref.shape[1]
        shard[:, first:] = small_ref[...].astype(low)
        greet(Gather.masks)
        moving = Gather(shard, weights, *sems)
        moving.start()
    else:
        copies = [
            pltpu.make_async_copy(shard_ref, weights, home.at[2]),
            pltpu.make_async_copy(before_hbm, before, home.at[3]),
        ]
        for copy in copies:
            copy.start()

    def normed(block):
        x = block.astype(full)
        return (x * lax.rsqrt(jnp.mean(x * x, axis=-1, keepdims=True) + 1e-06) * gain_ref[0:1, :]).astype(low)

    def norm(n, carry):
        span = pl.ds(pl.multiple_of(n * rows, rows), rows)
        first_ref[span, :] = normed(tokens_ref[span, :])
        return carry

    here.wait()
    lax.fori_loop(0, length // rows, norm, 0)

    def add(chip, fresh, done):
        start = pl.multiple_of(chip * half, half)

        def one(n, carry):
            span = pl.ds(pl.multiple_of(n * rows, rows), rows)
            part = mm(first_ref[span, pl.ds(start, half)], weights[pl.ds(start, half), :])
            if not fresh:
                part += total[span, :]
            if done:
                pre_ref[span, :] = part[:, :wide].astype(low)
                ab_ref[span, :] = part[:, wide:]
            else:
                total[span, :] = part
            return carry

        lax.fori_loop(0, length // rows, one, 0)

    if gathering:
        moving.local().wait()
        moving.traded((4,))
        add(partner(0) // 2, True, False)
        for copy in copies:
            copy.wait()
        gate, out, up, lift, down = buffers
        vals, size = gate.shape[1], up.shape[1]
        mix_ref[:, :vals] = gate[...].astype(low)
        for first in range(0, vals, 128):
            mix_ref[:, vals + first : vals + first + 128] = out[first : first + 128, :].T.astype(low)
        ffn_ref[:, :size] = up[...].astype(low)
        ffn_ref[:, size : 2 * size] = lift[...].astype(low)
        for first in range(0, size, 128):
            cols = slice(2 * size + first, 2 * size + first + 128)
            ffn_ref[:, cols] = down[first : first + 128, :].T.astype(low)
        moving.middle()
        moving.traded((5, 6))
        add(partner(2) // 2, False, False)
        moving.late()
        add(partner(4) // 2, False, False)
        moving.traded((7,))
        back.start()
        add(partner(6) // 2, False, True)
    else:
        for copy in copies:
            copy.wait()
        back.start()
        for chip in range(4):
            add(chip, chip == 0, chip == 3)
    edge_ref[...] = mm(normed(before[...]), weights[:, :wide]).astype(low)
    if gathering:
        moving.settle()
    back.wait()


def input_projection(tokens, before, gain, heavy, wide):
    length, width = tokens.shape
    gathering = len(heavy) > 1
    here = pl.BlockSpec(memory_space=pltpu.VMEM)
    away = pl.BlockSpec(**ANY)
    if gathering:
        operands = [*heavy, before, tokens]
        in_specs = [here] * 4 + [away] * 7
        rows = heavy[0].shape[0]
        columns = sum(a.shape[1] for a in heavy[:4])
        shards_out = [
            jax.ShapeDtypeStruct((rows, 2 * heavy[4].shape[1]), low),
            jax.ShapeDtypeStruct((rows, 3 * heavy[6].shape[1]), low),
        ]
        more = [pltpu.VMEM((rows, columns), low)] + [pltpu.VMEM(a.shape, full) for a in heavy[4:]]
        more += Gather.semaphores
        params = dict(collective_id=4, has_side_effects=True)
    else:
        operands = [*heavy, before, tokens]
        in_specs = [away] * 3
        columns = heavy[0].shape[1]
        shards_out, more, params = [], [], {}
    return pl.pallas_call(
        partial(input_kernel, wide, gathering),
        in_specs=[here] + in_specs,
        out_specs=[here] * 4 + [away] + [here] * len(shards_out),
        out_shape=[
            jax.ShapeDtypeStruct((length, width), low),
            jax.ShapeDtypeStruct((length, wide), low),
            jax.ShapeDtypeStruct((length, columns - wide), full),
            jax.ShapeDtypeStruct((16, wide), low),
            jax.ShapeDtypeStruct((width, columns), low),
        ]
        + shards_out,
        scratch_shapes=[
            pltpu.VMEM((width, columns), low),
            pltpu.VMEM((length, columns), full),
            pltpu.VMEM((length, width), low),
            pltpu.VMEM((16, width), low),
            pltpu.SemaphoreType.DMA((8,)),
        ]
        + more,
        compiler_params=pltpu.CompilerParams(vmem_limit_bytes=60 * MIB, **params),
        cost_estimate=FREE,
        name="input_projection",
    )(gain[None, :], *operands)


def weight_kernel(groups, adding, counts, place_ref, *refs):
    lefts, rights = refs[: counts[0]], refs[counts[0] : counts[0] + counts[1]]
    rest = refs[counts[0] + counts[1] :]
    parts = []
    n = 0
    for g, many in enumerate(groups):
        left = lefts[g][...]
        for _ in range(many):
            parts.append(mm_tn(left, rights[n][...]))
            n += 1
    first = 0
    for part in parts:
        cols = slice(first, first + part.shape[1])
        first += part.shape[1]
        if adding:
            part += rest[0][0, :, cols].astype(full)
        rest[-1][0, :, cols] = part.astype(low)


def weight_call(place, pairs, odd, count, stride, added=None, width=256):
    lefts = [a for a, _ in pairs]
    rights = [b for _, bs in pairs for b in bs]
    length = lefts[0].shape[0]
    columns = sum(b.shape[1] for b in rights)

    def pick(k, place_ref):
        return (0, jnp.bitwise_xor(place_ref[0], stride * k + odd))

    in_specs = [pl.BlockSpec((length, width), pick) for _ in lefts]
    in_specs += [pl.BlockSpec(b.shape, lambda k, p: (0, 0), **ONE) for b in rights]
    if added is not None:
        in_specs += [pl.BlockSpec((1, width, columns), lambda k, p: (k, 0, 0))]
    out_specs = [pl.BlockSpec((1, width, columns), lambda k, p: (k, 0, 0))]
    out_shape = [jax.ShapeDtypeStruct((count, width, columns), low)]
    return pl.pallas_call(
        partial(
            weight_kernel, [len(bs) for _, bs in pairs], added is not None, (len(lefts), len(rights))
        ),
        grid_spec=pltpu.PrefetchScalarGridSpec(
            num_scalar_prefetch=1, grid=(count,), in_specs=in_specs, out_specs=out_specs
        ),
        out_shape=out_shape,
        compiler_params=pltpu.CompilerParams(vmem_limit_bytes=56 * MIB),
        cost_estimate=FREE,
        name="weight_grads",
    )(place, *lefts, *rights, *(() if added is None else (added,)))


def pair_sums(place, pairs):
    (away,) = weight_call(place, pairs, 1, NEAR // 2, 2)
    (sums,) = weight_call(place, pairs, 0, NEAR // 2, 2, exchanged(away, 1))
    return sums


def plain_sums(place, pairs):
    width = pairs[0][0].shape[1]
    (grads,) = weight_call(jnp.zeros_like(place), pairs, 0, width // 256, 1)
    return lax.psum_scatter(grads.reshape(width, -1), "seq", scatter_dimension=0, tiled=True).astype(full)


def final_kernel(heads, keys, vals, size, middle_ref, sum_ref, dmiddle_ref, term_ref, in_own, in_got,
                 up_own, up_got, up_late, down_own, down_got, gate_own, gate_got, out_own, out_got, gains_ref,
                 tq_ref, tk_ref, tv_ref, result_ref, dtokens_ref, q_ref, k_ref, v_ref, a_ref, b_ref, up_ref, lift_ref, down_ref,
                 gate_ref, out_ref):
    def total(own, got, cols=slice(None)):
        return own[0, :, cols].astype(full) + sum(got[k, :, cols].astype(full) for k in range(3))

    @pl.when(pl.program_id(0) < 8)
    def _():
        result_ref[...] = (middle_ref[...] + sum_ref[...].astype(full)).astype(low)
        dtokens_ref[...] = dmiddle_ref[...] + term_ref[...].astype(full)
        wide = 2 * keys + vals
        q_ref[...] = total(in_own, in_got, slice(0, keys))
        k_ref[...] = total(in_own, in_got, slice(keys, 2 * keys))
        v_ref[...] = total(in_own, in_got, slice(2 * keys, wide))
        small = total(in_own, in_got, slice(wide, wide + LANES))
        a_ref[...] = small[:, :heads]
        b_ref[...] = small[:, heads : 2 * heads]
        split = up_got.shape[2]
        up_ref[...] = total(up_own, up_got, slice(0, size))
        lift_ref[:, : split - size] = total(up_own, up_got, slice(size, split))
        late = sum(up_late[k].astype(full) for k in range(3))
        lift_ref[:, split - size :] = up_own[0, :, split:].astype(full) + late
        gate_ref[...] = total(gate_own, gate_got)
        out_ref[...] = total(out_own, out_got).T

    @pl.when(pl.program_id(0) == 0)
    def _():
        tq_ref[...] = gains_ref[2:6, :keys]
        tk_ref[...] = gains_ref[2:6, keys : 2 * keys]
        tv_ref[...] = gains_ref[2:6, 2 * keys :]

    down_ref[...] = total(down_own, down_got).T


def final_sums(middle, narrow_sum, dmiddle, term, sums_in, got_in, sums_up, got_up, got_late, sums_rest, got_rest, gains, heads,
               keys, vals, size):
    length, width = dmiddle.shape
    rows = sums_in.shape[1]
    eight = lambda n: jnp.minimum(n, 7)
    many, few = length // 8, rows // 8

    def both(array, block, index):
        return [pl.BlockSpec((1,) + block, index), pl.BlockSpec((3,) + block, index)]

    wide_in = sums_in.shape[2]
    at_gate, at_out = size // LANES, (size + vals) // LANES
    tall = pl.BlockSpec((many, width), lambda n: (eight(n), 0))
    in_specs = [tall] * 4
    in_specs += both(sums_in, (few, wide_in), lambda n: (0, eight(n), 0))
    in_specs += [
        pl.BlockSpec((count, few, a.shape[2]), lambda n: (0, eight(n), 0))
        for count, a in ((1, sums_up), (3, got_up), (3, got_late))
    ]
    in_specs += both(sums_rest, (rows, LANES), lambda n: (0, 0, n))
    in_specs += both(sums_rest, (rows, LANES), lambda n: (0, 0, at_gate + eight(n)))
    in_specs += both(sums_rest, (rows, LANES), lambda n: (0, 0, at_out + eight(n)))
    once = lambda *shape: pl.BlockSpec(shape, lambda n: (0, 0))
    in_specs += [once(*gains.shape)]
    byrow = lambda columns: pl.BlockSpec((few, columns), lambda n: (eight(n), 0))
    outs = [
        ((4, keys), full), ((4, keys), full), ((4, vals), full), ((length, width), low), ((length, width), full), ((rows, keys), full), ((rows, keys), full),
        ((rows, vals), full), ((rows, heads), full), ((rows, heads), full), ((rows, size), full),
        ((rows, size), full), ((size, rows), full), ((rows, vals), full), ((vals, rows), full),
    ]
    return pl.pallas_call(
        partial(final_kernel, heads, keys, vals, size),
        grid=(size // LANES,),
        in_specs=in_specs,
        out_specs=[
            once(4, keys), once(4, keys), once(4, vals), tall, tall,
            byrow(keys), byrow(keys), byrow(vals), byrow(heads), byrow(heads), byrow(size), byrow(size),
            pl.BlockSpec((LANES, rows), lambda n: (n, 0)),
            pl.BlockSpec((rows, LANES), lambda n: (0, eight(n))),
            pl.BlockSpec((LANES, rows), lambda n: (eight(n), 0)),
        ],
        out_shape=[jax.ShapeDtypeStruct(shape, dtype) for shape, dtype in outs],
        compiler_params=pltpu.CompilerParams(vmem_limit_bytes=48 * MIB),
        cost_estimate=FREE,
        name="final_sums",
    )(middle, narrow_sum, dmiddle, term, sums_in, got_in, sums_up, got_up, got_late, sums_rest, got_rest, sums_rest,
      got_rest, sums_rest, got_rest, gains)


def small_sums(part):
    return lax.psum(part, "seq")


def passed_along(block, axis, distance):
    devices = range(lax.axis_size(axis))
    route = [(i - distance, i) for i in devices if i - distance in devices]
    return lax.ppermute(block, axis, route)


def shards(
    tokens,
    doc_lengths,
    mixer_gain,
    query_weight,
    key_weight,
    value_weight,
    gate_weight,
    alpha_weight,
    beta_weight,
    decay_log,
    decay_bias,
    query_taps,
    key_taps,
    value_taps,
    head_gain,
    output_weight,
    ffn_gain,
    ffn_gate,
    ffn_up,
    ffn_down,
    cotangent,
):
    length, width = tokens.shape
    heads = decay_log.shape[0]
    key = query_weight.shape[1] // heads
    value = head_gain.shape[0]
    keys, vals = heads * key, heads * value
    wide = 2 * keys + vals
    size = ffn_gate.shape[1]
    last = lax.axis_size("head") - 1
    near = lax.axis_size("seq") == NEAR
    shard = lax.axis_index("seq")
    place = jnp.full((1,), shard, jnp.int32)

    small = jnp.concatenate(
        [alpha_weight, beta_weight, jnp.zeros((alpha_weight.shape[0], LANES - 2 * heads), full)], axis=1
    )
    taps = jnp.concatenate([query_taps, key_taps, value_taps], axis=1)
    params = jnp.stack([-jnp.exp(decay_log), decay_bias])
    params = jnp.pad(params, ((0, 6), (0, LANES - heads)))
    gain = head_gain[None, :]

    if near:
        heavy = [query_weight, key_weight, value_weight, small, gate_weight, output_weight]
        heavy += [ffn_gate, ffn_up, ffn_down]
    else:
        shard_in = jnp.concatenate([query_weight, key_weight, value_weight, small], axis=1)
        heavy = [lax.all_gather(shard_in.astype(low), "seq", axis=0, tiled=True)]
    meta, edge_meta, segrow = segment_tables(doc_lengths, shard, length)
    first_in, pre, ab, edge, w_in, *laid = input_projection(
        tokens, passed_along(tokens[length - 16 :], "seq", 1), mixer_gain, heavy, wide
    )
    if near:
        shard_mix, shard_ffn = laid
    else:
        shard_mix = jnp.concatenate([gate_weight, output_weight.T], axis=1).astype(low)
        shard_ffn = jnp.concatenate([ffn_gate, ffn_up, ffn_down.T], axis=1).astype(low)
    edge = edge[8:]
    local, through, states, inverse, end, *moved = forward_chain(
        pre, ab, meta, segrow, edge, taps, params, heads, key, value, shard_mix if near else None
    )
    end = end.reshape(keys, value + key)
    if near:
        w_mix = moved[0]
        held, moving = [(w_mix, [(0, vals), (vals, vals)])], dict(early=end, gathers=[shard_ffn])
    else:
        w_mix = lax.all_gather(shard_mix, "seq", axis=0, tiled=True)
        ends = lax.all_gather(end, "seq", axis=0, tiled=True)
        held, moving = [(w_mix, [(0, vals), (vals, vals)]), (ends, [(0, ends.shape[1])])], {}
    mix_out, mixed, gate_pre, state_in, middle, second_in, *moved = line_call(
        partial(mixer_out_kernel, heads, key, value, last, None if near else 2), "mixer_out", 0, length, width, last,
        [gain, ffn_gain[None, :]], held, [first_in, local, through], [tokens],
        [((length, vals), low, "first"), ((length, vals), full, "first"),
         ((length, vals), full, "first"), ((heads, key, value), full, "all"),
         ((length, width), full, "second"), ((length, width), low, "second")],
        [], **moving,
    )
    if near:
        ends, w_ffn = moved
    else:
        w_ffn = lax.all_gather(shard_ffn, "seq", axis=0, tiled=True)
    hidden, gate_grad, lift_grad, narrow_part, middle_grad, middle_low, ffn_gain_part = line_call(
        partial(ffn_kernel, last, size), "ffn", 1, length, width, last,
        [ffn_gain[None, :]], [(w_ffn, [(n * size, size) for n in range(3)])], [second_in, cotangent], [middle, cotangent],
        [((length, size), low, "first")] * 3
        + [((length, width), low, "first"), ((length, width), full, "second"),
           ((length, width), low, "second"), ((8, width), full, "all")],
        [pltpu.VMEM((ROWS, size), full)] * 2,
    )
    narrow_sum = lax.psum_scatter(narrow_part, "head", scatter_dimension=0, tiled=True)
    gate_pgrad, mixed_grad, head_gain_part, adjoint = gate_back(
        middle_low, w_mix, mixed, gate_pre, gain, through, heads, key, value
    )
    if not near:
        head_gain_part = lax.psum(head_gain_part, "head")
    adjoint = adjoint.astype(low).reshape(keys, value)
    if not near:
        adjoint = lax.all_gather(adjoint, "seq", axis=0, tiled=True)
    split = 17 * LANES
    pairs_up = [(second_in, [gate_grad, lift_grad])]
    pairs_rest = [(cotangent, [hidden]), (first_in, [gate_pgrad]), (middle_low, [mix_out])]
    sums_up = pair_sums(place, pairs_up) if near else None
    sums_rest = pair_sums(place, pairs_rest) if near else None
    pre_grad, ab_grad, halo, taps_part, params_part, *moved = backward_chain(
        pre, ab, meta, segrow, edge, edge_meta, taps, params, states, inverse, state_in,
        mixed_grad, ends, adjoint, heads, key, value, sums_up, split,
    )
    got_up = moved
    if near:
        narrow_sum, halo = lax.optimization_barrier((narrow_sum, halo))
    narrow_sum = lax.all_gather(narrow_sum, "head", axis=0, tiled=True)
    halo = passed_along(halo, "seq", -1)
    tail = pre_grad[length - 8 :].astype(full) + halo
    pre_grad = lax.dynamic_update_slice(pre_grad, tail.astype(low), (length - 8, 0))
    pairs_in = [(first_in, [pre_grad, ab_grad])]
    sums_in = pair_sums(place, pairs_in) if near else None
    params_part = jnp.sum(params_part.reshape(2, 8, LANES), axis=1).reshape(1, -1)
    lines = jnp.concatenate(
        [
            jnp.zeros((1, width), full),
            jnp.sum(ffn_gain_part, axis=0, keepdims=True),
            jnp.sum(taps_part.reshape(4, 8, -1), axis=1),
            jnp.pad(params_part, ((0, 0), (0, width - params_part.shape[1]))),
            jnp.zeros((1, width), full)
            if near
            else jnp.pad(jnp.sum(head_gain_part, axis=0)[None], ((0, 0), (0, width - value))),
        ],
        axis=0,
    )
    term, gains, *moved = line_call(
        partial(input_grad_kernel, last, keys, vals, near), "input_grad", 2, length, width, last,
        [mixer_gain[None, :], lines, head_gain_part], [(w_in, [(0, w_in.shape[1])]), (w_mix, [(0, vals)])],
        [pre_grad, gate_pgrad, ab_grad], [tokens],
        [((length, width), low, "second"), ((8, width), full, "all")],
        [pltpu.VMEM((ROWS, width), full), pltpu.VMEM((8, width), full)]
        + ([pltpu.VMEM((NEAR, 8, width), full), *[pltpu.SemaphoreType.DMA((NEAR,))] * 2] if near else [])
        + ([pltpu.VMEM((last + 1, 8, value), full), *[pltpu.SemaphoreType.DMA((last + 1,))] * 2] if near else []),
        scatters=[(sums_rest, 0), (sums_in, 0), (sums_up, split)] if near else [], masks=range(1, NEAR) if near else (),
    )
    sums = gains if near else small_sums(gains)
    if near:
        (tq_grad, tk_grad, tv_grad, result, tokens_grad, query_grad, key_grad, value_grad, alpha_grad, beta_grad, up_grad, lift_grad,
         down_grad, gate_grad, out_grad) = final_sums(
            middle, narrow_sum, middle_grad, term, sums_in, moved[1], sums_up, got_up[0], moved[2], sums_rest, moved[0],
            gains, heads, keys, vals, size,
        )
    else:
        up, rest, into = (plain_sums(place, pairs) for pairs in (pairs_up, pairs_rest, pairs_in))
        tokens_grad = middle_grad + term.astype(full)
        query_grad, key_grad, value_grad = into[:, :keys], into[:, keys : 2 * keys], into[:, 2 * keys : wide]
        alpha_grad, beta_grad = into[:, wide : wide + heads], into[:, wide + heads : wide + 2 * heads]
        up_grad, lift_grad = up[:, :size], up[:, size:]
        down_grad, gate_grad, out_grad = (
            rest[:, :size].T, rest[:, size : size + vals], rest[:, size + vals :].T
        )
        result = (middle + narrow_sum.astype(full)).astype(low)
        taps_grad = sums[2:6]
        tq_grad, tk_grad, tv_grad = (
            taps_grad[:, :keys], taps_grad[:, keys : 2 * keys], taps_grad[:, 2 * keys :]
        )
    return (
        result,
        tokens_grad,
        sums[0],
        query_grad,
        key_grad,
        value_grad,
        gate_grad,
        alpha_grad,
        beta_grad,
        sums[6, LANES : LANES + heads],
        sums[6, :heads],
        tq_grad,
        tk_grad,
        tv_grad,
        sums[7, :value],
        out_grad,
        sums[1],
        up_grad,
        lift_grad,
        down_grad,
    )


def solution(mesh):
    rows, both = P("seq", None), P("seq", "head")
    in_specs = (
        rows, P(), P(), both, both, both, both, both, both, P("head"), P("head"),
        P(None, "head"), P(None, "head"), P(None, "head"), P(), P("head", "seq"), P(),
        both, both, P("head", "seq"), rows,
    )
    out_specs = (
        rows, rows, P(), both, both, both, both, both, both, P("head"), P("head"),
        P(None, "head"), P(None, "head"), P(None, "head"), P(), P("head", "seq"), P(),
        both, both, P("head", "seq"),
    )
    return jax.shard_map(shards, mesh=mesh, in_specs=in_specs, out_specs=out_specs, check_vma=False)
```

```python
from functools import partial

import jax
import jax.numpy as jnp
from jax import lax
from jax.experimental import pallas as pl
from jax.experimental.pallas import tpu as pltpu
from jax.sharding import PartitionSpec as P

BLOCK = 128
LANES = 128
low = jnp.bfloat16
full = jnp.float32
MIB = 1 << 20


NEAR = 8
ONE = dict(pipeline_mode=pl.Buffered(1))
ANY = dict(memory_space=pl.ANY)
FREE = pl.CostEstimate(flops=1, bytes_accessed=1, transcendentals=0)
MESH = pl.DeviceIdType.MESH


def partner(mask):
    index = lax.axis_index("seq")
    bits = (lax.rem(index, 2), lax.rem(index // 2, 2), index // 4)
    return sum((1 << i) * ((1 - b) if mask >> i & 1 else b) for i, b in enumerate(bits))


def greet(masks, last=None, all_heads=False):
    barrier = pltpu.get_barrier_semaphore()
    for mask in masks:
        pl.semaphore_signal(barrier, inc=1, device_id={"seq": partner(mask)}, device_id_type=MESH)
    count = len(masks)
    if all_heads:
        place = lax.axis_index("head")
        for k in range(1, last + 1):
            to = lax.rem(place + k, last + 1)
            pl.semaphore_signal(barrier, inc=1, device_id={"head": to}, device_id_type=MESH)
        count += last
    elif last is not None:
        place = lax.axis_index("head")
        for there, to in ((place > 0, place - 1), (place < last, place + 1)):

            @pl.when(there)
            def _(to=to):
                pl.semaphore_signal(barrier, inc=1, device_id={"head": to}, device_id_type=MESH)

        count += jnp.minimum(place, 1) + jnp.minimum(last - place, 1)
    pl.semaphore_wait(barrier, count)


class Gather:
    masks = (1, 2, 4)
    semaphores = [pltpu.SemaphoreType.DMA((8,)), pltpu.SemaphoreType.DMA((8,)), pltpu.SemaphoreType.DMA((1,))]

    def __init__(self, shard, whole, sent, got, home):
        self.shard, self.whole, self.sent, self.got, self.home = shard, whole, sent, got, home
        self.size = shard.shape[0]

    def rows(self, mask, first=0, count=None):
        start = pl.multiple_of(partner(mask) * self.size + first, self.size // 2)
        return self.whole.at[pl.ds(start, self.size if count is None else count), :]

    def push(self, slot):
        half = self.size // 2
        mask, src, dst = (
            (2, self.shard, self.rows(0)),
            (4, self.shard, self.rows(0)),
            (2, self.rows(4, 0, half), self.rows(4, 0, half)),
            (4, self.rows(2, half, half), self.rows(2, half, half)),
            (1, self.shard, self.rows(0)),
            (1, self.rows(2), self.rows(2)),
            (1, self.rows(4), self.rows(4)),
            (1, self.rows(6), self.rows(6)),
        )[slot]
        return pltpu.make_async_remote_copy(
            src_ref=src, dst_ref=dst, send_sem=self.sent.at[slot], recv_sem=self.got.at[slot],
            device_id={"seq": partner(mask)}, device_id_type=MESH,
        )

    def local(self):
        return pltpu.make_async_copy(self.shard, self.rows(0), self.home.at[0])

    def start(self):
        self.local().start()
        for slot in (0, 1, 4):
            self.push(slot).start()

    def middle(self):
        for slot in (0, 1):
            self.push(slot).wait_recv()
        for slot in (2, 3, 5, 6):
            self.push(slot).start()

    def late(self):
        for slot in (2, 3):
            self.push(slot).wait_recv()
        self.push(7).start()

    def traded(self, slots):
        for slot in slots:
            self.push(slot).wait_recv()

    def settle(self):
        for slot in range(8):
            self.push(slot).wait_send()

    def end(self):
        self.traded((4, 5, 6, 7))
        self.settle()
        self.local().wait()


class Scatter:
    masks = (2, 4, 6)
    semaphores = [pltpu.SemaphoreType.DMA((3,)), pltpu.SemaphoreType.DMA((3,))]

    def __init__(self, parts, got, sent, came, first=0):
        self.parts, self.got, self.sent, self.came = parts, got, sent, came
        self.columns = pl.ds(first, got.shape[2])

    def push(self, k):
        return pltpu.make_async_remote_copy(
            src_ref=self.parts.at[k + 1, :, self.columns], dst_ref=self.got.at[k], send_sem=self.sent.at[k],
            recv_sem=self.came.at[k], device_id={"seq": partner(2 * k + 2)}, device_id_type=MESH,
        )

    def start(self):
        for k in range(3):
            self.push(k).start()

    def end(self):
        for k in range(3):
            self.push(k).wait()


def load(step, pairs, sems):
    @pl.when(step == 0)
    def _():
        copies = [pltpu.make_async_copy(a, b, sems.at[n]) for n, (a, b) in enumerate(pairs)]
        for copy in copies:
            copy.start()
        for copy in copies:
            copy.wait()


def mm(a, b):
    return jnp.dot(a.astype(low), b.astype(low), preferred_element_type=full)


def mm_nt(a, b):
    return lax.dot_general(
        a.astype(low), b.astype(low), (((1,), (1,)), ((), ())), preferred_element_type=full
    )


def mm_tn(a, b):
    return lax.dot_general(
        a.astype(low), b.astype(low), (((0,), (0,)), ((), ())), preferred_element_type=full
    )


def exact(a, b):
    return jnp.dot(a, b, precision=lax.Precision.HIGHEST, preferred_element_type=full)


def sigmoid(t):
    return 1.0 / (1.0 + jnp.exp(-t))


def softplus(t):
    return jnp.maximum(t, 0.0) + jnp.log(1.0 + jnp.exp(-jnp.abs(t)))


def iotas(size):
    return (
        lax.broadcasted_iota(jnp.int32, (size, size), 0),
        lax.broadcasted_iota(jnp.int32, (size, size), 1),
    )


def conv_sum(ext, taps, meta, first, width, rows):
    total = taps[3:4, first : first + width] * ext[8 : 8 + rows, first : first + width]
    for lag in (1, 2, 3):
        total += (
            taps[3 - lag : 4 - lag, first : first + width]
            * meta[:, lag : lag + 1]
            * ext[8 - lag : 8 - lag + rows, first : first + width]
        )
    return total


def gates(ab, params, heads):
    log_decay = params[0:1, :] * softplus(ab + params[1:2, :])
    beta = sigmoid(ab)
    return log_decay, beta


def decay_parts(cum, cum_t, h, same_low, strict_low, meta):
    size = cum.shape[0]
    col = cum[:, h : h + 1]
    row = cum_t[h : h + 1, :]
    lower = jnp.where(same_low, jnp.exp(jnp.minimum(col - row, 0.0)), 0.0)
    strict = jnp.where(strict_low, lower, 0.0)
    last = cum[size - 1 : size, h : h + 1]
    from_start = jnp.exp(col) * meta[:, 4:5]
    to_end = jnp.exp(last - col) * meta[:, 5:6]
    carried = jnp.exp(last) * meta[size - 1 : size, 4:5]
    return lower, strict, from_start, to_end, carried


def unit_lower_inverse(strict, rows, cols):
    size = strict.shape[0]
    power = jnp.where((rows >> 3) == (cols >> 3), -strict, 0.0)
    inverse = jnp.where(rows == cols, 1.0, power)
    power = mm(power, power)
    inverse = inverse + mm(inverse, power)
    power = mm(power, power)
    inverse = inverse + mm(inverse, power)
    shift = 3
    while (1 << shift) < size:
        off = jnp.where(
            ((rows >> (shift + 1)) == (cols >> (shift + 1))) & ((rows >> shift) != (cols >> shift)),
            strict,
            0.0,
        )
        inverse = inverse - mm(inverse, mm(off, inverse))
        shift += 1
    return inverse


def inverses(stricts, rows, cols):
    size = stricts[0].shape[0]
    near = (rows >> 3) == (cols >> 3)
    powers = [jnp.where(near, -a, 0.0) for a in stricts]
    result = [jnp.where(rows == cols, 1.0, p) for p in powers]
    for _ in range(2):
        powers = [mm(p, p) for p in powers]
        result = [t + mm(t, p) for t, p in zip(result, powers)]
    shift = 3
    while (1 << shift) < size:
        pick = ((rows >> (shift + 1)) == (cols >> (shift + 1))) & (
            (rows >> shift) != (cols >> shift)
        )
        offs = [mm(jnp.where(pick, a, 0.0), t) for a, t in zip(stricts, result)]
        result = [t - mm(t, o) for t, o in zip(result, offs)]
        shift += 1
    return result


def masks(meta, segrow):
    size = meta.shape[0]
    rows, cols = iotas(size)
    same = meta[:, 0:1] == segrow[0:1, :]
    return rows, cols, same & (rows >= cols), same & (rows > cols)


def unit(post):
    return lax.rsqrt(jnp.sum(post * post, axis=-1, keepdims=True) + 1e-06)


def forward_kernel(
    heads, key, value, gathering,
    pre_ref, ab_ref, meta_ref, segrow_ref, edge_ref, taps_ref, params_ref, *refs
):
    step = pl.program_id(0)
    steps = pl.num_programs(0)
    if gathering:
        shard_ref, out_ref, through_ref, states_ref, inverse_ref, end_ref, whole_ref, ext, state, *sems = refs
        moving = Gather(shard_ref, whole_ref, *sems)

        @pl.when(step == 0)
        def _():
            greet(Gather.masks)
            moving.start()

        @pl.when(step == steps - 2)
        def _():
            moving.middle()

    else:
        out_ref, through_ref, states_ref, inverse_ref, end_ref, ext, state = refs
    size = pre_ref.shape[0]
    wide = value + key
    kfirst, vfirst = heads * key, 2 * heads * key

    @pl.when(step == 0)
    def _():
        ext[0:8, :] = edge_ref[...].astype(full)
        rows, cols = iotas(key)
        eye = (rows == cols).astype(full)
        for h in range(heads):
            state[h, :, :value] = jnp.zeros((key, value), full)
            state[h, :, value:] = eye

    @pl.when(step > 0)
    def _():
        ext[0:8, :] = ext[size : size + 8, :]

    ext[8:, :] = pre_ref[...].astype(full)
    meta = meta_ref[...]
    log_decay, beta = gates(ab_ref[...], params_ref, heads)
    rows, cols, same_low, strict_low = masks(meta, segrow_ref)
    cum = exact((rows >= cols).astype(full), log_decay)
    cum_t = cum.T
    qs, ks, vs, lowers, stricts, fs, es, cs = [], [], [], [], [], [], [], []
    for h in range(heads):
        u = conv_sum(ext, taps_ref, meta, h * key, key, size)
        post = u * sigmoid(u)
        q = (post * unit(post)).astype(low)
        u = conv_sum(ext, taps_ref, meta, kfirst + h * key, key, size)
        post = u * sigmoid(u)
        k = (post * unit(post)).astype(low)
        u = conv_sum(ext, taps_ref, meta, vfirst + h * value, value, size)
        v = u * sigmoid(u)
        lower, strict, f, e, c = decay_parts(cum, cum_t, h, same_low, strict_low, meta)
        bcol = beta[:, heads + h : heads + h + 1]
        gram = mm_nt(jnp.concatenate([k, q], axis=0), k)
        qs.append(q), ks.append(k), vs.append(v), fs.append(f), es.append(e), cs.append(c)
        stricts.append(bcol * strict * gram[:size])
        lowers.append(lower * gram[size:])
    ts = inverses(stricts, rows, cols)
    for h in range(heads):
        bcol = beta[:, heads + h : heads + h + 1]
        s = state[h]
        states_ref[0, h] = s.astype(low)
        t = ts[h].astype(low)
        inverse_ref[0, h] = t
        ks_s = mm(ks[h], s)
        fb = fs[h] * bcol
        target = jnp.concatenate(
            [bcol * vs[h] - fb * ks_s[:, :value], -fb * ks_s[:, value:]], axis=1
        )
        delta = mm(t, target).astype(low)
        left = jnp.concatenate([(fs[h] * qs[h].astype(full)).astype(low), lowers[h].astype(low)], axis=1)
        out = mm(left, jnp.concatenate([s.astype(low), delta], axis=0))
        out_ref[:, h * value : (h + 1) * value] = out[:, :value]
        through_ref[:, h * key : (h + 1) * key] = out[:, value:].astype(low)
        ke = es[h] * ks[h].astype(full)
        s = cs[h] * s + mm_tn(ke, delta)
        state[h] = s
        end_ref[h] = s.astype(low)

    if gathering:

        @pl.when(step == steps - 1)
        def _():
            moving.late()
            moving.end()


def forward_chain(pre, ab, meta, segrow, edge, taps, params, heads, key, value, shard=None):
    gathering = shard is not None
    moved = [jax.ShapeDtypeStruct((shard.shape[0] * NEAR, shard.shape[1]), low)] if gathering else []
    extra = dict(collective_id=5, has_side_effects=True) if gathering else {}
    length = pre.shape[0]
    blocks = length // BLOCK
    width = pre.shape[1]
    wide = value + key
    return pl.pallas_call(
        partial(forward_kernel, heads, key, value, gathering),
        grid=(blocks,),
        in_specs=[
            pl.BlockSpec((BLOCK, width), lambda n: (n, 0)),
            pl.BlockSpec((BLOCK, LANES), lambda n: (n, 0)),
            pl.BlockSpec((BLOCK, LANES), lambda n: (n, 0)),
            pl.BlockSpec((8, BLOCK), lambda n: (0, n)),
            pl.BlockSpec((8, width), lambda n: (0, 0)),
            pl.BlockSpec(taps.shape, lambda n: (0, 0)),
            pl.BlockSpec((8, LANES), lambda n: (0, 0)),
        ]
        + [pl.BlockSpec(**ANY) for _ in moved],
        out_specs=[
            pl.BlockSpec((BLOCK, heads * value), lambda n: (n, 0)),
            pl.BlockSpec((BLOCK, heads * key), lambda n: (n, 0)),
            pl.BlockSpec((1, heads, key, wide), lambda n: (n, 0, 0, 0)),
            pl.BlockSpec((1, heads, BLOCK, BLOCK), lambda n: (n, 0, 0, 0)),
            pl.BlockSpec((heads, key, wide), lambda n: (0, 0, 0)),
        ]
        + [pl.BlockSpec(**ANY) for _ in moved],
        out_shape=[
            jax.ShapeDtypeStruct((length, heads * value), full),
            jax.ShapeDtypeStruct((length, heads * key), low),
            jax.ShapeDtypeStruct((blocks, heads, key, wide), low),
            jax.ShapeDtypeStruct((blocks, heads, BLOCK, BLOCK), low),
            jax.ShapeDtypeStruct((heads, key, wide), low),
        ]
        + moved,
        scratch_shapes=[
            pltpu.VMEM((BLOCK + 8, width), full),
            pltpu.VMEM((heads, key, wide), full),
        ]
        + (Gather.semaphores if gathering else []),
        compiler_params=pltpu.CompilerParams(vmem_limit_bytes=48 * MIB, **extra),
        cost_estimate=FREE,
        name="chain_forward",
    )(pre, ab, meta, segrow, edge, taps, params, *([shard] if gathering else []))


def gate_back_kernel(heads, key, value, dz_ref, mixed_ref, gate_ref, gain_ref, through_ref, whole_ref,
                     dgz_ref, do_ref, gain_grad_ref, adjoint_ref, weights, dy_ref, sems):
    load(pl.program_id(0), [(whole_ref.at[:, heads * value :], weights)], sems)

    @pl.when(pl.program_id(0) == 0)
    def _():
        gain_grad_ref[...] = jnp.zeros_like(gain_grad_ref)
        adjoint_ref[...] = jnp.zeros_like(adjoint_ref)

    rows = dz_ref.shape[0]
    gain = gain_ref[0:1, :]
    dy_ref[...] = mm(dz_ref[...], weights[...])
    for h in range(heads):
        cols = slice(h * value, (h + 1) * value)
        o = mixed_ref[:, cols].astype(full)
        s3 = lax.rsqrt(jnp.mean(o * o, axis=-1, keepdims=True) + 1e-05)
        n3 = o * s3
        gz = gate_ref[:, cols]
        sig = sigmoid(gz)
        sg = gz * sig
        dy = dy_ref[:, cols]
        dyn = dy * n3
        part = dyn * sg
        gain_grad_ref[...] += jnp.sum(part.reshape(rows // 8, 8, value), axis=0)
        dgz_ref[:, cols] = (dyn * gain * (sig * (1.0 + gz * (1.0 - sig)))).astype(low)
        dn3 = dy * gain * sg
        do = s3 * (dn3 - n3 * jnp.mean(dn3 * n3, axis=-1, keepdims=True))
        do = do.astype(low)
        do_ref[:, cols] = do
        adjoint_ref[h] += mm_tn(through_ref[:, h * key : (h + 1) * key], do)


def gate_back(dz, w_mix, mixed, gate, gain, through, heads, key, value, rows=256):
    length, width = dz.shape
    wide = heads * value
    return pl.pallas_call(
        partial(gate_back_kernel, heads, key, value),
        grid=(length // rows,),
        in_specs=[
            pl.BlockSpec((rows, width), lambda n: (n, 0)),
            pl.BlockSpec((rows, wide), lambda n: (n, 0)),
            pl.BlockSpec((rows, wide), lambda n: (n, 0)),
            pl.BlockSpec((1, value), lambda n: (0, 0)),
            pl.BlockSpec((rows, heads * key), lambda n: (n, 0)),
        ]
        + [pl.BlockSpec(**ANY)],
        out_specs=[
            pl.BlockSpec((rows, wide), lambda n: (n, 0)),
            pl.BlockSpec((rows, wide), lambda n: (n, 0)),
            pl.BlockSpec((8, value), lambda n: (0, 0)),
            pl.BlockSpec((heads, key, value), lambda n: (0, 0, 0)),
        ],
        out_shape=[
            jax.ShapeDtypeStruct((length, wide), low),
            jax.ShapeDtypeStruct((length, wide), low),
            jax.ShapeDtypeStruct((8, value), full),
            jax.ShapeDtypeStruct((heads, key, value), full),
        ],
        scratch_shapes=[
            pltpu.VMEM((width, wide), low),
            pltpu.VMEM((rows, wide), full),
            pltpu.SemaphoreType.DMA((1,)),
        ],
        compiler_params=pltpu.CompilerParams(vmem_limit_bytes=48 * MIB),
        cost_estimate=FREE,
        name="gate_back",
    )(dz, mixed, gate, gain, through, w_mix)


def lane_sum(array):
    return jnp.sum(array, axis=-1, keepdims=True)


def backward_kernel(
    heads, key, value, devices, scattering,
    pre_ref, tail_ref, ab_ref, meta_ref, segrow_ref, edge_ref, edge_meta_ref, taps_ref, params_ref,
    states_ref, inverse_ref, state_in_ref, do_ref, ends_ref, *refs
):
    step = pl.program_id(0)
    steps = pl.num_programs(0)
    piece, *refs = refs
    parts_ref = refs.pop(0) if scattering else None
    dpre_ref, dab_ref, halo_ref, taps_grad_ref, params_grad_ref = refs[:5]
    refs = refs[5:]
    got_ref = refs.pop(0) if scattering else None
    ext, du, adjoint, adjoints, home, *sems = refs
    if scattering:
        moving = Scatter(parts_ref, got_ref, *sems[:2])
        lead = Gather(piece, adjoints, *sems[2:])

        @pl.when(step == 0)
        def _():
            greet(sorted({*Scatter.masks, *Gather.masks}))
            lead.start()

    size = pre_ref.shape[0]
    kfirst, vfirst = heads * key, 2 * heads * key

    @pl.when(step == 0)
    def _():
        adjoint[...] = jnp.zeros_like(adjoint)
        tall = heads * key
        if scattering:
            lead.middle()
            lead.late()
            moving.start()
            lead.end()
        else:
            copy = pltpu.make_async_copy(piece, adjoints, home.at[0])
            copy.start()
            copy.wait()

        def one(k, carry):
            j = devices - 1 - k
            for h in range(heads):
                rows = pl.ds(pl.multiple_of(j * tall + h * key, key), key)
                adjoint[h] = (
                    mm_tn(ends_ref[rows, value:], adjoint[h]) + adjoints[rows, :].astype(full)
                )
            return carry

        lax.fori_loop(0, devices - 1 - lax.axis_index("seq"), one, 0)
        du[8 + size :, :] = jnp.zeros((8, du.shape[1]), full)
        taps_grad_ref[...] = jnp.zeros_like(taps_grad_ref)
        params_grad_ref[...] = jnp.zeros_like(params_grad_ref)

    @pl.when(step > 0)
    def _():
        du[8 + size :, :] = du[8:16, :]

    du[0:8, :] = jnp.zeros((8, du.shape[1]), full)

    @pl.when(step < steps - 1)
    def _():
        ext[0:8, :] = tail_ref[8:16, :].astype(full)

    @pl.when(step == steps - 1)
    def _():
        ext[0:8, :] = edge_ref[...].astype(full)

    ext[8:, :] = pre_ref[...].astype(full)
    meta = meta_ref[...]
    ab = ab_ref[...]
    log_decay, beta = gates(ab, params_ref, heads)
    rows, cols, same_low, strict_low = masks(meta, segrow_ref)
    cum = exact((rows >= cols).astype(full), log_decay)
    cum_t = cum.T
    lane = lax.broadcasted_iota(jnp.int32, (size, LANES), 1)
    row8 = lax.broadcasted_iota(jnp.int32, (8, size), 0)
    dcum = jnp.zeros((size, LANES), full)
    dcum_rows = jnp.zeros((8, size), full)
    dcum_last = jnp.zeros((1, LANES), full)
    dbeta = jnp.zeros((size, LANES), full)
    lane1 = lax.broadcasted_iota(jnp.int32, (1, LANES), 1)

    for h in range(heads):
        qcols = slice(h * key, (h + 1) * key)
        kcols = slice(kfirst + h * key, kfirst + (h + 1) * key)
        vcols = slice(vfirst + h * value, vfirst + (h + 1) * value)
        uq = conv_sum(ext, taps_ref, meta, h * key, key, size)
        sq = sigmoid(uq)
        pq = uq * sq
        rq = unit(pq)
        qf = pq * rq
        q = qf.astype(low)
        uk = conv_sum(ext, taps_ref, meta, kfirst + h * key, key, size)
        sk = sigmoid(uk)
        pk = uk * sk
        rk = unit(pk)
        kf = pk * rk
        k = kf.astype(low)
        uv = conv_sum(ext, taps_ref, meta, vfirst + h * value, value, size)
        sv = sigmoid(uv)
        v = uv * sv
        lower, strict, f, e, c = decay_parts(cum, cum_t, h, same_low, strict_low, meta)
        b = beta[:, heads + h : heads + h + 1]
        kq = jnp.concatenate([k, q], axis=0)
        gram = mm_nt(kq, k)
        kk, qk = gram[:size], gram[size:]
        stored = states_ref[0, h]
        s = stored[:, :value].astype(full) + mm(stored[:, value:], state_in_ref[h])
        slow = s.astype(low)
        kqs = mm(kq, slow)
        ks, qs = kqs[:size], kqs[size:]
        rest = v - f * ks
        t = inverse_ref[0, h]
        delta = mm(t, b * rest).astype(low)
        do = do_ref[:, h * value : (h + 1) * value]
        dof = do.astype(full)
        ds = adjoint[h]
        dslow = ds.astype(low)
        ke = (e * kf).astype(low)
        p = lower * qk
        left = jnp.concatenate([p.T.astype(low), ke], axis=1)
        ddelta = mm(left, jnp.concatenate([do, dslow], axis=0))
        dtarget = mm_tn(t, ddelta)
        outer = mm_nt(jnp.concatenate([do, dtarget.astype(low)], axis=0), delta)
        dp, dan = outer[:size], outer[size:]
        eg = lower * dp
        hn = -strict * dan
        hg = b * hn
        x = eg * qk
        hk = hn * kk
        g1 = (b * f) * dtarget
        fdo = f * dof
        pair = jnp.concatenate([fdo.astype(low), (-g1).astype(low)], axis=0)
        both = mm_nt(pair, slow)
        dq = both[:size] + mm(eg, k)
        dsk = e * mm_nt(delta, dslow)
        left = jnp.concatenate([(hg + hg.T).astype(low), eg.T.astype(low)], axis=1)
        dk = both[size:] + dsk + mm(left, kq)
        dv = b * dtarget
        z = lane_sum(kf * dsk)
        dfrom = lane_sum(dof * qs) - b * lane_sum(dtarget * ks)
        hrow = lane_sum(hk)
        db = hrow + lane_sum(dtarget * rest)
        dbeta = dbeta + jnp.where(lane == heads + h, db, 0.0)
        dcum = dcum + jnp.where(lane == h, lane_sum(x) + b * hrow + f * dfrom - z, 0.0)
        drow = jnp.sum(x + b * hk, axis=0, keepdims=True)
        dcum_rows = dcum_rows + jnp.where(row8 == h, drow, 0.0)
        dlast = jnp.sum(z, axis=0, keepdims=True) + c * jnp.sum(
            lane_sum(ds * s), axis=0, keepdims=True
        )
        dcum_last = dcum_last + jnp.where(lane1 == h, dlast, 0.0)
        adjoint[h] = c * ds + mm_tn(jnp.concatenate([q, k], axis=0), pair)

        dpq = rq * (dq - qf * lane_sum(dq * qf))
        du[8 : 8 + size, qcols] = dpq * (sq * (1.0 + uq * (1.0 - sq)))
        dpk = rk * (dk - kf * lane_sum(dk * kf))
        du[8 : 8 + size, kcols] = dpk * (sk * (1.0 + uk * (1.0 - sk)))
        du[8 : 8 + size, vcols] = dv * (sv * (1.0 + uv * (1.0 - sv)))

    padded = jnp.concatenate([dcum_rows, jnp.zeros((LANES - 8, size), full)], axis=0)
    rowi = lax.broadcasted_iota(jnp.int32, (size, LANES), 0)
    dcum = dcum - padded.T + jnp.where(rowi == size - 1, dcum_last, 0.0)
    dlog = exact((rows <= cols).astype(full), dcum)
    dga = dlog * params_ref[0:1, :] * sigmoid(ab + params_ref[1:2, :])
    is_decay = lane < heads
    dga = jnp.where(is_decay, dga, 0.0)
    params_grad_ref[0:8, :] += jnp.sum(dga.reshape(size // 8, 8, LANES), axis=0)
    decay_part = jnp.where(is_decay, dlog * log_decay, 0.0)
    params_grad_ref[8:16, :] += jnp.sum(decay_part.reshape(size // 8, 8, LANES), axis=0)
    dab_ref[...] = jnp.where(is_decay, dga, dbeta * beta * (1.0 - beta)).astype(low)

    width = du.shape[1]
    for first in range(0, width, 512):
        cs = slice(first, first + 512)
        own = du[8 : 8 + size, cs]
        total = taps_ref[3:4, cs] * own
        taps_grad_ref[24:32, cs] += jnp.sum(
            (own * ext[8 : 8 + size, cs]).reshape(size // 8, 8, 512), axis=0
        )
        for lag in (1, 2, 3):
            total += taps_ref[3 - lag : 4 - lag, cs] * meta[:, 5 + lag : 6 + lag] * du[
                8 + lag : 8 + lag + size, cs
            ]
            taps_grad_ref[8 * (3 - lag) : 8 * (4 - lag), cs] += jnp.sum(
                (own * meta[:, lag : lag + 1] * ext[8 - lag : 8 - lag + size, cs]).reshape(
                    size // 8, 8, 512
                ),
                axis=0,
            )
        dpre_ref[:, cs] = total.astype(low)

    @pl.when(step == steps - 1)
    def _():
        edge_meta = edge_meta_ref[...]
        halo = jnp.zeros(halo_ref.shape, full)
        for lag in (1, 2, 3):
            halo += taps_ref[3 - lag : 4 - lag, :] * edge_meta[:, 5 + lag : 6 + lag] * du[
                lag : 8 + lag, :
            ]
        halo_ref[...] = halo
        if scattering:
            moving.end()


def backward_chain(pre, ab, meta, segrow, edge, edge_meta, taps, params, states, inverse,
                   state_in, do, ends, adjoints, heads, key, value, parts=None, sent=0):
    scattering = parts is not None
    moved = [jax.ShapeDtypeStruct((3, parts.shape[1], sent), low)] if scattering else []
    extra = dict(collective_id=6, has_side_effects=True) if scattering else {}
    devices = ends.shape[0] // (heads * key)
    length, width = pre.shape
    blocks = length // BLOCK
    wide = value + key
    once = dict(pipeline_mode=pl.Buffered(1))
    last = blocks - 1
    return pl.pallas_call(
        partial(backward_kernel, heads, key, value, devices, scattering),
        grid=(blocks,),
        in_specs=[
            pl.BlockSpec((BLOCK, width), lambda n: (last - n, 0)),
            pl.BlockSpec((16, width), lambda n: (jnp.maximum((last - n) * (BLOCK // 16) - 1, 0), 0)),
            pl.BlockSpec((BLOCK, LANES), lambda n: (last - n, 0)),
            pl.BlockSpec((BLOCK, LANES), lambda n: (last - n, 0)),
            pl.BlockSpec((8, BLOCK), lambda n: (0, last - n)),
            pl.BlockSpec((8, width), lambda n: (0, 0)),
            pl.BlockSpec((8, LANES), lambda n: (0, 0)),
            pl.BlockSpec(taps.shape, lambda n: (0, 0)),
            pl.BlockSpec((8, LANES), lambda n: (0, 0)),
            pl.BlockSpec((1, heads, key, wide), lambda n: (last - n, 0, 0, 0)),
            pl.BlockSpec((1, heads, BLOCK, BLOCK), lambda n: (last - n, 0, 0, 0)),
            pl.BlockSpec((heads, key, value), lambda n: (0, 0, 0)),
            pl.BlockSpec((BLOCK, heads * value), lambda n: (last - n, 0)),
            pl.BlockSpec(ends.shape, lambda n: (0, 0), **once),
        ]
        + [pl.BlockSpec(**ANY) for _ in (0, *moved)],
        out_specs=[
            pl.BlockSpec((BLOCK, width), lambda n: (last - n, 0)),
            pl.BlockSpec((BLOCK, LANES), lambda n: (last - n, 0)),
            pl.BlockSpec((8, width), lambda n: (0, 0)),
            pl.BlockSpec((32, width), lambda n: (0, 0)),
            pl.BlockSpec((16, LANES), lambda n: (0, 0)),
        ]
        + [pl.BlockSpec(**ANY) for _ in moved],
        out_shape=[
            jax.ShapeDtypeStruct((length, width), low),
            jax.ShapeDtypeStruct((length, LANES), low),
            jax.ShapeDtypeStruct((8, width), full),
            jax.ShapeDtypeStruct((32, width), full),
            jax.ShapeDtypeStruct((16, LANES), full),
        ]
        + moved,
        scratch_shapes=[
            pltpu.VMEM((BLOCK + 8, width), full),
            pltpu.VMEM((BLOCK + 16, width), full),
            pltpu.VMEM((heads, key, value), full),
            pltpu.VMEM((devices * heads * key, value), low),
            pltpu.SemaphoreType.DMA((1,)),
        ]
        + (Scatter.semaphores + Gather.semaphores if scattering else []),
        compiler_params=pltpu.CompilerParams(vmem_limit_bytes=56 * MIB, **extra),
        cost_estimate=FREE,
        name="chain_backward",
    )(pre, pre, ab, meta, segrow, edge, edge_meta, taps, params, states, inverse, state_in, do, ends,
      adjoints, *([parts] if scattering else []))


def segment_tables(doc_lengths, shard, length):
    starts = jnp.cumsum(doc_lengths, dtype=jnp.int32) - doc_lengths
    positions = shard * length + jnp.arange(-16, length + 8, dtype=jnp.int32)
    seg = jnp.sum((starts[None, :] <= positions[:, None]).astype(jnp.int32), axis=1)
    own = seg[16 : 16 + length]

    def lanes(first, count):
        base = seg[first : first + count]
        back = [seg[first - l : first - l + count] == base for l in (1, 2, 3)]
        ahead = [seg[first + l : first + l + count] == base for l in (1, 2, 3)]
        return base, back, ahead

    base, back, ahead = lanes(16, length)
    blocks = own.reshape(-1, BLOCK)
    before = seg[15 : 15 + length : BLOCK]
    alive = (blocks == before[:, None]).reshape(-1)
    to_last = (blocks == blocks[:, -1:]).reshape(-1)
    columns = [base, *back, alive, to_last, *ahead]
    meta = jnp.stack([a.astype(full) for a in columns], axis=1)
    meta = jnp.pad(meta, ((0, 0), (0, LANES - meta.shape[1])))
    base, back, ahead = lanes(8, 8)
    columns = [base, *back, base, base, *ahead]
    edge_meta = jnp.stack([a.astype(full) for a in columns], axis=1)
    edge_meta = jnp.pad(edge_meta, ((0, 0), (0, LANES - edge_meta.shape[1])))
    segrow = jnp.broadcast_to(own.astype(full)[None, :], (8, length))
    return meta, edge_meta, segrow


ROWS = 256
PIECE = 32
HOP = 2
EACH = ROWS // PIECE
AHEAD = 1 + (EACH - 1 + 3 * HOP) // EACH
RING = AHEAD + 1


def exchanged(block, mask):
    return lax.ppermute(block, "seq", [(i, i ^ mask) for i in range(lax.axis_size("seq"))])


def line_scratch(length, width):
    pieces = length // PIECE
    return [
        pltpu.VMEM((RING, ROWS, width), low),
        pltpu.VMEM((length, width), low),
        pltpu.VMEM((length, width), low),
        pltpu.SemaphoreType.DMA((pieces,)),
        pltpu.SemaphoreType.DMA((pieces,)),
        pltpu.SemaphoreType.DMA((pieces,)),
        pltpu.SemaphoreType.DMA((pieces,)),
    ]


def line_sum(step, last, stages, finish, scratch):
    own, from_left, from_right, got_left, got_right, sent_right, sent_left = scratch
    place = lax.axis_index("head")
    length, width = from_left.shape
    blocks, pieces = length // ROWS, length // PIECE
    left_there, right_there = place > 0, place < last

    def rows(piece):
        return pl.ds(pl.multiple_of(piece * PIECE, PIECE), PIECE)

    def hop(piece, rightwards):
        kept, sent, got, to = (
            (from_left, sent_right, got_left, place + 1)
            if rightwards
            else (from_right, sent_left, got_right, place - 1)
        )
        return pltpu.make_async_remote_copy(
            src_ref=kept.at[rows(piece)],
            dst_ref=kept.at[rows(piece)],
            send_sem=sent.at[piece],
            recv_sem=got.at[piece],
            device_id={"head": to},
            device_id_type=MESH,
        )

    def own_piece(piece):
        slot = lax.rem(piece // EACH, RING)
        first = pl.multiple_of(lax.rem(piece, EACH) * PIECE, PIECE)
        return own[slot, pl.ds(first, PIECE), :].astype(full)

    @pl.when(step == 0)
    def _():
        @pl.when(place == 0)
        def _():
            from_left[...] = jnp.zeros_like(from_left)

        @pl.when(place == last)
        def _():
            from_right[...] = jnp.zeros_like(from_right)

    def one(q, carry):
        now = (step - 1) * EACH + q
        for rightwards in (True, False):
            came, more = (left_there, right_there) if rightwards else (right_there, left_there)
            kept = from_left if rightwards else from_right
            piece = now - HOP * (place if rightwards else last - place)

            @pl.when((piece >= 0) & (piece < pieces))
            def _():
                @pl.when(came)
                def _():
                    hop(piece, rightwards).wait_recv()

                @pl.when(more)
                def _():
                    kept[rows(piece), :] = (
                        own_piece(piece) + kept[rows(piece), :].astype(full)
                    ).astype(low)
                    hop(piece, rightwards).start()

        return carry

    done = 0
    for n, stage in enumerate(stages):

        @pl.when(step < blocks)
        def _(n=n, stage=stage):
            value = stage()
            if n == len(stages) - 1:
                own[lax.rem(step, RING)] = value.astype(low)

        until = EACH * (n + 1) // len(stages)
        lax.fori_loop(done, until, one, 0)
        done = until

    @pl.when(step >= AHEAD)
    def _():
        block = step - AHEAD
        span = pl.ds(pl.multiple_of(block * ROWS, ROWS), ROWS)
        total = from_left[span, :].astype(full) + from_right[span, :].astype(full)
        twice = jnp.where(left_there & right_there, 1.0, 0.0)
        finish(total - twice * own[lax.rem(block, RING)].astype(full))

    @pl.when(step == blocks + AHEAD - 1)
    def _():
        def settle(piece, carry):
            @pl.when(right_there)
            def _():
                hop(piece, True).wait_send()

            @pl.when(left_there)
            def _():
                hop(piece, False).wait_send()

            return carry

        lax.fori_loop(0, pieces, settle, 0)


def union(kinds):
    return sorted({mask for kind in kinds for mask in kind.masks})


def line_call(kernel, name, collective, length, width, last, resident, weights, entering, leaving, outs,
              scratch, gathers=(), scatters=(), early=None, masks=()):
    blocks = length // ROWS
    steps = blocks + AHEAD
    cuts, weights = [c for _, c in weights], [a for a, _ in weights]

    def spec(array, stage):
        if stage == "first":
            return pl.BlockSpec((ROWS, array.shape[1]), lambda g: (jnp.minimum(g, blocks - 1), 0))
        if stage == "second":
            return pl.BlockSpec((ROWS, array.shape[1]), lambda g: (jnp.maximum(g - AHEAD, 0), 0))
        rank = len(array.shape)
        return pl.BlockSpec(array.shape, lambda g: (0,) * rank, **ONE)

    in_specs = [spec(a, "all") for a in resident]
    first_one = [] if early is None else [early]
    in_specs += [pl.BlockSpec(**ANY) for _ in (*weights, *first_one, *gathers, *scatters)]
    in_specs += [spec(a, "first") for a in entering] + [spec(a, "second") for a in leaving]
    shapes = [jax.ShapeDtypeStruct(shape, dtype) for shape, dtype, _ in outs]
    out_specs = [
        spec(s, stage) if stage != "all" else pl.BlockSpec(s.shape, lambda g, r=len(s.shape): (0,) * r)
        for s, (_, _, stage) in zip(shapes, outs)
    ]
    moved = [jax.ShapeDtypeStruct((a.shape[0] * NEAR, a.shape[1]), low) for a in (*first_one, *gathers)]
    firsts, scatters = [f for _, f in scatters], [a for a, _ in scatters]
    moved += [jax.ShapeDtypeStruct((3, a.shape[1], a.shape[2] - f), low) for a, f in zip(scatters, firsts)]
    kinds = [Gather] * len(gathers) + [Scatter] * len(scatters)
    whole_first = [pltpu.VMEM(s.shape, low) for s in moved[: len(first_one)]]
    held = [pltpu.VMEM(a.shape, low) for a in weights] + [pltpu.SemaphoreType.DMA((sum(len(c) for c in cuts),))]
    held += whole_first + [s for _ in first_one for s in Gather.semaphores]
    held += [s for kind in kinds for s in kind.semaphores]

    def body(*refs):
        refs = list(refs)

        def take(n):
            head, refs[:] = refs[:n], refs[n:]
            return head

        own_in, heavy = take(len(resident)), take(len(weights))
        ahead, sources = take(len(first_one)), take(len(kinds))
        chunks = take(len(entering) + len(leaving))
        own_out, handed, targets = take(len(outs)), take(len(first_one)), take(len(kinds))
        own_scratch = take(len(scratch) + 7)
        matrices, (sems,) = take(len(weights)), take(1)
        if first_one:
            (table,), signals = take(1), take(3)
            lead = Gather(ahead[0], table, *signals)
            back = pltpu.make_async_copy(table, handed[0], signals[2].at[0])
            matrices.append(table)
        begins = [()] * len(gathers) + [(first,) for first in firsts]
        carried = [
            kind(a, b, *take(len(kind.semaphores)), *first)
            for kind, a, b, first in zip(kinds, sources, targets, begins)
        ]
        step = pl.program_id(0)

        @pl.when(step == 0)
        def _():
            greet(sorted({*masks, *union(kinds + [Gather] * len(first_one))}), last, bool(masks))
            for c in [lead] if first_one else carried:
                c.start()

        waits = []
        for source, target, parts in zip(heavy, matrices, cuts):
            for first, count in parts:
                part = pl.ds(first, count)
                waits.append(
                    pltpu.make_async_copy(source.at[:, part], target.at[:, part], sems.at[len(waits)])
                )

        @pl.when(step == 0)
        def _():
            for copy in waits:
                copy.start()

        def ready(k):
            @pl.when(step == 0)
            def _():
                waits[k].wait()

        if first_one:

            @pl.when(step == 0)
            def _():
                lead.middle()
                lead.late()
                for c in carried:
                    c.start()
                lead.end()
                back.start()

        for at, turn in ((steps - 3, "middle"), (steps - 1, "late")):

            @pl.when(step == at)
            def _(turn=turn):
                for c in carried:
                    if isinstance(c, Gather):
                        getattr(c, turn)()

        kernel(ready, matrices, *own_in, *chunks, *own_out, *own_scratch)

        @pl.when(step == steps - 1)
        def _():
            for c in carried:
                c.end()
            if first_one:
                back.wait()

    return pl.pallas_call(
        body,
        grid=(steps,),
        in_specs=in_specs,
        out_specs=out_specs + [pl.BlockSpec(**ANY) for _ in moved],
        out_shape=shapes + moved,
        scratch_shapes=scratch + line_scratch(length, width) + held,
        compiler_params=pltpu.CompilerParams(
            collective_id=collective, has_side_effects=True, vmem_limit_bytes=60 * MIB
        ),
        cost_estimate=FREE,
        name=name,
    )(*resident, *weights, *first_one, *gathers, *scatters, *entering, *leaving)


def mixer_out_kernel(heads, key, value, last, handed, ready, matrices,
                     head_gain_ref, gain_ref,
                     first_ref, local_ref, through_ref, tokens_ref,
                     y_ref, mixed_ref, gate_ref, state_ref, middle_ref, second_ref, *scratch):
    step = pl.program_id(0)
    weights, ends = matrices
    vals = heads * value

    if handed is not None:
        ready(handed)

    @pl.when(step == 0)
    def _():
        state_ref[...] = jnp.zeros_like(state_ref)

        def one(j, carry):
            for h in range(heads):
                rows = pl.ds(pl.multiple_of((j * heads + h) * key, key), key)
                part = ends[rows, :]
                state_ref[h] = mm(part[:, value:], state_ref[h]) + part[:, :value].astype(full)
            return carry

        lax.fori_loop(0, lax.axis_index("seq"), one, 0)

    def gate():
        ready(0)
        gate_ref[...] = mm(first_ref[...], weights[:, :vals])

    def mix():
        for h in range(heads):
            cols = slice(h * value, (h + 1) * value)
            o = local_ref[:, cols] + mm(through_ref[:, h * key : (h + 1) * key], state_ref[h])
            mixed_ref[:, cols] = o
            s3 = lax.rsqrt(jnp.mean(o * o, axis=-1, keepdims=True) + 1e-05)
            gz = gate_ref[:, cols]
            y_ref[:, cols] = (o * s3 * head_gain_ref[0:1, :] * (gz * sigmoid(gz))).astype(low)

    def project():
        ready(1)
        return mm_nt(y_ref[...], weights[:, vals:])

    def finish(total):
        middle = tokens_ref[...].astype(full) + total
        middle_ref[...] = middle
        scale = lax.rsqrt(jnp.mean(middle * middle, axis=-1, keepdims=True) + 1e-06)
        second_ref[...] = (middle * scale * gain_ref[0:1, :]).astype(low)

    line_sum(step, last, [gate, mix, project], finish, scratch)


def ffn_kernel(last, size, ready, matrices, gain_ref,
               second_ref, cot_ref, middle_ref, cot_late_ref,
               hidden_ref, dgate_ref, dup_ref, partial_ref, dmiddle_ref, dlow_ref, gain_grad_ref,
               fg, fu, *scratch):
    step = pl.program_id(0)
    (weights,) = matrices
    w_gate, w_up, w_down = (slice(n * size, (n + 1) * size) for n in range(3))

    @pl.when(step == 0)
    def _():
        gain_grad_ref[...] = jnp.zeros_like(gain_grad_ref)

    def one():
        ready(0)
        fg[...] = mm(second_ref[...], weights[:, w_gate])

    def two():
        ready(1)
        fu[...] = mm(second_ref[...], weights[:, w_up])

    def three():
        ready(2)
        g, lift = fg[...], fu[...]
        sig = sigmoid(g)
        swish = g * sig
        hidden = (swish * lift).astype(low)
        hidden_ref[...] = hidden
        fg[...] = lift * (sig * (1.0 + g * (1.0 - sig)))
        fu[...] = swish
        partial_ref[...] = mm_nt(hidden, weights[:, w_down]).astype(low)

    def four():
        dhid = mm(cot_ref[...], weights[:, w_down])
        dgate_ref[...] = (dhid * fg[...]).astype(low)
        dup_ref[...] = (dhid * fu[...]).astype(low)

    def five():
        return mm_nt(dgate_ref[...], weights[:, w_gate]) + mm_nt(dup_ref[...], weights[:, w_up])

    def finish(grad):
        middle = middle_ref[...]
        scale = lax.rsqrt(jnp.mean(middle * middle, axis=-1, keepdims=True) + 1e-06)
        norm = middle * scale
        gain_grad_ref[...] += jnp.sum((grad * norm).reshape(ROWS // 8, 8, -1), axis=0)
        weighted = grad * gain_ref[0:1, :]
        dm = cot_late_ref[...].astype(full) + scale * (
            weighted - norm * jnp.mean(weighted * norm, axis=-1, keepdims=True)
        )
        dmiddle_ref[...] = dm
        dlow_ref[...] = dm.astype(low)

    line_sum(step, last, [one, two, three, four, five], finish, scratch)


def input_grad_kernel(last, keys, vals, near, ready, matrices, gain_ref, lines_ref, head_ref,
                      dpre_ref, dgz_ref, dab_ref, tokens_ref,
                      term_ref, gains_ref, part, gain_grad, *scratch):
    step = pl.program_id(0)
    w_in, w_mix = matrices
    wide = 2 * keys + vals
    if near:
        (got, sent, came, got_head, sent_head, came_head), scratch = scratch[:6], scratch[6:]
        place = lax.axis_index("head")

        def across(k):
            return pltpu.make_async_remote_copy(
                src_ref=head_ref, dst_ref=got_head.at[place], send_sem=sent_head.at[k],
                recv_sem=came_head.at[k], device_id={"head": lax.rem(place + k, last + 1)},
                device_id_type=MESH,
            )

    @pl.when(step == 0)
    def _():
        gain_grad[...] = jnp.zeros_like(gain_grad)
        if near:
            for k in range(1, last + 1):
                across(k).start()
            got_head[place] = head_ref[...]

    def one():
        ready(0)
        part[...] = mm_nt(dpre_ref[...], w_in[:, :wide])

    def two():
        ready(1)
        return (
            part[...]
            + mm_nt(dgz_ref[...], w_mix[:, :vals])
            + mm_nt(dab_ref[...], w_in[:, wide:])
        )

    def finish(grad):
        stream = tokens_ref[...].astype(full)
        scale = lax.rsqrt(jnp.mean(stream * stream, axis=-1, keepdims=True) + 1e-06)
        norm = stream * scale
        gain_grad[...] += jnp.sum((grad * norm).reshape(ROWS // 8, 8, -1), axis=0)
        weighted = grad * gain_ref[0:1, :]
        term_ref[...] = (
            scale * (weighted - norm * jnp.mean(weighted * norm, axis=-1, keepdims=True))
        ).astype(low)

    line_sum(step, last, [one, two], finish, scratch)

    @pl.when(step == pl.num_programs(0) - 1)
    def _():
        row = lax.broadcasted_iota(jnp.int32, gain_grad.shape, 0)
        first = jnp.sum(gain_grad[...], axis=0, keepdims=True)
        own = lines_ref[...] + jnp.where(row == 0, first, 0.0)
        if not near:
            gains_ref[...] = own
            return
        for k in range(1, last + 1):
            across(k).wait()
        heads_sum = sum((got_head[k] for k in range(1, last + 1)), start=got_head[0])
        gain_grad[...] = own
        gain_grad[7:8, : head_ref.shape[1]] = jnp.sum(heads_sum, axis=0, keepdims=True)
        me = lax.axis_index("seq")

        def push(mask):
            return pltpu.make_async_remote_copy(
                src_ref=gain_grad, dst_ref=got.at[me], send_sem=sent.at[mask], recv_sem=came.at[mask],
                device_id={"seq": partner(mask)}, device_id_type=MESH,
            )

        for mask in range(1, NEAR):
            push(mask).start()
        got[me] = gain_grad[...]
        for mask in range(1, NEAR):
            push(mask).wait()
        gains_ref[...] = sum((got[k] for k in range(1, NEAR)), start=got[0])


def input_kernel(wide, gathering, gain_ref, *refs):
    rows = 256
    if gathering:
        heavy, (before_hbm, tokens_hbm), refs = refs[:9], refs[9:11], refs[11:]
        small_ref, sources = heavy[3], heavy[4:]
    else:
        (shard_ref, before_hbm, tokens_hbm), refs = refs[:3], refs[3:]
    first_out, pre_ref, ab_ref, edge_ref, whole_ref = refs[:5]
    refs = refs[5:]
    if gathering:
        (mix_out, ffn_out), refs = refs[:2], refs[2:]
    weights, total, tokens_ref, before, first_ref, edge_total, home, *refs = refs
    length, width = tokens_ref.shape
    half = width // 4
    back = pltpu.make_async_copy(weights, whole_ref, home.at[0])
    handing = [pltpu.make_async_copy(first_ref, first_out, home.at[8])]
    here = pltpu.make_async_copy(tokens_hbm, tokens_ref, home.at[1])
    here.start()
    if gathering:
        shard, *buffers = refs[:6]
        mix_ref, ffn_ref, *sems = refs[6:]
        handing += [
            pltpu.make_async_copy(mix_ref, mix_out, home.at[9]),
            pltpu.make_async_copy(ffn_ref, ffn_out, home.at[10]),
        ]
        pairs = [(before_hbm, before), *zip(sources, buffers)]
        copies = [pltpu.make_async_copy(a, b, home.at[2 + n]) for n, (a, b) in enumerate(pairs)]
        for copy in copies:
            copy.start()
        first = 0
        for ref in heavy[:3]:
            shard[:, first : first + ref.shape[1]] = ref[...].astype(low)
            first += ref.shape[1]
        shard[:, first:] = small_ref[...].astype(low)
        greet(Gather.masks)
        moving = Gather(shard, weights, *sems)
        moving.start()
    else:
        copies = [
            pltpu.make_async_copy(shard_ref, weights, home.at[2]),
            pltpu.make_async_copy(before_hbm, before, home.at[3]),
        ]
        for copy in copies:
            copy.start()

    def normed(block):
        x = block.astype(full)
        return (x * lax.rsqrt(jnp.mean(x * x, axis=-1, keepdims=True) + 1e-06) * gain_ref[0:1, :]).astype(low)

    def norm(n, carry):
        span = pl.ds(pl.multiple_of(n * rows, rows), rows)
        first_ref[span, :] = normed(tokens_ref[span, :])
        return carry

    here.wait()
    lax.fori_loop(0, length // rows, norm, 0)
    handing[0].start()

    def add(chip, fresh, done):
        start = pl.multiple_of(chip * half, half)

        def one(n, carry):
            span = pl.ds(pl.multiple_of(n * rows, rows), rows)
            part = mm(first_ref[span, pl.ds(start, half)], weights[pl.ds(start, half), :])
            if not fresh:
                part += total[span, :]
            if done:
                pre_ref[span, :] = part[:, :wide].astype(low)
                ab_ref[span, :] = part[:, wide:]
            else:
                total[span, :] = part
            return carry

        lax.fori_loop(0, length // rows, one, 0)

    def edge_add(chip, fresh):
        start = pl.multiple_of(chip * half, half)
        part = mm(before[:, pl.ds(start, half)], weights[pl.ds(start, half), :wide])
        edge_total[...] = part if fresh else edge_total[...] + part

    if gathering:
        moving.local().wait()
        moving.traded((4,))
        add(partner(0) // 2, True, False)
        for copy in copies:
            copy.wait()
        gate, out, up, lift, down = buffers
        vals, size = gate.shape[1], up.shape[1]
        mix_ref[:, :vals] = gate[...].astype(low)
        for first in range(0, vals, 128):
            mix_ref[:, vals + first : vals + first + 128] = out[first : first + 128, :].T.astype(low)
        ffn_ref[:, :size] = up[...].astype(low)
        ffn_ref[:, size : 2 * size] = lift[...].astype(low)
        for first in range(0, size, 128):
            cols = slice(2 * size + first, 2 * size + first + 128)
            ffn_ref[:, cols] = down[first : first + 128, :].T.astype(low)
        for copy in handing[1:]:
            copy.start()
        moving.middle()
        before[...] = normed(before[...])
        edge_add(partner(0) // 2, True)
        moving.traded((5, 6))
        add(partner(2) // 2, False, False)
        moving.late()
        add(partner(4) // 2, False, False)
        edge_add(partner(2) // 2, False)
        edge_add(partner(4) // 2, False)
        moving.traded((7,))
        back.start()
        add(partner(6) // 2, False, True)
        edge_add(partner(6) // 2, False)
    else:
        for copy in copies:
            copy.wait()
        back.start()
        for chip in range(4):
            add(chip, chip == 0, chip == 3)
        before[...] = normed(before[...])
        for chip in range(4):
            edge_add(chip, chip == 0)
    edge_ref[...] = edge_total[...].astype(low)
    if gathering:
        moving.settle()
    for copy in handing:
        copy.wait()
    back.wait()


def input_projection(tokens, before, gain, heavy, wide):
    length, width = tokens.shape
    gathering = len(heavy) > 1
    here = pl.BlockSpec(memory_space=pltpu.VMEM)
    away = pl.BlockSpec(**ANY)
    if gathering:
        operands = [*heavy, before, tokens]
        in_specs = [here] * 4 + [away] * 7
        rows = heavy[0].shape[0]
        columns = sum(a.shape[1] for a in heavy[:4])
        shards_out = [
            jax.ShapeDtypeStruct((rows, 2 * heavy[4].shape[1]), low),
            jax.ShapeDtypeStruct((rows, 3 * heavy[6].shape[1]), low),
        ]
        more = [pltpu.VMEM((rows, columns), low)] + [pltpu.VMEM(a.shape, full) for a in heavy[4:]]
        more += [pltpu.VMEM(s.shape, low) for s in shards_out] + Gather.semaphores
        params = dict(collective_id=4, has_side_effects=True)
    else:
        operands = [*heavy, before, tokens]
        in_specs = [away] * 3
        columns = heavy[0].shape[1]
        shards_out, more, params = [], [], {}
    return pl.pallas_call(
        partial(input_kernel, wide, gathering),
        in_specs=[here] + in_specs,
        out_specs=[away] + [here] * 3 + [away] * (1 + len(shards_out)),
        out_shape=[
            jax.ShapeDtypeStruct((length, width), low),
            jax.ShapeDtypeStruct((length, wide), low),
            jax.ShapeDtypeStruct((length, columns - wide), full),
            jax.ShapeDtypeStruct((16, wide), low),
            jax.ShapeDtypeStruct((width, columns), low),
        ]
        + shards_out,
        scratch_shapes=[
            pltpu.VMEM((width, columns), low),
            pltpu.VMEM((length, columns), full),
            pltpu.VMEM((length, width), low),
            pltpu.VMEM((16, width), low),
            pltpu.VMEM((length, width), low),
            pltpu.VMEM((16, wide), full),
            pltpu.SemaphoreType.DMA((11,)),
        ]
        + more,
        compiler_params=pltpu.CompilerParams(vmem_limit_bytes=60 * MIB, **params),
        cost_estimate=FREE,
        name="input_projection",
    )(gain[None, :], *operands)


def weight_kernel(groups, adding, counts, place_ref, *refs):
    lefts, rights = refs[: counts[0]], refs[counts[0] : counts[0] + counts[1]]
    rest = refs[counts[0] + counts[1] :]
    parts = []
    n = 0
    for g, many in enumerate(groups):
        left = lefts[g][...]
        for _ in range(many):
            parts.append(mm_tn(left, rights[n][...]))
            n += 1
    first = 0
    for part in parts:
        cols = slice(first, first + part.shape[1])
        first += part.shape[1]
        if adding:
            part += rest[0][0, :, cols].astype(full)
        rest[-1][0, :, cols] = part.astype(low)


def weight_call(place, pairs, odd, count, stride, added=None, width=256):
    lefts = [a for a, _ in pairs]
    rights = [b for _, bs in pairs for b in bs]
    length = lefts[0].shape[0]
    columns = sum(b.shape[1] for b in rights)

    def pick(k, place_ref):
        return (0, jnp.bitwise_xor(place_ref[0], stride * k + odd))

    in_specs = [pl.BlockSpec((length, width), pick) for _ in lefts]
    in_specs += [pl.BlockSpec(b.shape, lambda k, p: (0, 0), **ONE) for b in rights]
    if added is not None:
        in_specs += [pl.BlockSpec((1, width, columns), lambda k, p: (k, 0, 0))]
    out_specs = [pl.BlockSpec((1, width, columns), lambda k, p: (k, 0, 0))]
    out_shape = [jax.ShapeDtypeStruct((count, width, columns), low)]
    return pl.pallas_call(
        partial(
            weight_kernel, [len(bs) for _, bs in pairs], added is not None, (len(lefts), len(rights))
        ),
        grid_spec=pltpu.PrefetchScalarGridSpec(
            num_scalar_prefetch=1, grid=(count,), in_specs=in_specs, out_specs=out_specs
        ),
        out_shape=out_shape,
        compiler_params=pltpu.CompilerParams(vmem_limit_bytes=56 * MIB),
        cost_estimate=FREE,
        name="weight_grads",
    )(place, *lefts, *rights, *(() if added is None else (added,)))


def pair_sums(place, pairs):
    (away,) = weight_call(place, pairs, 1, NEAR // 2, 2)
    (sums,) = weight_call(place, pairs, 0, NEAR // 2, 2, exchanged(away, 1))
    return sums


def plain_sums(place, pairs):
    width = pairs[0][0].shape[1]
    (grads,) = weight_call(jnp.zeros_like(place), pairs, 0, width // 256, 1)
    return lax.psum_scatter(grads.reshape(width, -1), "seq", scatter_dimension=0, tiled=True).astype(full)


def final_kernel(heads, keys, vals, size, middle_ref, sum_ref, dmiddle_ref, term_ref, in_own, in_got,
                 up_own, up_got, up_late, down_own, down_got, gate_own, gate_got, out_own, out_got, gains_ref,
                 tq_ref, tk_ref, tv_ref, result_ref, dtokens_ref, q_ref, k_ref, v_ref, a_ref, b_ref, up_ref, lift_ref, down_ref,
                 gate_ref, out_ref):
    def total(own, got, cols=slice(None)):
        return own[0, :, cols].astype(full) + sum(got[k, :, cols].astype(full) for k in range(3))

    @pl.when(pl.program_id(0) < 8)
    def _():
        result_ref[...] = (middle_ref[...] + sum_ref[...].astype(full)).astype(low)
        dtokens_ref[...] = dmiddle_ref[...] + term_ref[...].astype(full)
        wide = 2 * keys + vals
        q_ref[...] = total(in_own, in_got, slice(0, keys))
        k_ref[...] = total(in_own, in_got, slice(keys, 2 * keys))
        v_ref[...] = total(in_own, in_got, slice(2 * keys, wide))
        small = total(in_own, in_got, slice(wide, wide + LANES))
        a_ref[...] = small[:, :heads]
        b_ref[...] = small[:, heads : 2 * heads]
        split = up_got.shape[2]
        up_ref[...] = total(up_own, up_got, slice(0, size))
        lift_ref[:, : split - size] = total(up_own, up_got, slice(size, split))
        late = sum(up_late[k].astype(full) for k in range(3))
        lift_ref[:, split - size :] = up_own[0, :, split:].astype(full) + late
        gate_ref[...] = total(gate_own, gate_got)
        out_ref[...] = total(out_own, out_got).T

    @pl.when(pl.program_id(0) == 0)
    def _():
        tq_ref[...] = gains_ref[2:6, :keys]
        tk_ref[...] = gains_ref[2:6, keys : 2 * keys]
        tv_ref[...] = gains_ref[2:6, 2 * keys :]

    down_ref[...] = total(down_own, down_got).T


def final_sums(middle, narrow_sum, dmiddle, term, sums_in, got_in, sums_up, got_up, got_late, sums_rest, got_rest, gains, heads,
               keys, vals, size):
    length, width = dmiddle.shape
    rows = sums_in.shape[1]
    eight = lambda n: jnp.minimum(n, 7)
    many, few = length // 8, rows // 8

    def both(array, block, index):
        return [pl.BlockSpec((1,) + block, index), pl.BlockSpec((3,) + block, index)]

    wide_in = sums_in.shape[2]
    at_gate, at_out = size // LANES, (size + vals) // LANES
    tall = pl.BlockSpec((many, width), lambda n: (eight(n), 0))
    in_specs = [tall] * 4
    in_specs += both(sums_in, (few, wide_in), lambda n: (0, eight(n), 0))
    in_specs += [
        pl.BlockSpec((count, few, a.shape[2]), lambda n: (0, eight(n), 0))
        for count, a in ((1, sums_up), (3, got_up), (3, got_late))
    ]
    in_specs += both(sums_rest, (rows, LANES), lambda n: (0, 0, n))
    in_specs += both(sums_rest, (rows, LANES), lambda n: (0, 0, at_gate + eight(n)))
    in_specs += both(sums_rest, (rows, LANES), lambda n: (0, 0, at_out + eight(n)))
    once = lambda *shape: pl.BlockSpec(shape, lambda n: (0, 0))
    in_specs += [once(*gains.shape)]
    byrow = lambda columns: pl.BlockSpec((few, columns), lambda n: (eight(n), 0))
    outs = [
        ((4, keys), full), ((4, keys), full), ((4, vals), full), ((length, width), low), ((length, width), full), ((rows, keys), full), ((rows, keys), full),
        ((rows, vals), full), ((rows, heads), full), ((rows, heads), full), ((rows, size), full),
        ((rows, size), full), ((size, rows), full), ((rows, vals), full), ((vals, rows), full),
    ]
    return pl.pallas_call(
        partial(final_kernel, heads, keys, vals, size),
        grid=(size // LANES,),
        in_specs=in_specs,
        out_specs=[
            once(4, keys), once(4, keys), once(4, vals), tall, tall,
            byrow(keys), byrow(keys), byrow(vals), byrow(heads), byrow(heads), byrow(size), byrow(size),
            pl.BlockSpec((LANES, rows), lambda n: (n, 0)),
            pl.BlockSpec((rows, LANES), lambda n: (0, eight(n))),
            pl.BlockSpec((LANES, rows), lambda n: (eight(n), 0)),
        ],
        out_shape=[jax.ShapeDtypeStruct(shape, dtype) for shape, dtype in outs],
        compiler_params=pltpu.CompilerParams(vmem_limit_bytes=48 * MIB),
        cost_estimate=FREE,
        name="final_sums",
    )(middle, narrow_sum, dmiddle, term, sums_in, got_in, sums_up, got_up, got_late, sums_rest, got_rest, sums_rest,
      got_rest, sums_rest, got_rest, gains)


def small_sums(part):
    return lax.psum(part, "seq")


def passed_along(block, axis, distance):
    devices = range(lax.axis_size(axis))
    route = [(i - distance, i) for i in devices if i - distance in devices]
    return lax.ppermute(block, axis, route)


def shards(
    tokens,
    doc_lengths,
    mixer_gain,
    query_weight,
    key_weight,
    value_weight,
    gate_weight,
    alpha_weight,
    beta_weight,
    decay_log,
    decay_bias,
    query_taps,
    key_taps,
    value_taps,
    head_gain,
    output_weight,
    ffn_gain,
    ffn_gate,
    ffn_up,
    ffn_down,
    cotangent,
):
    length, width = tokens.shape
    heads = decay_log.shape[0]
    key = query_weight.shape[1] // heads
    value = head_gain.shape[0]
    keys, vals = heads * key, heads * value
    wide = 2 * keys + vals
    size = ffn_gate.shape[1]
    last = lax.axis_size("head") - 1
    near = lax.axis_size("seq") == NEAR
    shard = lax.axis_index("seq")
    place = jnp.full((1,), shard, jnp.int32)

    small = jnp.concatenate(
        [alpha_weight, beta_weight, jnp.zeros((alpha_weight.shape[0], LANES - 2 * heads), full)], axis=1
    )
    taps = jnp.concatenate([query_taps, key_taps, value_taps], axis=1)
    params = jnp.stack([-jnp.exp(decay_log), decay_bias])
    params = jnp.pad(params, ((0, 6), (0, LANES - heads)))
    gain = head_gain[None, :]

    if near:
        heavy = [query_weight, key_weight, value_weight, small, gate_weight, output_weight]
        heavy += [ffn_gate, ffn_up, ffn_down]
    else:
        shard_in = jnp.concatenate([query_weight, key_weight, value_weight, small], axis=1)
        heavy = [lax.all_gather(shard_in.astype(low), "seq", axis=0, tiled=True)]
    meta, edge_meta, segrow = segment_tables(doc_lengths, shard, length)
    first_in, pre, ab, edge, w_in, *laid = input_projection(
        tokens, passed_along(tokens[length - 16 :], "seq", 1), mixer_gain, heavy, wide
    )
    if near:
        shard_mix, shard_ffn = laid
    else:
        shard_mix = jnp.concatenate([gate_weight, output_weight.T], axis=1).astype(low)
        shard_ffn = jnp.concatenate([ffn_gate, ffn_up, ffn_down.T], axis=1).astype(low)
    edge = edge[8:]
    local, through, states, inverse, end, *moved = forward_chain(
        pre, ab, meta, segrow, edge, taps, params, heads, key, value, shard_mix if near else None
    )
    end = end.reshape(keys, value + key)
    if near:
        w_mix = moved[0]
        held, moving = [(w_mix, [(0, vals), (vals, vals)])], dict(early=end, gathers=[shard_ffn])
    else:
        w_mix = lax.all_gather(shard_mix, "seq", axis=0, tiled=True)
        ends = lax.all_gather(end, "seq", axis=0, tiled=True)
        held, moving = [(w_mix, [(0, vals), (vals, vals)]), (ends, [(0, ends.shape[1])])], {}
    mix_out, mixed, gate_pre, state_in, middle, second_in, *moved = line_call(
        partial(mixer_out_kernel, heads, key, value, last, None if near else 2), "mixer_out", 0, length, width, last,
        [gain, ffn_gain[None, :]], held, [first_in, local, through], [tokens],
        [((length, vals), low, "first"), ((length, vals), full, "first"),
         ((length, vals), full, "first"), ((heads, key, value), full, "all"),
         ((length, width), full, "second"), ((length, width), low, "second")],
        [], **moving,
    )
    if near:
        ends, w_ffn = moved
    else:
        w_ffn = lax.all_gather(shard_ffn, "seq", axis=0, tiled=True)
    hidden, gate_grad, lift_grad, narrow_part, middle_grad, middle_low, ffn_gain_part = line_call(
        partial(ffn_kernel, last, size), "ffn", 1, length, width, last,
        [ffn_gain[None, :]], [(w_ffn, [(n * size, size) for n in range(3)])], [second_in, cotangent], [middle, cotangent],
        [((length, size), low, "first")] * 3
        + [((length, width), low, "first"), ((length, width), full, "second"),
           ((length, width), low, "second"), ((8, width), full, "all")],
        [pltpu.VMEM((ROWS, size), full)] * 2,
    )
    narrow_sum = lax.psum_scatter(narrow_part, "head", scatter_dimension=0, tiled=True)
    gate_pgrad, mixed_grad, head_gain_part, adjoint = gate_back(
        middle_low, w_mix, mixed, gate_pre, gain, through, heads, key, value
    )
    if not near:
        head_gain_part = lax.psum(head_gain_part, "head")
    adjoint = adjoint.astype(low).reshape(keys, value)
    if not near:
        adjoint = lax.all_gather(adjoint, "seq", axis=0, tiled=True)
    split = 17 * LANES
    pairs_up = [(second_in, [gate_grad, lift_grad])]
    pairs_rest = [(cotangent, [hidden]), (first_in, [gate_pgrad]), (middle_low, [mix_out])]
    sums_up = pair_sums(place, pairs_up) if near else None
    sums_rest = pair_sums(place, pairs_rest) if near else None
    pre_grad, ab_grad, halo, taps_part, params_part, *moved = backward_chain(
        pre, ab, meta, segrow, edge, edge_meta, taps, params, states, inverse, state_in,
        mixed_grad, ends, adjoint, heads, key, value, sums_up, split,
    )
    got_up = moved
    if near:
        narrow_sum, halo = lax.optimization_barrier((narrow_sum, halo))
    narrow_sum = lax.all_gather(narrow_sum, "head", axis=0, tiled=True)
    halo = passed_along(halo, "seq", -1)
    tail = pre_grad[length - 8 :].astype(full) + halo
    pre_grad = lax.dynamic_update_slice(pre_grad, tail.astype(low), (length - 8, 0))
    pairs_in = [(first_in, [pre_grad, ab_grad])]
    sums_in = pair_sums(place, pairs_in) if near else None
    params_part = jnp.sum(params_part.reshape(2, 8, LANES), axis=1).reshape(1, -1)
    lines = jnp.concatenate(
        [
            jnp.zeros((1, width), full),
            jnp.sum(ffn_gain_part, axis=0, keepdims=True),
            jnp.sum(taps_part.reshape(4, 8, -1), axis=1),
            jnp.pad(params_part, ((0, 0), (0, width - params_part.shape[1]))),
            jnp.zeros((1, width), full)
            if near
            else jnp.pad(jnp.sum(head_gain_part, axis=0)[None], ((0, 0), (0, width - value))),
        ],
        axis=0,
    )
    term, gains, *moved = line_call(
        partial(input_grad_kernel, last, keys, vals, near), "input_grad", 2, length, width, last,
        [mixer_gain[None, :], lines, head_gain_part], [(w_in, [(0, w_in.shape[1])]), (w_mix, [(0, vals)])],
        [pre_grad, gate_pgrad, ab_grad], [tokens],
        [((length, width), low, "second"), ((8, width), full, "all")],
        [pltpu.VMEM((ROWS, width), full), pltpu.VMEM((8, width), full)]
        + ([pltpu.VMEM((NEAR, 8, width), full), *[pltpu.SemaphoreType.DMA((NEAR,))] * 2] if near else [])
        + ([pltpu.VMEM((last + 1, 8, value), full), *[pltpu.SemaphoreType.DMA((last + 1,))] * 2] if near else []),
        scatters=[(sums_rest, 0), (sums_in, 0), (sums_up, split)] if near else [], masks=range(1, NEAR) if near else (),
    )
    sums = gains if near else small_sums(gains)
    if near:
        (tq_grad, tk_grad, tv_grad, result, tokens_grad, query_grad, key_grad, value_grad, alpha_grad, beta_grad, up_grad, lift_grad,
         down_grad, gate_grad, out_grad) = final_sums(
            middle, narrow_sum, middle_grad, term, sums_in, moved[1], sums_up, got_up[0], moved[2], sums_rest, moved[0],
            gains, heads, keys, vals, size,
        )
    else:
        up, rest, into = (plain_sums(place, pairs) for pairs in (pairs_up, pairs_rest, pairs_in))
        tokens_grad = middle_grad + term.astype(full)
        query_grad, key_grad, value_grad = into[:, :keys], into[:, keys : 2 * keys], into[:, 2 * keys : wide]
        alpha_grad, beta_grad = into[:, wide : wide + heads], into[:, wide + heads : wide + 2 * heads]
        up_grad, lift_grad = up[:, :size], up[:, size:]
        down_grad, gate_grad, out_grad = (
            rest[:, :size].T, rest[:, size : size + vals], rest[:, size + vals :].T
        )
        result = (middle + narrow_sum.astype(full)).astype(low)
        taps_grad = sums[2:6]
        tq_grad, tk_grad, tv_grad = (
            taps_grad[:, :keys], taps_grad[:, keys : 2 * keys], taps_grad[:, 2 * keys :]
        )
    return (
        result,
        tokens_grad,
        sums[0],
        query_grad,
        key_grad,
        value_grad,
        gate_grad,
        alpha_grad,
        beta_grad,
        sums[6, LANES : LANES + heads],
        sums[6, :heads],
        tq_grad,
        tk_grad,
        tv_grad,
        sums[7, :value],
        out_grad,
        sums[1],
        up_grad,
        lift_grad,
        down_grad,
    )


def solution(mesh):
    rows, both = P("seq", None), P("seq", "head")
    in_specs = (
        rows, P(), P(), both, both, both, both, both, both, P("head"), P("head"),
        P(None, "head"), P(None, "head"), P(None, "head"), P(), P("head", "seq"), P(),
        both, both, P("head", "seq"), rows,
    )
    out_specs = (
        rows, rows, P(), both, both, both, both, both, both, P("head"), P("head"),
        P(None, "head"), P(None, "head"), P(None, "head"), P(), P("head", "seq"), P(),
        both, both, P("head", "seq"),
    )
    return jax.shard_map(shards, mesh=mesh, in_specs=in_specs, out_specs=out_specs, check_vma=False)
```
